32 devices in a mesh: dp: 8 (over y, x, core), mp: 4 (over z).
Axes of the slice: x: 2, y: 2, z: 4, core: 2. Of those that a mesh axis runs over, the one named last changes fastest.
Arguments:
- tokens: bfloat16 [128, 542, 768], P(('dp', 'mp')), may hold values from -6 to 6
- cotangent: bfloat16 [128, 542, 768], P(('dp', 'mp')), may hold values from -6 to 6
- kept_index: int32 [128, 268], P(('dp', 'mp')), may hold values from 0 to 541, as said below
- attention_weights: float32 [768, 3072], P(None, ('dp', 'mp')), may hold values from -0.4082483 to 0.4082483
- attention_first: float32 [768, 3072], P(None, ('dp', 'mp')), may hold values from -224 to 224
- attention_second: float32 [768, 3072], P(None, ('dp', 'mp')), may hold values from 1372.16 to 5488.64
- attention_average: float32 [768, 3072], P(None, ('dp', 'mp')), may hold values from -0.4082483 to 0.4082483
- feedforward_weights: float32 [2, 768, 3072], P(None, 'dp', 'mp'), may hold values from -0.14433757 to 0.14433757
- feedforward_first: float32 [2, 768, 3072], P(None, 'dp', 'mp'), may hold values from -448 to 448
- feedforward_second: float32 [2, 768, 3072], P(None, 'dp', 'mp'), may hold values from 5488.64 to 21954.56
- feedforward_average: float32 [2, 768, 3072], P(None, 'dp', 'mp'), may hold values from -0.14433757 to 0.14433757
- vector_weights: float32 [13, 768], replicated, may hold values from -1.2 to 1.3
- vector_first: float32 [13, 768], replicated, may hold values from -1024 to 1024
- vector_second: float32 [13, 768], replicated, may hold values from 34304 to 137216
- vector_average: float32 [13, 768], replicated, may hold values from -1.2 to 1.3
Outputs:
- block_output: bfloat16 [128, 542, 768], P(('dp', 'mp'))
- input_gradient: float32 [128, 542, 768], P(('dp', 'mp'))
- attention_gradient: float32 [768, 3072], P(None, ('dp', 'mp'))
- attention_first_new: float32 [768, 3072], P(None, ('dp', 'mp'))
- attention_second_new: float32 [768, 3072], P(None, ('dp', 'mp'))
- attention_weights_new: float32 [768, 3072], P(None, ('dp', 'mp'))
- attention_average_new: float32 [768, 3072], P(None, ('dp', 'mp'))
- attention_copy: bfloat16 [768, 3072], P(None, ('dp', 'mp'))
- feedforward_gradient: float32 [2, 768, 3072], P(None, 'dp', 'mp')
- feedforward_first_new: float32 [2, 768, 3072], P(None, 'dp', 'mp')
- feedforward_second_new: float32 [2, 768, 3072], P(None, 'dp', 'mp')
- feedforward_weights_new: float32 [2, 768, 3072], P(None, 'dp', 'mp')
- feedforward_average_new: float32 [2, 768, 3072], P(None, 'dp', 'mp')
- feedforward_copy: bfloat16 [2, 768, 3072], P(None, 'dp', 'mp')
- vector_gradient: float32 [13, 768], replicated
- vector_first_new: float32 [13, 768], replicated
- vector_second_new: float32 [13, 768], replicated
- vector_weights_new: float32 [13, 768], replicated
- vector_average_new: float32 [13, 768], replicated
- query_bias_gradient: float32 [768], replicated
The draws below stay inside these ranges and needn't reach their ends.
Inputs may be any that keep to these rules, and one draw needn't show every extreme that they name: `kept_index`: for each image and each of its six crops in order, 197//2 (global crops) or 37//2 (local crops) distinct increasing positions inside that crop; the crop's first and last positions are always among them.
All inputs are finite; a program needn't handle non-finite values.
Results may differ from the reference program's by a relative error of at most 0.0098.
The reference program's roundings to bfloat16 on the way count: a program that leaves them out, or rounds other values in their place, can miss the bound.
Values may be sent and summed in bfloat16 or wider, within the bound.
A program may use at most 192 MiB of HBM per device.

```python
import math
from functools import partial
import jax
import jax.numpy as jnp
import numpy as np
from jax import lax

D = 768
H = 12
HD = 64
FF = 3072
LG = 197
LL = 37
TOK_IMG = 542
IMAGES = 128
KEPT_ALL = 34304
NVEC = 13


def bounded(key, shape):
    return jnp.clip(jax.random.normal(key, shape, jnp.float32), -4.0, 4.0)


def attention_law(key):
    noise = bounded(key, (D, 4 * D))
    column = jnp.arange(4 * D)
    factor = jnp.where(column < 3 * D, D ** (-0.5), (D // 8) ** (-0.5))
    return (noise * factor[None, :]).astype(jnp.float32)


def feedforward_law(key):
    noise = bounded(key, (2, D, FF))
    factor = jnp.array([D ** (-0.5), FF ** (-0.5)], jnp.float32)
    return (noise * factor[:, None, None]).astype(jnp.float32)


def vector_law(key):
    gains = np.array([1.0 if row in (0, 6) else 0.0 for row in range(NVEC)], np.float32)
    spreads = np.array([0.0, 0.2, D ** (-0.5), 0.3, 0.3, 0.3, 0.0, 0.2, 0.3] + [0.2] * (NVEC - 9), np.float32)
    uniform = jax.random.uniform(jax.random.fold_in(key, 1), (NVEC, D), jnp.float32, -1.0, 1.0)
    noise = bounded(jax.random.fold_in(key, 2), (NVEC, D))
    value = jnp.asarray(gains)[:, None] * (1.0 + 0.3 * uniform) + jnp.asarray(spreads)[:, None] * noise
    return value.astype(jnp.float32)


def draw_attention_weights(key, part):
    return attention_law(jax.random.fold_in(key, 11))


def draw_attention_average(key, part):
    return attention_law(jax.random.fold_in(key, 12))


def draw_feedforward_weights(key, part):
    return feedforward_law(jax.random.fold_in(key, 21))


def draw_feedforward_average(key, part):
    return feedforward_law(jax.random.fold_in(key, 22))


def draw_vector_weights(key, part):
    return vector_law(jax.random.fold_in(key, 31))


def draw_vector_average(key, part):
    return vector_law(jax.random.fold_in(key, 32))


def draw_kept_index(key, part):

    def one_image(image_key):
        pieces = []
        offset = 0
        for crop in range(6):
            span = LG if crop < 2 else LL
            keep = span // 2
            order = jax.random.permutation(jax.random.fold_in(image_key, crop), span - 2).astype(jnp.int32) + 1
            chosen = jnp.concatenate([jnp.zeros((1,), jnp.int32), order[:keep - 2], jnp.full((1,), span - 1, jnp.int32)])
            pieces.append(jnp.sort(chosen) + offset)
            offset = offset + span
        return jnp.concatenate(pieces)
    image_keys = jax.random.split(jax.random.fold_in(key, 41), IMAGES)
    return jax.vmap(one_image)(image_keys).astype(jnp.int32)


def block_scale(stream_key, extent, cuts, least, largest):
    factor_of = 1.0
    for position, blocks in cuts:
        draws = jax.random.uniform(jax.random.fold_in(jax.random.fold_in(stream_key, 6), position), (blocks,), jnp.float32, least / len(cuts), largest / len(cuts))
        factor_of = factor_of * jnp.repeat(jnp.exp(draws), extent[position] // blocks).reshape((-1,) + (1,) * (len(extent) - 1 - position))
    return factor_of


def normal_values(rng, extent, scale, limit, shards=(), kind=jnp.bfloat16):
    values = scale * jax.random.normal(rng, extent, jnp.float32)
    if shards:
        values = values * block_scale(rng, extent, shards, -0.22, 0.18)
    return jnp.clip(values, -limit, limit).astype(kind)


def setup_inputs(seed: int = 0) -> dict:
    arg_keys = jax.random.split(jax.random.key(seed), 16)
    return {
        "tokens": normal_values(arg_keys[0], (IMAGES, TOK_IMG, D), 1.0, 6.0, ((0, 32),)),
        "cotangent": normal_values(arg_keys[1], (IMAGES, TOK_IMG, D), 1.0, 6.0, ((0, 32),)),
        "kept_index": draw_kept_index(jax.random.fold_in(arg_keys[15], 71), 0),
        "attention_weights": draw_attention_weights(jax.random.fold_in(arg_keys[15], 71), 0),
        "attention_first": normal_values(arg_keys[4], (D, 4 * D), (0.2 * KEPT_ALL ** 0.5), 224.0, ((1, 32),), jnp.float32),
        "attention_second": jnp.clip(jnp.exp(math.log(5488.64) - 1.3862944 * jax.random.uniform(arg_keys[5], (D, 4 * D), jnp.float32) ** block_scale(arg_keys[5], (D, 4 * D), ((1, 32),), -0.2, 0.2)), 1372.16, 5488.64),
        "attention_average": draw_attention_average(jax.random.fold_in(arg_keys[15], 71), 0),
        "feedforward_weights": draw_feedforward_weights(jax.random.fold_in(arg_keys[15], 71), 0),
        "feedforward_first": normal_values(arg_keys[8], (2, D, FF), (0.4 * KEPT_ALL ** 0.5), 448.0, ((1, 8), (2, 4)), jnp.float32),
        "feedforward_second": jnp.clip(jnp.exp(math.log(21954.56) - 1.3862944 * jax.random.uniform(arg_keys[9], (2, D, FF), jnp.float32) ** block_scale(arg_keys[9], (2, D, FF), ((1, 8), (2, 4)), -0.2, 0.2)), 5488.64, 21954.56),
        "feedforward_average": draw_feedforward_average(jax.random.fold_in(arg_keys[15], 71), 0),
        "vector_weights": draw_vector_weights(jax.random.fold_in(arg_keys[15], 71), 0),
        "vector_first": normal_values(arg_keys[12], (NVEC, D), (1.0 * KEPT_ALL ** 0.5), 1024.0, (), jnp.float32),
        "vector_second": jnp.clip(jnp.exp(jax.random.uniform(arg_keys[13], (NVEC, D), jnp.float32, math.log(34304.0), math.log(137216.0))), 34304.0, 137216.0),
        "vector_average": draw_vector_average(jax.random.fold_in(arg_keys[15], 71), 0),
    }


HIGHEST = lax.Precision.HIGHEST

@jax.custom_vjp
def low(v):
    return lax.optimization_barrier(v.astype(jnp.bfloat16)).astype(jnp.float32)

@jax.custom_vjp
def low_back(v):
    return v

def low_keep(v):
    return (low(v), None)

def low_pass(kept, grad):
    return (grad,)

def back_keep(v):
    return (v, None)

def back_low(kept, grad):
    return (low(grad),)
low.defvjp(low_keep, low_pass)
low_back.defvjp(back_keep, back_low)

def crop_labels():
    labels = [0] * (LG // 2) + [1] * (LG // 2)
    for crop in range(2, 6):
        labels = labels + [crop] * (LL // 2)
    return np.array(labels, np.int32)

def layer_norm(rows, gain, shift):
    center = rows - lax.optimization_barrier(jnp.mean(rows, axis=-1, keepdims=True))
    spread = lax.optimization_barrier(jnp.mean(center * center, axis=-1, keepdims=True))
    return center * lax.rsqrt(spread + 1e-06) * gain + shift

def block_forward(same_crop, kept_rows, attention_weights, feedforward_weights, vector_weights):
    attention_low = low(attention_weights)
    feedforward_low = low(feedforward_weights)
    width = kept_rows.shape[-1]

    def one_image(rows):
        count = rows.shape[0]
        normed = low(layer_norm(rows, vector_weights[0], vector_weights[1]))
        score = jax.nn.sigmoid(jnp.dot(normed, vector_weights[2], precision=HIGHEST))
        bias_three = jnp.concatenate([vector_weights[3], jnp.zeros_like(vector_weights[3]), vector_weights[4]])
        project = low_back(low(jnp.dot(normed, attention_low[:, :3 * width], precision=HIGHEST) + bias_three))
        query = project[:, :width].reshape(count, H, HD)
        keys = project[:, width:2 * width].reshape(count, H, HD)
        values = project[:, 2 * width:].reshape(count, H, HD)
        scores = low_back(HD ** (-0.5) * jnp.einsum('khd,jhd->hkj', query, keys, precision=HIGHEST))
        scores = jnp.where(same_crop[None], scores, -1000000000.0)
        probs = low(jax.nn.softmax(scores, axis=-1))
        mixed = jnp.einsum('hkj,jhd->khd', probs, values, precision=HIGHEST).reshape(count, width)
        mixed = low_back(low(mixed))
        branch = low_back(jnp.dot(mixed, attention_low[:, 3 * width:], precision=HIGHEST) + vector_weights[5])
        residual = rows + score[:, None] * branch
        normed_two = low(layer_norm(residual, vector_weights[6], vector_weights[7]))
        inner = low_back(jnp.dot(normed_two, feedforward_low[0], precision=HIGHEST) + vector_weights[9:].reshape(-1))
        activated = low(jax.nn.gelu(inner, approximate=False))
        output = jnp.dot(activated, feedforward_low[1].T, precision=HIGHEST) + vector_weights[8]
        return residual + output
    return lax.map(jax.checkpoint(one_image), kept_rows)

def adamw(grad, first, second, master, average, rate, decay):
    first_new = 0.5 * first + 0.5 * grad
    second_new = 0.5 * second + 0.5 * grad * grad
    update = first_new / (jnp.sqrt(second_new) + 1e-08)
    master_new = master - rate * (update + decay * master)
    average_new = 0.9 * average + 0.1 * master_new
    return (first_new, second_new, master_new, average_new)

def reference(tokens, cotangent, kept_index, attention_weights, attention_first, attention_second, attention_average, feedforward_weights, feedforward_first, feedforward_second, feedforward_average, vector_weights, vector_first, vector_second, vector_average):
    labels = crop_labels()
    same_crop = jnp.asarray(labels[:, None] == labels[None, :])
    tokens_float = tokens.astype(jnp.float32)
    cot_float = cotangent.astype(jnp.float32)
    kept_rows = jnp.take_along_axis(tokens_float, kept_index[:, :, None], axis=1)
    cot_rows = jnp.take_along_axis(cot_float, kept_index[:, :, None], axis=1)
    forward = partial(block_forward, same_crop)
    result, backward = jax.vjp(forward, kept_rows, attention_weights, feedforward_weights, vector_weights)
    kept_grad, attention_gradient, feedforward_gradient, vector_gradient = backward(cot_rows)
    image_index = jnp.arange(tokens.shape[0])[:, None]
    block_output = tokens_float.at[image_index, kept_index].set(result).astype(jnp.bfloat16)
    input_gradient = cot_float.at[image_index, kept_index].set(kept_grad)
    attention_new = adamw(attention_gradient, attention_first, attention_second, attention_weights, attention_average, 0.02, 0.05)
    feedforward_new = adamw(feedforward_gradient, feedforward_first, feedforward_second, feedforward_weights, feedforward_average, 0.02, 0.05)
    vector_new = adamw(vector_gradient, vector_first, vector_second, vector_weights, vector_average, 0.2, 0.0)
    return (block_output, input_gradient, attention_gradient, attention_new[0], attention_new[1], attention_new[2], attention_new[3], attention_new[2].astype(jnp.bfloat16), feedforward_gradient, feedforward_new[0], feedforward_new[1], feedforward_new[2], feedforward_new[3], feedforward_new[2].astype(jnp.bfloat16), vector_gradient, vector_new[0], vector_new[1], vector_new[2], vector_new[3], vector_gradient[3])
```

```python
import functools

import jax
import jax.numpy as jnp
import numpy as np
from jax import lax
from jax.experimental import pallas as pl
from jax.experimental.pallas import tpu as pltpu
from jax.sharding import PartitionSpec as P

H = 12
HD = 64
LG = 197
LL = 37
KG = LG // 2
KL = LL // 2
LOC = 4 * KL
GP = -(-KG // 16) * 16
LP = -(-LOC // 16) * 16
RI = 2 * GP + LP
UNITS = ((0, GP), (GP, GP), (2 * GP, LP))
PAIRS = H // 2
W2L = 2 * HD

bf16 = jnp.bfloat16
f32 = jnp.float32


def params(limit=56, **kw):
    return pltpu.CompilerParams(vmem_limit_bytes=limit << 20, **kw)


def full(shape):
    return pl.BlockSpec(shape, lambda *_: (0,) * len(shape))


def per_image(*shape):
    return pl.BlockSpec((1,) + shape, lambda i, *_: (i,) + (0,) * len(shape))


def nn(a, b):
    return lax.dot_general(a, b, (((1,), (0,)), ((), ())), preferred_element_type=f32)


def nt(a, b):
    return lax.dot_general(a, b, (((1,), (1,)), ((), ())), preferred_element_type=f32)


def tn(a, b):
    return lax.dot_general(a, b, (((0,), (0,)), ((), ())), preferred_element_type=f32)


def normalize(rows):
    center = rows - jnp.mean(rows, axis=-1, keepdims=True)
    spread = jnp.mean(center * center, axis=-1, keepdims=True)
    inverse = lax.rsqrt(spread + 1e-06)
    return center * inverse, inverse


def norm_backward(upstream, standard, inverse, gain):
    scaled = upstream * gain
    return inverse * (
        scaled
        - jnp.mean(scaled, axis=-1, keepdims=True)
        - standard * jnp.mean(scaled * standard, axis=-1, keepdims=True)
    )


def colsum(v):
    return jnp.sum(v, axis=0, keepdims=True)


def masks():
    key = np.arange(GP)[:, None]
    query = np.zeros((1, GP), np.int64)
    mg = np.where((key < KG) & (query == 0), 0.0, -1e9)
    key = np.arange(LP)[:, None]
    query = np.arange(LP)[None, :]
    ml = np.where((key < LOC) & (key // KL == query // KL), 0.0, -1e9)
    two = lambda m: jnp.asarray(np.concatenate([m, m], 1), f32)
    return two(mg), two(ml)


def lane_half(shape):
    return lax.broadcasted_iota(jnp.int32, shape, len(shape) - 1) < HD


def split_heads(v, scale):
    first = lane_half(v.shape)
    zero = jnp.zeros_like(v)
    if scale != 1.0:
        v = v * jnp.asarray(scale, v.dtype)
    return jnp.concatenate([jnp.where(first, v, zero), jnp.where(first, zero, v)], axis=0)


def join_heads(v):
    n = v.shape[0] // 2
    return jnp.where(lane_half((n, v.shape[1])), v[:n], v[n:])


def softmax_keys(st):
    p = jnp.exp(st - jnp.max(st, axis=0, keepdims=True))
    return p * (1.0 / jnp.sum(p, axis=0, keepdims=True))


def gather_kernel(tok_ref, cot_ref, idx_ref, vec_ref, kept_ref, normed_ref, cotk_ref):
    hot = (
        lax.broadcasted_iota(jnp.int32, (RI, tok_ref.shape[1]), 1) == idx_ref[0]
    ).astype(f32).astype(bf16)
    kept = nn(hot, tok_ref[0])
    kept_ref[0] = kept.astype(bf16)
    cotk_ref[0] = nn(hot, cot_ref[0]).astype(bf16)
    standard, _ = normalize(kept)
    normed_ref[0] = (standard * vec_ref[0:1] + vec_ref[1:2]).astype(bf16)


def router_score(normed, vec_ref):
    logit = jnp.sum(normed.astype(f32) * vec_ref[2:3], axis=-1, keepdims=True)
    return jax.nn.sigmoid(logit)


def forward_kernel(
    normed_ref, kept_ref, watt_ref, vec_ref, mg_ref, ml_ref,
    proj_ref, mixed_ref, branch_ref, n2_ref,
):
    d = normed_ref.shape[2]
    normed = normed_ref[0]
    for j, row in ((0, 3), (1, None), (2, 4)):
        part = nt(normed, watt_ref[j * d : (j + 1) * d, :])
        if row is not None:
            part = part + vec_ref[row : row + 1]
        proj_ref[0, :, j * d : (j + 1) * d] = part.astype(bf16)
    for start, n in UNITS:
        mask_ref = mg_ref if n == GP else ml_ref
        for pair in range(PAIRS):
            cols = lambda j: slice(j * d + pair * W2L, j * d + (pair + 1) * W2L)
            rows = slice(start, start + n)
            qs = split_heads(proj_ref[0, rows, cols(0)], HD ** -0.5)
            st = nt(proj_ref[0, rows, cols(1)], qs) + mask_ref[...]
            pt = softmax_keys(st).astype(bf16)
            out = tn(pt, proj_ref[0, rows, cols(2)])
            mixed_ref[0, rows, pair * W2L : (pair + 1) * W2L] = join_heads(out).astype(bf16)
    branch = nt(mixed_ref[0], watt_ref[3 * d :, :]) + vec_ref[5:6]
    branch_ref[0] = branch
    residual = kept_ref[0].astype(f32) + router_score(normed, vec_ref) * branch
    standard, _ = normalize(residual)
    n2_ref[0] = (standard * vec_ref[6:7] + vec_ref[7:8]).astype(bf16)


def feed_kernel(
    n2_ref, cot_ref, w_ref, bias_ref, out_ref, n2g_ref, gff_ref, bg_ref, act_s, ig_s,
):
    step = pl.program_id(0)
    images = n2_ref.shape[0]
    d, hb = w_ref.shape[2], w_ref.shape[3]
    bg_ref[0] = jnp.zeros((1, hb), f32)

    @pl.when(step == 0)
    def _():
        out_ref[...] = jnp.zeros_like(out_ref)
        n2g_ref[...] = jnp.zeros_like(n2g_ref)

    @pl.loop(0, images)
    def _(i):
        inner = nn(n2_ref[i], w_ref[0, 0]) + bias_ref[0]
        ag = nn(cot_ref[i], w_ref[0, 1])
        phi = 0.5 * (1.0 + lax.erf(inner * 0.7071067811865476))
        act = (inner * phi).astype(bf16)
        slope = phi + inner * jnp.exp(-0.5 * inner * inner) * 0.3989422804014327
        ig = (ag * slope).astype(bf16)
        rows = pl.ds(pl.multiple_of(i * RI, 16), RI)
        act_s[rows, :] = act
        ig_s[rows, :] = ig
        bg_ref[0] += colsum(ig.astype(f32))
        out_ref[i] += nt(act, w_ref[0, 1])
        n2g_ref[i] += nt(ig, w_ref[0, 0])

    n2 = n2_ref[...].reshape(images * RI, d)
    cot = cot_ref[...].reshape(images * RI, d)
    gff_ref[0, 0] = tn(n2, ig_s[...]).astype(bf16)
    gff_ref[0, 1] = tn(cot, act_s[...]).astype(bf16)


def backward_kernel(
    n2g_ref, cotk_ref, branch_ref, kept_ref, normed_ref, proj_ref, mixed_ref, watt_ref,
    vec_ref, mg_ref, ml_ref, dp_ref, resg_ref, rg_ref, vecg_ref, dproj_s, mg_s,
):
    d = normed_ref.shape[2]
    normed = normed_ref[0]
    score = router_score(normed, vec_ref)
    branch = branch_ref[0]
    residual = kept_ref[0].astype(f32) + score * branch
    standard, inverse = normalize(residual)
    n2g = n2g_ref[0]
    cot = cotk_ref[0].astype(f32)
    resg = cot + norm_backward(n2g, standard, inverse, vec_ref[6:7])
    resg_ref[0] = resg
    bg = (score * resg).astype(bf16)
    rg = jnp.sum(resg * branch, axis=-1, keepdims=True) * score * (1.0 - score)
    rg_ref[0] = rg
    dp_ref[0, :, 3 * d :] = bg
    mg_s[...] = nn(bg, watt_ref[3 * d :, :]).astype(bf16)
    for start, n in UNITS:
        mask_ref = mg_ref if n == GP else ml_ref
        rows = slice(start, start + n)
        for pair in range(PAIRS):
            cols = lambda j: slice(j * d + pair * W2L, j * d + (pair + 1) * W2L)
            qs = split_heads(proj_ref[0, rows, cols(0)], HD ** -0.5)
            kk = proj_ref[0, rows, cols(1)]
            pt = softmax_keys(nt(kk, qs) + mask_ref[...])
            ds = split_heads(mg_s[rows, cols(0)], 1.0)
            gpt = nt(proj_ref[0, rows, cols(2)], ds)
            sg = (pt * (gpt - jnp.sum(pt * gpt, axis=0, keepdims=True))).astype(bf16)
            qg = join_heads(tn(sg, kk)) * HD ** -0.5
            dp_ref[0, rows, cols(0)] = qg.astype(bf16)
            dp_ref[0, rows, cols(1)] = nn(sg, qs).astype(bf16)
            dp_ref[0, rows, cols(2)] = nn(pt.astype(bf16), ds).astype(bf16)
    zero = jnp.zeros((1, d), f32)
    sums = jnp.concatenate(
        [
            colsum(rg * normed.astype(f32)),
            colsum(dp_ref[0, :, :d].astype(f32)),
            colsum(dp_ref[0, :, 2 * d : 3 * d].astype(f32)),
            colsum(bg.astype(f32)),
            colsum(n2g * standard),
            colsum(n2g),
            colsum(cot),
            zero,
        ],
        axis=0,
    )

    @pl.when(pl.program_id(0) == 0)
    def _():
        vecg_ref[...] = jnp.zeros_like(vecg_ref)

    vecg_ref[...] += sums


def grad_kernel(dp_ref, normed_ref, mixed_ref, g_ref):
    rows = dp_ref.shape[0] * dp_ref.shape[1]
    left = dp_ref[...].reshape(rows, dp_ref.shape[2])
    d = normed_ref.shape[2]

    @pl.when(pl.program_id(0) < 3)
    def _():
        g_ref[...] = tn(left, normed_ref[...].reshape(rows, d)).astype(bf16)

    @pl.when(pl.program_id(0) == 3)
    def _():
        g_ref[...] = tn(left, mixed_ref[...].reshape(rows, d)).astype(bf16)


def input_kernel(
    dp_ref, rg_ref, resg_ref, kept_ref, cot_ref, idx_ref, watt_ref, vec_ref, ing_ref, vecg_ref,
):
    d = kept_ref.shape[2]
    standard, inverse = normalize(kept_ref[0].astype(f32))
    ng = rg_ref[0] * vec_ref[2:3] + nn(dp_ref[0, :, : 3 * d], watt_ref[: 3 * d, :])
    grad = resg_ref[0] + norm_backward(ng, standard, inverse, vec_ref[0:1])
    hot, taken = scatter_matrix(idx_ref, cot_ref.shape[1])
    high = grad.astype(bf16)
    low = (grad - high.astype(f32)).astype(bf16)
    spread = nn(hot, high) + nn(hot, low)
    ing_ref[0] = jnp.where(taken, spread, cot_ref[0].astype(f32))
    sums = jnp.concatenate(
        [colsum(ng * standard), colsum(ng), jnp.zeros((6, d), f32)], axis=0
    )

    @pl.when(pl.program_id(0) == 0)
    def _():
        vecg_ref[...] = jnp.zeros_like(vecg_ref)

    vecg_ref[...] += sums


def scatter_matrix(idx_ref, length):
    hot = (lax.broadcasted_iota(jnp.int32, (length, RI), 0) == idx_ref[0]).astype(f32)
    taken = jnp.sum(hot, axis=-1, keepdims=True) > 0.5
    return hot.astype(bf16), taken


def output_kernel(out_ref, branch_ref, kept_ref, normed_ref, tok_ref, idx_ref, vec_ref, o_ref):
    score = router_score(normed_ref[0], vec_ref)
    residual = kept_ref[0].astype(f32) + score * branch_ref[0]
    result = (residual + out_ref[0] + vec_ref[8:9]).astype(bf16)
    hot, taken = scatter_matrix(idx_ref, tok_ref.shape[1])
    o_ref[0] = jnp.where(taken, nn(hot, result), tok_ref[0].astype(f32)).astype(bf16)


def adamw(grad, first, second, master, average, rate, decay):
    first_new = 0.5 * first + 0.5 * grad
    second_new = 0.5 * second + 0.5 * grad * grad
    update = first_new / (jnp.sqrt(second_new) + 1e-08)
    master_new = master - rate * (update + decay * master)
    average_new = 0.9 * average + 0.1 * master_new
    return (first_new, second_new, master_new, average_new)


def sds(*shape_dtype):
    return jax.ShapeDtypeStruct(shape_dtype[:-1], shape_dtype[-1])


def gather_weights(att_t, ff):
    watt = lax.all_gather(att_t, ("dp", "mp"), axis=0, tiled=True)
    wff = lax.all_gather(ff, "dp", axis=1, tiled=True)
    wff = lax.all_gather(wff, "mp", axis=0, tiled=False)
    return watt, wff


def reduce_grads(gatt, gff):
    gatt = lax.psum_scatter(gatt, ("dp", "mp"), scatter_dimension=0, tiled=True)
    gff = lax.psum_scatter(gff, "mp", scatter_dimension=0, tiled=False)
    gff = lax.psum_scatter(gff, "dp", scatter_dimension=1, tiled=True)
    return gatt.astype(f32), gff.astype(f32)


def per_device(
    tokens, cotangent, kept_index,
    attention_weights, attention_first, attention_second, attention_average,
    feedforward_weights, feedforward_first, feedforward_second, feedforward_average,
    vector_weights, vector_first, vector_second, vector_average,
):
    images, length, d = tokens.shape
    vec = vector_weights
    nmp = lax.axis_size("mp")
    hb = feedforward_weights.shape[2]
    ff = nmp * hb
    fill = lambda n: jnp.full((images, n), -1, jnp.int32)
    idx = jnp.concatenate(
        [
            kept_index[:, :KG], fill(GP - KG),
            kept_index[:, KG : 2 * KG], fill(GP - KG),
            kept_index[:, 2 * KG :], fill(LP - LOC),
        ],
        axis=1,
    )
    idx_col, idx_row = idx[:, :, None], idx[:, None, :]
    mg, ml = masks()

    watt, wff = gather_weights(
        attention_weights.T.astype(bf16), feedforward_weights.astype(bf16)
    )

    kept, normed, cotk = pl.pallas_call(
        gather_kernel,
        grid=(images,),
        in_specs=[per_image(length, d), per_image(length, d), per_image(RI, 1), full(vec.shape)],
        out_specs=[per_image(RI, d)] * 3,
        out_shape=[sds(images, RI, d, bf16)] * 3,
        compiler_params=params(),
        name="gather_norm",
    )(tokens, cotangent, idx_col, vec)

    proj, mixed, branch, n2 = pl.pallas_call(
        forward_kernel,
        grid=(images,),
        in_specs=[
            per_image(RI, d), per_image(RI, d), full(watt.shape), full(vec.shape),
            full(mg.shape), full(ml.shape),
        ],
        out_specs=[per_image(RI, 3 * d), per_image(RI, d), per_image(RI, d), per_image(RI, d)],
        out_shape=[
            sds(images, RI, 3 * d, bf16), sds(images, RI, d, bf16),
            sds(images, RI, d, f32), sds(images, RI, d, bf16),
        ],
        compiler_params=params(),
        name="attention_forward",
    )(normed, kept, watt, vec, mg, ml)

    bias = vec[9:].reshape(nmp, 1, hb)
    whole = lambda *s: pl.BlockSpec(s, lambda j: (0,) * len(s), pipeline_mode=pl.Buffered(1))
    out_acc, n2g, gff, bg = pl.pallas_call(
        feed_kernel,
        grid=(nmp,),
        in_specs=[
            whole(images, RI, d), whole(images, RI, d),
            pl.BlockSpec((1, 2, d, hb), lambda j: (j, 0, 0, 0)),
            pl.BlockSpec((1, 1, hb), lambda j: (j, 0, 0)),
        ],
        out_specs=[
            full((images, RI, d)), full((images, RI, d)),
            pl.BlockSpec((1, 2, d, hb), lambda j: (j, 0, 0, 0)),
            pl.BlockSpec((1, 1, hb), lambda j: (j, 0, 0)),
        ],
        out_shape=[
            sds(images, RI, d, f32), sds(images, RI, d, f32),
            sds(nmp, 2, d, hb, bf16), sds(nmp, 1, hb, f32),
        ],
        scratch_shapes=[pltpu.VMEM((images * RI, hb), bf16), pltpu.VMEM((images * RI, hb), bf16)],
        compiler_params=params(),
        name="feedforward",
    )(n2, cotk, wff, bias)

    dp, resg, rg, vecg = pl.pallas_call(
        backward_kernel,
        grid=(images,),
        in_specs=[
            per_image(RI, d), per_image(RI, d), per_image(RI, d), per_image(RI, d),
            per_image(RI, d), per_image(RI, 3 * d), per_image(RI, d),
            full(watt.shape), full(vec.shape), full(mg.shape), full(ml.shape),
        ],
        out_specs=[per_image(RI, 4 * d), per_image(RI, d), per_image(RI, 1), full((8, d))],
        out_shape=[
            sds(images, RI, 4 * d, bf16), sds(images, RI, d, f32), sds(images, RI, 1, f32),
            sds(8, d, f32),
        ],
        scratch_shapes=[pltpu.VMEM((16, 128), f32), pltpu.VMEM((RI, d), bf16)],
        compiler_params=params(),
        name="attention_backward",
    )(n2g, cotk, branch, kept, normed, proj, mixed, watt, vec, mg, ml)

    gatt = pl.pallas_call(
        grad_kernel,
        grid=(4,),
        in_specs=[
            pl.BlockSpec((images, RI, d), lambda j: (0, 0, j)),
            whole(images, RI, d), whole(images, RI, d),
        ],
        out_specs=pl.BlockSpec((d, d), lambda j: (j, 0)),
        out_shape=sds(4 * d, d, bf16),
        compiler_params=params(),
        name="attention_grads",
    )(dp, normed, mixed)

    input_gradient, vecg_in = pl.pallas_call(
        input_kernel,
        grid=(images,),
        in_specs=[
            per_image(RI, 4 * d), per_image(RI, 1), per_image(RI, d), per_image(RI, d),
            per_image(length, d), per_image(1, RI), full(watt.shape), full(vec.shape),
        ],
        out_specs=[per_image(length, d), full((8, d))],
        out_shape=[sds(images, length, d, f32), sds(8, d, f32)],
        compiler_params=params(),
        name="input_grad",
    )(dp, rg, resg, kept, cotangent, idx_row, watt, vec)

    block_output = pl.pallas_call(
        output_kernel,
        grid=(images,),
        in_specs=[
            per_image(RI, d), per_image(RI, d), per_image(RI, d), per_image(RI, d),
            per_image(length, d), per_image(1, RI), full(vec.shape),
        ],
        out_specs=per_image(length, d),
        out_shape=sds(images, length, d, bf16),
        compiler_params=params(),
        name="block_output",
    )(out_acc, branch, kept, normed, tokens, idx_row, vec)

    gatt, feedforward_gradient = reduce_grads(gatt, gff)
    attention_gradient = gatt.T
    vector_local = jnp.concatenate([vecg_in[:2], vecg[:7], bg.reshape(ff // d, d)], axis=0)
    vector_gradient = lax.psum(vector_local, ("dp", "mp"))
    attention_new = adamw(
        attention_gradient, attention_first, attention_second,
        attention_weights, attention_average, 0.02, 0.05,
    )
    feedforward_new = adamw(
        feedforward_gradient, feedforward_first, feedforward_second,
        feedforward_weights, feedforward_average, 0.02, 0.05,
    )
    vector_new = adamw(
        vector_gradient, vector_first, vector_second, vector_weights, vector_average, 0.2, 0.0
    )
    return (
        block_output, input_gradient,
        attention_gradient, *attention_new, attention_new[2].astype(bf16),
        feedforward_gradient, *feedforward_new, feedforward_new[2].astype(bf16),
        vector_gradient, *vector_new, vector_gradient[3],
    )


def solution(mesh):
    rows = P(("dp", "mp"), None, None)
    att = P(None, ("dp", "mp"))
    feed = P(None, "dp", "mp")
    in_specs = (rows, rows, P(("dp", "mp"), None)) + (att,) * 4 + (feed,) * 4 + (P(),) * 4
    out_specs = (rows, rows) + (att,) * 6 + (feed,) * 6 + (P(),) * 6
    return jax.shard_map(
        per_device, mesh=mesh, in_specs=in_specs, out_specs=out_specs, check_vma=False
    )
```

```python
import functools

import jax
import jax.numpy as jnp
import numpy as np
from jax import lax
from jax.experimental import pallas as pl
from jax.experimental.pallas import tpu as pltpu
from jax.sharding import PartitionSpec as P

H = 12
HD = 64
LG = 197
LL = 37
KG = LG // 2
KL = LL // 2
LOC = 4 * KL
KEPT = 2 * KG + LOC
RI = -(-KEPT // 16) * 16
SPANS = ((0, KG), (KG, 2 * KG), (2 * KG, KEPT))
UNITS = tuple((a // 16 * 16, -(-b // 16) * 16) for a, b in SPANS)
PAIRS = H // 2
W2L = 2 * HD

bf16 = jnp.bfloat16
f32 = jnp.float32


def params(limit=56, **kw):
    return pltpu.CompilerParams(vmem_limit_bytes=limit << 20, **kw)


def full(shape):
    return pl.BlockSpec(shape, lambda *_: (0,) * len(shape))


def per_image(*shape):
    return pl.BlockSpec((1,) + shape, lambda i, *_: (i,) + (0,) * len(shape))


def nn(a, b):
    return lax.dot_general(a, b, (((1,), (0,)), ((), ())), preferred_element_type=f32)


def nt(a, b):
    return lax.dot_general(a, b, (((1,), (1,)), ((), ())), preferred_element_type=f32)


def tn(a, b):
    return lax.dot_general(a, b, (((0,), (0,)), ((), ())), preferred_element_type=f32)


def normalize(rows):
    center = rows - jnp.mean(rows, axis=-1, keepdims=True)
    spread = jnp.mean(center * center, axis=-1, keepdims=True)
    inverse = lax.rsqrt(spread + 1e-06)
    return center * inverse, inverse


def norm_backward(upstream, standard, inverse, gain):
    scaled = upstream * gain
    return inverse * (
        scaled
        - jnp.mean(scaled, axis=-1, keepdims=True)
        - standard * jnp.mean(scaled * standard, axis=-1, keepdims=True)
    )


def colsum(v):
    return jnp.sum(v, axis=0, keepdims=True)


def masks():
    crop = np.full(RI, -1)
    crop[:KG], crop[KG : 2 * KG] = 0, 1
    for c in range(4):
        crop[2 * KG + c * KL : 2 * KG + (c + 1) * KL] = 2 + c
    adds, valids = [], []
    for (a, b), (lo, hi) in zip(SPANS, UNITS):
        rows = np.arange(lo, hi)
        inside = (rows >= a) & (rows < b)
        same = (crop[lo:hi, None] == crop[None, lo:hi]) & inside[:, None] & inside[None, :]
        adds.append(np.tile(np.where(same, 0.0, -1e9), (1, 2)).astype(np.float32))
        valids.append(np.tile(inside[None, :].astype(np.float32), (8, 2)))
    return [jnp.asarray(m) for m in adds + valids]


def lane_half(shape):
    return lax.broadcasted_iota(jnp.int32, shape, len(shape) - 1) < HD


def split_heads(v, scale):
    first = lane_half(v.shape)
    zero = jnp.zeros_like(v)
    if scale != 1.0:
        v = v * jnp.asarray(scale, v.dtype)
    return jnp.concatenate([jnp.where(first, v, zero), jnp.where(first, zero, v)], axis=0)


def join_heads(v):
    n = v.shape[0] // 2
    return jnp.where(lane_half((n, v.shape[1])), v[:n], v[n:])


def softmax_keys(st, valid):
    p = jnp.exp(st - jnp.max(st, axis=0, keepdims=True))
    return p * (valid / jnp.sum(p, axis=0, keepdims=True))


def store_window(ref, lo, hi, last, cols, value, tail):
    value = value.astype(bf16)
    if tail is not None:
        value = jnp.concatenate([value[:16] + tail, value[16:]], axis=0)
    end = hi if last else hi - 16
    ref[0, lo:end, cols] = value[: end - lo]
    return None if last else value[end - lo :]


def gather_kernel(tok_ref, cot_ref, idx_ref, vec_ref, kept_ref, normed_ref, cotk_ref):
    hot = (
        lax.broadcasted_iota(jnp.int32, (RI, tok_ref.shape[1]), 1) == idx_ref[0]
    ).astype(f32).astype(bf16)
    kept = nn(hot, tok_ref[0])
    kept_ref[0] = kept.astype(bf16)
    cotk_ref[0] = nn(hot, cot_ref[0]).astype(bf16)
    standard, _ = normalize(kept)
    normed_ref[0] = (standard * vec_ref[0:1] + vec_ref[1:2]).astype(bf16)


def router_score(normed, vec_ref):
    logit = jnp.sum(normed.astype(f32) * vec_ref[2:3], axis=-1, keepdims=True)
    return jax.nn.sigmoid(logit)


def forward_kernel(
    normed_ref, kept_ref, watt_ref, vec_ref, m0_ref, m1_ref, m2_ref, v0_ref, v1_ref, v2_ref,
    proj_ref, mixed_ref, branch_ref, n2_ref,
):
    d = normed_ref.shape[2]
    normed = normed_ref[0]
    for j, row in ((0, 3), (1, None), (2, 4)):
        part = nt(normed, watt_ref[j * d : (j + 1) * d, :])
        if row is not None:
            part = part + vec_ref[row : row + 1]
        proj_ref[0, :, j * d : (j + 1) * d] = part.astype(bf16)
    mrefs, vrefs = (m0_ref, m1_ref, m2_ref), (v0_ref, v1_ref, v2_ref)
    for pair in range(PAIRS):
        cols = lambda j: slice(j * d + pair * W2L, j * d + (pair + 1) * W2L)
        tail = None
        for unit, (lo, hi) in enumerate(UNITS):
            qs = split_heads(proj_ref[0, lo:hi, cols(0)], HD ** -0.5)
            st = nt(proj_ref[0, lo:hi, cols(1)], qs) + mrefs[unit][...]
            pt = softmax_keys(st, vrefs[unit][0:1]).astype(bf16)
            out = join_heads(tn(pt, proj_ref[0, lo:hi, cols(2)]))
            tail = store_window(mixed_ref, lo, hi, unit == 2, cols(0), out, tail)
    branch = nt(mixed_ref[0], watt_ref[3 * d :, :]) + vec_ref[5:6]
    branch_ref[0] = branch
    residual = kept_ref[0].astype(f32) + router_score(normed, vec_ref) * branch
    standard, _ = normalize(residual)
    n2_ref[0] = (standard * vec_ref[6:7] + vec_ref[7:8]).astype(bf16)


def feed_kernel(
    n2_ref, cot_ref, w_ref, bias_ref, out_ref, n2g_ref, gff_ref, bg_ref, act_s, ig_s,
):
    step = pl.program_id(0)
    images = n2_ref.shape[0]
    d, hb = w_ref.shape[2], w_ref.shape[3]
    bg_ref[0] = jnp.zeros((1, hb), f32)

    @pl.when(step == 0)
    def _():
        out_ref[...] = jnp.zeros_like(out_ref)
        n2g_ref[...] = jnp.zeros_like(n2g_ref)

    @pl.loop(0, images)
    def _(i):
        inner = nn(n2_ref[i], w_ref[0, 0]) + bias_ref[0]
        ag = nn(cot_ref[i], w_ref[0, 1])
        phi = 0.5 * (1.0 + lax.erf(inner * 0.7071067811865476))
        act = (inner * phi).astype(bf16)
        slope = phi + inner * jnp.exp(-0.5 * inner * inner) * 0.3989422804014327
        ig = (ag * slope).astype(bf16)
        rows = pl.ds(pl.multiple_of(i * RI, 16), RI)
        act_s[rows, :] = act
        ig_s[rows, :] = ig
        bg_ref[0] += colsum(ig.astype(f32))
        out_ref[i] += nt(act, w_ref[0, 1])
        n2g_ref[i] += nt(ig, w_ref[0, 0])

    n2 = n2_ref[...].reshape(images * RI, d)
    cot = cot_ref[...].reshape(images * RI, d)
    gff_ref[0, 0] = tn(n2, ig_s[...]).astype(bf16)
    gff_ref[0, 1] = tn(cot, act_s[...]).astype(bf16)


def backward_kernel(
    n2g_ref, cotk_ref, branch_ref, kept_ref, normed_ref, proj_ref, mixed_ref, watt_ref,
    vec_ref, m0_ref, m1_ref, m2_ref, v0_ref, v1_ref, v2_ref, dp_ref, resg_ref, rg_ref, vecg_ref,
    mg_s,
):
    d = normed_ref.shape[2]
    normed = normed_ref[0]
    score = router_score(normed, vec_ref)
    branch = branch_ref[0]
    residual = kept_ref[0].astype(f32) + score * branch
    standard, inverse = normalize(residual)
    n2g = n2g_ref[0]
    cot = cotk_ref[0].astype(f32)
    resg = cot + norm_backward(n2g, standard, inverse, vec_ref[6:7])
    resg_ref[0] = resg
    bg = (score * resg).astype(bf16)
    rg = jnp.sum(resg * branch, axis=-1, keepdims=True) * score * (1.0 - score)
    rg_ref[0] = rg
    dp_ref[0, :, 3 * d :] = bg
    mg_s[...] = nn(bg, watt_ref[3 * d :, :]).astype(bf16)
    mrefs, vrefs = (m0_ref, m1_ref, m2_ref), (v0_ref, v1_ref, v2_ref)
    for pair in range(PAIRS):
        cols = lambda j: slice(j * d + pair * W2L, j * d + (pair + 1) * W2L)
        tails = [None] * 3
        for unit, (lo, hi) in enumerate(UNITS):
            qs = split_heads(proj_ref[0, lo:hi, cols(0)], HD ** -0.5)
            kk = proj_ref[0, lo:hi, cols(1)]
            pt = softmax_keys(nt(kk, qs) + mrefs[unit][...], vrefs[unit][0:1])
            ds = split_heads(mg_s[lo:hi, cols(0)], 1.0)
            gpt = nt(proj_ref[0, lo:hi, cols(2)], ds)
            sg = (pt * (gpt - jnp.sum(pt * gpt, axis=0, keepdims=True))).astype(bf16)
            grads = (
                join_heads(tn(sg, kk)) * HD ** -0.5, nn(sg, qs), nn(pt.astype(bf16), ds)
            )
            for j in range(3):
                tails[j] = store_window(dp_ref, lo, hi, unit == 2, cols(j), grads[j], tails[j])
    zero = jnp.zeros((1, d), f32)
    sums = jnp.concatenate(
        [
            colsum(rg * normed.astype(f32)),
            colsum(dp_ref[0, :, :d].astype(f32)),
            colsum(dp_ref[0, :, 2 * d : 3 * d].astype(f32)),
            colsum(bg.astype(f32)),
            colsum(n2g * standard),
            colsum(n2g),
            colsum(cot),
            zero,
        ],
        axis=0,
    )

    @pl.when(pl.program_id(0) == 0)
    def _():
        vecg_ref[...] = jnp.zeros_like(vecg_ref)

    vecg_ref[...] += sums


def grad_kernel(dp_ref, normed_ref, mixed_ref, g_ref):
    rows = dp_ref.shape[0] * dp_ref.shape[1]
    left = dp_ref[...].reshape(rows, dp_ref.shape[2])
    d = normed_ref.shape[2]

    @pl.when(pl.program_id(0) < 3)
    def _():
        g_ref[...] = tn(left, normed_ref[...].reshape(rows, d)).astype(bf16)

    @pl.when(pl.program_id(0) == 3)
    def _():
        g_ref[...] = tn(left, mixed_ref[...].reshape(rows, d)).astype(bf16)


def input_kernel(
    dp_ref, rg_ref, resg_ref, kept_ref, cot_ref, idx_ref, watt_ref, vec_ref, ing_ref, vecg_ref,
):
    d = kept_ref.shape[2]
    standard, inverse = normalize(kept_ref[0].astype(f32))
    ng = rg_ref[0] * vec_ref[2:3] + nn(dp_ref[0, :, : 3 * d], watt_ref[: 3 * d, :])
    grad = resg_ref[0] + norm_backward(ng, standard, inverse, vec_ref[0:1])
    hot, taken = scatter_matrix(idx_ref, cot_ref.shape[1])
    high = grad.astype(bf16)
    low = (grad - high.astype(f32)).astype(bf16)
    spread = nn(hot, high) + nn(hot, low)
    ing_ref[0] = jnp.where(taken, spread, cot_ref[0].astype(f32))
    sums = jnp.concatenate(
        [colsum(ng * standard), colsum(ng), jnp.zeros((6, d), f32)], axis=0
    )

    @pl.when(pl.program_id(0) == 0)
    def _():
        vecg_ref[...] = jnp.zeros_like(vecg_ref)

    vecg_ref[...] += sums


def scatter_matrix(idx_ref, length):
    hot = (lax.broadcasted_iota(jnp.int32, (length, RI), 0) == idx_ref[0]).astype(f32)
    taken = jnp.sum(hot, axis=-1, keepdims=True) > 0.5
    return hot.astype(bf16), taken


def output_kernel(out_ref, branch_ref, kept_ref, normed_ref, tok_ref, idx_ref, vec_ref, o_ref):
    score = router_score(normed_ref[0], vec_ref)
    residual = kept_ref[0].astype(f32) + score * branch_ref[0]
    result = (residual + out_ref[0] + vec_ref[8:9]).astype(bf16)
    hot, taken = scatter_matrix(idx_ref, tok_ref.shape[1])
    o_ref[0] = jnp.where(taken, nn(hot, result), tok_ref[0].astype(f32)).astype(bf16)


def adamw(grad, first, second, master, average, rate, decay):
    first_new = 0.5 * first + 0.5 * grad
    second_new = 0.5 * second + 0.5 * grad * grad
    update = first_new / (jnp.sqrt(second_new) + 1e-08)
    master_new = master - rate * (update + decay * master)
    average_new = 0.9 * average + 0.1 * master_new
    return (first_new, second_new, master_new, average_new)


def sds(*shape_dtype):
    return jax.ShapeDtypeStruct(shape_dtype[:-1], shape_dtype[-1])


MESH = pl.DeviceIdType.MESH
ANY = pl.BlockSpec(memory_space=pl.ANY)
MP = 4

def flip(index, bit):
    return index + bit * (1 - 2 * lax.rem(lax.div(index, bit), 2))


class Place:
    def __init__(self):
        self.dp = lax.axis_index("dp")
        self.z = lax.axis_index("mp")
        core, x, y = flip(self.dp, 1), flip(self.dp, 2), flip(self.dp, 4)
        self.core, self.x, self.y = (core, self.z), (x, self.z), (y, self.z)
        self.chips = (self.dp, x, y, flip(x, 4))
        self.mates = tuple(flip(c, 1) for c in self.chips)

    def up(self, k):
        return lax.rem(self.z + k, MP)

    def down(self, k):
        return lax.rem(self.z + MP - k, MP)

    def line(self, k):
        return (self.dp, self.up(k))

    def barrier(self):
        sem = pltpu.get_barrier_semaphore()
        others = [self.core, self.x, self.y] + [self.line(k) for k in range(1, MP)]
        for other in others:
            pl.semaphore_signal(sem, inc=1, device_id=other, device_id_type=MESH)
        pl.semaphore_wait(sem, len(others))


def att_block(ref, dp, z, rows):
    return ref.at[pl.ds(pl.multiple_of((dp * MP + z) * rows, 32), rows), :]


def ff_block(ref, dp, z, rows):
    return ref.at[z, :, pl.ds(pl.multiple_of(dp * rows, 32), rows), :]


Z0, X0, Y0, D0, C0 = 0, 3, 7, 11, 15
SLOTS = 31


def gather_links_kernel(att_ref, ff_ref, watt_ref, wff_ref, send, recv, local):
    at = Place()
    at.barrier()
    rows = att_ref.shape[0]
    tensors = ((att_ref, watt_ref, att_block), (ff_ref, wff_ref, ff_block))
    started = []

    def copy(t, slot, r, k, to):
        mine, out, block = tensors[t]
        dst = block(out, at.chips[r], at.down(k), rows)
        src = mine if (r, k) == (0, 0) else dst
        c = pltpu.make_async_remote_copy(
            src_ref=src, dst_ref=dst, send_sem=send.at[t, slot], recv_sem=recv.at[t, slot],
            device_id=to, device_id_type=MESH,
        )
        c.start()
        started.append(c)

    def arrived(t, slot, dp, k):
        mine, out, block = tensors[t]
        dst = block(out, dp, at.down(k), rows)
        pltpu.make_async_remote_copy(
            src_ref=dst, dst_ref=dst, send_sem=send.at[t, slot], recv_sem=recv.at[t, slot],
            device_id=at.core, device_id_type=MESH,
        ).wait_recv()

    def spread(t, k):
        copy(t, X0 + k, 0, k, at.x)
        copy(t, Y0 + k, 0, k, at.y)
        copy(t, C0 + k, 0, k, at.core)

    def begin(t):
        for k in range(1, MP):
            copy(t, Z0 + k - 1, 0, 0, at.line(k))
        spread(t, 0)

    locals_ = []
    for t, (mine, out, block) in enumerate(tensors):
        c = pltpu.make_async_copy(mine, block(out, at.dp, at.z, rows), local.at[t])
        c.start()
        locals_.append(c)
    begin(0)
    begin(1)
    for t in range(2):
        for k in range(1, MP):
            arrived(t, Z0 + k - 1, at.dp, k)
            spread(t, k)
        for k in range(MP):
            arrived(t, X0 + k, at.chips[1], k)
            copy(t, C0 + 4 + k, 1, k, at.core)
            if k < 2:
                copy(t, D0 + k, 1, k, at.y)
            arrived(t, Y0 + k, at.chips[2], k)
            copy(t, C0 + 8 + k, 2, k, at.core)
            if k >= 2:
                copy(t, D0 + k, 2, k, at.x)
        for k in range(MP):
            arrived(t, D0 + k, at.chips[3], k)
            copy(t, C0 + 12 + k, 3, k, at.core)
    for t in range(2):
        for r in range(4):
            for k in range(MP):
                arrived(t, C0 + 4 * r + k, at.mates[r], k)
    for c in started:
        c.wait_send()
    for c in locals_:
        c.wait()


def gather_weights_links(att, ff):
    rows, d = att.shape
    hb = ff.shape[2]
    n = rows * 32
    return pl.pallas_call(
        gather_links_kernel,
        in_specs=[ANY, ANY],
        out_specs=[ANY, ANY],
        out_shape=[
            jax.ShapeDtypeStruct((n, d), bf16), jax.ShapeDtypeStruct((MP, 2, 8 * rows, hb), bf16)
        ],
        scratch_shapes=[
            pltpu.SemaphoreType.DMA((2, SLOTS)), pltpu.SemaphoreType.DMA((2, SLOTS)),
            pltpu.SemaphoreType.DMA((2,)),
        ],
        compiler_params=pltpu.CompilerParams(collective_id=0, has_side_effects=True),
        name="gather_weights",
    )(att, ff)


def add_into(dst, *srcs, out=None):
    step = 32
    rows = dst.shape[0]
    target = dst if out is None else out

    def body(i, _):
        s = pl.ds(pl.multiple_of(i * step, step), step)
        total = dst[s, :].astype(f32)
        for r in srcs:
            total = total + r[s, :].astype(f32)
        target[s, :] = total.astype(target.dtype)
        return 0

    lax.fori_loop(0, rows // step, body, 0)


def scatter_links_kernel(
    gatt_ref, gff_ref, vec_ref, oatt_ref, off_ref, ovec_ref,
    a0, a1, c0, c1, d0, d1, x0, x1, y0, y1, z0, z1, vbuf, send, recv, local, vsend, vrecv,
):
    at = Place()
    at.barrier()
    rows = oatt_ref.shape[0]
    tensors = (
        (gatt_ref, att_block, a0, c0, d0, x0, y0, z0, oatt_ref),
        (gff_ref, ff_block, a1, c1, d1, x1, y1, z1, off_ref),
    )
    started = []

    def remote(t, slot, src, dst, to):
        c = pltpu.make_async_remote_copy(
            src_ref=src, dst_ref=dst, send_sem=send.at[t, slot], recv_sem=recv.at[t, slot],
            device_id=to, device_id_type=MESH,
        )
        c.start()
        started.append(c)

    def arrived(t, slot, dst):
        pltpu.make_async_remote_copy(
            src_ref=dst, dst_ref=dst, send_sem=send.at[t, slot], recv_sem=recv.at[t, slot],
            device_id=at.core, device_id_type=MESH,
        ).wait_recv()

    loads = {}
    for t in range(2):
        g, block, a, c = tensors[t][:4]
        for r in (3, 1, 2, 0):
            for k in range(MP):
                i = 4 * r + k
                src = block(g, at.mates[r], at.down(k), rows)
                remote(t, C0 + i, src, c.at[i], at.core)
                own = pltpu.make_async_copy(
                    block(g, at.chips[r], at.down(k), rows), a.at[i], local.at[t, i]
                )
                own.start()
                loads[t, i] = own

    vbuf[0] = vec_ref[...]
    for step, to in enumerate((at.core, at.x, at.y)):
        c = pltpu.make_async_remote_copy(
            src_ref=vbuf.at[step], dst_ref=vbuf.at[8 + step], send_sem=vsend.at[step],
            recv_sem=vrecv.at[step], device_id=to, device_id_type=MESH,
        )
        c.start()
        c.wait()
        vbuf[step + 1] = vbuf[step] + vbuf[8 + step]
    zc = []
    for k in range(1, MP):
        c = pltpu.make_async_remote_copy(
            src_ref=vbuf.at[3], dst_ref=vbuf.at[10 + k], send_sem=vsend.at[2 + k],
            recv_sem=vrecv.at[2 + k], device_id=at.line(k), device_id_type=MESH,
        )
        c.start()
        zc.append(c)

    def ref2(buf, i):
        return buf.at[i]

    for t in range(2):
        g, block, a, c, d, x, y, z, o = tensors[t]

        def gather_in(i):
            loads[t, i].wait()
            arrived(t, C0 + i, c.at[i])

        segs = range(1) if t == 0 else range(2)
        view = (lambda b, i: [b.at[i]]) if t == 0 else (lambda b, i: [b.at[i, 0], b.at[i, 1]])

        def accumulate(i, *bufs):
            for s, dst in enumerate(view(a, i)):
                add_into(dst, *[view(b, j)[s] for b, j in bufs])

        for k in range(MP):
            i = 12 + k
            gather_in(i)
            accumulate(i, (c, i))
            remote(t, D0 + k, a.at[i], d.at[k], at.x if k < 2 else at.y)
        for k in (0, 1):
            i = 4 + k
            gather_in(i)
            accumulate(i, (c, i))
            remote(t, X0 + k, a.at[i], x.at[k], at.x)
        for k in (2, 3):
            i = 8 + k
            gather_in(i)
            accumulate(i, (c, i))
            remote(t, Y0 + k, a.at[i], y.at[k], at.y)
        for k in (2, 3):
            i = 4 + k
            gather_in(i)
            arrived(t, D0 + k, d.at[k])
            accumulate(i, (c, i), (d, k))
            remote(t, X0 + k, a.at[i], x.at[k], at.x)
        for k in (0, 1):
            i = 8 + k
            gather_in(i)
            arrived(t, D0 + k, d.at[k])
            accumulate(i, (c, i), (d, k))
            remote(t, Y0 + k, a.at[i], y.at[k], at.y)
        for k in (1, 2, 3, 0):
            gather_in(k)
            arrived(t, X0 + k, x.at[k])
            arrived(t, Y0 + k, y.at[k])
            if k:
                accumulate(k, (c, k), (x, k), (y, k))
                remote(t, Z0 + k - 1, a.at[k], z.at[k - 1], (at.dp, at.down(k)))
        for k in range(1, MP):
            arrived(t, Z0 + k - 1, z.at[k - 1])
        for s in segs:
            out = o if t == 0 else o.at[s]
            add_into(
                view(a, 0)[s], view(c, 0)[s], view(x, 0)[s], view(y, 0)[s],
                *[view(z, k)[s] for k in range(3)], out=out,
            )
    for c in zc:
        c.wait()
    total = None
    own = at.z
    parts = [vbuf[3], vbuf[11], vbuf[12], vbuf[13]]
    for zz in range(MP):
        k = lax.rem(own + MP - zz, MP)
        term = jnp.where(k == 0, parts[0], jnp.where(k == 1, parts[1], jnp.where(k == 2, parts[2], parts[3])))
        total = term if total is None else total + term
    ovec_ref[...] = total
    for c in started:
        c.wait_send()


def reduce_grads_links(gatt, gff, vec):
    d = gatt.shape[1]
    rows = gatt.shape[0] // 32
    hb = gff.shape[3]
    V = pltpu.VMEM
    shapes = []
    for n in (16, 16, 4, 4, 4, 3):
        shapes += [V((n, rows, d), bf16), V((n, 2, rows, hb), bf16)]
    vm = pl.BlockSpec(memory_space=pltpu.VMEM)
    return pl.pallas_call(
        scatter_links_kernel,
        in_specs=[ANY, ANY, vm],
        out_specs=[vm, vm, vm],
        out_shape=[
            jax.ShapeDtypeStruct((rows, d), f32), jax.ShapeDtypeStruct((2, rows, hb), f32),
            jax.ShapeDtypeStruct(vec.shape, f32),
        ],
        scratch_shapes=shapes + [
            V((14,) + vec.shape, f32),
            pltpu.SemaphoreType.DMA((2, SLOTS)), pltpu.SemaphoreType.DMA((2, SLOTS)),
            pltpu.SemaphoreType.DMA((2, 16)),
            pltpu.SemaphoreType.DMA((6,)), pltpu.SemaphoreType.DMA((6,)),
        ],
        compiler_params=pltpu.CompilerParams(
            collective_id=1, has_side_effects=True, vmem_limit_bytes=56 << 20
        ),
        name="reduce_grads",
    )(gatt, gff, vec)


def on_links():
    return (lax.axis_size("dp"), lax.axis_size("mp")) == (8, 4)


def gather_weights(att_t, ff):
    if on_links():
        return gather_weights_links(att_t, ff)
    watt = lax.all_gather(att_t, ("dp", "mp"), axis=0, tiled=True)
    wff = lax.all_gather(ff, "dp", axis=1, tiled=True)
    wff = lax.all_gather(wff, "mp", axis=0, tiled=False)
    return watt, wff


def reduce_grads(gatt, gff, vec):
    if on_links():
        return reduce_grads_links(gatt, gff, vec)
    gatt = lax.psum_scatter(gatt, ("dp", "mp"), scatter_dimension=0, tiled=True)
    gff = lax.psum_scatter(gff, "mp", scatter_dimension=0, tiled=False)
    gff = lax.psum_scatter(gff, "dp", scatter_dimension=1, tiled=True)
    return gatt.astype(f32), gff.astype(f32), lax.psum(vec, ("dp", "mp"))


def per_device(
    tokens, cotangent, kept_index,
    attention_weights, attention_first, attention_second, attention_average,
    feedforward_weights, feedforward_first, feedforward_second, feedforward_average,
    vector_weights, vector_first, vector_second, vector_average,
):
    images, length, d = tokens.shape
    vec = vector_weights
    nmp = lax.axis_size("mp")
    hb = feedforward_weights.shape[2]
    ff = nmp * hb
    idx = jnp.concatenate(
        [kept_index, jnp.full((images, RI - KEPT), -1, jnp.int32)], axis=1
    )
    idx_col, idx_row = idx[:, :, None], idx[:, None, :]
    mask = masks()
    mask_specs = [full(m.shape) for m in mask]

    watt, wff = gather_weights(
        attention_weights.T.astype(bf16), feedforward_weights.astype(bf16)
    )

    kept, normed, cotk = pl.pallas_call(
        gather_kernel,
        grid=(images,),
        in_specs=[per_image(length, d), per_image(length, d), per_image(RI, 1), full(vec.shape)],
        out_specs=[per_image(RI, d)] * 3,
        out_shape=[sds(images, RI, d, bf16)] * 3,
        compiler_params=params(),
        name="gather_norm",
    )(tokens, cotangent, idx_col, vec)

    proj, mixed, branch, n2 = pl.pallas_call(
        forward_kernel,
        grid=(images,),
        in_specs=[
            per_image(RI, d), per_image(RI, d), full(watt.shape), full(vec.shape),
            *mask_specs,
        ],
        out_specs=[per_image(RI, 3 * d), per_image(RI, d), per_image(RI, d), per_image(RI, d)],
        out_shape=[
            sds(images, RI, 3 * d, bf16), sds(images, RI, d, bf16),
            sds(images, RI, d, f32), sds(images, RI, d, bf16),
        ],
        compiler_params=params(),
        name="attention_forward",
    )(normed, kept, watt, vec, *mask)

    bias = vec[9:].reshape(nmp, 1, hb)
    whole = lambda *s: pl.BlockSpec(s, lambda j: (0,) * len(s), pipeline_mode=pl.Buffered(1))
    out_acc, n2g, gff, bg = pl.pallas_call(
        feed_kernel,
        grid=(nmp,),
        in_specs=[
            whole(images, RI, d), whole(images, RI, d),
            pl.BlockSpec((1, 2, d, hb), lambda j: (j, 0, 0, 0)),
            pl.BlockSpec((1, 1, hb), lambda j: (j, 0, 0)),
        ],
        out_specs=[
            full((images, RI, d)), full((images, RI, d)),
            pl.BlockSpec((1, 2, d, hb), lambda j: (j, 0, 0, 0)),
            pl.BlockSpec((1, 1, hb), lambda j: (j, 0, 0)),
        ],
        out_shape=[
            sds(images, RI, d, f32), sds(images, RI, d, f32),
            sds(nmp, 2, d, hb, bf16), sds(nmp, 1, hb, f32),
        ],
        scratch_shapes=[pltpu.VMEM((images * RI, hb), bf16), pltpu.VMEM((images * RI, hb), bf16)],
        compiler_params=params(),
        name="feedforward",
    )(n2, cotk, wff, bias)

    dp, resg, rg, vecg = pl.pallas_call(
        backward_kernel,
        grid=(images,),
        in_specs=[
            per_image(RI, d), per_image(RI, d), per_image(RI, d), per_image(RI, d),
            per_image(RI, d), per_image(RI, 3 * d), per_image(RI, d),
            full(watt.shape), full(vec.shape), *mask_specs,
        ],
        out_specs=[per_image(RI, 4 * d), per_image(RI, d), per_image(RI, 1), full((8, d))],
        out_shape=[
            sds(images, RI, 4 * d, bf16), sds(images, RI, d, f32), sds(images, RI, 1, f32),
            sds(8, d, f32),
        ],
        scratch_shapes=[pltpu.VMEM((RI, d), bf16)],
        compiler_params=params(),
        name="attention_backward",
    )(n2g, cotk, branch, kept, normed, proj, mixed, watt, vec, *mask)

    gatt = pl.pallas_call(
        grad_kernel,
        grid=(4,),
        in_specs=[
            pl.BlockSpec((images, RI, d), lambda j: (0, 0, j)),
            whole(images, RI, d), whole(images, RI, d),
        ],
        out_specs=pl.BlockSpec((d, d), lambda j: (j, 0)),
        out_shape=sds(4 * d, d, bf16),
        compiler_params=params(),
        name="attention_grads",
    )(dp, normed, mixed)

    input_gradient, vecg_in = pl.pallas_call(
        input_kernel,
        grid=(images,),
        in_specs=[
            per_image(RI, 4 * d), per_image(RI, 1), per_image(RI, d), per_image(RI, d),
            per_image(length, d), per_image(1, RI), full(watt.shape), full(vec.shape),
        ],
        out_specs=[per_image(length, d), full((8, d))],
        out_shape=[sds(images, length, d, f32), sds(8, d, f32)],
        compiler_params=params(),
        name="input_grad",
    )(dp, rg, resg, kept, cotangent, idx_row, watt, vec)

    block_output = pl.pallas_call(
        output_kernel,
        grid=(images,),
        in_specs=[
            per_image(RI, d), per_image(RI, d), per_image(RI, d), per_image(RI, d),
            per_image(length, d), per_image(1, RI), full(vec.shape),
        ],
        out_specs=per_image(length, d),
        out_shape=sds(images, length, d, bf16),
        compiler_params=params(),
        name="block_output",
    )(out_acc, branch, kept, normed, tokens, idx_row, vec)

    vector_local = jnp.concatenate([vecg_in[:2], vecg[:7], bg.reshape(ff // d, d)], axis=0)
    gatt, feedforward_gradient, vector_gradient = reduce_grads(gatt, gff, vector_local)
    attention_gradient = gatt.T
    attention_new = adamw(
        attention_gradient, attention_first, attention_second,
        attention_weights, attention_average, 0.02, 0.05,
    )
    feedforward_new = adamw(
        feedforward_gradient, feedforward_first, feedforward_second,
        feedforward_weights, feedforward_average, 0.02, 0.05,
    )
    vector_new = adamw(
        vector_gradient, vector_first, vector_second, vector_weights, vector_average, 0.2, 0.0
    )
    return (
        block_output, input_gradient,
        attention_gradient, *attention_new, attention_new[2].astype(bf16),
        feedforward_gradient, *feedforward_new, feedforward_new[2].astype(bf16),
        vector_gradient, *vector_new, vector_gradient[3],
    )


def solution(mesh):
    rows = P(("dp", "mp"), None, None)
    att = P(None, ("dp", "mp"))
    feed = P(None, "dp", "mp")
    in_specs = (rows, rows, P(("dp", "mp"), None)) + (att,) * 4 + (feed,) * 4 + (P(),) * 4
    out_specs = (rows, rows) + (att,) * 6 + (feed,) * 6 + (P(),) * 6
    return jax.shard_map(
        per_device, mesh=mesh, in_specs=in_specs, out_specs=out_specs, check_vma=False
    )
```

```python
import functools

import jax
import jax.numpy as jnp
import numpy as np
from jax import lax
from jax.experimental import pallas as pl
from jax.experimental.pallas import tpu as pltpu
from jax.sharding import PartitionSpec as P

H = 12
HD = 64
LG = 197
LL = 37
KG = LG // 2
KL = LL // 2
LOC = 4 * KL
KEPT = 2 * KG + LOC
RI = -(-KEPT // 16) * 16
SPANS = ((0, KG), (KG, 2 * KG), (2 * KG, KEPT))
UNITS = tuple((a // 16 * 16, -(-b // 16) * 16) for a, b in SPANS)
PAIRS = H // 2
W2L = 2 * HD

bf16 = jnp.bfloat16
f32 = jnp.float32


def params(limit=56, **kw):
    return pltpu.CompilerParams(vmem_limit_bytes=limit << 20, **kw)


def full(shape):
    return pl.BlockSpec(shape, lambda *_: (0,) * len(shape))


def per_image(*shape):
    return pl.BlockSpec((1,) + shape, lambda i, *_: (i,) + (0,) * len(shape))


def nn(a, b):
    return lax.dot_general(a, b, (((1,), (0,)), ((), ())), preferred_element_type=f32)


def nt(a, b):
    return lax.dot_general(a, b, (((1,), (1,)), ((), ())), preferred_element_type=f32)


def tn(a, b):
    return lax.dot_general(a, b, (((0,), (0,)), ((), ())), preferred_element_type=f32)


def normalize(rows):
    center = rows - jnp.mean(rows, axis=-1, keepdims=True)
    spread = jnp.mean(center * center, axis=-1, keepdims=True)
    inverse = lax.rsqrt(spread + 1e-06)
    return center * inverse, inverse


def norm_backward(upstream, standard, inverse, gain):
    scaled = upstream * gain
    return inverse * (
        scaled
        - jnp.mean(scaled, axis=-1, keepdims=True)
        - standard * jnp.mean(scaled * standard, axis=-1, keepdims=True)
    )


def colsum(v):
    return jnp.sum(v, axis=0, keepdims=True)


def masks():
    crop = np.full(RI, -1)
    crop[:KG], crop[KG : 2 * KG] = 0, 1
    for c in range(4):
        crop[2 * KG + c * KL : 2 * KG + (c + 1) * KL] = 2 + c
    adds, valids = [], []
    for (a, b), (lo, hi) in zip(SPANS, UNITS):
        rows = np.arange(lo, hi)
        inside = (rows >= a) & (rows < b)
        same = (crop[lo:hi, None] == crop[None, lo:hi]) & inside[:, None] & inside[None, :]
        adds.append(np.tile(np.where(same, 0.0, -1e9), (1, 2)).astype(np.float32))
        valids.append(np.tile(inside[None, :].astype(np.float32), (8, 2)))
    return [jnp.asarray(m) for m in adds + valids]


def lane_half(shape):
    return lax.broadcasted_iota(jnp.int32, shape, len(shape) - 1) < HD


def split_heads(v, scale):
    first = lane_half(v.shape)
    zero = jnp.zeros_like(v)
    if scale != 1.0:
        v = v * jnp.asarray(scale, v.dtype)
    return jnp.concatenate([jnp.where(first, v, zero), jnp.where(first, zero, v)], axis=0)


def join_heads(v):
    n = v.shape[0] // 2
    return jnp.where(lane_half((n, v.shape[1])), v[:n], v[n:])


def softmax_keys(st, valid):
    p = jnp.exp(st - jnp.max(st, axis=0, keepdims=True))
    return p * (valid / jnp.sum(p, axis=0, keepdims=True))


def store_window(ref, image, lo, hi, last, cols, value, tail):
    value = value.astype(bf16)
    if tail is not None:
        value = jnp.concatenate([value[:16] + tail, value[16:]], axis=0)
    end = hi if last else hi - 16
    ref[image, lo:end, cols] = value[: end - lo]
    return None if last else value[end - lo :]


MESH = pl.DeviceIdType.MESH
ANY = pl.BlockSpec(memory_space=pl.ANY)
MP = 4
CROPS = ((0, LG), (LG, 2 * LG), (2 * LG, 2 * LG + 4 * LL))
ORDER = ((0, 1, 2, 3), (1, 0, 1, 2), (2, 2, 3, 1), (3, 3, 0, 0))


def flip(index, bit):
    return index + bit * (1 - 2 * lax.rem(lax.div(index, bit), 2))


def remote(src, dst, send, recv, to):
    return pltpu.make_async_remote_copy(
        src_ref=src, dst_ref=dst, send_sem=send, recv_sem=recv, device_id=to, device_id_type=MESH
    )


class Sends:
    def __init__(self):
        self.made = []

    def start(self, make, when=None):
        def go():
            make().start()

        go() if when is None else pl.when(when)(go)
        self.made.append((make, when))

    def finish(self):
        for make, when in self.made:
            def wait(make=make):
                make().wait_send()

            wait() if when is None else pl.when(when)(wait)


class Place:
    def __init__(self):
        self.dp = lax.axis_index("dp")
        self.z = lax.axis_index("mp")
        x, y = flip(self.dp, 2), flip(self.dp, 4)
        self.core = (flip(self.dp, 1), self.z)
        self.x, self.y = (x, self.z), (y, self.z)
        self.chips = (self.dp, x, y, flip(x, 4))
        self.mates = tuple(flip(c, 1) for c in self.chips)
        power = (1 + 3 * lax.rem(self.z, 2)) * (1 + 15 * lax.div(self.z, 2))
        self.event = []
        for row in ORDER:
            code = sum(v << (2 * i) for i, v in enumerate(row))
            self.event.append(lax.rem(lax.div(0 * power + code, power), 4))
        self.low, self.high = self.z > 0, self.z < MP - 1
        self.middle = self.low & self.high
        self.line = [lax.rem(self.z + k, MP) for k in range(MP)]
        self.up, self.down = (self.dp, self.z + 1), (self.dp, self.z - 1)
        self.onward = (self.up, self.down, (self.dp, 3 * (self.z - 1)))

    def barrier(self):
        sem = pltpu.get_barrier_semaphore()
        others = [self.core, self.x, self.y]
        others += [(self.dp, k) for k in self.line[1:]]
        for other in others:
            pl.semaphore_signal(sem, inc=1, device_id=other, device_id_type=MESH)
        pl.semaphore_wait(sem, len(others))


def att_block(ref, dp, z, rows):
    return ref.at[pl.ds(pl.multiple_of((dp * MP + z) * rows, 32), rows), :]


def ff_block(ref, dp, z, rows):
    return ref.at[z, :, pl.ds(pl.multiple_of(dp * rows, 32), rows), :]


class Gather:
    ALONG, X, Y, D, C, SLOTS = 0, 4, 8, 12, 16, 32

    def __init__(self, at, tensors, send, recv, local, rows):
        self.at, self.tensors, self.rows = at, tensors, rows
        self.send, self.recv, self.local = send, recv, local
        self.sends = Sends()

    def copy(self, t, base, e, dp, to, own=False):
        mine, out, block = self.tensors[t]
        zb = self.at.event[e]
        dst = block(out, dp, zb, self.rows)
        sems = self.send.at[t, base + zb], self.recv.at[t, base + zb]
        return remote(mine if own else dst, dst, *sems, to)

    def put(self, t, base, e, r, to, own=False, when=None):
        self.sends.start(lambda: self.copy(t, base, e, self.at.chips[r], to, own), when)

    def got(self, t, base, e, dp):
        self.copy(t, base, e, dp, self.at.core).wait_recv()

    def keep(self, t):
        mine, out, block = self.tensors[t]
        return pltpu.make_async_copy(
            mine, block(out, self.at.dp, self.at.z, self.rows), self.local.at[t]
        )

    def spread(self, t, e):
        own = e == 0
        self.put(t, self.X, e, 0, self.at.x, own)
        self.put(t, self.Y, e, 0, self.at.y, own)
        self.put(t, self.C, e, 0, self.at.core, own)

    def begin(self, t):
        at = self.at
        self.keep(t).start()
        self.put(t, self.ALONG, 0, 0, at.up, True, at.high)
        self.put(t, self.ALONG, 0, 0, at.down, True, at.low)
        self.spread(t, 0)

    def along(self, t, e):
        at = self.at
        self.got(t, self.ALONG, e, at.dp)
        self.put(t, self.ALONG, e, 0, at.onward[e - 1], False, at.middle)
        self.spread(t, e)

    def plane(self, t, e):
        at = self.at
        self.got(t, self.X, e, at.chips[1])
        if e % 2 == 0:
            self.put(t, self.D, e, 1, at.y)
        self.put(t, self.C + 4, e, 1, at.core)
        self.got(t, self.Y, e, at.chips[2])
        if e % 2 == 1:
            self.put(t, self.D, e, 2, at.x)
        self.put(t, self.C + 8, e, 2, at.core)

    def corner(self, t, e):
        self.got(t, self.D, e, self.at.chips[3])
        self.put(t, self.C + 12, e, 3, self.at.core)

    def actions(self, t):
        do = lambda f, e: lambda: f(t, e)
        order = [
            (self.along, 1), (self.plane, 0), (self.along, 2), (self.plane, 1), (self.along, 3),
            (self.plane, 2), (self.plane, 3),
        ]
        return [do(f, e) for f, e in order] + [do(self.corner, e) for e in range(4)]

    def finish(self, t):
        for r in range(4):
            for e in range(4):
                self.got(t, self.C + 4 * r, e, self.at.mates[r])
        self.keep(t).wait()


def add_into(target, first, *others):
    step = 32

    @pl.loop(0, first.shape[0] // step)
    def _(i):
        s = pl.ds(pl.multiple_of(i * step, step), step)
        total = first[s, :].astype(f32)
        for ref in others:
            total = total + ref[s, :].astype(f32)
        target[s, :] = total.astype(target.dtype)


class Reduce:
    C, D, X, Y, ALONG, SLOTS = 0, 16, 20, 24, 28, 32

    def __init__(self, at, source, own, parts, bufs, send, recv, load=None):
        self.at, self.source, self.own, self.parts = at, source, own, parts
        self.c, self.d, self.x, self.y, self.line = bufs
        self.send, self.recv, self.load = send, recv, load
        self.sends = Sends()

    def put(self, slot, src, dst, to):
        self.sends.start(
            lambda: remote(src(), dst(), self.send.at[slot], self.recv.at[slot], to)
        )

    def got(self, slot, dst):
        remote(dst, dst, self.send.at[slot], self.recv.at[slot], self.at.core).wait_recv()

    def cross(self, e, r):
        i = 4 * e + r
        self.put(self.C + i, lambda: self.source(e, self.at.mates[r]), lambda: self.c.at[i], self.at.core)
        if self.load is not None:
            self.load(e, r).start()

    def add(self, e, r, *others, target=None):
        i = 4 * e + r
        self.got(self.C + i, self.c.at[i])
        if self.load is not None:
            self.load(e, r).wait()
        refs = [self.own(e, r), self.c.at[i]] + list(others)
        target = refs[0] if target is None else target
        for t, *rest in zip(self.parts(target), *[self.parts(ref) for ref in refs]):
            add_into(t, *rest)

    def corner(self, e):
        at = self.at
        self.add(e, 3)
        to = at.y if e % 2 else at.x
        self.put(self.D + e, lambda: self.own(e, 3), lambda: self.d.at[e], to)
        r, base, buf, to = (2, self.Y, self.y, at.y) if e % 2 else (1, self.X, self.x, at.x)
        self.add(e, r)
        self.put(base + e, lambda: self.own(e, r), lambda: buf.at[e], to)

    def plane(self, e):
        at = self.at
        r, base, buf, to = (1, self.X, self.x, at.x) if e % 2 else (2, self.Y, self.y, at.y)
        self.got(self.D + e, self.d.at[e])
        self.add(e, r, self.d.at[e])
        self.put(base + e, lambda: self.own(e, r), lambda: buf.at[e], to)

    def along(self, e, out=None):
        at = self.at
        self.got(self.X + e, self.x.at[e])
        self.got(self.Y + e, self.y.at[e])
        if e:
            self.add(e, 0, self.x.at[e], self.y.at[e])
            zb = at.event[e]
            self.sends.start(
                lambda: remote(
                    self.own(e, 0), self.line.at[at.z], self.send.at[self.ALONG + zb],
                    self.recv.at[self.ALONG + at.z], (at.dp, zb),
                )
            )
        else:
            lines = []
            for k in range(1, MP):
                zb = at.line[k]
                dst = self.line.at[zb]
                self.got(self.ALONG + zb, dst)
                lines.append(dst)
            self.add(0, 0, self.x.at[0], self.y.at[0], *lines, target=out)


def pump(schedule, step, point):
    for (s, p), action in schedule:
        if p == point:
            pl.when(step == s)(action)


def forward_kernel(
    links, tok_ref, cot_ref, idx_ref, vec_ref, m0_ref, m1_ref, m2_ref, v0_ref, v1_ref, v2_ref,
    att_ref, ff_ref,
    kept_ref, normed_ref, cotk_ref, proj_ref, mixed_ref, branch_ref, resid_ref, n2_ref,
    watt_out, *rest,
):
    if links:
        wff_ref, watt_ref, tok_s, cot_s, load, send, recv, local = rest
    else:
        watt_ref, tok_s, cot_s, load = rest
    step = pl.program_id(0)
    images, _, d = kept_ref.shape
    loads = [
        pltpu.make_async_copy(tok_ref, tok_s, load.at[0]),
        pltpu.make_async_copy(cot_ref, cot_s, load.at[1]),
    ]
    if links:
        at = Place()
        rows = att_ref.shape[0]
        tensors = ((att_ref, watt_ref, att_block), (ff_ref, wff_ref, ff_block))
        gather = Gather(at, tensors, send, recv, local, rows)
        store = pltpu.make_async_copy(watt_ref, watt_out, load.at[2])
        att, feed = gather.actions(0), gather.actions(1)
        spots = [(1, 1), (1, 1), (1, 4), (2, 2), (2, 3), (3, 1), (4, 2), (4, 4), (4, 4), (4, 4), (4, 4)]
        schedule = list(zip(spots, feed))
    else:
        att, schedule = [lambda: None] * 11, []
        fetch = pltpu.make_async_copy(att_ref, watt_ref, load.at[2])

    @pl.when(step == 0)
    def _():
        if links:
            at.barrier()
            gather.begin(0)
        else:
            fetch.start()
        for c in loads:
            c.start()
        offset = 0
        loads[0].wait()
        loads[1].wait()
        for crop, ((a, b), (lo, hi)) in enumerate(zip(CROPS, UNITS)):
            n, k = hi - lo, images * (b - a)
            index = idx_ref[offset : offset + images * n, :]
            offset += images * n
            hot = (lax.broadcasted_iota(jnp.int32, (images * n, k), 1) == index)
            hot = hot.astype(f32).astype(bf16)
            for src, dst in ((tok_s, kept_ref), (cot_s, cotk_ref)):
                got = nn(hot, src[a:b].reshape(k, d)).astype(bf16)
                for i in range(images):
                    part = got[i * n : (i + 1) * n]
                    if crop:
                        dst[i, lo : lo + 16] = dst[i, lo : lo + 16] + part[:16]
                        dst[i, lo + 16 : hi] = part[16:]
                    else:
                        dst[i, lo:hi] = part
            att[crop]()
        for i in range(images):
            standard, _ = normalize(kept_ref[i].astype(f32))
            normed_ref[i] = (standard * vec_ref[0:1] + vec_ref[1:2]).astype(bf16)
            if i == 1:
                att[3]()
        for action in att[4:6]:
            action()
        if links:
            gather.begin(1)
        for action in att[6:]:
            action()
        if links:
            gather.finish(0)
            store.start()
        else:
            fetch.wait()
            done = pltpu.make_async_copy(watt_ref, watt_out, load.at[2])
            done.start()
            done.wait()

    @pl.when(step > 0)
    def _():
        image = step - 1
        normed = normed_ref[image]
        for j, row in ((0, 3), (1, None), (2, 4)):
            part = nt(normed, watt_ref[j * d : (j + 1) * d, :])
            if row is not None:
                part = part + vec_ref[row : row + 1]
            proj_ref[0, :, j * d : (j + 1) * d] = part.astype(bf16)
        pump(schedule, step, 1)
        mrefs, vrefs = (m0_ref, m1_ref, m2_ref), (v0_ref, v1_ref, v2_ref)
        for pair in range(PAIRS):
            cols = lambda j: slice(j * d + pair * W2L, j * d + (pair + 1) * W2L)
            tail = None
            for unit, (lo, hi) in enumerate(UNITS):
                qs = split_heads(proj_ref[0, lo:hi, cols(0)], HD ** -0.5)
                st = nt(proj_ref[0, lo:hi, cols(1)], qs) + mrefs[unit][...]
                pt = softmax_keys(st, vrefs[unit][0:1]).astype(bf16)
                out = join_heads(tn(pt, proj_ref[0, lo:hi, cols(2)]))
                tail = store_window(mixed_ref, 0, lo, hi, unit == 2, cols(0), out, tail)
            if pair == 1:
                pump(schedule, step, 2)
            if pair == 3:
                pump(schedule, step, 3)
        branch = nt(mixed_ref[0], watt_ref[3 * d :, :]) + vec_ref[5:6]
        branch_ref[0] = branch
        residual = kept_ref[image].astype(f32) + router_score(normed, vec_ref) * branch
        resid_ref[0] = residual
        standard, _ = normalize(residual)
        n2_ref[0] = (standard * vec_ref[6:7] + vec_ref[7:8]).astype(bf16)
        pump(schedule, step, 4)

    if links:
        @pl.when(step == images)
        def _():
            gather.finish(1)
            gather.sends.finish()
            store.wait()


def router_score(normed, vec_ref):
    logit = jnp.sum(normed.astype(f32) * vec_ref[2:3], axis=-1, keepdims=True)
    return jax.nn.sigmoid(logit)


def feed_kernel(
    n2_ref, cot_ref, resid_ref, w_ref, bias_ref, vec_ref,
    result_ref, n2g_ref, gff_ref, bg_ref, out_s, act_s, ig_s,
):
    step = pl.program_id(0)
    images = n2_ref.shape[0]
    d, hb = w_ref.shape[2], w_ref.shape[3]
    bg_ref[0] = jnp.zeros((1, hb), f32)

    @pl.when(step == 0)
    def _():
        out_s[...] = resid_ref[...] + vec_ref[8:9]
        n2g_ref[...] = jnp.zeros_like(n2g_ref)

    @pl.loop(0, images)
    def _(i):
        inner = nn(n2_ref[i], w_ref[0, 0]) + bias_ref[0]
        ag = nn(cot_ref[i], w_ref[0, 1])
        phi = 0.5 * (1.0 + lax.erf(inner * 0.7071067811865476))
        act = (inner * phi).astype(bf16)
        slope = phi + inner * jnp.exp(-0.5 * inner * inner) * 0.3989422804014327
        ig = (ag * slope).astype(bf16)
        rows = pl.ds(pl.multiple_of(i * RI, 16), RI)
        act_s[rows, :] = act
        ig_s[rows, :] = ig
        bg_ref[0] += colsum(ig.astype(f32))
        out_s[i] += nt(act, w_ref[0, 1])
        n2g_ref[i] += nt(ig, w_ref[0, 0])

    n2 = n2_ref[...].reshape(images * RI, d)
    cot = cot_ref[...].reshape(images * RI, d)
    gff_ref[0, 0] = tn(n2, ig_s[...]).astype(bf16)
    gff_ref[0, 1] = tn(cot, act_s[...]).astype(bf16)

    @pl.when(step == pl.num_programs(0) - 1)
    def _():
        result_ref[...] = out_s[...].astype(bf16)


def backward_kernel(
    links, n2g_ref, cotk_ref, branch_ref, resid_ref, normed_ref, proj_ref, watt_ref,
    vec_ref, m0_ref, m1_ref, m2_ref, v0_ref, v1_ref, v2_ref, *rest,
):
    if links:
        gff_ref, dp_ref, resg_ref, rg_ref, vecg_ref, gout_ref = rest[:6]
        mg_s, a, c, dd, x, y, line, send, recv, local = rest[6:]
    else:
        dp_ref, resg_ref, rg_ref, vecg_ref, mg_s = rest
    step = pl.program_id(0)
    schedule = []
    if links:
        at = Place()
        rows = gout_ref.shape[1]
        load = lambda e, r: pltpu.make_async_copy(
            ff_block(gff_ref, at.chips[r], at.event[e], rows), a.at[4 * e + r], local.at[4 * e + r]
        )
        reduce = Reduce(
            at, lambda e, dp: ff_block(gff_ref, dp, at.event[e], rows), lambda e, r: a.at[4 * e + r],
            lambda ref: (ref.at[0], ref.at[1]), (c, dd, x, y, line), send, recv, load,
        )

        def cross(e):
            for r in (3, 1, 2, 0):
                reduce.cross(e, r)

        def start():
            at.barrier()
            for e in (3, 2, 1, 0):
                cross(e)

        do = lambda f, e: lambda: f(e)
        schedule = [
            ((0, 0), start),
            ((0, 1), do(reduce.corner, 3)),
            ((0, 3), do(reduce.corner, 2)),
            ((1, 1), do(reduce.plane, 3)),
            ((1, 2), do(reduce.corner, 1)),
            ((2, 0), do(reduce.plane, 2)),
            ((2, 1), do(reduce.along, 3)),
            ((2, 2), do(reduce.corner, 0)),
            ((3, 0), do(reduce.plane, 1)),
            ((3, 2), do(reduce.along, 2)),
        ]

    pump(schedule, step, 0)
    d = normed_ref.shape[2]
    normed = normed_ref[0]
    score = router_score(normed, vec_ref)
    branch = branch_ref[0]
    standard, inverse = normalize(resid_ref[0])
    n2g = n2g_ref[0]
    cot = cotk_ref[0].astype(f32)
    resg = cot + norm_backward(n2g, standard, inverse, vec_ref[6:7])
    resg_ref[0] = resg
    bg = (score * resg).astype(bf16)
    rg = jnp.sum(resg * branch, axis=-1, keepdims=True) * score * (1.0 - score)
    rg_ref[0] = rg
    dp_ref[0, :, 3 * d :] = bg
    mg_s[...] = nn(bg, watt_ref[3 * d :, :]).astype(bf16)
    pump(schedule, step, 1)
    mrefs, vrefs = (m0_ref, m1_ref, m2_ref), (v0_ref, v1_ref, v2_ref)
    for pair in range(PAIRS):
        cols = lambda j: slice(j * d + pair * W2L, j * d + (pair + 1) * W2L)
        tails = [None] * 3
        for unit, (lo, hi) in enumerate(UNITS):
            qs = split_heads(proj_ref[0, lo:hi, cols(0)], HD ** -0.5)
            kk = proj_ref[0, lo:hi, cols(1)]
            pt = softmax_keys(nt(kk, qs) + mrefs[unit][...], vrefs[unit][0:1])
            ds = split_heads(mg_s[lo:hi, cols(0)], 1.0)
            gpt = nt(proj_ref[0, lo:hi, cols(2)], ds)
            sg = (pt * (gpt - jnp.sum(pt * gpt, axis=0, keepdims=True))).astype(bf16)
            grads = (
                join_heads(tn(sg, kk)) * HD ** -0.5, nn(sg, qs), nn(pt.astype(bf16), ds)
            )
            for j in range(3):
                tails[j] = store_window(dp_ref, 0, lo, hi, unit == 2, cols(j), grads[j], tails[j])
        if pair == 1:
            pump(schedule, step, 2)
        if pair == 3:
            pump(schedule, step, 3)
    sums = jnp.concatenate(
        [
            colsum(rg * normed.astype(f32)),
            colsum(dp_ref[0, :, :d].astype(f32)),
            colsum(dp_ref[0, :, 2 * d : 3 * d].astype(f32)),
            colsum(bg.astype(f32)),
            colsum(n2g * standard),
            colsum(n2g),
            colsum(cot),
            jnp.zeros((1, d), f32),
        ],
        axis=0,
    )

    @pl.when(step == 0)
    def _():
        vecg_ref[...] = jnp.zeros_like(vecg_ref)

    vecg_ref[...] += sums
    if links:
        @pl.when(step == pl.num_programs(0) - 1)
        def _():
            reduce.plane(0)
            reduce.along(1)
            reduce.along(0, gout_ref)
            reduce.sends.finish()


def grads_kernel(
    links, dp_ref, normed_ref, mixed_ref, rg_ref, resg_ref, kept_ref, vec_ref, watt_ref, *rest,
):
    if links:
        vecb_ref, bias_ref, high_ref, low_ref, gout_ref, vecout_ref = rest[:6]
        watt_s, gatt_s, vecg_s, load, c, dd, x, y, line, send, recv, vbuf, vsend, vrecv = rest[6:]
    else:
        high_ref, low_ref, gatt_s, vecg_s, watt_s, load = rest
    step = pl.program_id(0)
    images, _, d = normed_ref.shape
    fetch = pltpu.make_async_copy(watt_ref.at[: 3 * d], watt_s, load.at[0])
    schedule = []
    turn = step
    if links:
        at = Place()
        rows = gout_ref.shape[0]
        block = lambda e, dp: att_block(gatt_s, dp, at.event[e], rows)
        reduce = Reduce(
            at, block, lambda e, r: block(e, at.chips[r]), lambda ref: (ref,),
            (c, dd, x, y, line), send, recv,
        )

        def cross(r):
            for e in (3, 2, 1, 0):
                reduce.cross(e, r)

        chip = lax.div(at.dp, 2)
        turn = jnp.where(step == 0, 3 - chip, jnp.where(step == 1, flip(chip, 1), jnp.where(step == 2, flip(chip, 2), chip)))
        do = lambda f, e: lambda: f(e)
        schedule = [
            ((0, 1), do(cross, 3)),
            ((1, 1), do(cross, 1)),
            ((2, 1), do(cross, 2)),
            ((3, 1), do(cross, 0)),
            ((3, 1), do(reduce.corner, 3)),
            ((4, 1), do(reduce.corner, 2)),
            ((4, 1), do(reduce.plane, 3)),
            ((5, 1), do(reduce.corner, 1)),
            ((5, 1), do(reduce.plane, 2)),
            ((6, 1), do(reduce.along, 3)),
            ((6, 1), do(reduce.corner, 0)),
            ((7, 1), do(reduce.plane, 1)),
        ]

    @pl.when(step == 0)
    def _():
        if links:
            at.barrier()
        fetch.start()
        vecg_s[...] = jnp.zeros_like(vecg_s)

    @pl.when(step < 4)
    def _():
        total = images * RI
        left = dp_ref[:, :, pl.ds(pl.multiple_of(turn * d, 128), d)].reshape(total, d)
        where = pl.ds(pl.multiple_of(turn * d, 128), d)

        @pl.when(turn < 3)
        def _():
            gatt_s[where, :] = tn(left, normed_ref[...].reshape(total, d)).astype(bf16)

        @pl.when(turn == 3)
        def _():
            gatt_s[where, :] = tn(left, mixed_ref[...].reshape(total, d)).astype(bf16)

    @pl.when(step == 3)
    def _():
        fetch.wait()

    @pl.when(step > 3)
    def _():
        image = step - 4
        standard, inverse = normalize(kept_ref[image].astype(f32))
        ng = rg_ref[image] * vec_ref[2:3] + nn(dp_ref[image, :, : 3 * d], watt_s[...])
        grad = resg_ref[image] + norm_backward(ng, standard, inverse, vec_ref[0:1])
        high = grad.astype(bf16)
        high_ref[image] = high
        low_ref[image] = (grad - high.astype(f32)).astype(bf16)
        vecg_s[...] += jnp.concatenate([colsum(ng * standard), colsum(ng), jnp.zeros((6, d), f32)], axis=0)

    pump(schedule, step, 1)
    if links:
        @pl.when(step == 3 + images)
        def _():
            vbuf[0, 0:2] = vecg_s[0:2]
            vbuf[0, 2:9] = vecb_ref[0:7]
            vbuf[0, 9:13] = bias_ref[...]
            vbuf[0, 13:16] = jnp.zeros((3, d), f32)
            exchange = lambda k, to: remote(
                vbuf.at[k], vbuf.at[8 + k], vsend.at[k], vrecv.at[k], to
            )
            exchange(0, at.core).start()
            reduce.plane(0)
            exchange(0, at.core).wait()
            vbuf[1] = vbuf[0] + vbuf[8]
            exchange(1, at.x).start()
            reduce.along(2)
            exchange(1, at.x).wait()
            vbuf[2] = vbuf[1] + vbuf[9]
            exchange(2, at.y).start()
            reduce.along(1)
            exchange(2, at.y).wait()
            vbuf[3] = vbuf[2] + vbuf[10]
            lines = [
                lambda k=k: remote(
                    vbuf.at[3], vbuf.at[4 + at.z], vsend.at[2 + k], vrecv.at[3 + at.z],
                    (at.dp, at.line[k]),
                )
                for k in range(1, MP)
            ]
            for make in lines:
                make().start()
            vbuf[4 + at.z] = vbuf[3]
            reduce.along(0, gout_ref)
            for k in range(1, MP):
                zb = at.line[k]
                remote(
                    vbuf.at[3], vbuf.at[4 + zb], vsend.at[2 + k], vrecv.at[3 + zb], at.core
                ).wait_recv()
            total = vbuf[4] + vbuf[5] + vbuf[6] + vbuf[7]
            vecout_ref[...] = total[: vecout_ref.shape[0]]
            for make in lines:
                make().wait_send()
            reduce.sends.finish()
    else:
        @pl.when(step == 3 + images)
        def _():
            pass


def scatter_kernel(
    high_ref, low_ref, result_ref, idx_ref, tok_ref, cot_ref, ing_ref, out_ref,
    tok_s, cot_s, ing_s, out_s, load, store,
):
    images, _, d = high_ref.shape
    loads = []
    for k, (a, b) in enumerate(CROPS):
        for j, (src, dst) in enumerate(((cot_ref, cot_s), (tok_ref, tok_s))):
            c = pltpu.make_async_copy(src.at[a:b], dst.at[a:b], load.at[j, k])
            c.start()
            loads.append(c)
    stores = []
    offset = 0
    for k, ((a, b), (lo, hi)) in enumerate(zip(CROPS, UNITS)):
        n, rows = hi - lo, images * (b - a)
        index = idx_ref[0:1, offset : offset + images * n]
        offset += images * n
        hot = (lax.broadcasted_iota(jnp.int32, (rows, images * n), 0) == index).astype(f32)
        taken = jnp.sum(hot, axis=-1, keepdims=True) > 0.5
        hot = hot.astype(bf16)
        window = lambda ref: jnp.concatenate([ref[i, lo:hi] for i in range(images)], axis=0)
        spread = nn(hot, window(high_ref)) + nn(hot, window(low_ref))
        loads[2 * k].wait()
        old = cot_s[a:b].reshape(rows, d).astype(f32)
        ing_s[a:b] = jnp.where(taken, spread, old).reshape(b - a, images, d)
        stores.append(pltpu.make_async_copy(ing_s.at[a:b], ing_ref.at[a:b], store.at[0, k]))
        stores[-1].start()
        loads[2 * k + 1].wait()
        old = tok_s[a:b].reshape(rows, d).astype(f32)
        new = jnp.where(taken, nn(hot, window(result_ref)), old).astype(bf16)
        out_s[a:b] = new.reshape(b - a, images, d)
        stores.append(pltpu.make_async_copy(out_s.at[a:b], out_ref.at[a:b], store.at[1, k]))
        stores[-1].start()
    for c in stores:
        c.wait()


def adamw(grad, first, second, master, average, rate, decay):
    first_new = 0.5 * first + 0.5 * grad
    second_new = 0.5 * second + 0.5 * grad * grad
    update = first_new / (jnp.sqrt(second_new) + 1e-08)
    master_new = master - rate * (update + decay * master)
    average_new = 0.9 * average + 0.1 * master_new
    return (first_new, second_new, master_new, average_new)


def sds(*shape_dtype):
    return jax.ShapeDtypeStruct(shape_dtype[:-1], shape_dtype[-1])


def window_index(kept_index):
    images = kept_index.shape[0]
    padded = jnp.concatenate([kept_index, jnp.full((images, RI - KEPT), -1, jnp.int32)], axis=1)
    pieces = []
    for (a, b), (s, e), (lo, hi) in zip(CROPS, SPANS, UNITS):
        row = lax.broadcasted_iota(jnp.int32, (images, hi - lo), 1) + lo
        image = lax.broadcasted_iota(jnp.int32, (images, hi - lo), 0)
        place = (padded[:, lo:hi] - a) * images + image
        pieces.append(jnp.where((row >= s) & (row < e), place, -1).reshape(-1))
    return jnp.concatenate(pieces)


def scratch(*shape_dtype):
    return pltpu.VMEM(shape_dtype[:-1], shape_dtype[-1])


def dma(*shape):
    return pltpu.SemaphoreType.DMA(shape)


def per_device(
    tokens, cotangent, kept_index,
    attention_weights, attention_first, attention_second, attention_average,
    feedforward_weights, feedforward_first, feedforward_second, feedforward_average,
    vector_weights, vector_first, vector_second, vector_average,
):
    images, length, d = tokens.shape
    ndp, nmp = lax.axis_size("dp"), lax.axis_size("mp")
    links = (ndp, nmp) == (8, MP)
    vec = vector_weights
    rows, hb = feedforward_weights.shape[1:]
    hidden = nmp * hb
    mask = masks()
    mask_specs = [full(m.shape) for m in mask]
    places = window_index(kept_index)
    index_col, index_row = places[:, None], places[None, :]
    tok, cot = tokens.transpose(1, 0, 2), cotangent.transpose(1, 0, 2)
    comm = (lambda i: dict(collective_id=i, has_side_effects=True)) if links else (lambda i: {})

    att, ff = attention_weights.T.astype(bf16), feedforward_weights.astype(bf16)
    if not links:
        att = lax.all_gather(att, ("dp", "mp"), axis=0, tiled=True)
        wff = lax.all_gather(lax.all_gather(ff, "dp", axis=1, tiled=True), "mp", axis=0)
    now = lambda *s: pl.BlockSpec((1,) + s, lambda i: (jnp.maximum(i - 1, 0), 0, 0))
    whole = lambda *s: pl.BlockSpec(s, lambda j: (0,) * len(s), pipeline_mode=pl.Buffered(1))
    rowspec = (images, RI, d)
    outs = pl.pallas_call(
        functools.partial(forward_kernel, links),
        grid=(1 + images,),
        in_specs=[ANY, ANY, full(index_col.shape), full(vec.shape), *mask_specs, ANY, ANY],
        out_specs=[full(rowspec)] * 3 + [
            now(RI, 3 * d), now(RI, d), now(RI, d), now(RI, d), now(RI, d), ANY,
        ] + [ANY] * links,
        out_shape=[sds(*rowspec, bf16)] * 3 + [
            sds(images, RI, 3 * d, bf16), sds(*rowspec, bf16), sds(*rowspec, f32),
            sds(*rowspec, f32), sds(*rowspec, bf16), sds(4 * d, d, bf16),
        ] + [sds(nmp, 2, d, hb, bf16)] * links,
        scratch_shapes=[
            scratch(4 * d, d, bf16), scratch(length, images, d, bf16), scratch(length, images, d, bf16),
            dma(3),
        ] + ([dma(2, Gather.SLOTS), dma(2, Gather.SLOTS), dma(2)] if links else []),
        compiler_params=params(**comm(0)),
        name="forward",
    )(tok, cot, index_col, vec, *mask, att, ff)
    kept, normed, cotk, proj, mixed, branch, resid, n2, watt = outs[:9]
    if links:
        wff = outs[9]

    bias = vec[9:].reshape(nmp, 1, hb)
    result, n2g, gff, bg = pl.pallas_call(
        feed_kernel,
        grid=(nmp,),
        in_specs=[
            whole(*rowspec), whole(*rowspec), whole(*rowspec),
            pl.BlockSpec((1, 2, d, hb), lambda j: (j, 0, 0, 0)),
            pl.BlockSpec((1, 1, hb), lambda j: (j, 0, 0)),
            full(vec.shape),
        ],
        out_specs=[
            full(rowspec), full(rowspec),
            pl.BlockSpec((1, 2, d, hb), lambda j: (j, 0, 0, 0)),
            pl.BlockSpec((1, 1, hb), lambda j: (j, 0, 0)),
        ],
        out_shape=[
            sds(*rowspec, bf16), sds(*rowspec, f32),
            sds(nmp, 2, d, hb, bf16), sds(nmp, 1, hb, f32),
        ],
        scratch_shapes=[
            scratch(*rowspec, f32), scratch(images * RI, hb, bf16), scratch(images * RI, hb, bf16),
        ],
        compiler_params=params(),
        name="feedforward",
    )(n2, cotk, resid, wff, bias, vec)

    spans = (16, 16, 4, 4, 4, 4)
    outs = pl.pallas_call(
        functools.partial(backward_kernel, links),
        grid=(images,),
        in_specs=[
            per_image(RI, d), per_image(RI, d), per_image(RI, d), per_image(RI, d),
            per_image(RI, d), per_image(RI, 3 * d),
            full(watt.shape), full(vec.shape), *mask_specs,
        ] + [ANY] * links,
        out_specs=[per_image(RI, 4 * d), per_image(RI, d), per_image(RI, 1), full((8, d))]
        + [full((2, rows, hb))] * links,
        out_shape=[
            sds(images, RI, 4 * d, bf16), sds(*rowspec, f32), sds(images, RI, 1, f32), sds(8, d, f32),
        ] + [sds(2, rows, hb, f32)] * links,
        scratch_shapes=[scratch(RI, d, bf16)] + (
            [scratch(n, 2, rows, hb, bf16) for n in spans]
            + [dma(Reduce.SLOTS), dma(Reduce.SLOTS), dma(16)] if links else []
        ),
        compiler_params=params(**comm(1)),
        name="attention_backward",
    )(n2g, cotk, branch, resid, normed, proj, watt, vec, *mask, *([gff] if links else []))
    dp, resg, rg, vecg = outs[:4]
    if links:
        feedforward_gradient = outs[4]

    full_d = (4 * d, d)
    outs = pl.pallas_call(
        functools.partial(grads_kernel, links),
        grid=(4 + images,),
        in_specs=[
            whole(images, RI, 4 * d), whole(*rowspec), whole(*rowspec), whole(images, RI, 1),
            whole(*rowspec), whole(*rowspec), full(vec.shape), ANY,
        ] + [full((8, d)), full((hidden // d, d))] * links,
        out_specs=[full(rowspec), full(rowspec)]
        + ([full((rows, d)), full(vec.shape)] if links else [full(full_d), full((8, d))]),
        out_shape=[sds(*rowspec, bf16), sds(*rowspec, bf16)]
        + ([sds(rows, d, f32), sds(*vec.shape, f32)] if links else [sds(*full_d, bf16), sds(8, d, f32)]),
        scratch_shapes=[scratch(3 * d, d, bf16)] + (
            [scratch(*full_d, bf16), scratch(8, d, f32), dma(1)]
            + [scratch(n, rows, d, bf16) for n in spans[1:]]
            + [dma(Reduce.SLOTS), dma(Reduce.SLOTS), scratch(11, 16, d, f32), dma(8), dma(8)]
            if links else [dma(1)]
        ),
        compiler_params=params(**comm(2)),
        name="attention_grads",
    )(
        dp, normed, mixed, rg, resg, kept, vec, watt,
        *([vecg, bg.reshape(hidden // d, d)] if links else []),
    )
    high, low = outs[:2]
    if links:
        gatt, vector_gradient = outs[2:]
    else:
        gatt, vecg_in = outs[2:]
        local = jnp.concatenate([vecg_in[:2], vecg[:7], bg.reshape(hidden // d, d)], axis=0)
        gatt = lax.psum_scatter(gatt, ("dp", "mp"), scatter_dimension=0, tiled=True).astype(f32)
        gff = lax.psum_scatter(gff, "mp", scatter_dimension=0, tiled=False)
        gff = lax.psum_scatter(gff, "dp", scatter_dimension=1, tiled=True)
        feedforward_gradient, vector_gradient = gff.astype(f32), lax.psum(local, ("dp", "mp"))

    ing, out = pl.pallas_call(
        scatter_kernel,
        in_specs=[pl.BlockSpec(memory_space=pltpu.VMEM)] * 4 + [ANY, ANY],
        out_specs=[ANY, ANY],
        out_shape=[sds(length, images, d, f32), sds(length, images, d, bf16)],
        scratch_shapes=[
            scratch(length, images, d, bf16), scratch(length, images, d, bf16),
            scratch(length, images, d, f32), scratch(length, images, d, bf16), dma(2, 3), dma(2, 3),
        ],
        compiler_params=params(),
        name="scatter_rows",
    )(high, low, result, index_row, tok, cot)
    input_gradient, block_output = ing.transpose(1, 0, 2), out.transpose(1, 0, 2)

    attention_gradient = gatt.T
    attention_new = adamw(
        attention_gradient, attention_first, attention_second,
        attention_weights, attention_average, 0.02, 0.05,
    )
    feedforward_new = adamw(
        feedforward_gradient, feedforward_first, feedforward_second,
        feedforward_weights, feedforward_average, 0.02, 0.05,
    )
    vector_new = adamw(
        vector_gradient, vector_first, vector_second, vector_weights, vector_average, 0.2, 0.0
    )
    return (
        block_output, input_gradient,
        attention_gradient, *attention_new, attention_new[2].astype(bf16),
        feedforward_gradient, *feedforward_new, feedforward_new[2].astype(bf16),
        vector_gradient, *vector_new, vector_gradient[3],
    )


def solution(mesh):
    rows = P(("dp", "mp"), None, None)
    att = P(None, ("dp", "mp"))
    feed = P(None, "dp", "mp")
    in_specs = (rows, rows, P(("dp", "mp"), None)) + (att,) * 4 + (feed,) * 4 + (P(),) * 4
    out_specs = (rows, rows) + (att,) * 6 + (feed,) * 6 + (P(),) * 6
    return jax.shard_map(
        per_device, mesh=mesh, in_specs=in_specs, out_specs=out_specs, check_vma=False
    )
```

```python
import functools

import jax
import jax.numpy as jnp
import numpy as np
from jax import lax
from jax.experimental import pallas as pl
from jax.experimental.pallas import tpu as pltpu
from jax.sharding import PartitionSpec as P

H = 12
HD = 64
LG = 197
LL = 37
KG = LG // 2
KL = LL // 2
LOC = 4 * KL
KEPT = 2 * KG + LOC
RI = -(-KEPT // 16) * 16
SPANS = ((0, KG), (KG, 2 * KG), (2 * KG, KEPT))
UNITS = tuple((a // 16 * 16, -(-b // 16) * 16) for a, b in SPANS)
PAIRS = H // 2
W2L = 2 * HD

bf16 = jnp.bfloat16
f32 = jnp.float32


def params(limit=56, **kw):
    return pltpu.CompilerParams(vmem_limit_bytes=limit << 20, **kw)


def full(shape):
    return pl.BlockSpec(shape, lambda *_: (0,) * len(shape))


def per_image(*shape):
    return pl.BlockSpec((1,) + shape, lambda i, *_: (i,) + (0,) * len(shape))


def nn(a, b):
    return lax.dot_general(a, b, (((1,), (0,)), ((), ())), preferred_element_type=f32)


def nt(a, b):
    return lax.dot_general(a, b, (((1,), (1,)), ((), ())), preferred_element_type=f32)


def tn(a, b):
    return lax.dot_general(a, b, (((0,), (0,)), ((), ())), preferred_element_type=f32)


def normalize(rows):
    center = rows - jnp.mean(rows, axis=-1, keepdims=True)
    spread = jnp.mean(center * center, axis=-1, keepdims=True)
    inverse = lax.rsqrt(spread + 1e-06)
    return center * inverse, inverse


def norm_backward(upstream, standard, inverse, gain):
    scaled = upstream * gain
    return inverse * (
        scaled
        - jnp.mean(scaled, axis=-1, keepdims=True)
        - standard * jnp.mean(scaled * standard, axis=-1, keepdims=True)
    )


def colsum(v):
    return jnp.sum(v, axis=0, keepdims=True)


def masks():
    crop = np.full(RI, -1)
    crop[:KG], crop[KG : 2 * KG] = 0, 1
    for c in range(4):
        crop[2 * KG + c * KL : 2 * KG + (c + 1) * KL] = 2 + c
    adds, valids = [], []
    for (a, b), (lo, hi) in zip(SPANS, UNITS):
        rows = np.arange(lo, hi)
        inside = (rows >= a) & (rows < b)
        same = (crop[lo:hi, None] == crop[None, lo:hi]) & inside[:, None] & inside[None, :]
        adds.append(np.tile(np.where(same, 0.0, -1e9), (1, 2)).astype(np.float32))
        valids.append(np.tile(inside[None, :].astype(np.float32), (8, 2)))
    return [jnp.asarray(m) for m in adds + valids]


def lane_half(shape):
    return lax.broadcasted_iota(jnp.int32, shape, len(shape) - 1) < HD


def split_heads(v, scale):
    first = lane_half(v.shape)
    zero = jnp.zeros_like(v)
    if scale != 1.0:
        v = v * jnp.asarray(scale, v.dtype)
    return jnp.concatenate([jnp.where(first, v, zero), jnp.where(first, zero, v)], axis=0)


def join_heads(v):
    n = v.shape[0] // 2
    return jnp.where(lane_half((n, v.shape[1])), v[:n], v[n:])


def softmax_keys(st, valid):
    p = jnp.exp(st - jnp.max(st, axis=0, keepdims=True))
    return p * (valid / jnp.sum(p, axis=0, keepdims=True))


def store_window(ref, image, lo, hi, last, cols, value, tail):
    value = value.astype(bf16)
    if tail is not None:
        value = jnp.concatenate([value[:16] + tail, value[16:]], axis=0)
    end = hi if last else hi - 16
    ref[image, lo:end, cols] = value[: end - lo]
    return None if last else value[end - lo :]


MESH = pl.DeviceIdType.MESH
ANY = pl.BlockSpec(memory_space=pl.ANY)
MP = 4
CROPS = ((0, LG), (LG, 2 * LG), (2 * LG, 2 * LG + 4 * LL))
ORDER = ((0, 1, 2, 3), (1, 0, 1, 2), (2, 2, 3, 1), (3, 3, 0, 0))


def flip(index, bit):
    return index + bit * (1 - 2 * lax.rem(lax.div(index, bit), 2))


def remote(src, dst, send, recv, to):
    return pltpu.make_async_remote_copy(
        src_ref=src, dst_ref=dst, send_sem=send, recv_sem=recv, device_id=to, device_id_type=MESH
    )


class Sends:
    def __init__(self):
        self.made = []

    def start(self, make, when=None):
        def go():
            make().start()

        go() if when is None else pl.when(when)(go)
        self.made.append((make, when))

    def finish(self):
        for make, when in self.made:
            def wait(make=make):
                make().wait_send()

            wait() if when is None else pl.when(when)(wait)


class Place:
    def __init__(self):
        self.dp = lax.axis_index("dp")
        self.z = lax.axis_index("mp")
        x, y = flip(self.dp, 2), flip(self.dp, 4)
        self.core = (flip(self.dp, 1), self.z)
        self.x, self.y = (x, self.z), (y, self.z)
        self.chips = (self.dp, x, y, flip(x, 4))
        self.mates = tuple(flip(c, 1) for c in self.chips)
        power = (1 + 3 * lax.rem(self.z, 2)) * (1 + 15 * lax.div(self.z, 2))
        self.event = []
        for row in ORDER:
            code = sum(v << (2 * i) for i, v in enumerate(row))
            self.event.append(lax.rem(lax.div(0 * power + code, power), 4))
        self.low, self.high = self.z > 0, self.z < MP - 1
        self.middle = self.low & self.high
        self.line = [lax.rem(self.z + k, MP) for k in range(MP)]
        self.up, self.down = (self.dp, self.z + 1), (self.dp, self.z - 1)
        self.onward = (self.up, self.down, (self.dp, 3 * (self.z - 1)))

    def barrier(self):
        sem = pltpu.get_barrier_semaphore()
        others = [self.core, self.x, self.y]
        others += [(self.dp, k) for k in self.line[1:]]
        for other in others:
            pl.semaphore_signal(sem, inc=1, device_id=other, device_id_type=MESH)
        pl.semaphore_wait(sem, len(others))


def att_block(ref, dp, z, rows):
    return ref.at[pl.ds(pl.multiple_of((dp * MP + z) * rows, 32), rows), :]


def ff_block(ref, dp, z, rows):
    return ref.at[z, :, pl.ds(pl.multiple_of(dp * rows, 32), rows), :]


class Gather:
    ALONG, X, Y, D, C, SLOTS = 0, 4, 8, 12, 16, 32

    def __init__(self, at, first, place, send, recv, local):
        self.at, self.first, self.place = at, first, place
        self.send, self.recv, self.local = send, recv, local
        self.sends = Sends()

    def copy(self, slot, e, r, to):
        slot = self.ALONG + self.at.event[e] if slot is None else slot
        dst = self.place(e, self.at.chips[r])
        src = self.first(e) if r == 0 else dst
        return remote(src, dst, self.send.at[slot], self.recv.at[slot], to)

    def put(self, slot, e, r, to, when=None):
        self.sends.start(lambda: self.copy(slot, e, r, to), when)

    def got(self, slot, e, dp):
        dst = self.place(e, dp)
        remote(dst, dst, self.send.at[slot], self.recv.at[slot], self.at.core).wait_recv()

    def keep(self, e):
        return pltpu.make_async_copy(self.first(e), self.place(e, self.at.dp), self.local.at[e])

    def spread(self, e):
        self.put(self.X + e, e, 0, self.at.x)
        self.put(self.Y + e, e, 0, self.at.y)
        self.put(self.C + 4 * e, e, 0, self.at.core)

    def begin(self):
        at = self.at
        self.keep(0).start()
        for to, when in ((at.up, at.high), (at.down, at.low)):
            self.put(None, 0, 0, to, when)
        self.spread(0)

    def direct(self):
        self.keep(0).start()
        for zb in self.at.line[1:]:
            self.put(None, 0, 0, (self.at.dp, zb))

    def arrived(self, e):
        self.got(self.ALONG + self.at.event[e], e, self.at.dp)

    def along(self, e):
        at = self.at
        self.arrived(e)
        self.put(None, e, 0, at.onward[e - 1], at.middle)
        self.spread(e)

    def plane(self, e):
        at = self.at
        self.got(self.X + e, e, at.chips[1])
        if e % 2 == 0:
            self.put(self.D + e, e, 1, at.y)
        self.put(self.C + 4 * e + 1, e, 1, at.core)
        self.got(self.Y + e, e, at.chips[2])
        if e % 2 == 1:
            self.put(self.D + e, e, 2, at.x)
        self.put(self.C + 4 * e + 2, e, 2, at.core)

    def corner(self, e):
        self.got(self.D + e, e, self.at.chips[3])
        self.put(self.C + 4 * e + 3, e, 3, self.at.core)

    def finish(self, e):
        for r in range(4):
            self.got(self.C + 4 * e + r, e, self.at.mates[r])


def add_into(target, first, *others):
    if len(others) == 1 and target.dtype == bf16:
        target[...] = first[...] + others[0][...]
        return
    step = 48

    @pl.loop(0, first.shape[0] // step)
    def _(i):
        s = pl.ds(pl.multiple_of(i * step, step), step)
        total = first[s, :].astype(f32)
        for ref in others:
            total = total + ref[s, :].astype(f32)
        target[s, :] = total.astype(target.dtype)


class Reduce:
    C, D, X, Y, ALONG, SLOTS = 0, 16, 20, 24, 28, 32

    def __init__(self, at, source, own, parts, bufs, send, recv, load=None, base=0):
        self.at, self.source, self.own, self.parts, self.base = at, source, own, parts, base
        self.c, self.d, self.x, self.y, self.line = bufs
        self.send, self.recv, self.load = send, recv, load
        self.sends = Sends()

    def put(self, slot, src, dst, to):
        self.sends.start(
            lambda: remote(src(), dst(), self.send.at[slot], self.recv.at[slot], to)
        )

    def got(self, slot, dst):
        remote(dst, dst, self.send.at[slot], self.recv.at[slot], self.at.core).wait_recv()

    def slot(self, e, r):
        return 4 * (e - self.base) + r

    def cross(self, e, r):
        i = self.slot(e, r)
        self.put(self.C + i, lambda: self.source(e, self.at.mates[r]), lambda: self.c.at[i], self.at.core)
        if self.load is not None:
            self.load(e, r).start()

    def add(self, e, r, *others, target=None):
        i = self.slot(e, r)
        self.got(self.C + i, self.c.at[i])
        if self.load is not None:
            self.load(e, r).wait()
        refs = [self.own(e, r), self.c.at[i]] + list(others)
        self.total(refs[0] if target is None else target, *refs)

    def total(self, target, *refs):
        for t, *rest in zip(self.parts(target), *[self.parts(ref) for ref in refs]):
            add_into(t, *rest)

    def corner(self, e):
        at, i = self.at, e - self.base
        self.add(e, 3)
        self.put(
            self.D + i, lambda: self.own(e, 3), lambda: self.d.at[i], at.x if e % 2 else at.y
        )
        r, slot, buf, to = (1, self.X, self.x, at.x) if e % 2 else (2, self.Y, self.y, at.y)
        self.add(e, r)
        self.put(slot + i, lambda: self.own(e, r), lambda: buf.at[i], to)

    def plane(self, e):
        at, i = self.at, e - self.base
        r, slot, buf, to = (2, self.Y, self.y, at.y) if e % 2 else (1, self.X, self.x, at.x)
        self.got(self.D + i, self.d.at[i])
        self.add(e, r, self.d.at[i])
        self.put(slot + i, lambda: self.own(e, r), lambda: buf.at[i], to)

    def gathered(self, e, *others, target=None):
        i = e - self.base
        self.got(self.X + i, self.x.at[i])
        self.got(self.Y + i, self.y.at[i])
        self.add(e, 0, self.x.at[i], self.y.at[i], *others, target=target)

    def send_along(self, e, src):
        at = self.at
        zb = at.event[e]
        self.sends.start(
            lambda: remote(
                src(), self.line.at[at.z], self.send.at[self.ALONG + zb],
                self.recv.at[self.ALONG + at.z], (at.dp, zb),
            )
        )

    def along(self, e):
        self.gathered(e)
        self.send_along(e, lambda: self.own(e, 0))

    def lines(self):
        got = []
        for zb in self.at.line[1:]:
            got.append(self.line.at[zb])
            self.got(self.ALONG + zb, got[-1])
        return got


def pump(schedule, step, point):
    for (s, p), action in schedule:
        if isinstance(point, int):
            if p == point:
                pl.when(step == s)(action)
        else:
            pl.when((step == s) & (point == p))(action)


def do(action, *args):
    return lambda: action(*args)


def forward_kernel(
    links, tok_ref, cot_ref, idx_ref, vec_ref, m0_ref, m1_ref, m2_ref, v0_ref, v1_ref, v2_ref,
    att_ref, ff_ref,
    kept_ref, normed_ref, cotk_ref, proj_ref, mixed_ref, branch_ref, resid_ref, n2_ref,
    watt_out, *rest,
):
    if links:
        wff_ref, watt_ref, tok_s, cot_s, load, att_s, ff_s, send, recv, local = rest
    else:
        watt_ref, tok_s, cot_s, load = rest
    step = pl.program_id(0)
    images, _, d = kept_ref.shape
    loads = [
        pltpu.make_async_copy(tok_ref, tok_s, load.at[0]),
        pltpu.make_async_copy(cot_ref, cot_s, load.at[1]),
    ]
    acts, schedule = [[]] * 6, []
    if links:
        at = Place()
        rows = att_ref.shape[0]
        att = Gather(
            at, lambda e: att_block(watt_ref, at.dp, at.event[e], rows) if e else att_s,
            lambda e, dp: att_block(watt_ref, dp, at.event[e], rows),
            send.at[0], recv.at[0], local.at[0],
        )
        feed = Gather(
            at, lambda e: ff_block(wff_ref, at.dp, at.event[e], rows) if e else ff_s,
            lambda e, dp: ff_block(wff_ref, dp, at.event[e], rows),
            send.at[1], recv.at[1], local.at[1],
        )
        acts = [
            [do(att.along, 1), do(att.along, 2)],
            [],
            [do(att.along, 3), feed.direct, do(att.plane, 2)],
            [do(att.plane, 1)],
            [],
            [do(att.plane, 0), do(att.plane, 3)] + [do(att.corner, e) for e in (0, 3, 2, 1)],
        ]
        schedule = [
            ((2, 0), do(feed.arrived, 2)),
            ((2, 0), do(feed.spread, 2)),
            ((2, 1), do(feed.arrived, 3)),
            ((2, 1), do(feed.spread, 3)),
            ((3, 3), do(feed.plane, 2)),
            ((4, 0), do(feed.plane, 3)),
        ]
    else:
        fetch = pltpu.make_async_copy(att_ref, watt_ref, load.at[2])
    store = pltpu.make_async_copy(watt_ref, watt_out, load.at[2])

    @pl.when(step == 0)
    def _():
        if links:
            att_s[...] = att_ref[...].astype(bf16)
            at.barrier()
            att.begin()
        else:
            fetch.start()
        for c in loads:
            c.start()
        if links:
            ff_s[...] = ff_ref[...].astype(bf16)
        offset = 0
        run = lambda point: [action() for action in acts[point]]
        run(0)
        loads[0].wait()
        loads[1].wait()
        for crop, ((a, b), (lo, hi)) in enumerate(zip(CROPS, UNITS)):
            n, k = hi - lo, images * (b - a)
            index = idx_ref[offset : offset + images * n, :]
            offset += images * n
            hot = (lax.broadcasted_iota(jnp.int32, (images * n, k), 1) == index)
            hot = hot.astype(f32).astype(bf16)
            for src, dst in ((tok_s, kept_ref), (cot_s, cotk_ref)):
                got = nn(hot, src[a:b].reshape(k, d)).astype(bf16)
                for i in range(images):
                    part = got[i * n : (i + 1) * n]
                    if crop:
                        dst[i, lo : lo + 16] = dst[i, lo : lo + 16] + part[:16]
                        dst[i, lo + 16 : hi] = part[16:]
                    else:
                        dst[i, lo:hi] = part
            run(1 + crop)
        for i in range(images):
            standard, _ = normalize(kept_ref[i].astype(f32))
            normed_ref[i] = (standard * vec_ref[0:1] + vec_ref[1:2]).astype(bf16)
            if i == 1:
                run(4)
        run(5)
        if links:
            for e in range(4):
                att.finish(e)
            att.keep(0).wait()
        else:
            fetch.wait()
        store.start()

    pump(schedule, step, 0)

    @pl.when(step > 0)
    def _():
        image = step - 1
        normed = normed_ref[image]
        for j, row in ((0, 3), (1, None), (2, 4)):
            part = nt(normed, watt_ref[j * d : (j + 1) * d, :])
            if row is not None:
                part = part + vec_ref[row : row + 1]
            proj_ref[0, :, j * d : (j + 1) * d] = part.astype(bf16)
        pump(schedule, step, 1)
        mrefs, vrefs = (m0_ref, m1_ref, m2_ref), (v0_ref, v1_ref, v2_ref)
        for pair in range(PAIRS):
            cols = lambda j: slice(j * d + pair * W2L, j * d + (pair + 1) * W2L)
            tail = None
            for unit, (lo, hi) in enumerate(UNITS):
                qs = split_heads(proj_ref[0, lo:hi, cols(0)], HD ** -0.5)
                st = nt(proj_ref[0, lo:hi, cols(1)], qs) + mrefs[unit][...]
                pt = softmax_keys(st, vrefs[unit][0:1]).astype(bf16)
                out = join_heads(tn(pt, proj_ref[0, lo:hi, cols(2)]))
                tail = store_window(mixed_ref, 0, lo, hi, unit == 2, cols(0), out, tail)
            if pair == 2:
                pump(schedule, step, 3)
        branch = nt(mixed_ref[0], watt_ref[3 * d :, :]) + vec_ref[5:6]
        branch_ref[0] = branch
        residual = kept_ref[image].astype(f32) + router_score(normed, vec_ref) * branch
        resid_ref[0] = residual
        standard, _ = normalize(residual)
        n2_ref[0] = (standard * vec_ref[6:7] + vec_ref[7:8]).astype(bf16)

    @pl.when(step == images)
    def _():
        if links:
            feed.corner(2)
            feed.corner(3)
            feed.finish(2)
            feed.finish(3)
            feed.arrived(1)
            feed.keep(0).wait()
            att.sends.finish()
            feed.sends.finish()
        store.wait()


def router_score(normed, vec_ref):
    logit = jnp.sum(normed.astype(f32) * vec_ref[2:3], axis=-1, keepdims=True)
    return jax.nn.sigmoid(logit)


def feed_kernel(
    links, n2_ref, cot_ref, resid_ref, w_ref, bias_ref, vec_ref,
    result_ref, n2g_ref, gff_ref, bg_ref, *rest,
):
    if links:
        acc_ref, out_s, act_s, ig_s, w_s, g_s, load, store = rest[:8]
        send, recv, local, a, c, dd, x, y, rsend, rrecv, rlocal = rest[8:]
    else:
        out_s, act_s, ig_s, w_s, g_s, load, store = rest
    step = pl.program_id(0)
    last = pl.num_programs(0) - 1
    images, _, d = n2_ref.shape
    hb = w_ref.shape[3]
    block, schedule = step, []
    if links:
        at = Place()
        rows = acc_ref.shape[2]
        block = at.event[0]
        for e in (1, 2, 3):
            block = jnp.where(step == 3 - e, at.event[e], block)
        gather = Gather(
            at, lambda e: ff_block(w_ref, at.dp, at.event[e], rows),
            lambda e, dp: w_s.at[3 - e, :, pl.ds(pl.multiple_of(dp * rows, 32), rows), :],
            send, recv, local,
        )
        reduce = Reduce(
            at, lambda e, dp: ff_block(gff_ref, dp, at.event[e], rows),
            lambda e, r: a.at[4 * (e - 2) + r],
            lambda ref: (ref.at[0], ref.at[1]), (c, dd, x, y, None), rsend, rrecv,
            lambda e, r: pltpu.make_async_copy(
                ff_block(gff_ref, at.chips[r], at.event[e], rows), a.at[4 * (e - 2) + r],
                rlocal.at[4 * (e - 2) + r],
            ),
            2,
        )

        def start():
            at.barrier()
            for e in (1, 0):
                gather.spread(e)
                gather.keep(e).start()

        def ready(e):
            gather.finish(e)
            gather.keep(e).wait()

        def cross(e):
            for r in (3, 1, 2, 0):
                reduce.cross(e, r)

        schedule = [
            ((1, 0), do(gather.plane, 1)),
            ((1, 3), do(gather.plane, 0)),
            ((1, 4), do(cross, 3)),
            ((2, 0), do(gather.corner, 1)),
            ((2, 0), do(reduce.corner, 3)),
            ((2, 0), do(cross, 2)),
            ((2, 0), do(ready, 1)),
            ((2, 2), do(reduce.corner, 2)),
            ((2, 2), do(gather.corner, 0)),
            ((2, 5), do(reduce.plane, 3)),
            ((3, 0), do(ready, 0)),
            ((3, 0), do(reduce.plane, 2)),
        ]

    def fetch(e):
        return pltpu.make_async_copy(
            w_ref.at[at.event[3 - e] if links else e], w_s.at[e], load.at[e]
        )

    def save(slot, which):
        return pltpu.make_async_copy(g_s.at[slot], gff_ref.at[which], store.at[slot])

    early = (0, 1) if links else range(w_s.shape[0])

    @pl.when(step == 0)
    def _():
        for e in early:
            fetch(e).start()
        if links:
            start()
        out_s[...] = resid_ref[...] + vec_ref[8:9]
        n2g_ref[...] = jnp.zeros_like(n2g_ref)
        bg_ref[...] = jnp.zeros_like(bg_ref)
        fetch(0).wait()

    for e in early[1:]:
        @pl.when(step == e)
        def _(e=e):
            fetch(e).wait()

    slot = lax.rem(step, 2)

    @pl.when(step > 0)
    def _():
        save(1 - slot, 0).wait()

    pump(schedule, step, 0)

    @pl.loop(0, images)
    def _(i):
        pump(schedule, step, i + 1)
        inner = nn(n2_ref[i], w_s[step, 0]) + bias_ref[block]
        ag = nn(cot_ref[i], w_s[step, 1])
        phi = 0.5 * (1.0 + lax.erf(inner * 0.7071067811865476))
        act = (inner * phi).astype(bf16)
        slope = phi + inner * jnp.exp(-0.5 * inner * inner) * 0.3989422804014327
        ig = (ag * slope).astype(bf16)
        rows_i = pl.ds(pl.multiple_of(i * RI, 16), RI)
        act_s[rows_i, :] = act
        ig_s[rows_i, :] = ig
        bg_ref[block] += colsum(ig.astype(f32))
        out_s[i] += nt(act, w_s[step, 1])
        n2g_ref[i] += nt(ig, w_s[step, 0])

    pump(schedule, step, 5)
    n2 = n2_ref[...].reshape(images * RI, d)
    cot = cot_ref[...].reshape(images * RI, d)
    g_s[slot, 0] = tn(n2, ig_s[...]).astype(bf16)
    g_s[slot, 1] = tn(cot, act_s[...]).astype(bf16)
    save(slot, block).start()

    @pl.when(step == last)
    def _():
        result_ref[...] = out_s[...].astype(bf16)
        if links:
            reduce.gathered(3, target=acc_ref.at[0])
            reduce.gathered(2, target=acc_ref.at[1])
            gather.sends.finish()
            reduce.sends.finish()
        save(slot, 0).wait()


def backward_kernel(
    links, n2g_ref, cotk_ref, branch_ref, resid_ref, normed_ref, proj_ref, watt_ref,
    vec_ref, m0_ref, m1_ref, m2_ref, v0_ref, v1_ref, v2_ref, *rest,
):
    if links:
        gff_ref, acc_ref, dp_ref, resg_ref, rg_ref, vecg_ref, gout_ref = rest[:7]
        mg_s, a, c, dd, x, y, line, send, recv, local = rest[7:]
    else:
        dp_ref, resg_ref, rg_ref, vecg_ref, mg_s = rest
    step = pl.program_id(0)
    schedule = []
    if links:
        at = Place()
        rows = gout_ref.shape[1]
        reduce = Reduce(
            at, lambda e, dp: ff_block(gff_ref, dp, at.event[e], rows),
            lambda e, r: a.at[4 * e + r],
            lambda ref: (ref.at[0], ref.at[1]), (c, dd, x, y, line), send, recv,
            lambda e, r: pltpu.make_async_copy(
                ff_block(gff_ref, at.chips[r], at.event[e], rows), a.at[4 * e + r],
                local.at[4 * e + r],
            ),
        )

        def start():
            at.barrier()
            reduce.send_along(2, lambda: acc_ref.at[1])
            for e in (1, 0):
                for r in (3, 1, 2, 0):
                    reduce.cross(e, r)

        schedule = [
            ((0, 0), start),
            ((0, 1), do(reduce.corner, 1)),
            ((0, 3), do(reduce.send_along, 3, lambda: acc_ref.at[0])),
            ((1, 1), do(reduce.plane, 1)),
            ((1, 3), do(reduce.corner, 0)),
            ((2, 1), do(reduce.along, 1)),
            ((3, 0), do(reduce.plane, 0)),
        ]

    pump(schedule, step, 0)
    d = normed_ref.shape[2]
    normed = normed_ref[0]
    score = router_score(normed, vec_ref)
    branch = branch_ref[0]
    standard, inverse = normalize(resid_ref[0])
    n2g = n2g_ref[0]
    cot = cotk_ref[0].astype(f32)
    resg = cot + norm_backward(n2g, standard, inverse, vec_ref[6:7])
    resg_ref[0] = resg
    bg = (score * resg).astype(bf16)
    rg = jnp.sum(resg * branch, axis=-1, keepdims=True) * score * (1.0 - score)
    rg_ref[0] = rg
    dp_ref[0, :, 3 * d :] = bg
    mg_s[...] = nn(bg, watt_ref[3 * d :, :]).astype(bf16)
    pump(schedule, step, 1)
    mrefs, vrefs = (m0_ref, m1_ref, m2_ref), (v0_ref, v1_ref, v2_ref)
    for pair in range(PAIRS):
        cols = lambda j: slice(j * d + pair * W2L, j * d + (pair + 1) * W2L)
        tails = [None] * 3
        for unit, (lo, hi) in enumerate(UNITS):
            qs = split_heads(proj_ref[0, lo:hi, cols(0)], HD ** -0.5)
            kk = proj_ref[0, lo:hi, cols(1)]
            pt = softmax_keys(nt(kk, qs) + mrefs[unit][...], vrefs[unit][0:1])
            ds = split_heads(mg_s[lo:hi, cols(0)], 1.0)
            gpt = nt(proj_ref[0, lo:hi, cols(2)], ds)
            sg = (pt * (gpt - jnp.sum(pt * gpt, axis=0, keepdims=True))).astype(bf16)
            grads = (
                join_heads(tn(sg, kk)) * HD ** -0.5, nn(sg, qs), nn(pt.astype(bf16), ds)
            )
            for j in range(3):
                tails[j] = store_window(dp_ref, 0, lo, hi, unit == 2, cols(j), grads[j], tails[j])
        if pair == 2:
            pump(schedule, step, 3)
    sums = jnp.concatenate(
        [
            colsum(rg * normed.astype(f32)),
            colsum(dp_ref[0, :, :d].astype(f32)),
            colsum(dp_ref[0, :, 2 * d : 3 * d].astype(f32)),
            colsum(bg.astype(f32)),
            colsum(n2g * standard),
            colsum(n2g),
            colsum(cot),
            jnp.zeros((1, d), f32),
        ],
        axis=0,
    )

    @pl.when(step == 0)
    def _():
        vecg_ref[...] = jnp.zeros_like(vecg_ref)

    vecg_ref[...] += sums
    if links:
        @pl.when(step == pl.num_programs(0) - 1)
        def _():
            reduce.gathered(0, *reduce.lines(), target=gout_ref)
            reduce.sends.finish()


def grads_kernel(
    links, dp_ref, normed_ref, mixed_ref, rg_ref, resg_ref, kept_ref, vec_ref, watt_ref, *rest,
):
    if links:
        vecb_ref, bias_ref, high_ref, low_ref, gout_ref, vecout_ref = rest[:6]
        gatt_s, vecg_s, watt_s, dp_s, act_s, resg_s, kept_s, load = rest[6:14]
        c, dd, x, y, line, send, recv, vbuf, vsend, vrecv = rest[14:]
    else:
        high_ref, low_ref, gatt_s, vecg_s, watt_s, dp_s, act_s, resg_s, kept_s, load = rest
    step = pl.program_id(0)
    images, _, d = high_ref.shape
    last = 3 + images
    total = images * RI
    chip, schedule = 0, []
    if links:
        at = Place()
        chip = lax.div(at.dp, 2)
        rows = gout_ref.shape[0]
        block = lambda e, dp: att_block(gatt_s, dp, at.event[e], rows)
        reduce = Reduce(
            at, block, lambda e, r: block(e, at.chips[r]), lambda ref: (ref,),
            (c, dd, x, y, line), send, recv,
        )

        def cross(r):
            for e in (3, 2, 1, 0):
                reduce.cross(e, r)

        turns = (3 - chip, flip(chip, 1), flip(chip, 2), chip)
        schedule = [
            ((1, 2), do(cross, 3)),
            ((1, 2), do(cross, 1)),
            ((2, 2), do(reduce.corner, 3)),
            ((2, 2), do(cross, 2)),
            ((3, 2), do(cross, 0)),
            ((4, 1), do(reduce.plane, 3)),
            ((5, 0), do(reduce.corner, 2)),
            ((6, 0), do(reduce.corner, 1)),
            ((6, 0), do(reduce.along, 3)),
            ((7, 0), do(reduce.plane, 2)),
        ]
    else:
        turns = (0, 1, 2, 3)
    turn = turns[3]
    for k in (2, 1, 0):
        turn = jnp.where(step == k, turns[k], turn)

    def columns(k):
        lanes = pl.ds(pl.multiple_of(turns[k] * d, 128), d) if links else pl.ds(k * d, d)
        return pltpu.make_async_copy(dp_ref.at[:, :, lanes], dp_s.at[turns[k]], load.at[k])

    acts = [
        pltpu.make_async_copy(normed_ref, act_s.at[0], load.at[4]),
        pltpu.make_async_copy(mixed_ref, act_s.at[1], load.at[5]),
    ]
    later = [
        pltpu.make_async_copy(watt_ref.at[: 3 * d], watt_s, load.at[6]),
        pltpu.make_async_copy(resg_ref, resg_s, load.at[7]),
        pltpu.make_async_copy(kept_ref, kept_s, load.at[8]),
    ]

    @pl.when(step == 0)
    def _():
        columns(0).start()
        for copy in acts:
            copy.start()
        for k in (1, 2, 3):
            columns(k).start()
        for copy in later:
            copy.start()
        vecg_s[...] = jnp.zeros_like(vecg_s)
        if links:
            at.barrier()
        for copy in acts:
            copy.wait()

    for k in range(4):
        @pl.when(step == k)
        def _(k=k):
            columns(k).wait()

    @pl.when(step < 4)
    def _():
        which = jnp.where(turn == 3, 1, 0)
        where = pl.ds(pl.multiple_of(turn * d, 128), d)
        left = dp_s[turn].reshape(total, d)
        gatt_s[where, :] = tn(left, act_s[which].reshape(total, d)).astype(bf16)

    @pl.when(step == 4)
    def _():
        for copy in later:
            copy.wait()

    pump(schedule, step, 0)

    @pl.when(step > 3)
    def _():
        image = step - 4
        standard, inverse = normalize(kept_s[image].astype(f32))
        ng = rg_ref[image] * vec_ref[2:3]
        for j in range(3):
            ng += nn(dp_s[j, image], watt_s[j * d : (j + 1) * d, :])
        pump(schedule, step, 1)
        grad = resg_s[image] + norm_backward(ng, standard, inverse, vec_ref[0:1])
        high = grad.astype(bf16)
        high_ref[image] = high
        low_ref[image] = (grad - high.astype(f32)).astype(bf16)
        vecg_s[0:1] += colsum(ng * standard)
        vecg_s[1:2] += colsum(ng)

    pump(schedule, step, 2)
    if links:
        exchange = lambda k, to: remote(
            vbuf.at[k + 1], vbuf.at[8 + k], vsend.at[k], vrecv.at[k], to
        )
        lines = [
            lambda k=k: remote(
                vbuf.at[0], vbuf.at[4 + at.z], vsend.at[2 + k], vrecv.at[3 + at.z],
                (at.dp, at.line[k]),
            )
            for k in range(1, MP)
        ]

        @pl.when(step == last)
        def _():
            vbuf[0, 0:2] = vecg_s[0:2]
            vbuf[0, 2:9] = vecb_ref[0:7]
            vbuf[0, 9:13] = bias_ref[...]
            vbuf[0, 13:16] = jnp.zeros((3, d), f32)
            for make in lines:
                make().start()
            vbuf[4 + at.z] = vbuf[0]
            reduce.plane(1)
            reduce.corner(0)
            reduce.along(2)
            for k in range(1, MP):
                zb = at.line[k]
                remote(
                    vbuf.at[0], vbuf.at[4 + zb], vsend.at[2 + k], vrecv.at[3 + zb], at.core
                ).wait_recv()
            vbuf[1] = vbuf[4] + vbuf[5] + vbuf[6] + vbuf[7]
            exchange(0, at.core).start()
            reduce.along(1)
            exchange(0, at.core).wait()
            vbuf[2] = vbuf[1] + vbuf[8]
            exchange(1, at.x).start()
            reduce.plane(0)
            exchange(1, at.x).wait()
            vbuf[3] = vbuf[2] + vbuf[9]
            exchange(2, at.y).start()
            exchange(2, at.y).wait()
            full_sum = vbuf[3] + vbuf[10]
            vecout_ref[...] = full_sum[: vecout_ref.shape[0]]
            reduce.gathered(0, *reduce.lines(), target=gout_ref)
            for make in lines:
                make().wait_send()
            reduce.sends.finish()


def scatter_kernel(
    high_ref, low_ref, result_ref, idx_ref, tok_ref, cot_ref, ing_ref, out_ref,
    tok_s, cot_s, ing_s, out_s, load, store,
):
    images, _, d = high_ref.shape
    loads = []
    for k, (a, b) in enumerate(CROPS):
        for j, (src, dst) in enumerate(((cot_ref, cot_s), (tok_ref, tok_s))):
            c = pltpu.make_async_copy(src.at[a:b], dst.at[a:b], load.at[j, k])
            c.start()
            loads.append(c)
    stores = []
    offset = 0
    for k, ((a, b), (lo, hi)) in enumerate(zip(CROPS, UNITS)):
        n, rows = hi - lo, images * (b - a)
        index = idx_ref[0:1, offset : offset + images * n]
        offset += images * n
        hot = (lax.broadcasted_iota(jnp.int32, (rows, images * n), 0) == index).astype(f32)
        taken = jnp.sum(hot, axis=-1, keepdims=True) > 0.5
        hot = hot.astype(bf16)
        window = lambda ref: jnp.concatenate([ref[i, lo:hi] for i in range(images)], axis=0)
        spread = nn(hot, window(high_ref)) + nn(hot, window(low_ref))
        loads[2 * k].wait()
        old = cot_s[a:b].reshape(rows, d).astype(f32)
        ing_s[a:b] = jnp.where(taken, spread, old).reshape(b - a, images, d)
        stores.append(pltpu.make_async_copy(ing_s.at[a:b], ing_ref.at[a:b], store.at[0, k]))
        stores[-1].start()
        loads[2 * k + 1].wait()
        old = tok_s[a:b].reshape(rows, d).astype(f32)
        new = jnp.where(taken, nn(hot, window(result_ref)), old).astype(bf16)
        out_s[a:b] = new.reshape(b - a, images, d)
        stores.append(pltpu.make_async_copy(out_s.at[a:b], out_ref.at[a:b], store.at[1, k]))
        stores[-1].start()
    for c in stores:
        c.wait()


def adamw(grad, first, second, master, average, rate, decay):
    first_new = 0.5 * first + 0.5 * grad
    second_new = 0.5 * second + 0.5 * grad * grad
    update = first_new / (jnp.sqrt(second_new) + 1e-08)
    master_new = master - rate * (update + decay * master)
    average_new = 0.9 * average + 0.1 * master_new
    return (first_new, second_new, master_new, average_new)


def sds(*shape_dtype):
    return jax.ShapeDtypeStruct(shape_dtype[:-1], shape_dtype[-1])


def window_index(kept_index):
    images = kept_index.shape[0]
    padded = jnp.concatenate([kept_index, jnp.full((images, RI - KEPT), -1, jnp.int32)], axis=1)
    pieces = []
    for (a, b), (s, e), (lo, hi) in zip(CROPS, SPANS, UNITS):
        row = lax.broadcasted_iota(jnp.int32, (images, hi - lo), 1) + lo
        image = lax.broadcasted_iota(jnp.int32, (images, hi - lo), 0)
        place = (padded[:, lo:hi] - a) * images + image
        pieces.append(jnp.where((row >= s) & (row < e), place, -1).reshape(-1))
    return jnp.concatenate(pieces)


def scratch(*shape_dtype):
    return pltpu.VMEM(shape_dtype[:-1], shape_dtype[-1])


def dma(*shape):
    return pltpu.SemaphoreType.DMA(shape)


def per_device(
    tokens, cotangent, kept_index,
    attention_weights, attention_first, attention_second, attention_average,
    feedforward_weights, feedforward_first, feedforward_second, feedforward_average,
    vector_weights, vector_first, vector_second, vector_average,
):
    images, length, d = tokens.shape
    ndp, nmp = lax.axis_size("dp"), lax.axis_size("mp")
    links = (ndp, nmp) == (8, MP)
    vec = vector_weights
    rows, hb = feedforward_weights.shape[1:]
    hidden = nmp * hb
    mask = masks()
    mask_specs = [full(m.shape) for m in mask]
    places = window_index(kept_index)
    index_col, index_row = places[:, None], places[None, :]
    tok, cot = tokens.transpose(1, 0, 2), cotangent.transpose(1, 0, 2)
    comm = (lambda i: dict(collective_id=i, has_side_effects=True)) if links else (lambda i: {})

    att, ff = attention_weights.T, feedforward_weights
    if not links:
        att, ff = att.astype(bf16), ff.astype(bf16)
        att = lax.all_gather(att, ("dp", "mp"), axis=0, tiled=True)
        wff = lax.all_gather(lax.all_gather(ff, "dp", axis=1, tiled=True), "mp", axis=0)
    now = lambda *s: pl.BlockSpec((1,) + s, lambda i: (jnp.maximum(i - 1, 0), 0, 0))
    whole = lambda *s: pl.BlockSpec(s, lambda j: (0,) * len(s), pipeline_mode=pl.Buffered(1))
    rowspec = (images, RI, d)
    outs = pl.pallas_call(
        functools.partial(forward_kernel, links),
        grid=(1 + images,),
        in_specs=[ANY, ANY, full(index_col.shape), full(vec.shape), *mask_specs]
        + ([full(att.shape), full(ff.shape)] if links else [ANY, ANY]),
        out_specs=[full(rowspec)] * 3 + [
            now(RI, 3 * d), now(RI, d), now(RI, d), now(RI, d), now(RI, d), ANY,
        ] + [ANY] * links,
        out_shape=[sds(*rowspec, bf16)] * 3 + [
            sds(images, RI, 3 * d, bf16), sds(*rowspec, bf16), sds(*rowspec, f32),
            sds(*rowspec, f32), sds(*rowspec, bf16), sds(4 * d, d, bf16),
        ] + [sds(nmp, 2, d, hb, bf16)] * links,
        scratch_shapes=[
            scratch(4 * d, d, bf16), scratch(length, images, d, bf16), scratch(length, images, d, bf16),
            dma(3),
        ] + (
            [scratch(rows, d, bf16), scratch(2, rows, hb, bf16)]
            + [dma(2, Gather.SLOTS), dma(2, Gather.SLOTS), dma(2, 1)] if links else []
        ),
        compiler_params=params(**comm(0)),
        name="forward",
    )(tok, cot, index_col, vec, *mask, att, ff)
    kept, normed, cotk, proj, mixed, branch, resid, n2, watt = outs[:9]
    if links:
        wff = outs[9]

    bias = vec[9:].reshape(nmp, 1, hb)
    outs = pl.pallas_call(
        functools.partial(feed_kernel, links),
        grid=(nmp,),
        in_specs=[
            whole(*rowspec), whole(*rowspec), whole(*rowspec), ANY, full((nmp, 1, hb)), full(vec.shape),
        ],
        out_specs=[full(rowspec), full(rowspec), ANY, full((nmp, 1, hb))]
        + [full((2, 2, rows, hb))] * links,
        out_shape=[
            sds(*rowspec, bf16), sds(*rowspec, f32),
            sds(nmp, 2, d, hb, bf16), sds(nmp, 1, hb, f32),
        ] + [sds(2, 2, rows, hb, bf16)] * links,
        scratch_shapes=[
            scratch(*rowspec, f32), scratch(images * RI, hb, bf16), scratch(images * RI, hb, bf16),
            scratch(nmp, 2, d, hb, bf16), scratch(2, 2, d, hb, bf16), dma(nmp), dma(2),
        ] + (
            [dma(Gather.SLOTS), dma(Gather.SLOTS), dma(4)]
            + [scratch(n, 2, rows, hb, bf16) for n in (8, 8, 2, 2, 2)]
            + [dma(Reduce.SLOTS), dma(Reduce.SLOTS), dma(8)] if links else []
        ),
        compiler_params=params(**comm(3)),
        name="feedforward",
    )(n2, cotk, resid, wff, bias, vec)
    result, n2g, gff, bg = outs[:4]

    spans = (16, 16, 4, 4, 4, 4)
    outs = pl.pallas_call(
        functools.partial(backward_kernel, links),
        grid=(images,),
        in_specs=[
            per_image(RI, d), per_image(RI, d), per_image(RI, d), per_image(RI, d),
            per_image(RI, d), per_image(RI, 3 * d),
            full(watt.shape), full(vec.shape), *mask_specs,
        ] + [ANY, full((2, 2, rows, hb))] * links,
        out_specs=[per_image(RI, 4 * d), per_image(RI, d), per_image(RI, 1), full((8, d))]
        + [full((2, rows, hb))] * links,
        out_shape=[
            sds(images, RI, 4 * d, bf16), sds(*rowspec, f32), sds(images, RI, 1, f32), sds(8, d, f32),
        ] + [sds(2, rows, hb, f32)] * links,
        scratch_shapes=[scratch(RI, d, bf16)] + (
            [scratch(n, 2, rows, hb, bf16) for n in (8, 8, 2, 2, 2, 4)]
            + [dma(Reduce.SLOTS), dma(Reduce.SLOTS), dma(8)] if links else []
        ),
        compiler_params=params(**comm(1)),
        name="attention_backward",
    )(n2g, cotk, branch, resid, normed, proj, watt, vec, *mask, *([gff, outs[4]] if links else []))
    dp, resg, rg, vecg = outs[:4]
    if links:
        feedforward_gradient = outs[4]

    full_d = (4 * d, d)
    outs = pl.pallas_call(
        functools.partial(grads_kernel, links),
        grid=(4 + images,),
        in_specs=[ANY, ANY, ANY, full((images, RI, 1)), ANY, ANY, full(vec.shape), ANY]
        + [full((8, d)), full((hidden // d, d))] * links,
        out_specs=[full(rowspec), full(rowspec)]
        + ([full((rows, d)), full(vec.shape)] if links else [full(full_d), full((8, d))]),
        out_shape=[sds(*rowspec, bf16), sds(*rowspec, bf16)]
        + ([sds(rows, d, f32), sds(*vec.shape, f32)] if links else [sds(*full_d, bf16), sds(8, d, f32)]),
        scratch_shapes=([scratch(*full_d, bf16), scratch(8, d, f32)] if links else []) + [
            scratch(3 * d, d, bf16), scratch(4, *rowspec, bf16), scratch(2, *rowspec, bf16),
            scratch(*rowspec, f32), scratch(*rowspec, bf16), dma(9),
        ] + (
            [scratch(n, rows, d, bf16) for n in spans[1:]]
            + [dma(Reduce.SLOTS), dma(Reduce.SLOTS), scratch(11, 16, d, f32), dma(8), dma(8)]
            if links else []
        ),
        compiler_params=params(**comm(2)),
        name="attention_grads",
    )(
        dp, normed, mixed, rg, resg, kept, vec, watt,
        *([vecg, bg.reshape(hidden // d, d)] if links else []),
    )
    high, low = outs[:2]
    if links:
        gatt, vector_gradient = outs[2:]
    else:
        gatt, vecg_in = outs[2:]
        local = jnp.concatenate([vecg_in[:2], vecg[:7], bg.reshape(hidden // d, d)], axis=0)
        gatt = lax.psum_scatter(gatt, ("dp", "mp"), scatter_dimension=0, tiled=True).astype(f32)
        gff = lax.psum_scatter(gff, "mp", scatter_dimension=0, tiled=False)
        gff = lax.psum_scatter(gff, "dp", scatter_dimension=1, tiled=True)
        feedforward_gradient, vector_gradient = gff.astype(f32), lax.psum(local, ("dp", "mp"))

    ing, out = pl.pallas_call(
        scatter_kernel,
        in_specs=[pl.BlockSpec(memory_space=pltpu.VMEM)] * 4 + [ANY, ANY],
        out_specs=[ANY, ANY],
        out_shape=[sds(length, images, d, f32), sds(length, images, d, bf16)],
        scratch_shapes=[
            scratch(length, images, d, bf16), scratch(length, images, d, bf16),
            scratch(length, images, d, f32), scratch(length, images, d, bf16), dma(2, 3), dma(2, 3),
        ],
        compiler_params=params(),
        name="scatter_rows",
    )(high, low, result, index_row, tok, cot)
    input_gradient, block_output = ing.transpose(1, 0, 2), out.transpose(1, 0, 2)

    attention_gradient = gatt.T
    attention_new = adamw(
        attention_gradient, attention_first, attention_second,
        attention_weights, attention_average, 0.02, 0.05,
    )
    feedforward_new = adamw(
        feedforward_gradient, feedforward_first, feedforward_second,
        feedforward_weights, feedforward_average, 0.02, 0.05,
    )
    vector_new = adamw(
        vector_gradient, vector_first, vector_second, vector_weights, vector_average, 0.2, 0.0
    )
    return (
        block_output, input_gradient,
        attention_gradient, *attention_new, attention_new[2].astype(bf16),
        feedforward_gradient, *feedforward_new, feedforward_new[2].astype(bf16),
        vector_gradient, *vector_new, vector_gradient[3],
    )


def solution(mesh):
    rows = P(("dp", "mp"), None, None)
    att = P(None, ("dp", "mp"))
    feed = P(None, "dp", "mp")
    in_specs = (rows, rows, P(("dp", "mp"), None)) + (att,) * 4 + (feed,) * 4 + (P(),) * 4
    out_specs = (rows, rows) + (att,) * 6 + (feed,) * 6 + (P(),) * 6
    return jax.shard_map(
        per_device, mesh=mesh, in_specs=in_specs, out_specs=out_specs, check_vma=False
    )
```

```python
import functools

import jax
import jax.numpy as jnp
import numpy as np
from jax import lax
from jax.experimental import pallas as pl
from jax.experimental.pallas import tpu as pltpu
from jax.sharding import PartitionSpec as P

H = 12
HD = 64
LG = 197
LL = 37
KG = LG // 2
KL = LL // 2
LOC = 4 * KL
KEPT = 2 * KG + LOC
RI = -(-KEPT // 16) * 16
SPANS = ((0, KG), (KG, 2 * KG), (2 * KG, KEPT))
UNITS = tuple((a // 16 * 16, -(-b // 16) * 16) for a, b in SPANS)
PAIRS = H // 2
W2L = 2 * HD

bf16 = jnp.bfloat16
f32 = jnp.float32


def params(limit=56, **kw):
    return pltpu.CompilerParams(vmem_limit_bytes=limit << 20, **kw)


def full(shape):
    return pl.BlockSpec(shape, lambda *_: (0,) * len(shape))


def per_image(*shape):
    return pl.BlockSpec((1,) + shape, lambda i, *_: (i,) + (0,) * len(shape))


def nn(a, b):
    return lax.dot_general(a, b, (((1,), (0,)), ((), ())), preferred_element_type=f32)


def nt(a, b):
    return lax.dot_general(a, b, (((1,), (1,)), ((), ())), preferred_element_type=f32)


def tn(a, b):
    return lax.dot_general(a, b, (((0,), (0,)), ((), ())), preferred_element_type=f32)


def normalize(rows):
    center = rows - jnp.mean(rows, axis=-1, keepdims=True)
    spread = jnp.mean(center * center, axis=-1, keepdims=True)
    inverse = lax.rsqrt(spread + 1e-06)
    return center * inverse, inverse


def norm_backward(upstream, standard, inverse, gain):
    scaled = upstream * gain
    return inverse * (
        scaled
        - jnp.mean(scaled, axis=-1, keepdims=True)
        - standard * jnp.mean(scaled * standard, axis=-1, keepdims=True)
    )


def colsum(v):
    return jnp.sum(v, axis=0, keepdims=True)


def masks():
    crop = np.full(RI, -1)
    crop[:KG], crop[KG : 2 * KG] = 0, 1
    for c in range(4):
        crop[2 * KG + c * KL : 2 * KG + (c + 1) * KL] = 2 + c
    adds, valids = [], []
    for (a, b), (lo, hi) in zip(SPANS, UNITS):
        rows = np.arange(lo, hi)
        inside = (rows >= a) & (rows < b)
        same = (crop[lo:hi, None] == crop[None, lo:hi]) & inside[:, None] & inside[None, :]
        adds.append(np.tile(np.where(same, 0.0, -1e9), (1, 2)).astype(np.float32))
        valids.append(np.tile(inside[None, :].astype(np.float32), (8, 2)))
    return [jnp.asarray(m) for m in adds + valids]


def lane_half(shape):
    return lax.broadcasted_iota(jnp.int32, shape, len(shape) - 1) < HD


def split_heads(v, scale):
    first = lane_half(v.shape)
    zero = jnp.zeros_like(v)
    if scale != 1.0:
        v = v * jnp.asarray(scale, v.dtype)
    return jnp.concatenate([jnp.where(first, v, zero), jnp.where(first, zero, v)], axis=0)


def join_heads(v):
    n = v.shape[0] // 2
    return jnp.where(lane_half((n, v.shape[1])), v[:n], v[n:])


def softmax_keys(st, valid):
    p = jnp.exp(st - jnp.max(st, axis=0, keepdims=True))
    return p * (valid / jnp.sum(p, axis=0, keepdims=True))


def store_window(ref, image, lo, hi, last, cols, value, tail):
    value = value.astype(bf16)
    if tail is not None:
        value = jnp.concatenate([value[:16] + tail, value[16:]], axis=0)
    end = hi if last else hi - 16
    ref[image, lo:end, cols] = value[: end - lo]
    return None if last else value[end - lo :]


MESH = pl.DeviceIdType.MESH
ANY = pl.BlockSpec(memory_space=pl.ANY)
MP = 4
CROPS = ((0, LG), (LG, 2 * LG), (2 * LG, 2 * LG + 4 * LL))
ORDER = ((0, 1, 2, 3), (1, 0, 1, 2), (2, 2, 3, 1), (3, 3, 0, 0))


def flip(index, bit):
    return index + bit * (1 - 2 * lax.rem(lax.div(index, bit), 2))


def remote(src, dst, send, recv, to):
    return pltpu.make_async_remote_copy(
        src_ref=src, dst_ref=dst, send_sem=send, recv_sem=recv, device_id=to, device_id_type=MESH
    )


class Sends:
    def __init__(self):
        self.made = []

    def start(self, make, when=None):
        def go():
            make().start()

        go() if when is None else pl.when(when)(go)
        self.made.append((make, when))

    def finish(self):
        for make, when in self.made:
            def wait(make=make):
                make().wait_send()

            wait() if when is None else pl.when(when)(wait)


class Place:
    def __init__(self):
        self.dp = lax.axis_index("dp")
        self.z = lax.axis_index("mp")
        x, y = flip(self.dp, 2), flip(self.dp, 4)
        self.core = (flip(self.dp, 1), self.z)
        self.x, self.y = (x, self.z), (y, self.z)
        self.chips = (self.dp, x, y, flip(x, 4))
        self.mates = tuple(flip(c, 1) for c in self.chips)
        power = (1 + 3 * lax.rem(self.z, 2)) * (1 + 15 * lax.div(self.z, 2))
        self.event = []
        for row in ORDER:
            code = sum(v << (2 * i) for i, v in enumerate(row))
            self.event.append(lax.rem(lax.div(0 * power + code, power), 4))
        self.low, self.high = self.z > 0, self.z < MP - 1
        self.middle = self.low & self.high
        self.line = [lax.rem(self.z + k, MP) for k in range(MP)]
        self.up, self.down = (self.dp, self.z + 1), (self.dp, self.z - 1)
        self.onward = (self.up, self.down, (self.dp, 3 * (self.z - 1)))

    def barrier(self):
        sem = pltpu.get_barrier_semaphore()
        others = [self.core, self.x, self.y]
        others += [(self.dp, k) for k in self.line[1:]]
        for other in others:
            pl.semaphore_signal(sem, inc=1, device_id=other, device_id_type=MESH)
        pl.semaphore_wait(sem, len(others))


def att_block(ref, dp, z, rows):
    return ref.at[pl.ds(pl.multiple_of((dp * MP + z) * rows, 32), rows), :]


def att_part(ref, dp, z, rows, h):
    half = rows // 2
    return ref.at[pl.ds(pl.multiple_of((dp * MP + z) * rows + h * half, 16), half), :]


def ff_part(ref, dp, z, rows, h):
    return ref.at[z, h, pl.ds(pl.multiple_of(dp * rows, 32), rows), :]


def ff_block(ref, dp, z, rows):
    return ref.at[z, :, pl.ds(pl.multiple_of(dp * rows, 32), rows), :]


class Gather:
    ALONG, X, Y, D, C, SLOTS = 0, 4, 8, 12, 16, 32

    def __init__(self, at, first, place, send, recv, local):
        self.at, self.first, self.place = at, first, place
        self.send, self.recv, self.local = send, recv, local
        self.sends = Sends()

    def copy(self, slot, e, r, to):
        slot = self.ALONG + self.at.event[e] if slot is None else slot
        dst = self.place(e, self.at.chips[r])
        src = self.first(e) if r == 0 else dst
        return remote(src, dst, self.send.at[slot], self.recv.at[slot], to)

    def put(self, slot, e, r, to, when=None):
        self.sends.start(lambda: self.copy(slot, e, r, to), when)

    def got(self, slot, e, dp):
        dst = self.place(e, dp)
        remote(dst, dst, self.send.at[slot], self.recv.at[slot], self.at.core).wait_recv()

    def keep(self, e):
        return pltpu.make_async_copy(self.first(e), self.place(e, self.at.dp), self.local.at[e])

    def spread(self, e):
        self.put(self.X + e, e, 0, self.at.x)
        self.put(self.Y + e, e, 0, self.at.y)
        self.put(self.C + 4 * e, e, 0, self.at.core)

    def begin(self):
        at = self.at
        self.keep(0).start()
        for to, when in ((at.up, at.high), (at.down, at.low)):
            self.put(None, 0, 0, to, when)
        self.spread(0)

    def direct(self):
        self.keep(0).start()
        for zb in self.at.line[1:]:
            self.put(None, 0, 0, (self.at.dp, zb))

    def arrived(self, e):
        self.got(self.ALONG + self.at.event[e], e, self.at.dp)

    def along(self, e):
        at = self.at
        self.arrived(e)
        self.put(None, e, 0, at.onward[e - 1], at.middle)
        self.spread(e)

    def plane(self, e):
        at = self.at
        self.got(self.X + e, e, at.chips[1])
        if e % 2 == 0:
            self.put(self.D + e, e, 1, at.y)
        self.put(self.C + 4 * e + 1, e, 1, at.core)
        self.got(self.Y + e, e, at.chips[2])
        if e % 2 == 1:
            self.put(self.D + e, e, 2, at.x)
        self.put(self.C + 4 * e + 2, e, 2, at.core)

    def corner(self, e):
        self.got(self.D + e, e, self.at.chips[3])
        self.put(self.C + 4 * e + 3, e, 3, self.at.core)

    def finish(self, e):
        for r in range(4):
            self.got(self.C + 4 * e + r, e, self.at.mates[r])


def add_into(target, first, *others):
    if len(others) == 1 and target.dtype == bf16:
        target[...] = first[...] + others[0][...]
        return
    step = 48

    @pl.loop(0, first.shape[0] // step)
    def _(i):
        s = pl.ds(pl.multiple_of(i * step, step), step)
        total = first[s, :].astype(f32)
        for ref in others:
            total = total + ref[s, :].astype(f32)
        target[s, :] = total.astype(target.dtype)


class Reduce:
    C, D, X, Y, ALONG, SLOTS = 0, 16, 20, 24, 28, 32

    def __init__(self, at, source, own, parts, bufs, send, recv, load=None, base=0):
        self.at, self.source, self.own, self.parts, self.base = at, source, own, parts, base
        self.c, self.d, self.x, self.y, self.line = bufs
        self.send, self.recv, self.load = send, recv, load
        self.sends = Sends()

    def put(self, slot, src, dst, to):
        self.sends.start(
            lambda: remote(src(), dst(), self.send.at[slot], self.recv.at[slot], to)
        )

    def got(self, slot, dst):
        remote(dst, dst, self.send.at[slot], self.recv.at[slot], self.at.core).wait_recv()

    def slot(self, e, r):
        return 4 * (e - self.base) + r

    def cross(self, e, r):
        i = self.slot(e, r)
        self.put(self.C + i, lambda: self.source(e, self.at.mates[r]), lambda: self.c.at[i], self.at.core)
        if self.load is not None:
            self.load(e, r).start()

    def add(self, e, r, *others, target=None):
        i = self.slot(e, r)
        self.got(self.C + i, self.c.at[i])
        if self.load is not None:
            self.load(e, r).wait()
        refs = [self.own(e, r), self.c.at[i]] + list(others)
        self.total(refs[0] if target is None else target, *refs)

    def total(self, target, *refs):
        for t, *rest in zip(self.parts(target), *[self.parts(ref) for ref in refs]):
            add_into(t, *rest)

    def corner(self, e):
        at, i = self.at, e - self.base
        self.add(e, 3)
        self.put(
            self.D + i, lambda: self.own(e, 3), lambda: self.d.at[i], at.x if e % 2 else at.y
        )
        r, slot, buf, to = (1, self.X, self.x, at.x) if e % 2 else (2, self.Y, self.y, at.y)
        self.add(e, r)
        self.put(slot + i, lambda: self.own(e, r), lambda: buf.at[i], to)

    def plane(self, e):
        at, i = self.at, e - self.base
        r, slot, buf, to = (2, self.Y, self.y, at.y) if e % 2 else (1, self.X, self.x, at.x)
        self.got(self.D + i, self.d.at[i])
        self.add(e, r, self.d.at[i])
        self.put(slot + i, lambda: self.own(e, r), lambda: buf.at[i], to)

    def gathered(self, e, *others, target=None):
        i = e - self.base
        self.got(self.X + i, self.x.at[i])
        self.got(self.Y + i, self.y.at[i])
        self.add(e, 0, self.x.at[i], self.y.at[i], *others, target=target)

    def send_along(self, e, src):
        at = self.at
        zb = at.event[e]
        self.sends.start(
            lambda: remote(
                src(), self.line.at[at.z], self.send.at[self.ALONG + zb],
                self.recv.at[self.ALONG + at.z], (at.dp, zb),
            )
        )

    def along(self, e):
        self.gathered(e)
        self.send_along(e, lambda: self.own(e, 0))

    def lines(self):
        got = []
        for zb in self.at.line[1:]:
            got.append(self.line.at[zb])
            self.got(self.ALONG + zb, got[-1])
        return got


def pump(schedule, step, point):
    for (s, p), action in schedule:
        if isinstance(point, int):
            if p == point:
                pl.when(step == s)(action)
        else:
            pl.when((step == s) & (point == p))(action)


def do(action, *args):
    return lambda: action(*args)


def token_columns(idx_ref, idx_s):
    idx_s[...] = jnp.full(idx_s.shape, -1.0, f32)
    idx_s[0 : idx_ref.shape[0], 0 : idx_ref.shape[1]] = idx_ref[...].astype(f32)
    return idx_s[...].T


def one_hot(columns, crop, images):
    (a, b), (s, e), (lo, hi) = CROPS[crop], SPANS[crop], UNITS[crop]
    row = lax.broadcasted_iota(jnp.int32, (hi - lo, 1), 0) + lo
    pieces = []
    for i in range(images):
        place = (columns[lo:hi, i : i + 1].astype(jnp.int32) - a) * images + i
        pieces.append(jnp.where((row >= s) & (row < e), place, -1))
    index = jnp.concatenate(pieces, axis=0)
    count = images * (b - a)
    hot = lax.broadcasted_iota(jnp.int32, (index.shape[0], count), 1) == index
    return hot.astype(f32).astype(bf16)


def forward_kernel(
    links, tok_ref, cot_ref, idx_ref, vec_ref, m0_ref, m1_ref, m2_ref, v0_ref, v1_ref, v2_ref,
    att_ref, ff_ref,
    kept_ref, normed_ref, cotk_ref, proj_ref, mixed_ref, branch_ref, resid_ref, n2_ref,
    watt_out, *rest,
):
    if links:
        wff_ref, watt_ref, tok_s, cot_s, idx_s, load, att_s, ff_s, send, recv, local = rest
    else:
        watt_ref, tok_s, cot_s, idx_s, load = rest
    step = pl.program_id(0)
    images, _, d = kept_ref.shape
    loads = [
        pltpu.make_async_copy(tok_ref, tok_s, load.at[0]),
        pltpu.make_async_copy(cot_ref, cot_s, load.at[1]),
    ]
    acts, schedule = [[]] * 6, []
    if links:
        at = Place()
        rows = att_ref.shape[0]
        half = rows // 2

        def att_half(h):
            return Gather(
                at,
                lambda e: att_part(watt_ref, at.dp, at.event[e], rows, h) if e
                else att_s.at[h * half : (h + 1) * half],
                lambda e, dp: att_part(watt_ref, dp, at.event[e], rows, h),
                send.at[h], recv.at[h], local.at[h],
            )

        def feed_half(h):
            return Gather(
                at, lambda e: ff_part(wff_ref, at.dp, at.event[e], rows, h) if e else ff_s.at[h],
                lambda e, dp: ff_part(wff_ref, dp, at.event[e], rows, h),
                send.at[2 + h], recv.at[2 + h], local.at[2 + h],
            )

        (a0, a1), (f0, f1) = [att_half(h) for h in (0, 1)], [feed_half(h) for h in (0, 1)]
        acts = [
            [a1.begin, a0.begin],
            [do(a1.along, 1), do(a1.plane, 0), do(a0.along, 1), do(a0.along, 2), do(a1.along, 2)],
            [do(a0.along, 3)],
            [do(a1.along, 3), f0.direct, do(a1.plane, 1), do(a0.plane, 2)],
            [do(a0.plane, 0)],
            [
                do(a0.plane, 3), do(a0.plane, 1), do(a1.plane, 3), do(a1.plane, 2),
                do(a0.corner, 0), do(a1.corner, 1), do(a0.corner, 3), do(a1.corner, 2),
                do(a1.corner, 0), f1.direct, do(a0.corner, 1), do(a0.corner, 2), do(a1.corner, 3),
                do(f0.arrived, 2), do(f0.spread, 2),
            ],
        ]
        schedule = [
            ((1, 3), do(f0.arrived, 3)),
            ((1, 3), do(f0.spread, 3)),
            ((2, 1), do(f1.arrived, 2)),
            ((2, 1), do(f1.spread, 2)),
            ((3, 0), do(f1.arrived, 3)),
            ((3, 0), do(f1.spread, 3)),
            ((3, 0), do(f0.plane, 2)),
            ((3, 1), do(f1.plane, 2)),
            ((3, 1), do(f0.plane, 3)),
            ((3, 3), do(f1.plane, 3)),
            ((4, 3), do(f1.corner, 3)),
            ((4, 3), do(f0.corner, 3)),
            ((4, 3), do(f1.corner, 2)),
            ((4, 3), do(f0.corner, 2)),
        ]
    else:
        fetch = pltpu.make_async_copy(att_ref, watt_ref, load.at[2])
    store = pltpu.make_async_copy(watt_ref, watt_out, load.at[2])
    run = lambda point: [action() for action in acts[point]]

    @pl.when(step == 0)
    def _():
        if links:
            att_s[...] = att_ref[...].astype(bf16)
            at.barrier()
            run(0)
        else:
            fetch.start()
        for c in loads:
            c.start()
        if links:
            ff_s[...] = ff_ref[...].astype(bf16)
        columns = token_columns(idx_ref, idx_s)
        loads[0].wait()
        loads[1].wait()
        for crop, ((a, b), (lo, hi)) in enumerate(zip(CROPS, UNITS)):
            n, k = hi - lo, images * (b - a)
            hot = one_hot(columns, crop, images)
            for src, dst in ((tok_s, kept_ref), (cot_s, cotk_ref)):
                got = nn(hot, src[a:b].reshape(k, d)).astype(bf16)
                for i in range(images):
                    part = got[i * n : (i + 1) * n]
                    if crop:
                        dst[i, lo : lo + 16] = dst[i, lo : lo + 16] + part[:16]
                        dst[i, lo + 16 : hi] = part[16:]
                    else:
                        dst[i, lo:hi] = part
            run(1 + crop)
        for i in range(images):
            standard, _ = normalize(kept_ref[i].astype(f32))
            normed_ref[i] = (standard * vec_ref[0:1] + vec_ref[1:2]).astype(bf16)
            if i == 1:
                run(4)
        run(5)
        if links:
            for e in range(4):
                a0.finish(e)
                a1.finish(e)
            a0.keep(0).wait()
            a1.keep(0).wait()
        else:
            fetch.wait()
        store.start()

    pump(schedule, step, 0)

    @pl.when(step > 0)
    def _():
        image = step - 1
        normed = normed_ref[image]
        for j, row in ((0, 3), (1, None), (2, 4)):
            part = nt(normed, watt_ref[j * d : (j + 1) * d, :])
            if row is not None:
                part = part + vec_ref[row : row + 1]
            proj_ref[0, :, j * d : (j + 1) * d] = part.astype(bf16)
        pump(schedule, step, 1)
        mrefs, vrefs = (m0_ref, m1_ref, m2_ref), (v0_ref, v1_ref, v2_ref)
        for pair in range(PAIRS):
            cols = lambda j: slice(j * d + pair * W2L, j * d + (pair + 1) * W2L)
            tail = None
            for unit, (lo, hi) in enumerate(UNITS):
                qs = split_heads(proj_ref[0, lo:hi, cols(0)], HD ** -0.5)
                st = nt(proj_ref[0, lo:hi, cols(1)], qs) + mrefs[unit][...]
                pt = softmax_keys(st, vrefs[unit][0:1]).astype(bf16)
                out = join_heads(tn(pt, proj_ref[0, lo:hi, cols(2)]))
                tail = store_window(mixed_ref, 0, lo, hi, unit == 2, cols(0), out, tail)
            if pair == 2:
                pump(schedule, step, 3)
        branch = nt(mixed_ref[0], watt_ref[3 * d :, :]) + vec_ref[5:6]
        branch_ref[0] = branch
        residual = kept_ref[image].astype(f32) + router_score(normed, vec_ref) * branch
        resid_ref[0] = residual
        standard, _ = normalize(residual)
        n2_ref[0] = (standard * vec_ref[6:7] + vec_ref[7:8]).astype(bf16)

    @pl.when(step == images)
    def _():
        if links:
            for feed in (f0, f1):
                feed.finish(2)
                feed.finish(3)
                feed.arrived(1)
                feed.keep(0).wait()
            for part in (a0, a1, f0, f1):
                part.sends.finish()
        store.wait()


def router_score(normed, vec_ref):
    logit = jnp.sum(normed.astype(f32) * vec_ref[2:3], axis=-1, keepdims=True)
    return jax.nn.sigmoid(logit)


def feed_kernel(
    links, n2_ref, cot_ref, resid_ref, w_ref, vec_ref,
    result_ref, n2g_ref, gff_ref, bg_ref, *rest,
):
    if links:
        acc_ref, out_s, act_s, ig_s, i0, i1, a0, a1, w_s, g_s, load, store = rest[:12]
        send, recv, local, a, c, dd, x, y, rsend, rrecv, rlocal = rest[12:]
    else:
        out_s, act_s, ig_s, i0, i1, a0, a1, w_s, g_s, load, store = rest
    inner_s, ag_s = (i0, i1), (a0, a1)
    step = pl.program_id(0)
    last = pl.num_programs(0) - 1
    images, _, d = n2_ref.shape
    nload = w_s.shape[0]
    hb = w_ref.shape[3]
    block, schedule = step, []
    if links:
        at = Place()
        rows = acc_ref.shape[2]
        block = at.event[0]
        for e in (1, 2, 3):
            block = jnp.where(step == 3 - e, at.event[e], block)
        gather = Gather(
            at, lambda e: ff_block(w_ref, at.dp, at.event[e], rows),
            lambda e, dp: w_s.at[3 - e, :, pl.ds(pl.multiple_of(dp * rows, 32), rows), :],
            send, recv, local,
        )
        reduce = Reduce(
            at, lambda e, dp: ff_block(gff_ref, dp, at.event[e], rows),
            lambda e, r: a.at[4 * (e - 2) + r],
            lambda ref: (ref.at[0], ref.at[1]), (c, dd, x, y, None), rsend, rrecv,
            lambda e, r: pltpu.make_async_copy(
                ff_block(gff_ref, at.chips[r], at.event[e], rows), a.at[4 * (e - 2) + r],
                rlocal.at[4 * (e - 2) + r],
            ),
            2,
        )

        def start():
            at.barrier()
            for e in (1, 0):
                gather.spread(e)
                gather.keep(e).start()

        def ready(e):
            gather.finish(e)
            gather.keep(e).wait()

        def cross(e):
            for r in (3, 1, 2, 0):
                reduce.cross(e, r)

        schedule = [
            ((1, 0), do(gather.plane, 1)),
            ((1, 3), do(gather.plane, 0)),
            ((1, 4), do(cross, 3)),
            ((2, 0), do(gather.corner, 1)),
            ((2, 0), do(reduce.corner, 3)),
            ((2, 0), do(cross, 2)),
            ((2, 0), do(ready, 1)),
            ((2, 2), do(reduce.corner, 2)),
            ((2, 2), do(gather.corner, 0)),
            ((2, 5), do(reduce.plane, 3)),
            ((3, 0), do(ready, 0)),
            ((3, 0), do(reduce.plane, 2)),
        ]

    def fetch(e):
        return pltpu.make_async_copy(
            w_ref.at[at.event[3 - e] if links else e], w_s.at[e], load.at[e]
        )

    def save(slot, which):
        return pltpu.make_async_copy(g_s.at[slot], gff_ref.at[which], store.at[slot])

    residual = pltpu.make_async_copy(resid_ref, out_s, load.at[nload])
    early = (0, 1) if links else range(w_s.shape[0])

    @pl.when(step == 0)
    def _():
        for e in early:
            fetch(e).start()
        if links:
            start()
        residual.start()
        n2g_ref[...] = jnp.zeros_like(n2g_ref)
        bg_ref[...] = jnp.zeros_like(bg_ref)
        fetch(0).wait()
        residual.wait()

    for e in early[1:]:
        @pl.when(step == e)
        def _(e=e):
            fetch(e).wait()

    slot = lax.rem(step, 2)

    @pl.when(step > 0)
    def _():
        save(1 - slot, 0).wait()

    pump(schedule, step, 0)

    def first(i):
        inner_s[i % 2][...] = nn(n2_ref[i], w_s[step, 0]) + vec_ref[pl.ds(9 + block, 1), :]
        ag_s[i % 2][...] = nn(cot_ref[i], w_s[step, 1])

    def second(i):
        inner = inner_s[i % 2][...]
        phi = 0.5 * (1.0 + lax.erf(inner * 0.7071067811865476))
        act = (inner * phi).astype(bf16)
        slope = phi + inner * jnp.exp(-0.5 * inner * inner) * 0.3989422804014327
        ig = (ag_s[i % 2][...] * slope).astype(bf16)
        rows_i = slice(i * RI, (i + 1) * RI)
        act_s[rows_i, :] = act
        ig_s[rows_i, :] = ig
        bg_ref[pl.ds(block, 1), :] += colsum(ig.astype(f32))
        out_s[i] += nt(act, w_s[step, 1])
        n2g_ref[i] += nt(ig, w_s[step, 0])

    first(0)
    for i in range(images):
        pump(schedule, step, i + 1)
        if i + 1 < images:
            first(i + 1)
        second(i)

    pump(schedule, step, 5)
    n2 = n2_ref[...].reshape(images * RI, d)
    cot = cot_ref[...].reshape(images * RI, d)
    g_s[slot, 0] = tn(n2, ig_s[...]).astype(bf16)
    g_s[slot, 1] = tn(cot, act_s[...]).astype(bf16)
    save(slot, block).start()

    @pl.when(step == last)
    def _():
        result_ref[...] = (out_s[...] + vec_ref[8:9]).astype(bf16)
        if links:
            reduce.gathered(3, target=acc_ref.at[0])
            reduce.gathered(2, target=acc_ref.at[1])
            gather.sends.finish()
            reduce.sends.finish()
        save(slot, 0).wait()


def backward_kernel(
    links, n2g_ref, cotk_ref, branch_ref, resid_ref, normed_ref, proj_ref, wout_ref,
    vec_ref, m0_ref, m1_ref, m2_ref, v0_ref, v1_ref, v2_ref, *rest,
):
    if links:
        gff_ref, acc_ref, dp_ref, resg_ref, rg_ref, vecg_ref, gout_ref = rest[:7]
        mg_s, a, c, dd, x, y, line, send, recv, local = rest[7:]
    else:
        dp_ref, resg_ref, rg_ref, vecg_ref, mg_s = rest
    step = pl.program_id(0)
    schedule = []
    if links:
        at = Place()
        rows = gout_ref.shape[1]
        reduce = Reduce(
            at, lambda e, dp: ff_block(gff_ref, dp, at.event[e], rows),
            lambda e, r: a.at[4 * e + r],
            lambda ref: (ref.at[0], ref.at[1]), (c, dd, x, y, line), send, recv,
            lambda e, r: pltpu.make_async_copy(
                ff_block(gff_ref, at.chips[r], at.event[e], rows), a.at[4 * e + r],
                local.at[4 * e + r],
            ),
        )

        def start():
            at.barrier()
            reduce.send_along(2, lambda: acc_ref.at[1])
            for e in (1, 0):
                for r in (3, 1, 2, 0):
                    reduce.cross(e, r)

        schedule = [
            ((0, 0), start),
            ((0, 1), do(reduce.corner, 1)),
            ((0, 3), do(reduce.send_along, 3, lambda: acc_ref.at[0])),
            ((1, 1), do(reduce.plane, 1)),
            ((1, 3), do(reduce.corner, 0)),
            ((2, 1), do(reduce.along, 1)),
            ((3, 0), do(reduce.plane, 0)),
        ]

    pump(schedule, step, 0)
    d = normed_ref.shape[2]
    normed = normed_ref[0]
    score = router_score(normed, vec_ref)
    branch = branch_ref[0]
    standard, inverse = normalize(resid_ref[0])
    n2g = n2g_ref[0]
    cot = cotk_ref[0].astype(f32)
    resg = cot + norm_backward(n2g, standard, inverse, vec_ref[6:7])
    resg_ref[0] = resg
    bg = (score * resg).astype(bf16)
    rg = jnp.sum(resg * branch, axis=-1, keepdims=True) * score * (1.0 - score)
    rg_ref[0] = rg
    dp_ref[0, :, 3 * d :] = bg
    mg_s[...] = nn(bg, wout_ref[...]).astype(bf16)
    pump(schedule, step, 1)
    mrefs, vrefs = (m0_ref, m1_ref, m2_ref), (v0_ref, v1_ref, v2_ref)
    for pair in range(PAIRS):
        cols = lambda j: slice(j * d + pair * W2L, j * d + (pair + 1) * W2L)
        tails = [None] * 3
        for unit, (lo, hi) in enumerate(UNITS):
            qs = split_heads(proj_ref[0, lo:hi, cols(0)], HD ** -0.5)
            kk = proj_ref[0, lo:hi, cols(1)]
            pt = softmax_keys(nt(kk, qs) + mrefs[unit][...], vrefs[unit][0:1])
            ds = split_heads(mg_s[lo:hi, cols(0)], 1.0)
            gpt = nt(proj_ref[0, lo:hi, cols(2)], ds)
            sg = (pt * (gpt - jnp.sum(pt * gpt, axis=0, keepdims=True))).astype(bf16)
            grads = (
                join_heads(tn(sg, kk)) * HD ** -0.5, nn(sg, qs), nn(pt.astype(bf16), ds)
            )
            for j in range(3):
                tails[j] = store_window(dp_ref, 0, lo, hi, unit == 2, cols(j), grads[j], tails[j])
        if pair == 2:
            pump(schedule, step, 3)
    sums = jnp.concatenate(
        [
            colsum(rg * normed.astype(f32)),
            colsum(dp_ref[0, :, :d].astype(f32)),
            colsum(dp_ref[0, :, 2 * d : 3 * d].astype(f32)),
            colsum(bg.astype(f32)),
            colsum(n2g * standard),
            colsum(n2g),
            colsum(cot),
            jnp.zeros((1, d), f32),
        ],
        axis=0,
    )

    @pl.when(step == 0)
    def _():
        vecg_ref[...] = jnp.zeros_like(vecg_ref)

    vecg_ref[...] += sums
    if links:
        @pl.when(step == pl.num_programs(0) - 1)
        def _():
            reduce.gathered(0, *reduce.lines(), target=gout_ref)
            reduce.sends.finish()


def grads_kernel(
    links, dp_ref, normed_ref, mixed_ref, rg_ref, resg_ref, kept_ref, vec_ref, watt_ref, *rest,
):
    if links:
        vecb_ref, bias_ref, high_ref, low_ref, gout_ref, vecout_ref = rest[:6]
        gatt_s, vecg_s, watt_s, dp_s, act_s, resg_s, kept_s, load = rest[6:14]
        c, dd, x, y, line, send, recv, vbuf, vsend, vrecv = rest[14:]
    else:
        high_ref, low_ref, gatt_s, vecg_s, watt_s, dp_s, act_s, resg_s, kept_s, load = rest
    step = pl.program_id(0)
    images, _, d = high_ref.shape
    last = 3 + images
    total = images * RI
    chip, schedule = 0, []
    if links:
        at = Place()
        chip = lax.div(at.dp, 2)
        rows = gout_ref.shape[0]
        block = lambda e, dp: att_block(gatt_s, dp, at.event[e], rows)
        reduce = Reduce(
            at, block, lambda e, r: block(e, at.chips[r]), lambda ref: (ref,),
            (c, dd, x, y, line), send, recv,
        )

        def cross(r):
            for e in (3, 2, 1, 0):
                reduce.cross(e, r)

        turns = (3 - chip, flip(chip, 1), flip(chip, 2), chip)
        schedule = [
            ((1, 2), do(cross, 3)),
            ((1, 2), do(cross, 1)),
            ((2, 2), do(reduce.corner, 3)),
            ((2, 2), do(cross, 2)),
            ((3, 2), do(cross, 0)),
            ((4, 1), do(reduce.plane, 3)),
            ((5, 0), do(reduce.corner, 2)),
            ((6, 0), do(reduce.corner, 1)),
            ((6, 0), do(reduce.along, 3)),
            ((7, 0), do(reduce.plane, 2)),
        ]
    else:
        turns = (0, 1, 2, 3)
    turn = turns[3]
    for k in (2, 1, 0):
        turn = jnp.where(step == k, turns[k], turn)

    def columns(k):
        lanes = pl.ds(pl.multiple_of(turns[k] * d, 128), d) if links else pl.ds(k * d, d)
        return pltpu.make_async_copy(dp_ref.at[:, :, lanes], dp_s.at[turns[k]], load.at[k])

    acts = [
        pltpu.make_async_copy(normed_ref, act_s.at[0], load.at[4]),
        pltpu.make_async_copy(mixed_ref, act_s.at[1], load.at[5]),
    ]
    later = [
        pltpu.make_async_copy(watt_ref.at[: 3 * d], watt_s, load.at[6]),
        pltpu.make_async_copy(resg_ref, resg_s, load.at[7]),
        pltpu.make_async_copy(kept_ref, kept_s, load.at[8]),
    ]

    @pl.when(step == 0)
    def _():
        columns(0).start()
        for copy in acts:
            copy.start()
        for k in (1, 2, 3):
            columns(k).start()
        for copy in later:
            copy.start()
        vecg_s[...] = jnp.zeros_like(vecg_s)
        if links:
            at.barrier()
        for copy in acts:
            copy.wait()

    for k in range(4):
        @pl.when(step == k)
        def _(k=k):
            columns(k).wait()

    @pl.when(step < 4)
    def _():
        which = jnp.where(turn == 3, 1, 0)
        where = pl.ds(pl.multiple_of(turn * d, 128), d)
        left = dp_s[turn].reshape(total, d)
        gatt_s[where, :] = tn(left, act_s[which].reshape(total, d)).astype(bf16)

    @pl.when(step == 4)
    def _():
        for copy in later:
            copy.wait()

    pump(schedule, step, 0)

    @pl.when(step > 3)
    def _():
        image = step - 4
        standard, inverse = normalize(kept_s[image].astype(f32))
        ng = rg_ref[image] * vec_ref[2:3]
        for j in range(3):
            ng += nn(dp_s[j, image], watt_s[j * d : (j + 1) * d, :])
        pump(schedule, step, 1)
        grad = resg_s[image] + norm_backward(ng, standard, inverse, vec_ref[0:1])
        high = grad.astype(bf16)
        high_ref[image] = high
        low_ref[image] = (grad - high.astype(f32)).astype(bf16)
        vecg_s[0:1] += colsum(ng * standard)
        vecg_s[1:2] += colsum(ng)

    pump(schedule, step, 2)
    if links:
        exchange = lambda k, to: remote(
            vbuf.at[k + 1], vbuf.at[8 + k], vsend.at[k], vrecv.at[k], to
        )
        lines = [
            lambda k=k: remote(
                vbuf.at[0], vbuf.at[4 + at.z], vsend.at[2 + k], vrecv.at[3 + at.z],
                (at.dp, at.line[k]),
            )
            for k in range(1, MP)
        ]

        @pl.when(step == last)
        def _():
            vbuf[0, 0:2] = vecg_s[0:2]
            vbuf[0, 2:9] = vecb_ref[0:7]
            vbuf[0, 9:13] = bias_ref[...]
            vbuf[0, 13:16] = jnp.zeros((3, d), f32)
            for make in lines:
                make().start()
            vbuf[4 + at.z] = vbuf[0]
            reduce.plane(1)
            reduce.corner(0)
            reduce.along(2)
            for k in range(1, MP):
                zb = at.line[k]
                remote(
                    vbuf.at[0], vbuf.at[4 + zb], vsend.at[2 + k], vrecv.at[3 + zb], at.core
                ).wait_recv()
            vbuf[1] = vbuf[4] + vbuf[5] + vbuf[6] + vbuf[7]
            exchange(0, at.core).start()
            reduce.along(1)
            exchange(0, at.core).wait()
            vbuf[2] = vbuf[1] + vbuf[8]
            exchange(1, at.x).start()
            reduce.plane(0)
            exchange(1, at.x).wait()
            vbuf[3] = vbuf[2] + vbuf[9]
            exchange(2, at.y).start()
            exchange(2, at.y).wait()
            full_sum = vbuf[3] + vbuf[10]
            vecout_ref[...] = full_sum[: vecout_ref.shape[0]]
            reduce.gathered(0, *reduce.lines(), target=gout_ref)
            for make in lines:
                make().wait_send()
            reduce.sends.finish()


def adamw(grad, first, second, master, average, rate, decay):
    first_new = 0.5 * first + 0.5 * grad
    second_new = 0.5 * second + 0.5 * grad * grad
    update = first_new / (jnp.sqrt(second_new) + 1e-08)
    master_new = master - rate * (update + decay * master)
    average_new = 0.9 * average + 0.1 * master_new
    return (first_new, second_new, master_new, average_new)


GROUPS = ((0.02, 0.05), (0.02, 0.05), (0.2, 0.0))


def final_kernel(
    high_ref, low_ref, result_ref, idx_ref, tok_ref, cot_ref, *rest,
):
    groups_in, rest = rest[:15], rest[15:]
    ing_ref, out_ref, qb_ref = rest[:3]
    groups_out, rest = rest[3:20], rest[20:]
    idx_s, tok_s, cot_s, high_s, low_s, result_s, ing_s, out_s, load, store = rest[:10]
    state_s, state_load, fresh, fresh_store = rest[10:25], rest[25], rest[26:40], rest[40]
    images, _, d = high_ref.shape
    state = [
        pltpu.make_async_copy(src, dst, state_load.at[i])
        for i, (src, dst) in enumerate(zip(groups_in, state_s))
    ]
    rows = [
        pltpu.make_async_copy(src, dst, load.at[2, i])
        for i, (src, dst) in enumerate(
            ((high_ref, high_s), (low_ref, low_s), (result_ref, result_s))
        )
    ]
    loads = []
    for k, (a, b) in enumerate(CROPS):
        for j, (src, dst) in enumerate(((cot_ref, cot_s), (tok_ref, tok_s))):
            loads.append(pltpu.make_async_copy(src.at[a:b], dst.at[a:b], load.at[j, k]))
    for c in rows[:2] + loads[:1] + rows[2:] + loads[1:] + state:
        c.start()
    stores = []

    def update(g):
        grad, first, second, master, average = [ref[...] for ref in state_s[5 * g : 5 * g + 5]]
        new = adamw(grad, first, second, master, average, *GROUPS[g])
        if g < 2:
            new = new + (new[2].astype(bf16),)
        base = 5 * g if g < 2 else 10
        stores.append(
            pltpu.make_async_copy(state_s[5 * g], groups_out[14 + g], fresh_store.at[14 + g])
        )
        stores[-1].start()
        for i, value in enumerate(new):
            fresh[base + i][...] = value
            c = pltpu.make_async_copy(fresh[base + i], groups_out[base + i], fresh_store.at[base + i])
            c.start()
            stores.append(c)

    columns = token_columns(idx_ref, idx_s)
    ones = jnp.ones((images * (UNITS[0][1] - UNITS[0][0]), 128), bf16)
    for c in rows[:2]:
        c.wait()
    for k, ((a, b), (lo, hi)) in enumerate(zip(CROPS, UNITS)):
        n, count = hi - lo, images * (b - a)
        hot = one_hot(columns, k, images)
        taken = tn(hot, ones[: images * n])[:, 0:1] > 0.5
        window = lambda ref: jnp.concatenate([ref[i, lo:hi] for i in range(images)], axis=0)
        spread = tn(hot, window(high_s)) + tn(hot, window(low_s))
        loads[2 * k].wait()
        old = cot_s[a:b].reshape(count, d).astype(f32)
        ing_s[a:b] = jnp.where(taken, spread, old).reshape(b - a, images, d)
        stores.append(pltpu.make_async_copy(ing_s.at[a:b], ing_ref.at[a:b], store.at[0, k]))
        stores[-1].start()
        if k == 0:
            rows[2].wait()
        loads[2 * k + 1].wait()
        old = tok_s[a:b].reshape(count, d).astype(f32)
        new = jnp.where(taken, tn(hot, window(result_s)), old).astype(bf16)
        out_s[a:b] = new.reshape(b - a, images, d)
        stores.append(pltpu.make_async_copy(out_s.at[a:b], out_ref.at[a:b], store.at[1, k]))
        stores[-1].start()
        if k == 0:
            for c in state:
                c.wait()
        update(k)
    qb_ref[...] = state_s[10][3]
    for c in stores:
        c.wait()


def sds(*shape_dtype):
    return jax.ShapeDtypeStruct(shape_dtype[:-1], shape_dtype[-1])


def scratch(*shape_dtype):
    return pltpu.VMEM(shape_dtype[:-1], shape_dtype[-1])


def dma(*shape):
    return pltpu.SemaphoreType.DMA(shape)


def per_device(
    tokens, cotangent, kept_index,
    attention_weights, attention_first, attention_second, attention_average,
    feedforward_weights, feedforward_first, feedforward_second, feedforward_average,
    vector_weights, vector_first, vector_second, vector_average,
):
    images, length, d = tokens.shape
    ndp, nmp = lax.axis_size("dp"), lax.axis_size("mp")
    links = (ndp, nmp) == (8, MP)
    vec = vector_weights
    rows, hb = feedforward_weights.shape[1:]
    hidden = nmp * hb
    mask = masks()
    mask_specs = [full(m.shape) for m in mask]
    tok, cot = tokens.transpose(1, 0, 2), cotangent.transpose(1, 0, 2)
    comm = (lambda i: dict(collective_id=i, has_side_effects=True)) if links else (lambda i: {})

    att, ff = attention_weights.T, feedforward_weights
    if not links:
        att, ff = att.astype(bf16), ff.astype(bf16)
        att = lax.all_gather(att, ("dp", "mp"), axis=0, tiled=True)
        wff = lax.all_gather(lax.all_gather(ff, "dp", axis=1, tiled=True), "mp", axis=0)
    now = lambda *s: pl.BlockSpec((1,) + s, lambda i: (jnp.maximum(i - 1, 0), 0, 0))
    whole = lambda *s: pl.BlockSpec(s, lambda j: (0,) * len(s), pipeline_mode=pl.Buffered(1))
    rowspec = (images, RI, d)
    outs = pl.pallas_call(
        functools.partial(forward_kernel, links),
        grid=(1 + images,),
        in_specs=[ANY, ANY, full(kept_index.shape), full(vec.shape), *mask_specs]
        + ([full(att.shape), full(ff.shape)] if links else [ANY, ANY]),
        out_specs=[full(rowspec)] * 3 + [
            now(RI, 3 * d), now(RI, d), now(RI, d), now(RI, d), now(RI, d), ANY,
        ] + [ANY] * links,
        out_shape=[sds(*rowspec, bf16)] * 3 + [
            sds(images, RI, 3 * d, bf16), sds(*rowspec, bf16), sds(*rowspec, f32),
            sds(*rowspec, f32), sds(*rowspec, bf16), sds(4 * d, d, bf16),
        ] + [sds(nmp, 2, d, hb, bf16)] * links,
        scratch_shapes=[
            scratch(4 * d, d, bf16), scratch(length, images, d, bf16), scratch(length, images, d, bf16),
            scratch(8, 384, f32), dma(3),
        ] + (
            [scratch(rows, d, bf16), scratch(2, rows, hb, bf16)]
            + [dma(4, Gather.SLOTS), dma(4, Gather.SLOTS), dma(4, 1)] if links else []
        ),
        compiler_params=params(**comm(0)),
        name="forward",
    )(tok, cot, kept_index, vec, *mask, att, ff)
    kept, normed, cotk, proj, mixed, branch, resid, n2, watt = outs[:9]
    if links:
        wff = outs[9]

    outs = pl.pallas_call(
        functools.partial(feed_kernel, links),
        grid=(nmp,),
        in_specs=[
            whole(*rowspec), whole(*rowspec), ANY, ANY, full(vec.shape),
        ],
        out_specs=[full(rowspec), full(rowspec), ANY, full((nmp, hb))]
        + [full((2, 2, rows, hb))] * links,
        out_shape=[
            sds(*rowspec, bf16), sds(*rowspec, f32),
            sds(nmp, 2, d, hb, bf16), sds(nmp, hb, f32),
        ] + [sds(2, 2, rows, hb, bf16)] * links,
        scratch_shapes=[
            scratch(*rowspec, f32), scratch(images * RI, hb, bf16), scratch(images * RI, hb, bf16),
            *[scratch(RI, hb, f32)] * 4,
            scratch(nmp, 2, d, hb, bf16), scratch(2, 2, d, hb, bf16), dma(nmp + 1), dma(2),
        ] + (
            [dma(Gather.SLOTS), dma(Gather.SLOTS), dma(4)]
            + [scratch(n, 2, rows, hb, bf16) for n in (8, 8, 2, 2, 2)]
            + [dma(Reduce.SLOTS), dma(Reduce.SLOTS), dma(8)] if links else []
        ),
        compiler_params=params(**comm(3)),
        name="feedforward",
    )(n2, cotk, resid, wff, vec)
    result, n2g, gff, bg = outs[:4]

    spans = (16, 16, 4, 4, 4, 4)
    outs = pl.pallas_call(
        functools.partial(backward_kernel, links),
        grid=(images,),
        in_specs=[
            per_image(RI, d), per_image(RI, d), per_image(RI, d), per_image(RI, d),
            per_image(RI, d), per_image(RI, 3 * d),
            pl.BlockSpec((d, d), lambda i: (3, 0)), full(vec.shape), *mask_specs,
        ] + [ANY, full((2, 2, rows, hb))] * links,
        out_specs=[per_image(RI, 4 * d), per_image(RI, d), per_image(RI, 1), full((8, d))]
        + [full((2, rows, hb))] * links,
        out_shape=[
            sds(images, RI, 4 * d, bf16), sds(*rowspec, f32), sds(images, RI, 1, f32), sds(8, d, f32),
        ] + [sds(2, rows, hb, f32)] * links,
        scratch_shapes=[scratch(RI, d, bf16)] + (
            [scratch(n, 2, rows, hb, bf16) for n in (8, 8, 2, 2, 2, 4)]
            + [dma(Reduce.SLOTS), dma(Reduce.SLOTS), dma(8)] if links else []
        ),
        compiler_params=params(**comm(1)),
        name="attention_backward",
    )(n2g, cotk, branch, resid, normed, proj, watt, vec, *mask, *([gff, outs[4]] if links else []))
    dp, resg, rg, vecg = outs[:4]
    if links:
        feedforward_gradient = outs[4]

    full_d = (4 * d, d)
    outs = pl.pallas_call(
        functools.partial(grads_kernel, links),
        grid=(4 + images,),
        in_specs=[ANY, ANY, ANY, full((images, RI, 1)), ANY, ANY, full(vec.shape), ANY]
        + [full((8, d)), full((hidden // d, d))] * links,
        out_specs=[full(rowspec), full(rowspec)]
        + ([full((rows, d)), full(vec.shape)] if links else [full(full_d), full((8, d))]),
        out_shape=[sds(*rowspec, bf16), sds(*rowspec, bf16)]
        + ([sds(rows, d, f32), sds(*vec.shape, f32)] if links else [sds(*full_d, bf16), sds(8, d, f32)]),
        scratch_shapes=([scratch(*full_d, bf16), scratch(8, d, f32)] if links else []) + [
            scratch(3 * d, d, bf16), scratch(4, *rowspec, bf16), scratch(2, *rowspec, bf16),
            scratch(*rowspec, f32), scratch(*rowspec, bf16), dma(9),
        ] + (
            [scratch(n, rows, d, bf16) for n in spans[1:]]
            + [dma(Reduce.SLOTS), dma(Reduce.SLOTS), scratch(11, 16, d, f32), dma(8), dma(8)]
            if links else []
        ),
        compiler_params=params(**comm(2)),
        name="attention_grads",
    )(
        dp, normed, mixed, rg, resg, kept, vec, watt,
        *([vecg, bg] if links else []),
    )
    high, low = outs[:2]
    if links:
        gatt, vector_gradient = outs[2:]
    else:
        gatt, vecg_in = outs[2:]
        local = jnp.concatenate([vecg_in[:2], vecg[:7], bg], axis=0)
        gatt = lax.psum_scatter(gatt, ("dp", "mp"), scatter_dimension=0, tiled=True).astype(f32)
        gff = lax.psum_scatter(gff, "mp", scatter_dimension=0, tiled=False)
        gff = lax.psum_scatter(gff, "dp", scatter_dimension=1, tiled=True)
        feedforward_gradient, vector_gradient = gff.astype(f32), lax.psum(local, ("dp", "mp"))

    state = []
    for grad, *rest in (
        (gatt, attention_first.T, attention_second.T, attention_weights.T, attention_average.T),
        (
            feedforward_gradient, feedforward_first, feedforward_second, feedforward_weights,
            feedforward_average,
        ),
        (vector_gradient, vector_first, vector_second, vector_weights, vector_average),
    ):
        state += [grad, *rest]
    fresh = []
    for g in range(3):
        fresh += [(state[5 * g].shape, f32)] * 4 + [(state[5 * g].shape, bf16)] * (g < 2)
    ing, out, qb, *new = pl.pallas_call(
        final_kernel,
        in_specs=[ANY, ANY, ANY, pl.BlockSpec(memory_space=pltpu.VMEM), ANY, ANY] + [ANY] * 15,
        out_specs=[ANY, ANY, pl.BlockSpec(memory_space=pltpu.VMEM)] + [ANY] * (len(fresh) + 3),
        out_shape=[sds(length, images, d, f32), sds(length, images, d, bf16), sds(d, f32)]
        + [jax.ShapeDtypeStruct(*f) for f in fresh]
        + [sds(*state[5 * g].shape, f32) for g in range(3)],
        scratch_shapes=[
            scratch(8, 384, f32),
            scratch(length, images, d, bf16), scratch(length, images, d, bf16),
            *[scratch(*rowspec, bf16)] * 3,
            scratch(length, images, d, f32), scratch(length, images, d, bf16), dma(3, 3), dma(2, 3),
            *[pltpu.VMEM(v.shape, f32) for v in state], dma(15),
            *[pltpu.VMEM(*f) for f in fresh], dma(len(fresh) + 3),
        ],
        compiler_params=params(),
        name="finish",
    )(high, low, result, kept_index, tok, cot, *state)
    att_new, ff_new, vec_new = [v.T for v in new[:5]], new[5:10], new[10:14]
    gatt, feedforward_gradient, vector_gradient = new[14:]
    return (
        out.transpose(1, 0, 2), ing.transpose(1, 0, 2),
        gatt.T, *att_new, feedforward_gradient, *ff_new, vector_gradient, *vec_new, qb,
    )


def solution(mesh):
    rows = P(("dp", "mp"), None, None)
    att = P(None, ("dp", "mp"))
    feed = P(None, "dp", "mp")
    in_specs = (rows, rows, P(("dp", "mp"), None)) + (att,) * 4 + (feed,) * 4 + (P(),) * 4
    out_specs = (rows, rows) + (att,) * 6 + (feed,) * 6 + (P(),) * 6
    return jax.shard_map(
        per_device, mesh=mesh, in_specs=in_specs, out_specs=out_specs, check_vma=False
    )
```

```python
import functools

import jax
import jax.numpy as jnp
import numpy as np
from jax import lax
from jax.experimental import pallas as pl
from jax.experimental.pallas import tpu as pltpu
from jax.sharding import PartitionSpec as P

H = 12
HD = 64
LG = 197
LL = 37
KG = LG // 2
KL = LL // 2
LOC = 4 * KL
KEPT = 2 * KG + LOC
RI = -(-KEPT // 16) * 16
SPANS = ((0, KG), (KG, 2 * KG), (2 * KG, KEPT))
UNITS = tuple((a // 16 * 16, -(-b // 16) * 16) for a, b in SPANS)
PAIRS = H // 2
W2L = 2 * HD

bf16 = jnp.bfloat16
f32 = jnp.float32


def params(limit=56, **kw):
    return pltpu.CompilerParams(vmem_limit_bytes=limit << 20, **kw)


def full(shape):
    return pl.BlockSpec(shape, lambda *_: (0,) * len(shape))


def per_image(*shape):
    return pl.BlockSpec((1,) + shape, lambda i, *_: (i,) + (0,) * len(shape))


def nn(a, b):
    return lax.dot_general(a, b, (((1,), (0,)), ((), ())), preferred_element_type=f32)


def nt(a, b):
    return lax.dot_general(a, b, (((1,), (1,)), ((), ())), preferred_element_type=f32)


def tn(a, b):
    return lax.dot_general(a, b, (((0,), (0,)), ((), ())), preferred_element_type=f32)


def normalize(rows):
    center = rows - jnp.mean(rows, axis=-1, keepdims=True)
    spread = jnp.mean(center * center, axis=-1, keepdims=True)
    inverse = lax.rsqrt(spread + 1e-06)
    return center * inverse, inverse


def norm_backward(upstream, standard, inverse, gain):
    scaled = upstream * gain
    return inverse * (
        scaled
        - jnp.mean(scaled, axis=-1, keepdims=True)
        - standard * jnp.mean(scaled * standard, axis=-1, keepdims=True)
    )


def colsum(v):
    return jnp.sum(v, axis=0, keepdims=True)


def masks():
    crop = np.full(RI, -1)
    crop[:KG], crop[KG : 2 * KG] = 0, 1
    for c in range(4):
        crop[2 * KG + c * KL : 2 * KG + (c + 1) * KL] = 2 + c
    adds, valids = [], []
    for (a, b), (lo, hi) in zip(SPANS, UNITS):
        rows = np.arange(lo, hi)
        inside = (rows >= a) & (rows < b)
        same = (crop[lo:hi, None] == crop[None, lo:hi]) & inside[:, None] & inside[None, :]
        adds.append(np.tile(np.where(same, 0.0, -1e9), (1, 2)).astype(np.float32))
        valids.append(np.tile(inside[None, :].astype(np.float32), (8, 2)))
    return [jnp.asarray(m) for m in adds + valids]


def lane_half(shape):
    return lax.broadcasted_iota(jnp.int32, shape, len(shape) - 1) < HD


def split_heads(v, scale):
    first = lane_half(v.shape)
    zero = jnp.zeros_like(v)
    if scale != 1.0:
        v = v * jnp.asarray(scale, v.dtype)
    return jnp.concatenate([jnp.where(first, v, zero), jnp.where(first, zero, v)], axis=0)


def join_heads(v):
    n = v.shape[0] // 2
    return jnp.where(lane_half((n, v.shape[1])), v[:n], v[n:])


def softmax_keys(st, valid):
    p = jnp.exp(st - jnp.max(st, axis=0, keepdims=True))
    return p * (valid / jnp.sum(p, axis=0, keepdims=True))


def store_window(ref, image, lo, hi, last, cols, value, tail):
    value = value.astype(bf16)
    if tail is not None:
        value = jnp.concatenate([value[:16] + tail, value[16:]], axis=0)
    end = hi if last else hi - 16
    ref[image, lo:end, cols] = value[: end - lo]
    return None if last else value[end - lo :]


MESH = pl.DeviceIdType.MESH
ANY = pl.BlockSpec(memory_space=pl.ANY)
MP = 4
CROPS = ((0, LG), (LG, 2 * LG), (2 * LG, 2 * LG + 4 * LL))
ORDER = ((0, 1, 2, 3), (1, 0, 1, 2), (2, 2, 3, 1), (3, 3, 0, 0))


def flip(index, bit):
    return index + bit * (1 - 2 * lax.rem(lax.div(index, bit), 2))


def remote(src, dst, send, recv, to):
    return pltpu.make_async_remote_copy(
        src_ref=src, dst_ref=dst, send_sem=send, recv_sem=recv, device_id=to, device_id_type=MESH
    )


class Sends:
    def __init__(self):
        self.made = []

    def start(self, make, when=None):
        def go():
            make().start()

        go() if when is None else pl.when(when)(go)
        self.made.append((make, when))

    def finish(self):
        for make, when in self.made:
            def wait(make=make):
                make().wait_send()

            wait() if when is None else pl.when(when)(wait)


class Place:
    def __init__(self):
        self.dp = lax.axis_index("dp")
        self.z = lax.axis_index("mp")
        x, y = flip(self.dp, 2), flip(self.dp, 4)
        self.core = (flip(self.dp, 1), self.z)
        self.x, self.y = (x, self.z), (y, self.z)
        self.chips = (self.dp, x, y, flip(x, 4))
        self.mates = tuple(flip(c, 1) for c in self.chips)
        power = (1 + 3 * lax.rem(self.z, 2)) * (1 + 15 * lax.div(self.z, 2))
        self.event = []
        for row in ORDER:
            code = sum(v << (2 * i) for i, v in enumerate(row))
            self.event.append(lax.rem(lax.div(0 * power + code, power), 4))
        self.low, self.high = self.z > 0, self.z < MP - 1
        self.middle = self.low & self.high
        self.line = [lax.rem(self.z + k, MP) for k in range(MP)]
        self.up, self.down = (self.dp, self.z + 1), (self.dp, self.z - 1)
        self.onward = (self.up, self.down, (self.dp, 3 * (self.z - 1)))

    def barrier(self):
        sem = pltpu.get_barrier_semaphore()
        others = [self.core, self.x, self.y]
        others += [(self.dp, k) for k in self.line[1:]]
        for other in others:
            pl.semaphore_signal(sem, inc=1, device_id=other, device_id_type=MESH)
        pl.semaphore_wait(sem, len(others))


def att_block(ref, dp, z, rows):
    return ref.at[pl.ds(pl.multiple_of((dp * MP + z) * rows, 32), rows), :]


def att_part(ref, dp, z, rows, h):
    half = rows // 2
    return ref.at[pl.ds(pl.multiple_of((dp * MP + z) * rows + h * half, 16), half), :]


def ff_part(ref, dp, z, rows, h):
    return ref.at[z, h, pl.ds(pl.multiple_of(dp * rows, 32), rows), :]


def ff_block(ref, dp, z, rows):
    return ref.at[z, :, pl.ds(pl.multiple_of(dp * rows, 32), rows), :]


class Gather:
    ALONG, X, Y, D, C, SLOTS = 0, 4, 8, 12, 16, 32

    def __init__(self, at, first, place, send, recv, local):
        self.at, self.first, self.place = at, first, place
        self.send, self.recv, self.local = send, recv, local
        self.sends = Sends()

    def copy(self, slot, e, r, to):
        slot = self.ALONG + self.at.event[e] if slot is None else slot
        dst = self.place(e, self.at.chips[r])
        src = self.first(e) if r == 0 else dst
        return remote(src, dst, self.send.at[slot], self.recv.at[slot], to)

    def put(self, slot, e, r, to, when=None):
        self.sends.start(lambda: self.copy(slot, e, r, to), when)

    def got(self, slot, e, dp):
        dst = self.place(e, dp)
        remote(dst, dst, self.send.at[slot], self.recv.at[slot], self.at.core).wait_recv()

    def keep(self, e):
        return pltpu.make_async_copy(self.first(e), self.place(e, self.at.dp), self.local.at[e])

    def spread(self, e):
        self.put(self.X + e, e, 0, self.at.x)
        self.put(self.Y + e, e, 0, self.at.y)
        self.put(self.C + 4 * e, e, 0, self.at.core)

    def begin(self):
        at = self.at
        self.keep(0).start()
        for to, when in ((at.up, at.high), (at.down, at.low)):
            self.put(None, 0, 0, to, when)
        self.spread(0)

    def direct(self):
        self.keep(0).start()
        for zb in self.at.line[1:]:
            self.put(None, 0, 0, (self.at.dp, zb))

    def arrived(self, e):
        self.got(self.ALONG + self.at.event[e], e, self.at.dp)

    def along(self, e):
        at = self.at
        self.arrived(e)
        self.put(None, e, 0, at.onward[e - 1], at.middle)
        self.spread(e)

    def plane(self, e):
        at = self.at
        self.got(self.X + e, e, at.chips[1])
        if e % 2 == 0:
            self.put(self.D + e, e, 1, at.y)
        self.put(self.C + 4 * e + 1, e, 1, at.core)
        self.got(self.Y + e, e, at.chips[2])
        if e % 2 == 1:
            self.put(self.D + e, e, 2, at.x)
        self.put(self.C + 4 * e + 2, e, 2, at.core)

    def corner(self, e):
        self.got(self.D + e, e, self.at.chips[3])
        self.put(self.C + 4 * e + 3, e, 3, self.at.core)

    def finish(self, e):
        for r in range(4):
            self.got(self.C + 4 * e + r, e, self.at.mates[r])


def add_into(target, first, *others):
    if len(others) == 1 and target.dtype == bf16:
        @pl.loop(0, first.shape[0] // 48)
        def _(i):
            s = pl.ds(pl.multiple_of(i * 48, 16), 48)
            target[s, :] = first[s, :] + others[0][s, :]

        return
    step = 48

    @pl.loop(0, first.shape[0] // step)
    def _(i):
        s = pl.ds(pl.multiple_of(i * step, 16), step)
        total = first[s, :].astype(f32)
        for ref in others:
            total = total + ref[s, :].astype(f32)
        target[s, :] = total.astype(target.dtype)


class Reduce:
    C, D, X, Y, ALONG, SLOTS = 0, 16, 20, 24, 28, 32

    def __init__(self, at, source, own, parts, bufs, send, recv, load=None, base=0):
        self.at, self.source, self.own, self.parts, self.base = at, source, own, parts, base
        self.c, self.d, self.x, self.y, self.line = bufs
        self.send, self.recv, self.load = send, recv, load
        self.sends = Sends()

    def put(self, slot, src, dst, to):
        self.sends.start(
            lambda: remote(src(), dst(), self.send.at[slot], self.recv.at[slot], to)
        )

    def got(self, slot, dst):
        remote(dst, dst, self.send.at[slot], self.recv.at[slot], self.at.core).wait_recv()

    def slot(self, e, r):
        return 4 * (e - self.base) + r

    def cross(self, e, r):
        i = self.slot(e, r)
        self.put(self.C + i, lambda: self.source(e, self.at.mates[r]), lambda: self.c.at[i], self.at.core)
        if self.load is not None:
            self.load(e, r).start()

    def add(self, e, r, *others, target=None):
        i = self.slot(e, r)
        self.got(self.C + i, self.c.at[i])
        if self.load is not None:
            self.load(e, r).wait()
        refs = [self.own(e, r), self.c.at[i]] + list(others)
        self.total(refs[0] if target is None else target, *refs)

    def total(self, target, *refs):
        for t, *rest in zip(self.parts(target), *[self.parts(ref) for ref in refs]):
            add_into(t, *rest)

    def corner(self, e):
        at, i = self.at, e - self.base
        self.add(e, 3)
        self.put(
            self.D + i, lambda: self.own(e, 3), lambda: self.d.at[i], at.x if e % 2 else at.y
        )
        r, slot, buf, to = (1, self.X, self.x, at.x) if e % 2 else (2, self.Y, self.y, at.y)
        self.add(e, r)
        self.put(slot + i, lambda: self.own(e, r), lambda: buf.at[i], to)

    def plane(self, e):
        at, i = self.at, e - self.base
        r, slot, buf, to = (2, self.Y, self.y, at.y) if e % 2 else (1, self.X, self.x, at.x)
        self.got(self.D + i, self.d.at[i])
        self.add(e, r, self.d.at[i])
        self.put(slot + i, lambda: self.own(e, r), lambda: buf.at[i], to)

    def gathered(self, e, *others, target=None):
        i = e - self.base
        self.got(self.X + i, self.x.at[i])
        self.got(self.Y + i, self.y.at[i])
        self.add(e, 0, self.x.at[i], self.y.at[i], *others, target=target)

    def send_along(self, e, src):
        at = self.at
        zb = at.event[e]
        self.sends.start(
            lambda: remote(
                src(), self.line.at[at.z], self.send.at[self.ALONG + zb],
                self.recv.at[self.ALONG + at.z], (at.dp, zb),
            )
        )

    def along(self, e):
        self.gathered(e)
        self.send_along(e, lambda: self.own(e, 0))

    def lines(self):
        got = []
        for zb in self.at.line[1:]:
            got.append(self.line.at[zb])
            self.got(self.ALONG + zb, got[-1])
        return got


def pump(schedule, step, point):
    for (s, p), action in schedule:
        if isinstance(point, int):
            if p == point:
                pl.when(step == s)(action)
        else:
            pl.when((step == s) & (point == p))(action)


def do(action, *args):
    return lambda: action(*args)


def token_columns(idx_ref, idx_s, col_s):
    idx_s[...] = jnp.full(idx_s.shape, -1.0, f32)
    idx_s[0 : idx_ref.shape[0], 0 : idx_ref.shape[1]] = idx_ref[...].astype(f32)
    col_s[...] = idx_s[...].T


def one_hot(col_s, crop, images, local):
    (a, b), (s, e), (lo, hi) = [v[2 if local else 0] for v in (CROPS, SPANS, UNITS)]
    n, size = hi - lo, b - a
    count = images * size
    if not local:
        a, s, e, lo = LG * crop, KG * crop, KG * (crop + 1), UNITS[1][0] * crop
        lo = pl.multiple_of(lo, 16)
    columns = col_s[pl.ds(lo, n), :]
    row = lax.broadcasted_iota(jnp.int32, (n, 1), 0) + lo
    pieces = []
    for i in range(images):
        place = (columns[:, i : i + 1].astype(jnp.int32) - a) * images + i
        pieces.append(jnp.where((row >= s) & (row < e), place, -1))
    index = jnp.concatenate(pieces, axis=0)
    hot = lax.broadcasted_iota(jnp.int32, (index.shape[0], count), 1) == index
    return hot.astype(f32).astype(bf16), pl.ds(a, size), lo, n, count


def forward_kernel(
    links, tok_ref, cot_ref, idx_ref, vec_ref, m0_ref, m1_ref, m2_ref, v0_ref, v1_ref, v2_ref,
    att_ref, ff_ref,
    kept_ref, normed_ref, cotk_ref, proj_ref, mixed_ref, branch_ref, resid_ref, n2_ref,
    watt_out, *rest,
):
    if links:
        wff_ref, watt_ref, tok_s, cot_s, idx_s, col_s, load, att_s, ff_s, send, recv, local = rest
    else:
        watt_ref, tok_s, cot_s, idx_s, col_s, load = rest
    step = pl.program_id(0)
    images, _, d = kept_ref.shape
    loads = [
        pltpu.make_async_copy(tok_ref, tok_s, load.at[0]),
        pltpu.make_async_copy(cot_ref, cot_s, load.at[1]),
    ]
    acts, schedule = [[]] * 6, []
    if links:
        at = Place()
        rows = att_ref.shape[0]
        half = rows // 2

        def att_half(h):
            return Gather(
                at,
                lambda e: att_part(watt_ref, at.dp, at.event[e], rows, h) if e
                else att_s.at[h * half : (h + 1) * half],
                lambda e, dp: att_part(watt_ref, dp, at.event[e], rows, h),
                send.at[h], recv.at[h], local.at[h],
            )

        def feed_half(h):
            return Gather(
                at, lambda e: ff_part(wff_ref, at.dp, at.event[e], rows, h) if e else ff_s.at[h],
                lambda e, dp: ff_part(wff_ref, dp, at.event[e], rows, h),
                send.at[2 + h], recv.at[2 + h], local.at[2 + h],
            )

        (a0, a1), (f0, f1) = [att_half(h) for h in (0, 1)], [feed_half(h) for h in (0, 1)]
        acts = [
            [a1.begin, a0.begin],
            [do(a1.along, 1), do(a1.plane, 0), do(a0.along, 1), do(a0.along, 2), do(a1.along, 2)],
            [do(a0.along, 3)],
            [do(a1.along, 3), f0.direct, do(a1.plane, 1), do(a0.plane, 2)],
            [do(a0.plane, 0)],
            [
                do(a0.plane, 3), do(a0.plane, 1), do(a1.plane, 3), do(a1.plane, 2),
                do(a0.corner, 0), do(a1.corner, 1), do(a0.corner, 3), do(a1.corner, 2),
                do(a1.corner, 0), f1.direct, do(a0.corner, 1), do(a0.corner, 2), do(a1.corner, 3),
                do(f0.arrived, 2), do(f0.spread, 2),
            ],
        ]
        schedule = [
            ((1, 3), do(f0.arrived, 3)),
            ((1, 3), do(f0.spread, 3)),
            ((2, 1), do(f1.arrived, 2)),
            ((2, 1), do(f1.spread, 2)),
            ((3, 0), do(f1.arrived, 3)),
            ((3, 0), do(f1.spread, 3)),
            ((3, 0), do(f0.plane, 2)),
            ((3, 1), do(f1.plane, 2)),
            ((3, 1), do(f0.plane, 3)),
            ((3, 3), do(f1.plane, 3)),
            ((4, 3), do(f1.corner, 3)),
            ((4, 3), do(f0.corner, 3)),
            ((4, 3), do(f1.corner, 2)),
            ((4, 3), do(f0.corner, 2)),
        ]
    else:
        fetch = pltpu.make_async_copy(att_ref, watt_ref, load.at[2])
    store = pltpu.make_async_copy(watt_ref, watt_out, load.at[2])

    def clear(dst):
        for i in range(images):
            for _, hi in UNITS[:2]:
                dst[i, hi - 16 : hi] = jnp.zeros((16, d), bf16)

    def pick(crop, local, src, dst):
        hot, span, lo, n, k = one_hot(col_s, crop, images, local)
        got = nn(hot, src[span].reshape(k, d)).astype(bf16)
        for i in range(images):
            part = got[i * n : (i + 1) * n]
            head = pl.ds(lo, 16)
            if local:
                dst[i, head, :] = dst[i, head, :] + part[:16]
            else:
                old = jnp.where(crop == 0, jnp.zeros_like(part[:16]), dst[i, head, :])
                dst[i, head, :] = old + part[:16]
            dst[i, pl.ds(lo + 16, n - 16), :] = part[16:]

    def run(point):
        for action in acts[point]:
            action()

    @pl.when(step == 0)
    def _():
        if links:
            att_s[...] = att_ref[...].astype(bf16)
            at.barrier()
            run(0)
        else:
            fetch.start()
        for c in loads:
            c.start()
        if links:
            ff_s[...] = ff_ref[...].astype(bf16)
        token_columns(idx_ref, idx_s, col_s)
        loads[0].wait()
        clear(kept_ref)

        @pl.loop(0, 2)
        def _(crop):
            pick(crop, False, tok_s, kept_ref)
            for point in (1, 2):
                pl.when(crop == point - 1)(do(run, point))

        pick(2, True, tok_s, kept_ref)
        run(3)
        for i in range(images):
            standard, _ = normalize(kept_ref[i].astype(f32))
            normed_ref[i] = (standard * vec_ref[0:1] + vec_ref[1:2]).astype(bf16)
            if i == 1:
                run(4)
        run(5)
        if links:
            for e in range(4):
                a0.finish(e)
                a1.finish(e)
            a0.keep(0).wait()
            a1.keep(0).wait()
        else:
            fetch.wait()
        store.start()

    pump(schedule, step, 0)

    @pl.when(step > 0)
    def _():
        image = step - 1
        normed = normed_ref[image]
        for j, row in ((0, 3), (1, None), (2, 4)):
            part = nt(normed, watt_ref[j * d : (j + 1) * d, :])
            if row is not None:
                part = part + vec_ref[row : row + 1]
            proj_ref[0, :, j * d : (j + 1) * d] = part.astype(bf16)
        pump(schedule, step, 1)

        @pl.when(step == 2)
        def _():
            loads[1].wait()
            clear(cotk_ref)

        @pl.when((step == 2) | (step == 3))
        def _():
            pick(step - 2, False, cot_s, cotk_ref)

        @pl.when(step == 4)
        def _():
            pick(2, True, cot_s, cotk_ref)

        mrefs, vrefs = (m0_ref, m1_ref, m2_ref), (v0_ref, v1_ref, v2_ref)
        for pair in range(PAIRS):
            cols = lambda j: slice(j * d + pair * W2L, j * d + (pair + 1) * W2L)
            tail = None
            for unit, (lo, hi) in enumerate(UNITS):
                qs = split_heads(proj_ref[0, lo:hi, cols(0)], HD ** -0.5)
                st = nt(proj_ref[0, lo:hi, cols(1)], qs) + mrefs[unit][...]
                pt = softmax_keys(st, vrefs[unit][0:1]).astype(bf16)
                out = join_heads(tn(pt, proj_ref[0, lo:hi, cols(2)]))
                tail = store_window(mixed_ref, 0, lo, hi, unit == 2, cols(0), out, tail)
            if pair == 2:
                pump(schedule, step, 3)
        branch = nt(mixed_ref[0], watt_ref[3 * d :, :]) + vec_ref[5:6]
        branch_ref[0] = branch
        residual = kept_ref[image].astype(f32) + router_score(normed, vec_ref) * branch
        resid_ref[0] = residual
        standard, _ = normalize(residual)
        n2_ref[0] = (standard * vec_ref[6:7] + vec_ref[7:8]).astype(bf16)

    @pl.when(step == images)
    def _():
        if links:
            for feed in (f0, f1):
                feed.finish(2)
                feed.finish(3)
                feed.arrived(1)
                feed.keep(0).wait()
            for part in (a0, a1, f0, f1):
                part.sends.finish()
        store.wait()


def router_score(normed, vec_ref):
    logit = jnp.sum(normed.astype(f32) * vec_ref[2:3], axis=-1, keepdims=True)
    return jax.nn.sigmoid(logit)


def feed_kernel(
    links, n2_ref, cot_ref, resid_ref, w_ref, vec_ref,
    result_ref, n2g_ref, gff_ref, bg_ref, *rest,
):
    if links:
        acc_ref, out_s, act_s, ig_s, i0, i1, a0, a1, w_s, g_s, load, store = rest[:12]
        send, recv, local, a, c, dd, x, y, rsend, rrecv, rlocal = rest[12:]
    else:
        out_s, act_s, ig_s, i0, i1, a0, a1, w_s, g_s, load, store = rest
    inner_s, ag_s = (i0, i1), (a0, a1)
    step = pl.program_id(0)
    last = pl.num_programs(0) - 1
    images, _, d = n2_ref.shape
    nload = w_s.shape[0]
    hb = w_ref.shape[3]
    block, schedule = step, []
    if links:
        at = Place()
        rows = acc_ref.shape[2]
        block = at.event[0]
        for e in (1, 2, 3):
            block = jnp.where(step == 3 - e, at.event[e], block)
        gather = Gather(
            at, lambda e: ff_block(w_ref, at.dp, at.event[e], rows),
            lambda e, dp: w_s.at[3 - e, :, pl.ds(pl.multiple_of(dp * rows, 32), rows), :],
            send, recv, local,
        )
        reduce = Reduce(
            at, lambda e, dp: ff_block(gff_ref, dp, at.event[e], rows),
            lambda e, r: a.at[4 * (e - 2) + r],
            lambda ref: (ref.at[0], ref.at[1]), (c, dd, x, y, None), rsend, rrecv,
            lambda e, r: pltpu.make_async_copy(
                ff_block(gff_ref, at.chips[r], at.event[e], rows), a.at[4 * (e - 2) + r],
                rlocal.at[4 * (e - 2) + r],
            ),
            2,
        )

        def start():
            at.barrier()
            for e in (1, 0):
                gather.spread(e)
                gather.keep(e).start()

        def ready(e):
            gather.finish(e)
            gather.keep(e).wait()

        def cross(e):
            for r in (3, 1, 2, 0):
                reduce.cross(e, r)

        schedule = [
            ((1, 0), do(gather.plane, 1)),
            ((1, 3), do(gather.plane, 0)),
            ((1, 4), do(cross, 3)),
            ((2, 0), do(gather.corner, 1)),
            ((2, 0), do(reduce.corner, 3)),
            ((2, 0), do(cross, 2)),
            ((2, 0), do(ready, 1)),
            ((2, 2), do(reduce.corner, 2)),
            ((2, 2), do(gather.corner, 0)),
            ((2, 5), do(reduce.plane, 3)),
            ((3, 0), do(ready, 0)),
            ((3, 0), do(reduce.plane, 2)),
        ]

    def fetch(e):
        return pltpu.make_async_copy(
            w_ref.at[at.event[3 - e] if links else e], w_s.at[e], load.at[e]
        )

    def save(slot, which):
        return pltpu.make_async_copy(g_s.at[slot], gff_ref.at[which], store.at[slot])

    residual = pltpu.make_async_copy(resid_ref, out_s, load.at[nload])
    early = (0, 1) if links else range(w_s.shape[0])

    @pl.when(step == 0)
    def _():
        for e in early:
            fetch(e).start()
        if links:
            start()
        residual.start()
        n2g_ref[...] = jnp.zeros_like(n2g_ref)
        bg_ref[...] = jnp.zeros_like(bg_ref)
        fetch(0).wait()
        residual.wait()

    for e in early[1:]:
        @pl.when(step == e)
        def _(e=e):
            fetch(e).wait()

    slot = lax.rem(step, 2)

    @pl.when(step > 0)
    def _():
        save(1 - slot, 0).wait()

    pump(schedule, step, 0)

    def first(i):
        inner_s[i % 2][...] = nn(n2_ref[i], w_s[step, 0]) + vec_ref[pl.ds(9 + block, 1), :]
        ag_s[i % 2][...] = nn(cot_ref[i], w_s[step, 1])

    def second(i):
        inner = inner_s[i % 2][...]
        phi = 0.5 * (1.0 + lax.erf(inner * 0.7071067811865476))
        act = (inner * phi).astype(bf16)
        slope = phi + inner * jnp.exp(-0.5 * inner * inner) * 0.3989422804014327
        ig = (ag_s[i % 2][...] * slope).astype(bf16)
        rows_i = slice(i * RI, (i + 1) * RI)
        act_s[rows_i, :] = act
        ig_s[rows_i, :] = ig
        bg_ref[pl.ds(block, 1), :] += colsum(ig.astype(f32))
        out_s[i] += nt(act, w_s[step, 1])
        n2g_ref[i] += nt(ig, w_s[step, 0])

    first(0)
    for i in range(images):
        pump(schedule, step, i + 1)
        if i + 1 < images:
            first(i + 1)
        second(i)

    pump(schedule, step, 5)
    n2 = n2_ref[...].reshape(images * RI, d)
    cot = cot_ref[...].reshape(images * RI, d)
    g_s[slot, 0] = tn(n2, ig_s[...]).astype(bf16)
    g_s[slot, 1] = tn(cot, act_s[...]).astype(bf16)
    save(slot, block).start()

    @pl.when(step == last)
    def _():
        result_ref[...] = (out_s[...] + vec_ref[8:9]).astype(bf16)
        if links:
            reduce.gathered(3, target=acc_ref.at[0])
            reduce.gathered(2, target=acc_ref.at[1])
            gather.sends.finish()
            reduce.sends.finish()
        save(slot, 0).wait()


def backward_kernel(
    links, n2g_ref, cotk_ref, branch_ref, resid_ref, normed_ref, proj_ref, wout_ref,
    vec_ref, m0_ref, m1_ref, m2_ref, v0_ref, v1_ref, v2_ref, *rest,
):
    if links:
        gff_ref, acc_ref, dp_ref, resg_ref, rg_ref, vecg_ref, gout_ref = rest[:7]
        mg_s, a, c, dd, x, y, line, send, recv, local = rest[7:]
    else:
        dp_ref, resg_ref, rg_ref, vecg_ref, mg_s = rest
    step = pl.program_id(0)
    schedule = []
    if links:
        at = Place()
        rows = gout_ref.shape[1]
        reduce = Reduce(
            at, lambda e, dp: ff_block(gff_ref, dp, at.event[e], rows),
            lambda e, r: a.at[4 * e + r],
            lambda ref: (ref.at[0], ref.at[1]), (c, dd, x, y, line), send, recv,
            lambda e, r: pltpu.make_async_copy(
                ff_block(gff_ref, at.chips[r], at.event[e], rows), a.at[4 * e + r],
                local.at[4 * e + r],
            ),
        )

        def start():
            at.barrier()
            reduce.send_along(2, lambda: acc_ref.at[1])
            for e in (1, 0):
                for r in (3, 1, 2, 0):
                    reduce.cross(e, r)

        schedule = [
            ((0, 0), start),
            ((0, 1), do(reduce.corner, 1)),
            ((0, 3), do(reduce.send_along, 3, lambda: acc_ref.at[0])),
            ((1, 1), do(reduce.plane, 1)),
            ((1, 3), do(reduce.corner, 0)),
            ((2, 1), do(reduce.along, 1)),
            ((3, 0), do(reduce.plane, 0)),
        ]

    pump(schedule, step, 0)
    d = normed_ref.shape[2]
    normed = normed_ref[0]
    score = router_score(normed, vec_ref)
    branch = branch_ref[0]
    standard, inverse = normalize(resid_ref[0])
    n2g = n2g_ref[0]
    cot = cotk_ref[0].astype(f32)
    resg = cot + norm_backward(n2g, standard, inverse, vec_ref[6:7])
    resg_ref[0] = resg
    bg = (score * resg).astype(bf16)
    rg = jnp.sum(resg * branch, axis=-1, keepdims=True) * score * (1.0 - score)
    rg_ref[0] = rg
    dp_ref[0, :, 3 * d :] = bg
    mg_s[...] = nn(bg, wout_ref[...]).astype(bf16)
    pump(schedule, step, 1)
    mrefs, vrefs = (m0_ref, m1_ref, m2_ref), (v0_ref, v1_ref, v2_ref)
    for pair in range(PAIRS):
        cols = lambda j: slice(j * d + pair * W2L, j * d + (pair + 1) * W2L)
        tails = [None] * 3
        for unit, (lo, hi) in enumerate(UNITS):
            qs = split_heads(proj_ref[0, lo:hi, cols(0)], HD ** -0.5)
            kk = proj_ref[0, lo:hi, cols(1)]
            pt = softmax_keys(nt(kk, qs) + mrefs[unit][...], vrefs[unit][0:1])
            ds = split_heads(mg_s[lo:hi, cols(0)], 1.0)
            gpt = nt(proj_ref[0, lo:hi, cols(2)], ds)
            sg = (pt * (gpt - jnp.sum(pt * gpt, axis=0, keepdims=True))).astype(bf16)
            grads = (
                join_heads(tn(sg, kk)) * HD ** -0.5, nn(sg, qs), nn(pt.astype(bf16), ds)
            )
            for j in range(3):
                tails[j] = store_window(dp_ref, 0, lo, hi, unit == 2, cols(j), grads[j], tails[j])
        if pair == 2:
            pump(schedule, step, 3)
    sums = jnp.concatenate(
        [
            colsum(rg * normed.astype(f32)),
            colsum(dp_ref[0, :, :d].astype(f32)),
            colsum(dp_ref[0, :, 2 * d : 3 * d].astype(f32)),
            colsum(bg.astype(f32)),
            colsum(n2g * standard),
            colsum(n2g),
            colsum(cot),
            jnp.zeros((1, d), f32),
        ],
        axis=0,
    )

    @pl.when(step == 0)
    def _():
        vecg_ref[...] = jnp.zeros_like(vecg_ref)

    vecg_ref[...] += sums
    if links:
        @pl.when(step == pl.num_programs(0) - 1)
        def _():
            reduce.gathered(0, *reduce.lines(), target=gout_ref)
            reduce.sends.finish()


def grads_kernel(
    links, dp_ref, normed_ref, mixed_ref, rg_ref, resg_ref, kept_ref, vec_ref, watt_ref,
    idx_ref, tok_ref, cot_ref, result_ref, *rest,
):
    if links:
        vecb_ref, bias_ref, ing_ref, out_ref, gout_ref, vecout_ref = rest[:6]
        gatt_s, vecg_s, *rest = rest[6:]
        c, dd, x, y, line, send, recv, vbuf, vsend, vrecv = rest[17:]
    else:
        ing_ref, out_ref, gatt_s, vecg_s, *rest = rest
    watt_s, dp_s, act_s, resg_s, kept_s, load, high_ref, low_ref, result_s = rest[:9]
    idx_s, col_s, tok_s, cot_s, ing_s, out_s, fetch, store = rest[9:17]
    step = pl.program_id(0)
    images, _, d = high_ref.shape
    last = 3 + images + 3
    total = images * RI
    chip, schedule = 0, []
    if links:
        at = Place()
        chip = lax.div(at.dp, 2)
        rows = gout_ref.shape[0]
        block = lambda e, dp: att_block(gatt_s, dp, at.event[e], rows)
        reduce = Reduce(
            at, block, lambda e, r: block(e, at.chips[r]), lambda ref: (ref,),
            (c, dd, x, y, line), send, recv,
        )

        def cross(r):
            for e in (3, 2, 1, 0):
                reduce.cross(e, r)

        exchange = lambda k, to: remote(
            vbuf.at[k + 1], vbuf.at[8 + k], vsend.at[k], vrecv.at[k], to
        )
        lines = [
            lambda k=k: remote(
                vbuf.at[0], vbuf.at[4 + at.z], vsend.at[2 + k], vrecv.at[3 + at.z],
                (at.dp, at.line[k]),
            )
            for k in range(1, MP)
        ]

        def spread_vectors():
            vbuf[0, 0:2] = vecg_s[0:2]
            vbuf[0, 2:9] = vecb_ref[0:7]
            vbuf[0, 9:13] = bias_ref[...]
            vbuf[0, 13:16] = jnp.zeros((3, d), f32)
            for make in lines:
                make().start()
            vbuf[4 + at.z] = vbuf[0]

        def line_vectors():
            for k in range(1, MP):
                zb = at.line[k]
                remote(
                    vbuf.at[0], vbuf.at[4 + zb], vsend.at[2 + k], vrecv.at[3 + zb], at.core
                ).wait_recv()
            vbuf[1] = vbuf[4] + vbuf[5] + vbuf[6] + vbuf[7]
            exchange(0, at.core).start()

        def core_vectors():
            exchange(0, at.core).wait()
            vbuf[2] = vbuf[1] + vbuf[8]
            exchange(1, at.x).start()

        def x_vectors():
            exchange(1, at.x).wait()
            vbuf[3] = vbuf[2] + vbuf[9]
            exchange(2, at.y).start()

        turns = (3 - chip, flip(chip, 1), flip(chip, 2), chip)
        schedule = [
            ((1, 2), do(cross, 3)),
            ((1, 2), do(cross, 1)),
            ((2, 2), do(reduce.corner, 3)),
            ((2, 2), do(cross, 2)),
            ((3, 2), do(cross, 0)),
            ((4, 1), do(reduce.plane, 3)),
            ((5, 0), do(reduce.corner, 2)),
            ((6, 0), do(reduce.corner, 1)),
            ((6, 0), do(reduce.along, 3)),
            ((7, 0), do(reduce.plane, 2)),
            ((8, 0), spread_vectors),
            ((8, 0), do(reduce.plane, 1)),
            ((8, 0), do(reduce.corner, 0)),
            ((8, 1), do(reduce.along, 2)),
            ((8, 2), line_vectors),
            ((9, 1), core_vectors),
            ((9, 1), do(reduce.along, 1)),
            ((9, 1), do(reduce.plane, 0)),
            ((9, 2), x_vectors),
        ]
    else:
        turns = (0, 1, 2, 3)
    turn = turns[3]
    for k in (2, 1, 0):
        turn = jnp.where(step == k, turns[k], turn)

    def columns(k):
        lanes = pl.ds(pl.multiple_of(turns[k] * d, 128), d) if links else pl.ds(k * d, d)
        return pltpu.make_async_copy(dp_ref.at[:, :, lanes], dp_s.at[turns[k]], load.at[k])

    acts = [
        pltpu.make_async_copy(normed_ref, act_s.at[0], load.at[4]),
        pltpu.make_async_copy(mixed_ref, act_s.at[1], load.at[5]),
    ]
    later = [
        pltpu.make_async_copy(watt_ref.at[: 3 * d], watt_s, load.at[6]),
        pltpu.make_async_copy(resg_ref, resg_s, load.at[7]),
        pltpu.make_async_copy(kept_ref, kept_s, load.at[8]),
        pltpu.make_async_copy(result_ref, result_s, load.at[9]),
    ]

    def crop_copies(crop, size):
        span = pl.ds(LG * crop, size)
        slot = lax.rem(crop, 2)
        here = pl.ds(0, size)
        return [
            pltpu.make_async_copy(cot_ref.at[span], cot_s.at[slot, here], fetch.at[0, slot]),
            pltpu.make_async_copy(tok_ref.at[span], tok_s.at[slot, here], fetch.at[1, slot]),
            pltpu.make_async_copy(ing_s.at[slot, here], ing_ref.at[span], store.at[0, slot]),
            pltpu.make_async_copy(out_s.at[slot, here], out_ref.at[span], store.at[1, slot]),
        ]

    def place(crop, local):
        hot, span, lo, n, count = one_hot(col_s, crop, images, local)
        size = count // images
        window = lambda ref: jnp.concatenate([ref[i, pl.ds(lo, n), :] for i in range(images)], axis=0)
        taken = tn(hot, jnp.ones((images * n, 128), bf16))[:, 0:1] > 0.5
        get_cot, get_tok, put_ing, put_out = crop_copies(crop, size)
        slot = lax.rem(crop, 2)
        get_tok.wait()
        old = tok_s[slot, 0:size].reshape(count, d).astype(f32)
        new = jnp.where(taken, tn(hot, window(result_s)), old).astype(bf16)
        out_s[slot, 0:size] = new.reshape(size, images, d)
        put_out.start()
        pump(schedule, step, 1)
        get_cot.wait()
        spread = tn(hot, window(high_ref)) + tn(hot, window(low_ref))
        old = cot_s[slot, 0:size].reshape(count, d).astype(f32)
        ing_s[slot, 0:size] = jnp.where(taken, spread, old).reshape(size, images, d)
        put_ing.start()

    @pl.when(step == 0)
    def _():
        columns(0).start()
        for copy in acts:
            copy.start()
        for k in (1, 2, 3):
            columns(k).start()
        for copy in later:
            copy.start()
        vecg_s[...] = jnp.zeros_like(vecg_s)
        if links:
            at.barrier()
        for copy in acts:
            copy.wait()

    for k in range(4):
        @pl.when(step == k)
        def _(k=k):
            columns(k).wait()

    @pl.when(step < 4)
    def _():
        which = jnp.where(turn == 3, 1, 0)
        where = pl.ds(pl.multiple_of(turn * d, 128), d)
        left = dp_s[turn].reshape(total, d)
        gatt_s[where, :] = tn(left, act_s[which].reshape(total, d)).astype(bf16)

    @pl.when(step == 4)
    def _():
        for copy in later:
            copy.wait()

    pump(schedule, step, 0)

    @pl.when((step > 3) & (step < 4 + images))
    def _():
        image = step - 4
        standard, inverse = normalize(kept_s[image].astype(f32))
        ng = rg_ref[image] * vec_ref[2:3]
        for j in range(3):
            ng += nn(dp_s[j, image], watt_s[j * d : (j + 1) * d, :])
        pump(schedule, step, 1)
        grad = resg_s[image] + norm_backward(ng, standard, inverse, vec_ref[0:1])
        high = grad.astype(bf16)
        high_ref[image] = high
        low_ref[image] = (grad - high.astype(f32)).astype(bf16)
        vecg_s[0:1] += colsum(ng * standard)
        vecg_s[1:2] += colsum(ng)

    first_crop = 4 + images

    @pl.when(step == 4)
    def _():
        token_columns(idx_ref, idx_s, col_s)
        for crop in range(2):
            for copy in crop_copies(crop, LG)[:2]:
                copy.start()

    @pl.when((step == first_crop) | (step == first_crop + 1))
    def _():
        place(step - first_crop, False)

    @pl.when(step == first_crop + 1)
    def _():
        for copy in crop_copies(2, 4 * LL)[:2]:
            copy.start()
        for copy in crop_copies(0, LG)[2:]:
            copy.wait()

    @pl.when(step == first_crop + 2)
    def _():
        place(2, True)

    pump(schedule, step, 2)

    @pl.when(step == last)
    def _():
        for copy in crop_copies(1, LG)[2:] + crop_copies(2, 4 * LL)[2:]:
            copy.wait()

    if links:
        @pl.when(step == last)
        def _():
            exchange(2, at.y).wait()
            full_sum = vbuf[3] + vbuf[10]
            vecout_ref[...] = full_sum[: vecout_ref.shape[0]]
            reduce.gathered(0, *reduce.lines(), target=gout_ref)
            for make in lines:
                make().wait_send()
            reduce.sends.finish()


def adamw(grad, first, second, master, average, rate, decay):
    first_new = 0.5 * first + 0.5 * grad
    second_new = 0.5 * second + 0.5 * grad * grad
    update = first_new / (jnp.sqrt(second_new) + 1e-08)
    master_new = master - rate * (update + decay * master)
    average_new = 0.9 * average + 0.1 * master_new
    return (first_new, second_new, master_new, average_new)


GROUPS = ((0.02, 0.05), (0.02, 0.05), (0.2, 0.0))


def final_kernel(*refs):
    groups_in, rest = refs[2:17], refs[19:]
    (ing_in, out_in), (ing_ref, out_ref) = refs[:2], refs[17:19]
    qb_ref, groups_out, rest = rest[0], rest[1:18], rest[18:]
    state_s, load, fresh, store, pass_on = rest[:15], rest[15], rest[16:30], rest[30], rest[31]
    bounce = rest[32:34]
    state = [
        pltpu.make_async_copy(src, dst, load.at[i])
        for i, (src, dst) in enumerate(zip(groups_in, state_s))
    ]
    for c in state:
        c.start()
    stores, passing = [], []
    for k, (a, b) in enumerate(CROPS):
        for j, (src, dst) in enumerate(((ing_in, ing_ref), (out_in, out_ref))):
            through = bounce[j].at[a:b]
            taken = pltpu.make_async_copy(src.at[a:b], through, pass_on.at[0, j, k])
            taken.start()
            given = pltpu.make_async_copy(through, dst.at[a:b], pass_on.at[1, j, k])
            passing.append((taken, given))
    for g in range(3):
        for taken, given in passing[2 * g : 2 * g + 2]:
            taken.wait()
            given.start()
            stores.append(given)
        for c in state[5 * g : 5 * g + 5]:
            c.wait()
        grad, first, second, master, average = [ref[...] for ref in state_s[5 * g : 5 * g + 5]]
        new = adamw(grad, first, second, master, average, *GROUPS[g])
        if g < 2:
            new = new + (new[2].astype(bf16),)
        base = 5 * g
        for i, value in enumerate(new):
            fresh[base + i][...] = value
        pairs = [(fresh[base + i], base + i) for i in range(len(new))] + [(state_s[5 * g], 14 + g)]
        for src, i in pairs:
            stores.append(pltpu.make_async_copy(src, groups_out[i], store.at[i]))
            stores[-1].start()
    qb_ref[...] = state_s[10][3]
    for c in stores:
        c.wait()


def sds(*shape_dtype):
    return jax.ShapeDtypeStruct(shape_dtype[:-1], shape_dtype[-1])


def scratch(*shape_dtype):
    return pltpu.VMEM(shape_dtype[:-1], shape_dtype[-1])


def dma(*shape):
    return pltpu.SemaphoreType.DMA(shape)


def per_device(
    tokens, cotangent, kept_index,
    attention_weights, attention_first, attention_second, attention_average,
    feedforward_weights, feedforward_first, feedforward_second, feedforward_average,
    vector_weights, vector_first, vector_second, vector_average,
):
    images, length, d = tokens.shape
    ndp, nmp = lax.axis_size("dp"), lax.axis_size("mp")
    links = (ndp, nmp) == (8, MP)
    vec = vector_weights
    rows, hb = feedforward_weights.shape[1:]
    hidden = nmp * hb
    mask = masks()
    mask_specs = [full(m.shape) for m in mask]
    tok, cot = tokens.transpose(1, 0, 2), cotangent.transpose(1, 0, 2)
    comm = (lambda i: dict(collective_id=i, has_side_effects=True)) if links else (lambda i: {})

    att, ff = attention_weights.T, feedforward_weights
    if not links:
        att, ff = att.astype(bf16), ff.astype(bf16)
        att = lax.all_gather(att, ("dp", "mp"), axis=0, tiled=True)
        wff = lax.all_gather(lax.all_gather(ff, "dp", axis=1, tiled=True), "mp", axis=0)
    now = lambda *s: pl.BlockSpec((1,) + s, lambda i: (jnp.maximum(i - 1, 0), 0, 0))
    whole = lambda *s: pl.BlockSpec(s, lambda j: (0,) * len(s), pipeline_mode=pl.Buffered(1))
    rowspec = (images, RI, d)
    outs = pl.pallas_call(
        functools.partial(forward_kernel, links),
        grid=(1 + images,),
        in_specs=[ANY, ANY, full(kept_index.shape), full(vec.shape), *mask_specs]
        + ([full(att.shape), full(ff.shape)] if links else [ANY, ANY]),
        out_specs=[full(rowspec)] * 3 + [
            now(RI, 3 * d), now(RI, d), now(RI, d), now(RI, d), now(RI, d), ANY,
        ] + [ANY] * links,
        out_shape=[sds(*rowspec, bf16)] * 3 + [
            sds(images, RI, 3 * d, bf16), sds(*rowspec, bf16), sds(*rowspec, f32),
            sds(*rowspec, f32), sds(*rowspec, bf16), sds(4 * d, d, bf16),
        ] + [sds(nmp, 2, d, hb, bf16)] * links,
        scratch_shapes=[
            scratch(4 * d, d, bf16), scratch(length, images, d, bf16), scratch(length, images, d, bf16),
            scratch(8, 384, f32), scratch(384, 8, f32), dma(3),
        ] + (
            [scratch(rows, d, bf16), scratch(2, rows, hb, bf16)]
            + [dma(4, Gather.SLOTS), dma(4, Gather.SLOTS), dma(4, 1)] if links else []
        ),
        compiler_params=params(**comm(0)),
        name="forward",
    )(tok, cot, kept_index, vec, *mask, att, ff)
    kept, normed, cotk, proj, mixed, branch, resid, n2, watt = outs[:9]
    if links:
        wff = outs[9]

    outs = pl.pallas_call(
        functools.partial(feed_kernel, links),
        grid=(nmp,),
        in_specs=[
            whole(*rowspec), whole(*rowspec), ANY, ANY, full(vec.shape),
        ],
        out_specs=[full(rowspec), full(rowspec), ANY, full((nmp, hb))]
        + [full((2, 2, rows, hb))] * links,
        out_shape=[
            sds(*rowspec, bf16), sds(*rowspec, f32),
            sds(nmp, 2, d, hb, bf16), sds(nmp, hb, f32),
        ] + [sds(2, 2, rows, hb, bf16)] * links,
        scratch_shapes=[
            scratch(*rowspec, f32), scratch(images * RI, hb, bf16), scratch(images * RI, hb, bf16),
            *[scratch(RI, hb, f32)] * 4,
            scratch(nmp, 2, d, hb, bf16), scratch(2, 2, d, hb, bf16), dma(nmp + 1), dma(2),
        ] + (
            [dma(Gather.SLOTS), dma(Gather.SLOTS), dma(4)]
            + [scratch(n, 2, rows, hb, bf16) for n in (8, 8, 2, 2, 2)]
            + [dma(Reduce.SLOTS), dma(Reduce.SLOTS), dma(8)] if links else []
        ),
        compiler_params=params(**comm(3)),
        name="feedforward",
    )(n2, cotk, resid, wff, vec)
    result, n2g, gff, bg = outs[:4]

    spans = (16, 16, 4, 4, 4, 4)
    outs = pl.pallas_call(
        functools.partial(backward_kernel, links),
        grid=(images,),
        in_specs=[
            per_image(RI, d), per_image(RI, d), per_image(RI, d), per_image(RI, d),
            per_image(RI, d), per_image(RI, 3 * d),
            pl.BlockSpec((d, d), lambda i: (3, 0)), full(vec.shape), *mask_specs,
        ] + [ANY, full((2, 2, rows, hb))] * links,
        out_specs=[per_image(RI, 4 * d), per_image(RI, d), per_image(RI, 1), full((8, d))]
        + [full((2, rows, hb))] * links,
        out_shape=[
            sds(images, RI, 4 * d, bf16), sds(*rowspec, f32), sds(images, RI, 1, f32), sds(8, d, f32),
        ] + [sds(2, rows, hb, f32)] * links,
        scratch_shapes=[scratch(RI, d, bf16)] + (
            [scratch(n, 2, rows, hb, bf16) for n in (8, 8, 2, 2, 2, 4)]
            + [dma(Reduce.SLOTS), dma(Reduce.SLOTS), dma(8)] if links else []
        ),
        compiler_params=params(**comm(1)),
        name="attention_backward",
    )(n2g, cotk, branch, resid, normed, proj, watt, vec, *mask, *([gff, outs[4]] if links else []))
    dp, resg, rg, vecg = outs[:4]
    if links:
        feedforward_gradient = outs[4]

    full_d = (4 * d, d)
    outs = pl.pallas_call(
        functools.partial(grads_kernel, links),
        grid=(4 + images + 3,),
        in_specs=[ANY, ANY, ANY, full((images, RI, 1)), ANY, ANY, full(vec.shape), ANY]
        + [full(kept_index.shape), ANY, ANY, ANY]
        + [full((8, d)), full((hidden // d, d))] * links,
        out_specs=[ANY, ANY]
        + ([full((rows, d)), full(vec.shape)] if links else [full(full_d), full((8, d))]),
        out_shape=[sds(length, images, d, f32), sds(length, images, d, bf16)]
        + ([sds(rows, d, f32), sds(*vec.shape, f32)] if links else [sds(*full_d, bf16), sds(8, d, f32)]),
        scratch_shapes=([scratch(*full_d, bf16), scratch(8, d, f32)] if links else []) + [
            scratch(3 * d, d, bf16), scratch(4, *rowspec, bf16), scratch(2, *rowspec, bf16),
            scratch(*rowspec, f32), scratch(*rowspec, bf16), dma(10),
            *[scratch(*rowspec, bf16)] * 3,
            scratch(8, 384, f32), scratch(384, 8, f32),
            scratch(2, LG, images, d, bf16), scratch(2, LG, images, d, bf16),
            scratch(2, LG, images, d, f32), scratch(2, LG, images, d, bf16), dma(2, 2), dma(2, 2),
        ] + (
            [scratch(n, rows, d, bf16) for n in spans[1:]]
            + [dma(Reduce.SLOTS), dma(Reduce.SLOTS), scratch(11, 16, d, f32), dma(8), dma(8)]
            if links else []
        ),
        compiler_params=params(60, **comm(2)),
        name="attention_grads",
    )(
        dp, normed, mixed, rg, resg, kept, vec, watt, kept_index, tok, cot, result,
        *([vecg, bg] if links else []),
    )
    ing, out = outs[:2]
    if links:
        gatt, vector_gradient = outs[2:]
    else:
        gatt, vecg_in = outs[2:]
        local = jnp.concatenate([vecg_in[:2], vecg[:7], bg], axis=0)
        gatt = lax.psum_scatter(gatt, ("dp", "mp"), scatter_dimension=0, tiled=True).astype(f32)
        gff = lax.psum_scatter(gff, "mp", scatter_dimension=0, tiled=False)
        gff = lax.psum_scatter(gff, "dp", scatter_dimension=1, tiled=True)
        feedforward_gradient, vector_gradient = gff.astype(f32), lax.psum(local, ("dp", "mp"))

    state = []
    for grad, *rest in (
        (gatt, attention_first.T, attention_second.T, attention_weights.T, attention_average.T),
        (
            feedforward_gradient, feedforward_first, feedforward_second, feedforward_weights,
            feedforward_average,
        ),
        (vector_gradient, vector_first, vector_second, vector_weights, vector_average),
    ):
        state += [grad, *rest]
    fresh = []
    for g in range(3):
        fresh += [(state[5 * g].shape, f32)] * 4 + [(state[5 * g].shape, bf16)] * (g < 2)
    ing, out, qb, *new = pl.pallas_call(
        final_kernel,
        in_specs=[ANY] * 17,
        out_specs=[ANY, ANY, pl.BlockSpec(memory_space=pltpu.VMEM)] + [ANY] * (len(fresh) + 3),
        out_shape=[sds(length, images, d, f32), sds(length, images, d, bf16), sds(d, f32)]
        + [jax.ShapeDtypeStruct(*f) for f in fresh]
        + [sds(*state[5 * g].shape, f32) for g in range(3)],
        scratch_shapes=[
            *[pltpu.VMEM(v.shape, f32) for v in state], dma(15),
            *[pltpu.VMEM(*f) for f in fresh], dma(len(fresh) + 3), dma(2, 2, 3),
            scratch(length, images, d, f32), scratch(length, images, d, bf16),
        ],
        compiler_params=params(),
        name="finish",
    )(ing, out, *state)
    att_new, ff_new, vec_new = [v.T for v in new[:5]], new[5:10], new[10:14]
    gatt, feedforward_gradient, vector_gradient = new[14:]
    return (
        out.transpose(1, 0, 2), ing.transpose(1, 0, 2),
        gatt.T, *att_new, feedforward_gradient, *ff_new, vector_gradient, *vec_new, qb,
    )


def solution(mesh):
    rows = P(("dp", "mp"), None, None)
    att = P(None, ("dp", "mp"))
    feed = P(None, "dp", "mp")
    in_specs = (rows, rows, P(("dp", "mp"), None)) + (att,) * 4 + (feed,) * 4 + (P(),) * 4
    out_specs = (rows, rows) + (att,) * 6 + (feed,) * 6 + (P(),) * 6
    return jax.shard_map(
        per_device, mesh=mesh, in_specs=in_specs, out_specs=out_specs, check_vma=False
    )
```

```python
import functools

import jax
import jax.numpy as jnp
import numpy as np
from jax import lax
from jax.experimental import pallas as pl
from jax.experimental.pallas import tpu as pltpu
from jax.sharding import PartitionSpec as P

H = 12
HD = 64
LG = 197
LL = 37
KG = LG // 2
KL = LL // 2
LOC = 4 * KL
KEPT = 2 * KG + LOC
RI = -(-KEPT // 16) * 16
SPANS = ((0, KG), (KG, 2 * KG), (2 * KG, KEPT))
UNITS = tuple((a // 16 * 16, -(-b // 16) * 16) for a, b in SPANS)
PAIRS = H // 2
W2L = 2 * HD

bf16 = jnp.bfloat16
f32 = jnp.float32


def params(limit=56, **kw):
    return pltpu.CompilerParams(vmem_limit_bytes=limit << 20, **kw)


def full(shape):
    return pl.BlockSpec(shape, lambda *_: (0,) * len(shape))


def per_image(*shape):
    return pl.BlockSpec((1,) + shape, lambda i, *_: (i,) + (0,) * len(shape))


def nn(a, b):
    return lax.dot_general(a, b, (((1,), (0,)), ((), ())), preferred_element_type=f32)


def nt(a, b):
    return lax.dot_general(a, b, (((1,), (1,)), ((), ())), preferred_element_type=f32)


def tn(a, b):
    return lax.dot_general(a, b, (((0,), (0,)), ((), ())), preferred_element_type=f32)


def normalize(rows):
    center = rows - jnp.mean(rows, axis=-1, keepdims=True)
    spread = jnp.mean(center * center, axis=-1, keepdims=True)
    inverse = lax.rsqrt(spread + 1e-06)
    return center * inverse, inverse


def norm_backward(upstream, standard, inverse, gain):
    scaled = upstream * gain
    return inverse * (
        scaled
        - jnp.mean(scaled, axis=-1, keepdims=True)
        - standard * jnp.mean(scaled * standard, axis=-1, keepdims=True)
    )


def colsum(v):
    return jnp.sum(v, axis=0, keepdims=True)


def masks():
    crop = np.full(RI, -1)
    crop[:KG], crop[KG : 2 * KG] = 0, 1
    for c in range(4):
        crop[2 * KG + c * KL : 2 * KG + (c + 1) * KL] = 2 + c
    adds, valids = [], []
    for (a, b), (lo, hi) in zip(SPANS, UNITS):
        rows = np.arange(lo, hi)
        inside = (rows >= a) & (rows < b)
        same = (crop[lo:hi, None] == crop[None, lo:hi]) & inside[:, None] & inside[None, :]
        adds.append(np.tile(np.where(same, 0.0, -1e9), (1, 2)).astype(np.float32))
        valids.append(np.tile(inside[None, :].astype(np.float32), (8, 2)))
    return [jnp.asarray(m) for m in adds + valids]


def lane_half(shape):
    return lax.broadcasted_iota(jnp.int32, shape, len(shape) - 1) < HD


def split_heads(v, scale):
    first = lane_half(v.shape)
    zero = jnp.zeros_like(v)
    if scale != 1.0:
        v = v * jnp.asarray(scale, v.dtype)
    return jnp.concatenate([jnp.where(first, v, zero), jnp.where(first, zero, v)], axis=0)


def join_heads(v):
    n = v.shape[0] // 2
    return jnp.where(lane_half((n, v.shape[1])), v[:n], v[n:])


def softmax_keys(st, valid):
    p = jnp.exp(st - jnp.max(st, axis=0, keepdims=True))
    return p * (valid / jnp.sum(p, axis=0, keepdims=True))


def store_window(ref, image, lo, hi, last, cols, value, tail):
    value = value.astype(bf16)
    if tail is not None:
        value = jnp.concatenate([value[:16] + tail, value[16:]], axis=0)
    end = hi if last else hi - 16
    ref[image, lo:end, cols] = value[: end - lo]
    return None if last else value[end - lo :]


MESH = pl.DeviceIdType.MESH
ANY = pl.BlockSpec(memory_space=pl.ANY)
MP = 4
CROPS = ((0, LG), (LG, 2 * LG), (2 * LG, 2 * LG + 4 * LL))
ORDER = ((0, 1, 2, 3), (1, 0, 1, 2), (2, 2, 3, 1), (3, 3, 0, 0))


def flip(index, bit):
    return index + bit * (1 - 2 * lax.rem(lax.div(index, bit), 2))


def remote(src, dst, send, recv, to):
    return pltpu.make_async_remote_copy(
        src_ref=src, dst_ref=dst, send_sem=send, recv_sem=recv, device_id=to, device_id_type=MESH
    )


class Sends:
    def __init__(self):
        self.made = []

    def start(self, make, when=None):
        def go():
            make().start()

        go() if when is None else pl.when(when)(go)
        self.made.append((make, when))

    def finish(self):
        for make, when in self.made:
            def wait(make=make):
                make().wait_send()

            wait() if when is None else pl.when(when)(wait)


class Place:
    def __init__(self):
        self.dp = lax.axis_index("dp")
        self.z = lax.axis_index("mp")
        x, y = flip(self.dp, 2), flip(self.dp, 4)
        self.core = (flip(self.dp, 1), self.z)
        self.x, self.y = (x, self.z), (y, self.z)
        self.chips = (self.dp, x, y, flip(x, 4))
        self.mates = tuple(flip(c, 1) for c in self.chips)
        power = (1 + 3 * lax.rem(self.z, 2)) * (1 + 15 * lax.div(self.z, 2))
        self.event = []
        for row in ORDER:
            code = sum(v << (2 * i) for i, v in enumerate(row))
            self.event.append(lax.rem(lax.div(0 * power + code, power), 4))
        self.low, self.high = self.z > 0, self.z < MP - 1
        self.middle = self.low & self.high
        self.line = [lax.rem(self.z + k, MP) for k in range(MP)]
        self.up, self.down = (self.dp, self.z + 1), (self.dp, self.z - 1)
        self.onward = (self.up, self.down, (self.dp, 3 * (self.z - 1)))

    def barrier(self):
        sem = pltpu.get_barrier_semaphore()
        others = [self.core, self.x, self.y]
        others += [(self.dp, k) for k in self.line[1:]]
        for other in others:
            pl.semaphore_signal(sem, inc=1, device_id=other, device_id_type=MESH)
        pl.semaphore_wait(sem, len(others))


def att_block(ref, dp, z, rows):
    return ref.at[pl.ds(pl.multiple_of((dp * MP + z) * rows, 32), rows), :]


def att_part(ref, dp, z, rows, h):
    half = rows // 2
    return ref.at[pl.ds(pl.multiple_of((dp * MP + z) * rows + h * half, 16), half), :]


def ff_part(ref, dp, z, rows, h):
    return ref.at[z, h, pl.ds(pl.multiple_of(dp * rows, 32), rows), :]


def ff_block(ref, dp, z, rows):
    return ref.at[z, :, pl.ds(pl.multiple_of(dp * rows, 32), rows), :]


class Gather:
    ALONG, X, Y, D, C, SLOTS = 0, 4, 8, 12, 16, 32

    def __init__(self, at, first, place, send, recv, local):
        self.at, self.first, self.place = at, first, place
        self.send, self.recv, self.local = send, recv, local
        self.sends = Sends()

    def copy(self, slot, e, r, to):
        slot = self.ALONG + self.at.event[e] if slot is None else slot
        dst = self.place(e, self.at.chips[r])
        src = self.first(e) if r == 0 else dst
        return remote(src, dst, self.send.at[slot], self.recv.at[slot], to)

    def put(self, slot, e, r, to, when=None):
        self.sends.start(lambda: self.copy(slot, e, r, to), when)

    def got(self, slot, e, dp):
        dst = self.place(e, dp)
        remote(dst, dst, self.send.at[slot], self.recv.at[slot], self.at.core).wait_recv()

    def keep(self, e):
        return pltpu.make_async_copy(self.first(e), self.place(e, self.at.dp), self.local.at[e])

    def spread(self, e):
        self.put(self.X + e, e, 0, self.at.x)
        self.put(self.Y + e, e, 0, self.at.y)
        self.put(self.C + 4 * e, e, 0, self.at.core)

    def begin(self):
        at = self.at
        self.keep(0).start()
        for to, when in ((at.up, at.high), (at.down, at.low)):
            self.put(None, 0, 0, to, when)
        self.spread(0)

    def direct(self):
        self.keep(0).start()
        for zb in self.at.line[1:]:
            self.put(None, 0, 0, (self.at.dp, zb))

    def arrived(self, e):
        self.got(self.ALONG + self.at.event[e], e, self.at.dp)

    def along(self, e):
        at = self.at
        self.arrived(e)
        self.put(None, e, 0, at.onward[e - 1], at.middle)
        self.spread(e)

    def plane(self, e):
        at = self.at
        self.got(self.X + e, e, at.chips[1])
        if e % 2 == 0:
            self.put(self.D + e, e, 1, at.y)
        self.put(self.C + 4 * e + 1, e, 1, at.core)
        self.got(self.Y + e, e, at.chips[2])
        if e % 2 == 1:
            self.put(self.D + e, e, 2, at.x)
        self.put(self.C + 4 * e + 2, e, 2, at.core)

    def corner(self, e):
        self.got(self.D + e, e, self.at.chips[3])
        self.put(self.C + 4 * e + 3, e, 3, self.at.core)

    def finish(self, e):
        for r in range(4):
            self.got(self.C + 4 * e + r, e, self.at.mates[r])


def add_into(target, first, *others):
    if len(others) == 1 and target.dtype == bf16:
        @pl.loop(0, first.shape[0] // 48)
        def _(i):
            s = pl.ds(pl.multiple_of(i * 48, 16), 48)
            target[s, :] = first[s, :] + others[0][s, :]

        return
    step = 48

    @pl.loop(0, first.shape[0] // step)
    def _(i):
        s = pl.ds(pl.multiple_of(i * step, 16), step)
        total = first[s, :].astype(f32)
        for ref in others:
            total = total + ref[s, :].astype(f32)
        target[s, :] = total.astype(target.dtype)


class Reduce:
    C, D, X, Y, ALONG, SLOTS = 0, 16, 20, 24, 28, 32

    def __init__(self, at, source, own, parts, bufs, send, recv, load=None, base=0):
        self.at, self.source, self.own, self.parts, self.base = at, source, own, parts, base
        self.c, self.d, self.x, self.y, self.line = bufs
        self.send, self.recv, self.load = send, recv, load
        self.sends = Sends()

    def put(self, slot, src, dst, to):
        self.sends.start(
            lambda: remote(src(), dst(), self.send.at[slot], self.recv.at[slot], to)
        )

    def got(self, slot, dst):
        remote(dst, dst, self.send.at[slot], self.recv.at[slot], self.at.core).wait_recv()

    def slot(self, e, r):
        return 4 * (e - self.base) + r

    def cross(self, e, r):
        i = self.slot(e, r)
        self.put(self.C + i, lambda: self.source(e, self.at.mates[r]), lambda: self.c.at[i], self.at.core)
        if self.load is not None:
            self.load(e, r).start()

    def add(self, e, r, *others, target=None):
        i = self.slot(e, r)
        self.got(self.C + i, self.c.at[i])
        if self.load is not None:
            self.load(e, r).wait()
        refs = [self.own(e, r), self.c.at[i]] + list(others)
        self.total(refs[0] if target is None else target, *refs)

    def total(self, target, *refs):
        for t, *rest in zip(self.parts(target), *[self.parts(ref) for ref in refs]):
            add_into(t, *rest)

    def corner(self, e):
        at, i = self.at, e - self.base
        self.add(e, 3)
        self.put(
            self.D + i, lambda: self.own(e, 3), lambda: self.d.at[i], at.x if e % 2 else at.y
        )
        r, slot, buf, to = (1, self.X, self.x, at.x) if e % 2 else (2, self.Y, self.y, at.y)
        self.add(e, r)
        self.put(slot + i, lambda: self.own(e, r), lambda: buf.at[i], to)

    def plane(self, e):
        at, i = self.at, e - self.base
        r, slot, buf, to = (2, self.Y, self.y, at.y) if e % 2 else (1, self.X, self.x, at.x)
        self.got(self.D + i, self.d.at[i])
        self.add(e, r, self.d.at[i])
        self.put(slot + i, lambda: self.own(e, r), lambda: buf.at[i], to)

    def gathered(self, e, *others, target=None):
        i = e - self.base
        self.got(self.X + i, self.x.at[i])
        self.got(self.Y + i, self.y.at[i])
        self.add(e, 0, self.x.at[i], self.y.at[i], *others, target=target)

    def send_along(self, e, src):
        at = self.at
        zb = at.event[e]
        self.sends.start(
            lambda: remote(
                src(), self.line.at[at.z], self.send.at[self.ALONG + zb],
                self.recv.at[self.ALONG + at.z], (at.dp, zb),
            )
        )

    def along(self, e):
        self.gathered(e)
        self.send_along(e, lambda: self.own(e, 0))

    def lines(self):
        got = []
        for zb in self.at.line[1:]:
            got.append(self.line.at[zb])
            self.got(self.ALONG + zb, got[-1])
        return got


def pump(schedule, step, point):
    for (s, p), action in schedule:
        if isinstance(point, int):
            if p == point:
                pl.when(step == s)(action)
        else:
            pl.when((step == s) & (point == p))(action)


def do(action, *args):
    return lambda: action(*args)


def token_columns(idx_ref, idx_s, col_s):
    idx_s[...] = jnp.full(idx_s.shape, -1.0, f32)
    idx_s[0 : idx_ref.shape[0], 0 : idx_ref.shape[1]] = idx_ref[...].astype(f32)
    col_s[...] = idx_s[...].T


def one_hot(col_s, crop, images, local):
    (a, b), (s, e), (lo, hi) = [v[2 if local else 0] for v in (CROPS, SPANS, UNITS)]
    n, size = hi - lo, b - a
    count = images * size
    if not local:
        a, s, e, lo = LG * crop, KG * crop, KG * (crop + 1), UNITS[1][0] * crop
        lo = pl.multiple_of(lo, 16)
    columns = col_s[pl.ds(lo, n), :]
    row = lax.broadcasted_iota(jnp.int32, (n, 1), 0) + lo
    pieces = []
    for i in range(images):
        place = (columns[:, i : i + 1].astype(jnp.int32) - a) * images + i
        pieces.append(jnp.where((row >= s) & (row < e), place, -1))
    index = jnp.concatenate(pieces, axis=0)
    hot = lax.broadcasted_iota(jnp.int32, (index.shape[0], count), 1) == index
    return hot.astype(f32).astype(bf16), pl.ds(a, size), lo, n, count


def forward_kernel(
    links, tok_ref, cot_ref, idx_ref, vec_ref, m0_ref, m1_ref, m2_ref, v0_ref, v1_ref, v2_ref,
    att_ref, ff_ref,
    kept_out, normed_out, cotk_out, proj_out, mixed_ref, branch_ref, resid_ref, n2_ref,
    watt_out, *rest,
):
    if links:
        wff_ref, *rest = rest
        att_s, ff_s, send, recv, local = rest[10:]
    watt_ref, tok_s, cot_s, idx_s, col_s, load, kept_ref, normed_ref, cotk_ref, proj_ref = rest[:10]
    step = pl.program_id(0)
    images, _, d = kept_ref.shape
    leave = [
        pltpu.make_async_copy(src, dst, load.at[3 + i])
        for i, (src, dst) in enumerate(
            (
                (kept_ref, kept_out), (normed_ref, normed_out), (cotk_ref, cotk_out),
                (proj_ref, proj_out),
            )
        )
    ]
    loads = [
        pltpu.make_async_copy(tok_ref, tok_s, load.at[0]),
        pltpu.make_async_copy(cot_ref, cot_s, load.at[1]),
    ]
    order = (0, 1, 2, 3)

    def clear(dst):
        for i in range(images):
            for _, hi in UNITS[:2]:
                dst[i, hi - 16 : hi] = jnp.zeros((16, d), bf16)

    def pick(crop, local, src, dst):
        hot, span, lo, n, k = one_hot(col_s, crop, images, local)
        got = nn(hot, src[span].reshape(k, d)).astype(bf16)
        for i in range(images):
            part = got[i * n : (i + 1) * n]
            head = pl.ds(lo, 16)
            if local:
                dst[i, head, :] = dst[i, head, :] + part[:16]
            else:
                old = jnp.where(crop == 0, jnp.zeros_like(part[:16]), dst[i, head, :])
                dst[i, head, :] = old + part[:16]
            dst[i, pl.ds(lo + 16, n - 16), :] = part[16:]

    def cot_rows():
        loads[1].wait()
        clear(cotk_ref)

        @pl.loop(0, 2)
        def _(crop):
            pick(crop, False, cot_s, cotk_ref)

        pick(2, True, cot_s, cotk_ref)

    def project(r):
        j = order[r]

        @pl.when(j < 3)
        def _():
            rows_j = pl.ds(pl.multiple_of(j * d, 128), d)
            bias = jnp.where(j == 1, 0.0, jnp.where(j == 0, vec_ref[3:4], vec_ref[4:5]))

            @pl.loop(0, images)
            def _(i):
                part = nt(normed_ref[i], watt_ref[rows_j, :]) + bias
                proj_ref[i, :, rows_j] = part.astype(bf16)

    acts, schedule = [[]] * 5 + [[cot_rows]], []
    if links:
        at = Place()
        rows = att_ref.shape[0]
        half = rows // 2

        def att_half(h):
            return Gather(
                at,
                lambda e: att_part(watt_ref, at.dp, at.event[e], rows, h) if e
                else att_s.at[h * half : (h + 1) * half],
                lambda e, dp: att_part(watt_ref, dp, at.event[e], rows, h),
                send.at[h], recv.at[h], local.at[h],
            )

        def feed_half(h):
            return Gather(
                at, lambda e: ff_part(wff_ref, at.dp, at.event[e], rows, h) if e else ff_s.at[h],
                lambda e, dp: ff_part(wff_ref, dp, at.event[e], rows, h),
                send.at[2 + h], recv.at[2 + h], local.at[2 + h],
            )

        (a0, a1), (f0, f1) = [att_half(h) for h in (0, 1)], [feed_half(h) for h in (0, 1)]
        chip = lax.div(at.dp, 2)
        order = (chip, flip(chip, 1), flip(chip, 2), 3 - chip)

        def ready(r):
            for part in (a0, a1):
                for e in range(4):
                    part.got(part.C + 4 * e + r, e, at.mates[r])
                if r == 0:
                    part.keep(0).wait()

        acts = [
            [a1.begin, a0.begin],
            [do(a1.along, 1), do(a1.plane, 0), do(a0.along, 1), do(a0.along, 2), do(a1.along, 2)],
            [do(a0.along, 3)],
            [do(a1.along, 3), f0.direct, do(a1.plane, 1), do(a0.plane, 2)],
            [do(a0.plane, 0)],
            [
                do(ready, 0), do(project, 0),
                do(a0.plane, 3), do(a0.plane, 1), do(a1.plane, 3), do(a1.plane, 2), cot_rows,
                do(ready, 1), do(project, 1),
                do(a0.corner, 0), do(a1.corner, 1), do(a0.corner, 3), do(a1.corner, 2),
                do(a1.corner, 0), f1.direct,
                do(ready, 2), do(project, 2),
                do(a0.corner, 1), do(a0.corner, 2), do(a1.corner, 3),
                do(f0.arrived, 2), do(f0.spread, 2),
                do(ready, 3), do(project, 3),
            ],
        ]
        schedule = [
            ((1, 3), do(f0.arrived, 3)),
            ((1, 3), do(f0.spread, 3)),
            ((2, 1), do(f1.arrived, 2)),
            ((2, 1), do(f1.spread, 2)),
            ((3, 0), do(f1.arrived, 3)),
            ((3, 0), do(f1.spread, 3)),
            ((3, 0), do(f0.plane, 2)),
            ((3, 1), do(f1.plane, 2)),
            ((3, 1), do(f0.plane, 3)),
            ((3, 3), do(f1.plane, 3)),
            ((4, 3), do(f1.corner, 3)),
            ((4, 3), do(f0.corner, 3)),
            ((4, 3), do(f1.corner, 2)),
            ((4, 3), do(f0.corner, 2)),
        ]
    else:
        fetch = pltpu.make_async_copy(att_ref, watt_ref, load.at[2])
    store = pltpu.make_async_copy(watt_ref, watt_out, load.at[2])

    def run(point):
        for action in acts[point]:
            action()

    @pl.when(step == 0)
    def _():
        if links:
            att_s[...] = att_ref[...].astype(bf16)
            at.barrier()
            run(0)
        else:
            fetch.start()
        for c in loads:
            c.start()
        if links:
            ff_s[...] = ff_ref[...].astype(bf16)
        token_columns(idx_ref, idx_s, col_s)
        loads[0].wait()
        clear(kept_ref)

        @pl.loop(0, 2)
        def _(crop):
            pick(crop, False, tok_s, kept_ref)
            for point in (1, 2):
                pl.when(crop == point - 1)(do(run, point))

        pick(2, True, tok_s, kept_ref)
        run(3)
        for i in range(images):
            standard, _ = normalize(kept_ref[i].astype(f32))
            normed_ref[i] = (standard * vec_ref[0:1] + vec_ref[1:2]).astype(bf16)
            if i == 1:
                run(4)
        run(5)
        if not links:
            fetch.wait()
            for r in range(3):
                project(r)
        store.start()
        for c in leave:
            c.start()

    pump(schedule, step, 0)

    @pl.when(step > 0)
    def _():
        image = step - 1
        normed = normed_ref[image]
        pump(schedule, step, 1)
        mrefs, vrefs = (m0_ref, m1_ref, m2_ref), (v0_ref, v1_ref, v2_ref)
        for pair in range(PAIRS):
            cols = lambda j: slice(j * d + pair * W2L, j * d + (pair + 1) * W2L)
            tail = None
            for unit, (lo, hi) in enumerate(UNITS):
                qs = split_heads(proj_ref[image, lo:hi, cols(0)], HD ** -0.5)
                st = nt(proj_ref[image, lo:hi, cols(1)], qs) + mrefs[unit][...]
                pt = softmax_keys(st, vrefs[unit][0:1]).astype(bf16)
                out = join_heads(tn(pt, proj_ref[image, lo:hi, cols(2)]))
                tail = store_window(mixed_ref, 0, lo, hi, unit == 2, cols(0), out, tail)
            if pair == 2:
                pump(schedule, step, 3)
        branch = nt(mixed_ref[0], watt_ref[3 * d :, :]) + vec_ref[5:6]
        branch_ref[0] = branch
        residual = kept_ref[image].astype(f32) + router_score(normed, vec_ref) * branch
        resid_ref[0] = residual
        standard, _ = normalize(residual)
        n2_ref[0] = (standard * vec_ref[6:7] + vec_ref[7:8]).astype(bf16)

    @pl.when(step == images)
    def _():
        if links:
            for feed in (f0, f1):
                feed.finish(2)
                feed.finish(3)
                feed.arrived(1)
                feed.keep(0).wait()
            for part in (a0, a1, f0, f1):
                part.sends.finish()
        for c in [store] + leave:
            c.wait()


def router_score(normed, vec_ref):
    logit = jnp.sum(normed.astype(f32) * vec_ref[2:3], axis=-1, keepdims=True)
    return jax.nn.sigmoid(logit)


def feed_kernel(
    links, n2_ref, cot_ref, resid_ref, w_ref, vec_ref,
    result_ref, n2g_ref, gff_ref, bg_ref, *rest,
):
    if links:
        acc_ref, out_s, act_s, ig_s, i0, i1, a0, a1, w_s, g_s, load, store = rest[:12]
        send, recv, local, a, c, dd, x, y, rsend, rrecv, rlocal = rest[12:]
    else:
        out_s, act_s, ig_s, i0, i1, a0, a1, w_s, g_s, load, store = rest
    inner_s, ag_s = (i0, i1), (a0, a1)
    step = pl.program_id(0)
    last = pl.num_programs(0) - 1
    images, _, d = n2_ref.shape
    nload = w_s.shape[0]
    hb = w_ref.shape[3]
    block, schedule = step, []
    if links:
        at = Place()
        rows = acc_ref.shape[2]
        block = at.event[0]
        for e in (1, 2, 3):
            block = jnp.where(step == 3 - e, at.event[e], block)
        gather = Gather(
            at, lambda e: ff_block(w_ref, at.dp, at.event[e], rows),
            lambda e, dp: w_s.at[3 - e, :, pl.ds(pl.multiple_of(dp * rows, 32), rows), :],
            send, recv, local,
        )
        reduce = Reduce(
            at, lambda e, dp: ff_block(gff_ref, dp, at.event[e], rows),
            lambda e, r: a.at[4 * (e - 2) + r],
            lambda ref: (ref.at[0], ref.at[1]), (c, dd, x, y, None), rsend, rrecv,
            lambda e, r: pltpu.make_async_copy(
                ff_block(gff_ref, at.chips[r], at.event[e], rows), a.at[4 * (e - 2) + r],
                rlocal.at[4 * (e - 2) + r],
            ),
            2,
        )

        def start():
            at.barrier()
            for e in (1, 0):
                gather.spread(e)
                gather.keep(e).start()

        def ready(e):
            gather.finish(e)
            gather.keep(e).wait()

        def cross(e):
            for r in (3, 1, 2, 0):
                reduce.cross(e, r)

        schedule = [
            ((1, 0), do(gather.plane, 1)),
            ((1, 0), do(gather.plane, 0)),
            ((1, 0), do(cross, 3)),
            ((2, 0), do(gather.corner, 1)),
            ((2, 0), do(reduce.corner, 3)),
            ((2, 0), do(cross, 2)),
            ((2, 0), do(ready, 1)),
            ((2, 0), do(reduce.corner, 2)),
            ((2, 0), do(gather.corner, 0)),
            ((3, 0), do(reduce.plane, 3)),
            ((3, 0), do(ready, 0)),
            ((3, 0), do(reduce.plane, 2)),
        ]

    def fetch(e):
        return pltpu.make_async_copy(
            w_ref.at[at.event[3 - e] if links else e], w_s.at[e], load.at[e]
        )

    def save(slot, which):
        return pltpu.make_async_copy(g_s.at[slot], gff_ref.at[which], store.at[slot])

    residual = pltpu.make_async_copy(resid_ref, out_s, load.at[nload])
    early = (0, 1) if links else range(w_s.shape[0])

    @pl.when(step == 0)
    def _():
        for e in early:
            fetch(e).start()
        if links:
            start()
        residual.start()
        n2g_ref[...] = jnp.zeros_like(n2g_ref)
        bg_ref[...] = jnp.zeros_like(bg_ref)
        fetch(0).wait()
        residual.wait()

    for e in early[1:]:
        @pl.when(step == e)
        def _(e=e):
            fetch(e).wait()

    slot = lax.rem(step, 2)

    @pl.when(step > 0)
    def _():
        save(1 - slot, 0).wait()

    pump(schedule, step, 0)

    def first(i):
        inner_s[i % 2][...] = nn(n2_ref[i], w_s[step, 0]) + vec_ref[pl.ds(9 + block, 1), :]
        ag_s[i % 2][...] = nn(cot_ref[i], w_s[step, 1])

    def second(i):
        inner = inner_s[i % 2][...]
        phi = 0.5 * (1.0 + lax.erf(inner * 0.7071067811865476))
        act = (inner * phi).astype(bf16)
        slope = phi + inner * jnp.exp(-0.5 * inner * inner) * 0.3989422804014327
        ig = (ag_s[i % 2][...] * slope).astype(bf16)
        rows_i = slice(i * RI, (i + 1) * RI)
        act_s[rows_i, :] = act
        ig_s[rows_i, :] = ig
        bg_ref[pl.ds(block, 1), :] += colsum(ig.astype(f32))
        out_s[i] += nt(act, w_s[step, 1])
        n2g_ref[i] += nt(ig, w_s[step, 0])

    first(0)
    for i in range(images):
        pump(schedule, step, i + 1)
        if i + 1 < images:
            first(i + 1)
        second(i)

    pump(schedule, step, 5)
    n2 = n2_ref[...].reshape(images * RI, d)
    cot = cot_ref[...].reshape(images * RI, d)
    g_s[slot, 0] = tn(n2, ig_s[...]).astype(bf16)
    g_s[slot, 1] = tn(cot, act_s[...]).astype(bf16)
    save(slot, block).start()

    @pl.when(step == last)
    def _():
        result_ref[...] = (out_s[...] + vec_ref[8:9]).astype(bf16)
        if links:
            reduce.gathered(3, target=acc_ref.at[0])
            reduce.gathered(2, target=acc_ref.at[1])
            gather.sends.finish()
            reduce.sends.finish()
        save(slot, 0).wait()


def backward_kernel(
    links, n2g_ref, cotk_ref, branch_ref, resid_ref, normed_ref, proj_ref, wout_ref,
    vec_ref, m0_ref, m1_ref, m2_ref, v0_ref, v1_ref, v2_ref, *rest,
):
    if links:
        gff_ref, acc_ref, dp_ref, resg_ref, rg_ref, vecg_ref, gout_ref = rest[:7]
        mg_s, a, c, dd, x, y, line, send, recv, local = rest[7:]
    else:
        dp_ref, resg_ref, rg_ref, vecg_ref, mg_s = rest
    step = pl.program_id(0)
    schedule = []
    if links:
        at = Place()
        rows = gout_ref.shape[1]
        reduce = Reduce(
            at, lambda e, dp: ff_block(gff_ref, dp, at.event[e], rows),
            lambda e, r: a.at[4 * e + r],
            lambda ref: (ref.at[0], ref.at[1]), (c, dd, x, y, line), send, recv,
            lambda e, r: pltpu.make_async_copy(
                ff_block(gff_ref, at.chips[r], at.event[e], rows), a.at[4 * e + r],
                local.at[4 * e + r],
            ),
        )

        def start():
            at.barrier()
            reduce.send_along(2, lambda: acc_ref.at[1])
            for e in (1, 0):
                for r in (3, 1, 2, 0):
                    reduce.cross(e, r)

        schedule = [
            ((0, 0), start),
            ((0, 1), do(reduce.corner, 1)),
            ((0, 3), do(reduce.send_along, 3, lambda: acc_ref.at[0])),
            ((1, 1), do(reduce.plane, 1)),
            ((1, 3), do(reduce.corner, 0)),
            ((2, 1), do(reduce.along, 1)),
            ((3, 0), do(reduce.plane, 0)),
        ]

    pump(schedule, step, 0)
    d = normed_ref.shape[2]
    normed = normed_ref[0]
    score = router_score(normed, vec_ref)
    branch = branch_ref[0]
    standard, inverse = normalize(resid_ref[0])
    n2g = n2g_ref[0]
    cot = cotk_ref[0].astype(f32)
    resg = cot + norm_backward(n2g, standard, inverse, vec_ref[6:7])
    resg_ref[0] = resg
    bg = (score * resg).astype(bf16)
    rg = jnp.sum(resg * branch, axis=-1, keepdims=True) * score * (1.0 - score)
    rg_ref[0] = rg
    dp_ref[0, :, 3 * d :] = bg
    mg_s[...] = nn(bg, wout_ref[...]).astype(bf16)
    pump(schedule, step, 1)
    mrefs, vrefs = (m0_ref, m1_ref, m2_ref), (v0_ref, v1_ref, v2_ref)
    for pair in range(PAIRS):
        cols = lambda j: slice(j * d + pair * W2L, j * d + (pair + 1) * W2L)
        tails = [None] * 3
        for unit, (lo, hi) in enumerate(UNITS):
            qs = split_heads(proj_ref[0, lo:hi, cols(0)], HD ** -0.5)
            kk = proj_ref[0, lo:hi, cols(1)]
            pt = softmax_keys(nt(kk, qs) + mrefs[unit][...], vrefs[unit][0:1])
            ds = split_heads(mg_s[lo:hi, cols(0)], 1.0)
            gpt = nt(proj_ref[0, lo:hi, cols(2)], ds)
            sg = (pt * (gpt - jnp.sum(pt * gpt, axis=0, keepdims=True))).astype(bf16)
            grads = (
                join_heads(tn(sg, kk)) * HD ** -0.5, nn(sg, qs), nn(pt.astype(bf16), ds)
            )
            for j in range(3):
                tails[j] = store_window(dp_ref, 0, lo, hi, unit == 2, cols(j), grads[j], tails[j])
        if pair == 2:
            pump(schedule, step, 3)
    sums = jnp.concatenate(
        [
            colsum(rg * normed.astype(f32)),
            colsum(dp_ref[0, :, :d].astype(f32)),
            colsum(dp_ref[0, :, 2 * d : 3 * d].astype(f32)),
            colsum(bg.astype(f32)),
            colsum(n2g * standard),
            colsum(n2g),
            colsum(cot),
            jnp.zeros((1, d), f32),
        ],
        axis=0,
    )

    @pl.when(step == 0)
    def _():
        vecg_ref[...] = jnp.zeros_like(vecg_ref)

    vecg_ref[...] += sums
    if links:
        @pl.when(step == pl.num_programs(0) - 1)
        def _():
            reduce.gathered(0, *reduce.lines(), target=gout_ref)
            reduce.sends.finish()


def grads_kernel(
    links, dp_ref, normed_ref, mixed_ref, rg_ref, resg_ref, kept_ref, vec_ref, watt_ref,
    idx_ref, tok_ref, cot_ref, result_ref, *rest,
):
    if links:
        vecb_ref, bias_ref, ing_ref, out_ref, gout_ref, vecout_ref = rest[:6]
        gatt_s, vecg_s, *rest = rest[6:]
        c, dd, x, y, line, send, recv, vbuf, vsend, vrecv = rest[17:]
    else:
        ing_ref, out_ref, gatt_s, vecg_s, *rest = rest
    watt_s, dp_s, act_s, resg_s, kept_s, load, high_ref, low_ref, result_s = rest[:9]
    idx_s, col_s, tok_s, cot_s, ing_s, out_s, fetch, store = rest[9:17]
    step = pl.program_id(0)
    images, _, d = high_ref.shape
    last = 3 + images + 3
    total = images * RI
    chip, schedule = 0, []
    if links:
        at = Place()
        chip = lax.div(at.dp, 2)
        rows = gout_ref.shape[0]
        block = lambda e, dp: att_block(gatt_s, dp, at.event[e], rows)
        reduce = Reduce(
            at, block, lambda e, r: block(e, at.chips[r]), lambda ref: (ref,),
            (c, dd, x, y, line), send, recv,
        )

        def cross(r):
            for e in (3, 2, 1, 0):
                reduce.cross(e, r)

        exchange = lambda k, to: remote(
            vbuf.at[k + 1], vbuf.at[8 + k], vsend.at[k], vrecv.at[k], to
        )
        lines = [
            lambda k=k: remote(
                vbuf.at[0], vbuf.at[4 + at.z], vsend.at[2 + k], vrecv.at[3 + at.z],
                (at.dp, at.line[k]),
            )
            for k in range(1, MP)
        ]

        def spread_vectors():
            vbuf[0, 0:2] = vecg_s[0:2]
            vbuf[0, 2:9] = vecb_ref[0:7]
            vbuf[0, 9:13] = bias_ref[...]
            vbuf[0, 13:16] = jnp.zeros((3, d), f32)
            for make in lines:
                make().start()
            vbuf[4 + at.z] = vbuf[0]

        def line_vectors():
            for k in range(1, MP):
                zb = at.line[k]
                remote(
                    vbuf.at[0], vbuf.at[4 + zb], vsend.at[2 + k], vrecv.at[3 + zb], at.core
                ).wait_recv()
            vbuf[1] = vbuf[4] + vbuf[5] + vbuf[6] + vbuf[7]
            exchange(0, at.core).start()

        def core_vectors():
            exchange(0, at.core).wait()
            vbuf[2] = vbuf[1] + vbuf[8]
            exchange(1, at.x).start()

        def x_vectors():
            exchange(1, at.x).wait()
            vbuf[3] = vbuf[2] + vbuf[9]
            exchange(2, at.y).start()

        turns = (3 - chip, flip(chip, 1), flip(chip, 2), chip)
        schedule = [
            ((1, 2), do(cross, 3)),
            ((1, 2), do(cross, 1)),
            ((2, 2), do(reduce.corner, 3)),
            ((2, 2), do(cross, 2)),
            ((3, 2), do(cross, 0)),
            ((4, 1), do(reduce.plane, 3)),
            ((5, 0), do(reduce.corner, 2)),
            ((6, 0), do(reduce.corner, 1)),
            ((6, 0), do(reduce.along, 3)),
            ((7, 0), do(reduce.plane, 2)),
            ((8, 0), spread_vectors),
            ((8, 0), do(reduce.plane, 1)),
            ((8, 0), do(reduce.corner, 0)),
            ((8, 1), do(reduce.along, 2)),
            ((8, 2), line_vectors),
            ((9, 1), core_vectors),
            ((9, 1), do(reduce.along, 1)),
            ((9, 1), do(reduce.plane, 0)),
            ((9, 2), x_vectors),
        ]
    else:
        turns = (0, 1, 2, 3)
    turn = turns[3]
    for k in (2, 1, 0):
        turn = jnp.where(step == k, turns[k], turn)

    def columns(k):
        lanes = pl.ds(pl.multiple_of(turns[k] * d, 128), d) if links else pl.ds(k * d, d)
        return pltpu.make_async_copy(dp_ref.at[:, :, lanes], dp_s.at[turns[k]], load.at[k])

    acts = [
        pltpu.make_async_copy(normed_ref, act_s.at[0], load.at[4]),
        pltpu.make_async_copy(mixed_ref, act_s.at[1], load.at[5]),
    ]
    later = [
        pltpu.make_async_copy(watt_ref.at[: 3 * d], watt_s, load.at[6]),
        pltpu.make_async_copy(resg_ref, resg_s, load.at[7]),
        pltpu.make_async_copy(kept_ref, kept_s, load.at[8]),
        pltpu.make_async_copy(result_ref, result_s, load.at[9]),
    ]

    def crop_copies(crop, size):
        span = pl.ds(LG * crop, size)
        slot = lax.rem(crop, 2)
        here = pl.ds(0, size)
        return [
            pltpu.make_async_copy(cot_ref.at[span], cot_s.at[slot, here], fetch.at[0, slot]),
            pltpu.make_async_copy(tok_ref.at[span], tok_s.at[slot, here], fetch.at[1, slot]),
            pltpu.make_async_copy(ing_s.at[slot, here], ing_ref.at[span], store.at[0, slot]),
            pltpu.make_async_copy(out_s.at[slot, here], out_ref.at[span], store.at[1, slot]),
        ]

    def place(crop, local):
        hot, span, lo, n, count = one_hot(col_s, crop, images, local)
        size = count // images
        window = lambda ref: jnp.concatenate([ref[i, pl.ds(lo, n), :] for i in range(images)], axis=0)
        taken = tn(hot, jnp.ones((images * n, 128), bf16))[:, 0:1] > 0.5
        get_cot, get_tok, put_ing, put_out = crop_copies(crop, size)
        slot = lax.rem(crop, 2)
        get_tok.wait()
        old = tok_s[slot, 0:size].reshape(count, d).astype(f32)
        new = jnp.where(taken, tn(hot, window(result_s)), old).astype(bf16)
        out_s[slot, 0:size] = new.reshape(size, images, d)
        put_out.start()
        pump(schedule, step, 1)
        get_cot.wait()
        spread = tn(hot, window(high_ref)) + tn(hot, window(low_ref))
        old = cot_s[slot, 0:size].reshape(count, d).astype(f32)
        ing_s[slot, 0:size] = jnp.where(taken, spread, old).reshape(size, images, d)
        put_ing.start()

    @pl.when(step == 0)
    def _():
        columns(0).start()
        for copy in acts:
            copy.start()
        for k in (1, 2, 3):
            columns(k).start()
        for copy in later:
            copy.start()
        vecg_s[...] = jnp.zeros_like(vecg_s)
        if links:
            at.barrier()
        for copy in acts:
            copy.wait()

    for k in range(4):
        @pl.when(step == k)
        def _(k=k):
            columns(k).wait()

    @pl.when(step < 4)
    def _():
        which = jnp.where(turn == 3, 1, 0)
        where = pl.ds(pl.multiple_of(turn * d, 128), d)
        left = dp_s[turn].reshape(total, d)
        gatt_s[where, :] = tn(left, act_s[which].reshape(total, d)).astype(bf16)

    @pl.when(step == 4)
    def _():
        for copy in later:
            copy.wait()

    pump(schedule, step, 0)

    @pl.when((step > 3) & (step < 4 + images))
    def _():
        image = step - 4
        standard, inverse = normalize(kept_s[image].astype(f32))
        ng = rg_ref[image] * vec_ref[2:3]
        for j in range(3):
            ng += nn(dp_s[j, image], watt_s[j * d : (j + 1) * d, :])
        pump(schedule, step, 1)
        grad = resg_s[image] + norm_backward(ng, standard, inverse, vec_ref[0:1])
        high = grad.astype(bf16)
        high_ref[image] = high
        low_ref[image] = (grad - high.astype(f32)).astype(bf16)
        vecg_s[0:1] += colsum(ng * standard)
        vecg_s[1:2] += colsum(ng)

    first_crop = 4 + images

    @pl.when(step == 4)
    def _():
        token_columns(idx_ref, idx_s, col_s)
        for crop in range(2):
            for copy in crop_copies(crop, LG)[:2]:
                copy.start()

    @pl.when((step == first_crop) | (step == first_crop + 1))
    def _():
        place(step - first_crop, False)

    @pl.when(step == first_crop + 1)
    def _():
        for copy in crop_copies(2, 4 * LL)[:2]:
            copy.start()
        for copy in crop_copies(0, LG)[2:]:
            copy.wait()

    @pl.when(step == first_crop + 2)
    def _():
        place(2, True)

    pump(schedule, step, 2)

    @pl.when(step == last)
    def _():
        for copy in crop_copies(1, LG)[2:] + crop_copies(2, 4 * LL)[2:]:
            copy.wait()

    if links:
        @pl.when(step == last)
        def _():
            exchange(2, at.y).wait()
            full_sum = vbuf[3] + vbuf[10]
            vecout_ref[...] = full_sum[: vecout_ref.shape[0]]
            reduce.gathered(0, *reduce.lines(), target=gout_ref)
            for make in lines:
                make().wait_send()
            reduce.sends.finish()


def adamw(grad, first, second, master, average, rate, decay):
    first_new = 0.5 * first + 0.5 * grad
    second_new = 0.5 * second + 0.5 * grad * grad
    update = first_new / (jnp.sqrt(second_new) + 1e-08)
    master_new = master - rate * (update + decay * master)
    average_new = 0.9 * average + 0.1 * master_new
    return (first_new, second_new, master_new, average_new)


GROUPS = ((0.02, 0.05), (0.02, 0.05), (0.2, 0.0))


def final_kernel(*refs):
    groups_in, rest = refs[2:17], refs[19:]
    (ing_in, out_in), (ing_ref, out_ref) = refs[:2], refs[17:19]
    qb_ref, groups_out, rest = rest[0], rest[1:18], rest[18:]
    state_s, load, fresh, store, pass_on = rest[:15], rest[15], rest[16:30], rest[30], rest[31]
    bounce = rest[32:34]
    state = [
        pltpu.make_async_copy(src, dst, load.at[i])
        for i, (src, dst) in enumerate(zip(groups_in, state_s))
    ]
    for c in state:
        c.start()
    stores, passing = [], []
    for k, (a, b) in enumerate(CROPS):
        for j, (src, dst) in enumerate(((ing_in, ing_ref), (out_in, out_ref))):
            through = bounce[j].at[a:b]
            taken = pltpu.make_async_copy(src.at[a:b], through, pass_on.at[0, j, k])
            taken.start()
            given = pltpu.make_async_copy(through, dst.at[a:b], pass_on.at[1, j, k])
            passing.append((taken, given))
    for g in range(3):
        for taken, given in passing[2 * g : 2 * g + 2]:
            taken.wait()
            given.start()
            stores.append(given)
        for c in state[5 * g : 5 * g + 5]:
            c.wait()
        grad, first, second, master, average = [ref[...] for ref in state_s[5 * g : 5 * g + 5]]
        new = adamw(grad, first, second, master, average, *GROUPS[g])
        if g < 2:
            new = new + (new[2].astype(bf16),)
        base = 5 * g
        for i, value in enumerate(new):
            fresh[base + i][...] = value
        pairs = [(fresh[base + i], base + i) for i in range(len(new))] + [(state_s[5 * g], 14 + g)]
        for src, i in pairs:
            stores.append(pltpu.make_async_copy(src, groups_out[i], store.at[i]))
            stores[-1].start()
    qb_ref[...] = state_s[10][3]
    for c in stores:
        c.wait()


def sds(*shape_dtype):
    return jax.ShapeDtypeStruct(shape_dtype[:-1], shape_dtype[-1])


def scratch(*shape_dtype):
    return pltpu.VMEM(shape_dtype[:-1], shape_dtype[-1])


def dma(*shape):
    return pltpu.SemaphoreType.DMA(shape)


def per_device(
    tokens, cotangent, kept_index,
    attention_weights, attention_first, attention_second, attention_average,
    feedforward_weights, feedforward_first, feedforward_second, feedforward_average,
    vector_weights, vector_first, vector_second, vector_average,
):
    images, length, d = tokens.shape
    ndp, nmp = lax.axis_size("dp"), lax.axis_size("mp")
    links = (ndp, nmp) == (8, MP)
    vec = vector_weights
    rows, hb = feedforward_weights.shape[1:]
    hidden = nmp * hb
    mask = masks()
    mask_specs = [full(m.shape) for m in mask]
    tok, cot = tokens.transpose(1, 0, 2), cotangent.transpose(1, 0, 2)
    comm = (lambda i: dict(collective_id=i, has_side_effects=True)) if links else (lambda i: {})

    att, ff = attention_weights.T, feedforward_weights
    if not links:
        att, ff = att.astype(bf16), ff.astype(bf16)
        att = lax.all_gather(att, ("dp", "mp"), axis=0, tiled=True)
        wff = lax.all_gather(lax.all_gather(ff, "dp", axis=1, tiled=True), "mp", axis=0)
    now = lambda *s: pl.BlockSpec((1,) + s, lambda i: (jnp.maximum(i - 1, 0), 0, 0))
    whole = lambda *s: pl.BlockSpec(s, lambda j: (0,) * len(s), pipeline_mode=pl.Buffered(1))
    rowspec = (images, RI, d)
    outs = pl.pallas_call(
        functools.partial(forward_kernel, links),
        grid=(1 + images,),
        in_specs=[ANY, ANY, full(kept_index.shape), full(vec.shape), *mask_specs]
        + ([full(att.shape), full(ff.shape)] if links else [ANY, ANY]),
        out_specs=[ANY] * 4 + [now(RI, d)] * 4 + [ANY] + [ANY] * links,
        out_shape=[sds(*rowspec, bf16)] * 3 + [
            sds(images, RI, 3 * d, bf16), sds(*rowspec, bf16), sds(*rowspec, f32),
            sds(*rowspec, f32), sds(*rowspec, bf16), sds(4 * d, d, bf16),
        ] + [sds(nmp, 2, d, hb, bf16)] * links,
        scratch_shapes=[
            scratch(4 * d, d, bf16), scratch(length, images, d, bf16), scratch(length, images, d, bf16),
            scratch(8, 384, f32), scratch(384, 8, f32), dma(7),
            *[scratch(*rowspec, bf16)] * 3, scratch(images, RI, 3 * d, bf16),
        ] + (
            [scratch(rows, d, bf16), scratch(2, rows, hb, bf16)]
            + [dma(4, Gather.SLOTS), dma(4, Gather.SLOTS), dma(4, 1)] if links else []
        ),
        compiler_params=params(**comm(0)),
        name="forward",
    )(tok, cot, kept_index, vec, *mask, att, ff)
    kept, normed, cotk, proj, mixed, branch, resid, n2, watt = outs[:9]
    if links:
        wff = outs[9]

    outs = pl.pallas_call(
        functools.partial(feed_kernel, links),
        grid=(nmp,),
        in_specs=[
            whole(*rowspec), whole(*rowspec), ANY, ANY, full(vec.shape),
        ],
        out_specs=[full(rowspec), full(rowspec), ANY, full((nmp, hb))]
        + [full((2, 2, rows, hb))] * links,
        out_shape=[
            sds(*rowspec, bf16), sds(*rowspec, f32),
            sds(nmp, 2, d, hb, bf16), sds(nmp, hb, f32),
        ] + [sds(2, 2, rows, hb, bf16)] * links,
        scratch_shapes=[
            scratch(*rowspec, f32), scratch(images * RI, hb, bf16), scratch(images * RI, hb, bf16),
            *[scratch(RI, hb, f32)] * 4,
            scratch(nmp, 2, d, hb, bf16), scratch(2, 2, d, hb, bf16), dma(nmp + 1), dma(2),
        ] + (
            [dma(Gather.SLOTS), dma(Gather.SLOTS), dma(4)]
            + [scratch(n, 2, rows, hb, bf16) for n in (8, 8, 2, 2, 2)]
            + [dma(Reduce.SLOTS), dma(Reduce.SLOTS), dma(8)] if links else []
        ),
        compiler_params=params(**comm(3)),
        name="feedforward",
    )(n2, cotk, resid, wff, vec)
    result, n2g, gff, bg = outs[:4]

    spans = (16, 16, 4, 4, 4, 4)
    outs = pl.pallas_call(
        functools.partial(backward_kernel, links),
        grid=(images,),
        in_specs=[
            per_image(RI, d), per_image(RI, d), per_image(RI, d), per_image(RI, d),
            per_image(RI, d), per_image(RI, 3 * d),
            pl.BlockSpec((d, d), lambda i: (3, 0)), full(vec.shape), *mask_specs,
        ] + [ANY, full((2, 2, rows, hb))] * links,
        out_specs=[per_image(RI, 4 * d), per_image(RI, d), per_image(RI, 1), full((8, d))]
        + [full((2, rows, hb))] * links,
        out_shape=[
            sds(images, RI, 4 * d, bf16), sds(*rowspec, f32), sds(images, RI, 1, f32), sds(8, d, f32),
        ] + [sds(2, rows, hb, f32)] * links,
        scratch_shapes=[scratch(RI, d, bf16)] + (
            [scratch(n, 2, rows, hb, bf16) for n in (8, 8, 2, 2, 2, 4)]
            + [dma(Reduce.SLOTS), dma(Reduce.SLOTS), dma(8)] if links else []
        ),
        compiler_params=params(**comm(1)),
        name="attention_backward",
    )(n2g, cotk, branch, resid, normed, proj, watt, vec, *mask, *([gff, outs[4]] if links else []))
    dp, resg, rg, vecg = outs[:4]
    if links:
        feedforward_gradient = outs[4]

    full_d = (4 * d, d)
    outs = pl.pallas_call(
        functools.partial(grads_kernel, links),
        grid=(4 + images + 3,),
        in_specs=[ANY, ANY, ANY, full((images, RI, 1)), ANY, ANY, full(vec.shape), ANY]
        + [full(kept_index.shape), ANY, ANY, ANY]
        + [full((8, d)), full((hidden // d, d))] * links,
        out_specs=[ANY, ANY]
        + ([full((rows, d)), full(vec.shape)] if links else [full(full_d), full((8, d))]),
        out_shape=[sds(length, images, d, f32), sds(length, images, d, bf16)]
        + ([sds(rows, d, f32), sds(*vec.shape, f32)] if links else [sds(*full_d, bf16), sds(8, d, f32)]),
        scratch_shapes=([scratch(*full_d, bf16), scratch(8, d, f32)] if links else []) + [
            scratch(3 * d, d, bf16), scratch(4, *rowspec, bf16), scratch(2, *rowspec, bf16),
            scratch(*rowspec, f32), scratch(*rowspec, bf16), dma(10),
            *[scratch(*rowspec, bf16)] * 3,
            scratch(8, 384, f32), scratch(384, 8, f32),
            scratch(2, LG, images, d, bf16), scratch(2, LG, images, d, bf16),
            scratch(2, LG, images, d, f32), scratch(2, LG, images, d, bf16), dma(2, 2), dma(2, 2),
        ] + (
            [scratch(n, rows, d, bf16) for n in spans[1:]]
            + [dma(Reduce.SLOTS), dma(Reduce.SLOTS), scratch(11, 16, d, f32), dma(8), dma(8)]
            if links else []
        ),
        compiler_params=params(60, **comm(2)),
        name="attention_grads",
    )(
        dp, normed, mixed, rg, resg, kept, vec, watt, kept_index, tok, cot, result,
        *([vecg, bg] if links else []),
    )
    ing, out = outs[:2]
    if links:
        gatt, vector_gradient = outs[2:]
    else:
        gatt, vecg_in = outs[2:]
        local = jnp.concatenate([vecg_in[:2], vecg[:7], bg], axis=0)
        gatt = lax.psum_scatter(gatt, ("dp", "mp"), scatter_dimension=0, tiled=True).astype(f32)
        gff = lax.psum_scatter(gff, "mp", scatter_dimension=0, tiled=False)
        gff = lax.psum_scatter(gff, "dp", scatter_dimension=1, tiled=True)
        feedforward_gradient, vector_gradient = gff.astype(f32), lax.psum(local, ("dp", "mp"))

    state = []
    for grad, *rest in (
        (gatt, attention_first.T, attention_second.T, attention_weights.T, attention_average.T),
        (
            feedforward_gradient, feedforward_first, feedforward_second, feedforward_weights,
            feedforward_average,
        ),
        (vector_gradient, vector_first, vector_second, vector_weights, vector_average),
    ):
        state += [grad, *rest]
    fresh = []
    for g in range(3):
        fresh += [(state[5 * g].shape, f32)] * 4 + [(state[5 * g].shape, bf16)] * (g < 2)
    ing, out, qb, *new = pl.pallas_call(
        final_kernel,
        in_specs=[ANY] * 17,
        out_specs=[ANY, ANY, pl.BlockSpec(memory_space=pltpu.VMEM)] + [ANY] * (len(fresh) + 3),
        out_shape=[sds(length, images, d, f32), sds(length, images, d, bf16), sds(d, f32)]
        + [jax.ShapeDtypeStruct(*f) for f in fresh]
        + [sds(*state[5 * g].shape, f32) for g in range(3)],
        scratch_shapes=[
            *[pltpu.VMEM(v.shape, f32) for v in state], dma(15),
            *[pltpu.VMEM(*f) for f in fresh], dma(len(fresh) + 3), dma(2, 2, 3),
            scratch(length, images, d, f32), scratch(length, images, d, bf16),
        ],
        compiler_params=params(),
        name="finish",
    )(ing, out, *state)
    att_new, ff_new, vec_new = [v.T for v in new[:5]], new[5:10], new[10:14]
    gatt, feedforward_gradient, vector_gradient = new[14:]
    return (
        out.transpose(1, 0, 2), ing.transpose(1, 0, 2),
        gatt.T, *att_new, feedforward_gradient, *ff_new, vector_gradient, *vec_new, qb,
    )


def solution(mesh):
    rows = P(("dp", "mp"), None, None)
    att = P(None, ("dp", "mp"))
    feed = P(None, "dp", "mp")
    in_specs = (rows, rows, P(("dp", "mp"), None)) + (att,) * 4 + (feed,) * 4 + (P(),) * 4
    out_specs = (rows, rows) + (att,) * 6 + (feed,) * 6 + (P(),) * 6
    return jax.shard_map(
        per_device, mesh=mesh, in_specs=in_specs, out_specs=out_specs, check_vma=False
    )
```

```python
import functools

import jax
import jax.numpy as jnp
import numpy as np
from jax import lax
from jax.experimental import pallas as pl
from jax.experimental.pallas import tpu as pltpu
from jax.sharding import PartitionSpec as P

H = 12
HD = 64
LG = 197
LL = 37
KG = LG // 2
KL = LL // 2
LOC = 4 * KL
KEPT = 2 * KG + LOC
RI = -(-KEPT // 16) * 16
SPANS = ((0, KG), (KG, 2 * KG), (2 * KG, KEPT))
UNITS = tuple((a // 16 * 16, -(-b // 16) * 16) for a, b in SPANS)
PAIRS = H // 2
W2L = 2 * HD

bf16 = jnp.bfloat16
f32 = jnp.float32


def params(limit=56, **kw):
    return pltpu.CompilerParams(vmem_limit_bytes=limit << 20, **kw)


def full(shape):
    return pl.BlockSpec(shape, lambda *_: (0,) * len(shape))


def per_image(*shape):
    return pl.BlockSpec((1,) + shape, lambda i, *_: (i,) + (0,) * len(shape))


def nn(a, b):
    return lax.dot_general(a, b, (((1,), (0,)), ((), ())), preferred_element_type=f32)


def nt(a, b):
    return lax.dot_general(a, b, (((1,), (1,)), ((), ())), preferred_element_type=f32)


def tn(a, b):
    return lax.dot_general(a, b, (((0,), (0,)), ((), ())), preferred_element_type=f32)


def normalize(rows):
    center = rows - jnp.mean(rows, axis=-1, keepdims=True)
    spread = jnp.mean(center * center, axis=-1, keepdims=True)
    inverse = lax.rsqrt(spread + 1e-06)
    return center * inverse, inverse


def norm_backward(upstream, standard, inverse, gain):
    scaled = upstream * gain
    return inverse * (
        scaled
        - jnp.mean(scaled, axis=-1, keepdims=True)
        - standard * jnp.mean(scaled * standard, axis=-1, keepdims=True)
    )


def colsum(v):
    return jnp.sum(v, axis=0, keepdims=True)


def masks():
    crop = np.full(RI, -1)
    crop[:KG], crop[KG : 2 * KG] = 0, 1
    for c in range(4):
        crop[2 * KG + c * KL : 2 * KG + (c + 1) * KL] = 2 + c
    adds, valids = [], []
    for (a, b), (lo, hi) in zip(SPANS, UNITS):
        rows = np.arange(lo, hi)
        inside = (rows >= a) & (rows < b)
        same = (crop[lo:hi, None] == crop[None, lo:hi]) & inside[:, None] & inside[None, :]
        adds.append(np.tile(np.where(same, 0.0, -1e9), (1, 2)).astype(np.float32))
        valids.append(np.tile(inside[None, :].astype(np.float32), (8, 2)))
    return [jnp.asarray(m) for m in adds + valids]


def lane_half(shape):
    return lax.broadcasted_iota(jnp.int32, shape, len(shape) - 1) < HD


def split_heads(v, scale):
    first = lane_half(v.shape)
    zero = jnp.zeros_like(v)
    if scale != 1.0:
        v = v * jnp.asarray(scale, v.dtype)
    return jnp.concatenate([jnp.where(first, v, zero), jnp.where(first, zero, v)], axis=0)


def join_heads(v):
    n = v.shape[0] // 2
    return jnp.where(lane_half((n, v.shape[1])), v[:n], v[n:])


def softmax_keys(st, valid):
    p = jnp.exp(st - jnp.max(st, axis=0, keepdims=True))
    return p * (valid / jnp.sum(p, axis=0, keepdims=True))


def store_window(ref, image, lo, hi, last, cols, value, tail):
    value = value.astype(bf16)
    if tail is not None:
        value = jnp.concatenate([value[:16] + tail, value[16:]], axis=0)
    end = hi if last else hi - 16
    ref[image, lo:end, cols] = value[: end - lo]
    return None if last else value[end - lo :]


MESH = pl.DeviceIdType.MESH
ANY = pl.BlockSpec(memory_space=pl.ANY)
MP = 4
CROPS = ((0, LG), (LG, 2 * LG), (2 * LG, 2 * LG + 4 * LL))
ORDER = ((0, 1, 2, 3), (1, 0, 1, 2), (2, 2, 3, 1), (3, 3, 0, 0))


def flip(index, bit):
    return index + bit * (1 - 2 * lax.rem(lax.div(index, bit), 2))


def remote(src, dst, send, recv, to):
    return pltpu.make_async_remote_copy(
        src_ref=src, dst_ref=dst, send_sem=send, recv_sem=recv, device_id=to, device_id_type=MESH
    )


class Sends:
    def __init__(self):
        self.made = []

    def start(self, make, when=None):
        def go():
            make().start()

        go() if when is None else pl.when(when)(go)
        self.made.append((make, when))

    def finish(self):
        for make, when in self.made:
            def wait(make=make):
                make().wait_send()

            wait() if when is None else pl.when(when)(wait)


class Place:
    def __init__(self):
        self.dp = lax.axis_index("dp")
        self.z = lax.axis_index("mp")
        x, y = flip(self.dp, 2), flip(self.dp, 4)
        self.core = (flip(self.dp, 1), self.z)
        self.x, self.y = (x, self.z), (y, self.z)
        self.chips = (self.dp, x, y, flip(x, 4))
        self.mates = tuple(flip(c, 1) for c in self.chips)
        power = (1 + 3 * lax.rem(self.z, 2)) * (1 + 15 * lax.div(self.z, 2))
        self.event = []
        for row in ORDER:
            code = sum(v << (2 * i) for i, v in enumerate(row))
            self.event.append(lax.rem(lax.div(0 * power + code, power), 4))
        self.low, self.high = self.z > 0, self.z < MP - 1
        self.middle = self.low & self.high
        self.line = [lax.rem(self.z + k, MP) for k in range(MP)]
        self.up, self.down = (self.dp, self.z + 1), (self.dp, self.z - 1)
        self.onward = (self.up, self.down, (self.dp, 3 * (self.z - 1)))

    def barrier(self):
        sem = pltpu.get_barrier_semaphore()
        others = [self.core, self.x, self.y]
        others += [(self.dp, k) for k in self.line[1:]]
        for other in others:
            pl.semaphore_signal(sem, inc=1, device_id=other, device_id_type=MESH)
        pl.semaphore_wait(sem, len(others))


def att_block(ref, dp, z, rows):
    return ref.at[pl.ds(pl.multiple_of((dp * MP + z) * rows, 32), rows), :]


def att_part(ref, dp, z, rows, h):
    half = rows // 2
    return ref.at[pl.ds(pl.multiple_of((dp * MP + z) * rows + h * half, 16), half), :]


def ff_part(ref, dp, z, rows, h):
    return ref.at[z, h, pl.ds(pl.multiple_of(dp * rows, 32), rows), :]


def ff_block(ref, dp, z, rows):
    return ref.at[z, :, pl.ds(pl.multiple_of(dp * rows, 32), rows), :]


class Gather:
    ALONG, X, Y, D, C, SLOTS = 0, 4, 8, 12, 16, 32

    def __init__(self, at, first, place, send, recv, local):
        self.at, self.first, self.place = at, first, place
        self.send, self.recv, self.local = send, recv, local
        self.sends = Sends()

    def copy(self, slot, e, r, to):
        slot = self.ALONG + self.at.event[e] if slot is None else slot
        dst = self.place(e, self.at.chips[r])
        src = self.first(e) if r == 0 else dst
        return remote(src, dst, self.send.at[slot], self.recv.at[slot], to)

    def put(self, slot, e, r, to, when=None):
        self.sends.start(lambda: self.copy(slot, e, r, to), when)

    def got(self, slot, e, dp):
        dst = self.place(e, dp)
        remote(dst, dst, self.send.at[slot], self.recv.at[slot], self.at.core).wait_recv()

    def keep(self, e):
        return pltpu.make_async_copy(self.first(e), self.place(e, self.at.dp), self.local.at[e])

    def spread(self, e):
        self.put(self.X + e, e, 0, self.at.x)
        self.put(self.Y + e, e, 0, self.at.y)
        self.put(self.C + 4 * e, e, 0, self.at.core)

    def begin(self):
        at = self.at
        self.keep(0).start()
        for to, when in ((at.up, at.high), (at.down, at.low)):
            self.put(None, 0, 0, to, when)
        self.spread(0)

    def direct(self):
        self.keep(0).start()
        for zb in self.at.line[1:]:
            self.put(None, 0, 0, (self.at.dp, zb))

    def arrived(self, e):
        self.got(self.ALONG + self.at.event[e], e, self.at.dp)

    def along(self, e):
        at = self.at
        self.arrived(e)
        self.put(None, e, 0, at.onward[e - 1], at.middle)
        self.spread(e)

    def plane(self, e):
        at = self.at
        self.got(self.X + e, e, at.chips[1])
        if e % 2 == 0:
            self.put(self.D + e, e, 1, at.y)
        self.put(self.C + 4 * e + 1, e, 1, at.core)
        self.got(self.Y + e, e, at.chips[2])
        if e % 2 == 1:
            self.put(self.D + e, e, 2, at.x)
        self.put(self.C + 4 * e + 2, e, 2, at.core)

    def corner(self, e):
        self.got(self.D + e, e, self.at.chips[3])
        self.put(self.C + 4 * e + 3, e, 3, self.at.core)

    def finish(self, e):
        for r in range(4):
            self.got(self.C + 4 * e + r, e, self.at.mates[r])


def add_into(target, first, *others):
    if len(others) == 1 and target.dtype == bf16:
        @pl.loop(0, first.shape[0] // 48)
        def _(i):
            s = pl.ds(pl.multiple_of(i * 48, 16), 48)
            target[s, :] = first[s, :] + others[0][s, :]

        return
    step = 48

    @pl.loop(0, first.shape[0] // step)
    def _(i):
        s = pl.ds(pl.multiple_of(i * step, 16), step)
        total = first[s, :].astype(f32)
        for ref in others:
            total = total + ref[s, :].astype(f32)
        target[s, :] = total.astype(target.dtype)


class Reduce:
    C, D, X, Y, ALONG, SLOTS = 0, 16, 20, 24, 28, 32

    def __init__(self, at, source, own, parts, bufs, send, recv, load=None, base=0):
        self.at, self.source, self.own, self.parts, self.base = at, source, own, parts, base
        self.c, self.d, self.x, self.y, self.line = bufs
        self.send, self.recv, self.load = send, recv, load
        self.sends = Sends()

    def put(self, slot, src, dst, to):
        self.sends.start(
            lambda: remote(src(), dst(), self.send.at[slot], self.recv.at[slot], to)
        )

    def got(self, slot, dst):
        remote(dst, dst, self.send.at[slot], self.recv.at[slot], self.at.core).wait_recv()

    def slot(self, e, r):
        return 4 * (e - self.base) + r

    def cross(self, e, r):
        i = self.slot(e, r)
        self.put(self.C + i, lambda: self.source(e, self.at.mates[r]), lambda: self.c.at[i], self.at.core)
        if self.load is not None:
            self.load(e, r).start()

    def add(self, e, r, *others, target=None):
        i = self.slot(e, r)
        self.got(self.C + i, self.c.at[i])
        if self.load is not None:
            self.load(e, r).wait()
        refs = [self.own(e, r), self.c.at[i]] + list(others)
        self.total(refs[0] if target is None else target, *refs)

    def total(self, target, *refs):
        for t, *rest in zip(self.parts(target), *[self.parts(ref) for ref in refs]):
            add_into(t, *rest)

    def corner(self, e):
        at, i = self.at, e - self.base
        self.add(e, 3)
        self.put(
            self.D + i, lambda: self.own(e, 3), lambda: self.d.at[i], at.x if e % 2 else at.y
        )
        r, slot, buf, to = (1, self.X, self.x, at.x) if e % 2 else (2, self.Y, self.y, at.y)
        self.add(e, r)
        self.put(slot + i, lambda: self.own(e, r), lambda: buf.at[i], to)

    def plane(self, e):
        at, i = self.at, e - self.base
        r, slot, buf, to = (2, self.Y, self.y, at.y) if e % 2 else (1, self.X, self.x, at.x)
        self.got(self.D + i, self.d.at[i])
        self.add(e, r, self.d.at[i])
        self.put(slot + i, lambda: self.own(e, r), lambda: buf.at[i], to)

    def gathered(self, e, *others, target=None):
        i = e - self.base
        self.got(self.X + i, self.x.at[i])
        self.got(self.Y + i, self.y.at[i])
        self.add(e, 0, self.x.at[i], self.y.at[i], *others, target=target)

    def send_along(self, e, src):
        at = self.at
        zb = at.event[e]
        self.sends.start(
            lambda: remote(
                src(), self.line.at[at.z], self.send.at[self.ALONG + zb],
                self.recv.at[self.ALONG + at.z], (at.dp, zb),
            )
        )

    def along(self, e):
        self.gathered(e)
        self.send_along(e, lambda: self.own(e, 0))

    def lines(self):
        got = []
        for zb in self.at.line[1:]:
            got.append(self.line.at[zb])
            self.got(self.ALONG + zb, got[-1])
        return got


def pump(schedule, step, point):
    for (s, p), action in schedule:
        if isinstance(point, int):
            if p == point:
                pl.when(step == s)(action)
        else:
            pl.when((step == s) & (point == p))(action)


def do(action, *args):
    return lambda: action(*args)


def token_columns(idx_ref, idx_s, col_s):
    idx_s[...] = jnp.full(idx_s.shape, -1.0, f32)
    idx_s[0 : idx_ref.shape[0], 0 : idx_ref.shape[1]] = idx_ref[...].astype(f32)
    col_s[...] = idx_s[...].T


def one_hot(col_s, crop, images, local):
    (a, b), (s, e), (lo, hi) = [v[2 if local else 0] for v in (CROPS, SPANS, UNITS)]
    n, size = hi - lo, b - a
    count = images * size
    if not local:
        a, s, e, lo = LG * crop, KG * crop, KG * (crop + 1), UNITS[1][0] * crop
        lo = pl.multiple_of(lo, 16)
    columns = col_s[pl.ds(lo, n), :]
    row = lax.broadcasted_iota(jnp.int32, (n, 1), 0) + lo
    pieces = []
    for i in range(images):
        place = (columns[:, i : i + 1].astype(jnp.int32) - a) * images + i
        pieces.append(jnp.where((row >= s) & (row < e), place, -1))
    index = jnp.concatenate(pieces, axis=0)
    hot = lax.broadcasted_iota(jnp.int32, (index.shape[0], count), 1) == index
    return hot.astype(f32).astype(bf16), pl.ds(a, size), lo, n, count


def forward_kernel(
    links, tok_ref, cot_ref, idx_ref, vec_ref, m0_ref, m1_ref, m2_ref, v0_ref, v1_ref, v2_ref,
    att_ref, ff_ref,
    kept_out, normed_out, cotk_out, proj_out, mixed_ref, branch_ref, resid_ref, n2_ref,
    watt_out, *rest,
):
    if links:
        wff_ref, *rest = rest
        att_s, ff_s, send, recv, local = rest[10:]
    watt_ref, tok_s, cot_s, idx_s, col_s, load, kept_ref, normed_ref, cotk_ref, proj_ref = rest[:10]
    step = pl.program_id(0)
    images, _, d = kept_ref.shape
    leave = [
        pltpu.make_async_copy(src, dst, load.at[3 + i])
        for i, (src, dst) in enumerate(
            (
                (kept_ref, kept_out), (normed_ref, normed_out), (cotk_ref, cotk_out),
                (proj_ref, proj_out),
            )
        )
    ]
    loads = [
        pltpu.make_async_copy(tok_ref, tok_s, load.at[0]),
        pltpu.make_async_copy(cot_ref, cot_s, load.at[1]),
    ]
    order = (0, 1, 2, 3)

    def clear(dst):
        for i in range(images):
            for _, hi in UNITS[:2]:
                dst[i, hi - 16 : hi] = jnp.zeros((16, d), bf16)

    def pick(crop, local, src, dst):
        hot, span, lo, n, k = one_hot(col_s, crop, images, local)
        got = nn(hot, src[span].reshape(k, d)).astype(bf16)
        for i in range(images):
            part = got[i * n : (i + 1) * n]
            head = pl.ds(lo, 16)
            if local:
                dst[i, head, :] = dst[i, head, :] + part[:16]
            else:
                old = jnp.where(crop == 0, jnp.zeros_like(part[:16]), dst[i, head, :])
                dst[i, head, :] = old + part[:16]
            dst[i, pl.ds(lo + 16, n - 16), :] = part[16:]

    def cot_rows():
        loads[1].wait()
        clear(cotk_ref)

        @pl.loop(0, 2)
        def _(crop):
            pick(crop, False, cot_s, cotk_ref)

        pick(2, True, cot_s, cotk_ref)

    def project(r):
        j = order[r]

        @pl.when(j < 3)
        def _():
            rows_j = pl.ds(pl.multiple_of(j * d, 128), d)
            bias = jnp.where(j == 1, 0.0, jnp.where(j == 0, vec_ref[3:4], vec_ref[4:5]))

            @pl.loop(0, images)
            def _(i):
                part = nt(normed_ref[i], watt_ref[rows_j, :]) + bias
                proj_ref[i, :, rows_j] = part.astype(bf16)

    acts, schedule = [[]] * 5 + [[cot_rows]], []
    if links:
        at = Place()
        rows = att_ref.shape[0]
        half = rows // 2

        def att_half(h):
            return Gather(
                at,
                lambda e: att_part(watt_ref, at.dp, at.event[e], rows, h) if e
                else att_s.at[h * half : (h + 1) * half],
                lambda e, dp: att_part(watt_ref, dp, at.event[e], rows, h),
                send.at[h], recv.at[h], local.at[h],
            )

        def feed_half(h):
            return Gather(
                at, lambda e: ff_part(wff_ref, at.dp, at.event[e], rows, h) if e else ff_s.at[h],
                lambda e, dp: ff_part(wff_ref, dp, at.event[e], rows, h),
                send.at[2 + h], recv.at[2 + h], local.at[2 + h],
            )

        (a0, a1), (f0, f1) = [att_half(h) for h in (0, 1)], [feed_half(h) for h in (0, 1)]
        chip = lax.div(at.dp, 2)
        order = (chip, flip(chip, 1), flip(chip, 2), 3 - chip)

        def ready(r):
            for part in (a0, a1):
                for e in range(4):
                    part.got(part.C + 4 * e + r, e, at.mates[r])
                if r == 0:
                    part.keep(0).wait()

        acts = [
            [a1.begin, a0.begin],
            [do(a1.along, 1), do(a1.plane, 0), do(a0.along, 1), do(a0.along, 2), do(a1.along, 2)],
            [do(a0.along, 3)],
            [do(a1.along, 3), f0.direct, f1.direct, do(a1.plane, 1), do(a0.plane, 2)],
            [do(a0.plane, 0)],
            [
                do(ready, 0), do(project, 0),
                do(a0.plane, 3), do(a0.plane, 1), do(a1.plane, 3), do(a1.plane, 2), cot_rows,
                do(ready, 1), do(project, 1),
                do(a0.corner, 0), do(a1.corner, 1), do(a0.corner, 3), do(a1.corner, 2),
                do(a1.corner, 0),
                do(ready, 2), do(project, 2),
                do(a0.corner, 1), do(a0.corner, 2), do(a1.corner, 3),
                do(f0.arrived, 2), do(f0.spread, 2), do(f0.arrived, 3), do(f0.spread, 3),
                do(ready, 3), do(project, 3),
            ],
        ]
        schedule = [
            ((1, 3), do(f1.arrived, 2)),
            ((1, 3), do(f1.spread, 2)),
            ((1, 3), do(f1.arrived, 3)),
            ((1, 3), do(f1.spread, 3)),
            ((2, 3), do(f0.plane, 2)),
            ((2, 3), do(f0.plane, 3)),
            ((3, 3), do(f1.plane, 2)),
            ((4, 1), do(f1.plane, 3)),
            ((4, 1), do(f0.corner, 2)),
            ((4, 1), do(f0.corner, 3)),
            ((4, 3), do(f1.corner, 2)),
            ((4, 3), do(f1.corner, 3)),
        ]
    else:
        fetch = pltpu.make_async_copy(att_ref, watt_ref, load.at[2])
    store = pltpu.make_async_copy(watt_ref, watt_out, load.at[2])

    def run(point):
        for action in acts[point]:
            action()

    @pl.when(step == 0)
    def _():
        if links:
            att_s[...] = att_ref[...].astype(bf16)
            at.barrier()
            run(0)
        else:
            fetch.start()
        for c in loads:
            c.start()
        if links:
            ff_s[...] = ff_ref[...].astype(bf16)
        token_columns(idx_ref, idx_s, col_s)
        loads[0].wait()
        clear(kept_ref)

        @pl.loop(0, 2)
        def _(crop):
            pick(crop, False, tok_s, kept_ref)
            for point in (1, 2):
                pl.when(crop == point - 1)(do(run, point))

        pick(2, True, tok_s, kept_ref)
        run(3)
        for i in range(images):
            standard, _ = normalize(kept_ref[i].astype(f32))
            normed_ref[i] = (standard * vec_ref[0:1] + vec_ref[1:2]).astype(bf16)
            if i == 1:
                run(4)
        run(5)
        if not links:
            fetch.wait()
            for r in range(3):
                project(r)
        store.start()
        for c in leave:
            c.start()

    pump(schedule, step, 0)

    @pl.when(step > 0)
    def _():
        image = step - 1
        normed = normed_ref[image]
        pump(schedule, step, 1)
        mrefs, vrefs = (m0_ref, m1_ref, m2_ref), (v0_ref, v1_ref, v2_ref)
        for pair in range(PAIRS):
            cols = lambda j: slice(j * d + pair * W2L, j * d + (pair + 1) * W2L)
            tail = None
            for unit, (lo, hi) in enumerate(UNITS):
                qs = split_heads(proj_ref[image, lo:hi, cols(0)], HD ** -0.5)
                st = nt(proj_ref[image, lo:hi, cols(1)], qs) + mrefs[unit][...]
                pt = softmax_keys(st, vrefs[unit][0:1]).astype(bf16)
                out = join_heads(tn(pt, proj_ref[image, lo:hi, cols(2)]))
                tail = store_window(mixed_ref, 0, lo, hi, unit == 2, cols(0), out, tail)
            if pair == 2:
                pump(schedule, step, 3)
        branch = nt(mixed_ref[0], watt_ref[3 * d :, :]) + vec_ref[5:6]
        branch_ref[0] = branch
        residual = kept_ref[image].astype(f32) + router_score(normed, vec_ref) * branch
        resid_ref[0] = residual
        standard, _ = normalize(residual)
        n2_ref[0] = (standard * vec_ref[6:7] + vec_ref[7:8]).astype(bf16)

    @pl.when(step == images)
    def _():
        if links:
            for feed in (f0, f1):
                feed.finish(2)
                feed.finish(3)
                feed.arrived(1)
                feed.keep(0).wait()
            for part in (a0, a1, f0, f1):
                part.sends.finish()
        for c in [store] + leave:
            c.wait()


def router_score(normed, vec_ref):
    logit = jnp.sum(normed.astype(f32) * vec_ref[2:3], axis=-1, keepdims=True)
    return jax.nn.sigmoid(logit)


def feed_kernel(
    links, n2_ref, cot_ref, resid_ref, w_ref, vec_ref,
    result_out, n2g_out, gff_ref, bg_ref, *rest,
):
    if links:
        acc_ref, *rest = rest
        send, recv, local, a, c, dd, x, y, rsend, rrecv, rlocal = rest[13:]
    result_ref, n2g_ref, out_s, act_s, ig_s, i0, i1, a0, a1, w_s, g_s, load, store = rest[:13]
    inner_s, ag_s = (i0, i1), (a0, a1)
    step = pl.program_id(0)
    last = pl.num_programs(0) - 1
    images, _, d = n2_ref.shape
    nload = w_s.shape[0]
    hb = w_ref.shape[3]
    block, schedule = step, []
    if links:
        at = Place()
        rows = acc_ref.shape[2]
        block = at.event[0]
        for e in (1, 2, 3):
            block = jnp.where(step == 3 - e, at.event[e], block)
        gather = Gather(
            at, lambda e: ff_block(w_ref, at.dp, at.event[e], rows),
            lambda e, dp: w_s.at[3 - e, :, pl.ds(pl.multiple_of(dp * rows, 32), rows), :],
            send, recv, local,
        )
        reduce = Reduce(
            at, lambda e, dp: ff_block(gff_ref, dp, at.event[e], rows),
            lambda e, r: a.at[4 * (e - 2) + r],
            lambda ref: (ref.at[0], ref.at[1]), (c, dd, x, y, None), rsend, rrecv,
            lambda e, r: pltpu.make_async_copy(
                ff_block(gff_ref, at.chips[r], at.event[e], rows), a.at[4 * (e - 2) + r],
                rlocal.at[4 * (e - 2) + r],
            ),
            2,
        )

        def start():
            at.barrier()
            for e in (1, 0):
                gather.spread(e)
                gather.keep(e).start()

        def ready(e):
            gather.finish(e)
            gather.keep(e).wait()

        def cross(e):
            for r in (3, 1, 2, 0):
                reduce.cross(e, r)

        schedule = [
            ((1, 0), do(gather.plane, 1)),
            ((1, 0), do(gather.plane, 0)),
            ((1, 0), do(cross, 3)),
            ((2, 0), do(gather.corner, 1)),
            ((2, 0), do(reduce.corner, 3)),
            ((2, 0), do(cross, 2)),
            ((2, 0), do(ready, 1)),
            ((2, 0), do(reduce.corner, 2)),
            ((2, 0), do(gather.corner, 0)),
            ((3, 0), do(reduce.plane, 3)),
            ((3, 0), do(ready, 0)),
            ((3, 0), do(reduce.plane, 2)),
        ]

    def fetch(e):
        return pltpu.make_async_copy(
            w_ref.at[at.event[3 - e] if links else e], w_s.at[e], load.at[e]
        )

    def save(slot, which):
        return pltpu.make_async_copy(g_s.at[slot], gff_ref.at[which], store.at[slot])

    residual = pltpu.make_async_copy(resid_ref, out_s, load.at[nload])
    early = (0, 1) if links else range(w_s.shape[0])

    @pl.when(step == 0)
    def _():
        for e in early:
            fetch(e).start()
        if links:
            start()
        residual.start()
        n2g_ref[...] = jnp.zeros_like(n2g_ref)
        bg_ref[...] = jnp.zeros_like(bg_ref)
        fetch(0).wait()
        residual.wait()

    for e in early[1:]:
        @pl.when(step == e)
        def _(e=e):
            fetch(e).wait()

    slot = lax.rem(step, 2)

    @pl.when(step > 0)
    def _():
        save(1 - slot, 0).wait()

    pump(schedule, step, 0)

    def first(i):
        inner_s[i % 2][...] = nn(n2_ref[i], w_s[step, 0]) + vec_ref[pl.ds(9 + block, 1), :]
        ag_s[i % 2][...] = nn(cot_ref[i], w_s[step, 1])

    def second(i):
        inner = inner_s[i % 2][...]
        phi = 0.5 * (1.0 + lax.erf(inner * 0.7071067811865476))
        act = (inner * phi).astype(bf16)
        slope = phi + inner * jnp.exp(-0.5 * inner * inner) * 0.3989422804014327
        ig = (ag_s[i % 2][...] * slope).astype(bf16)
        rows_i = slice(i * RI, (i + 1) * RI)
        act_s[rows_i, :] = act
        ig_s[rows_i, :] = ig
        bg_ref[pl.ds(block, 1), :] += colsum(ig.astype(f32))
        out_s[i] += nt(act, w_s[step, 1])
        n2g_ref[i] += nt(ig, w_s[step, 0])

    first(0)
    for i in range(images):
        pump(schedule, step, i + 1)
        if i + 1 < images:
            first(i + 1)
        second(i)

    leave = [
        pltpu.make_async_copy(n2g_ref, n2g_out, store.at[2]),
        pltpu.make_async_copy(result_ref, result_out, store.at[3]),
    ]

    @pl.when(step == last)
    def _():
        leave[0].start()
        result_ref[...] = (out_s[...] + vec_ref[8:9]).astype(bf16)
        leave[1].start()

    n2 = n2_ref[...].reshape(images * RI, d)
    cot = cot_ref[...].reshape(images * RI, d)
    g_s[slot, 0] = tn(n2, ig_s[...]).astype(bf16)
    g_s[slot, 1] = tn(cot, act_s[...]).astype(bf16)
    save(slot, block).start()

    @pl.when(step == last)
    def _():
        for c in leave:
            c.wait()
        if links:
            reduce.gathered(3, target=acc_ref.at[0])
            reduce.gathered(2, target=acc_ref.at[1])
            gather.sends.finish()
            reduce.sends.finish()
        save(slot, 0).wait()


def backward_kernel(
    links, n2g_ref, cotk_ref, branch_ref, resid_ref, normed_ref, proj_ref, wout_ref,
    vec_ref, m0_ref, m1_ref, m2_ref, v0_ref, v1_ref, v2_ref, *rest,
):
    if links:
        gff_ref, acc_ref, dp_ref, resg_ref, rg_ref, vecg_ref, gout_ref = rest[:7]
        mg_s, a, c, dd, x, y, line, send, recv, local = rest[7:]
    else:
        dp_ref, resg_ref, rg_ref, vecg_ref, mg_s = rest
    step = pl.program_id(0)
    schedule = []
    if links:
        at = Place()
        rows = gout_ref.shape[1]
        reduce = Reduce(
            at, lambda e, dp: ff_block(gff_ref, dp, at.event[e], rows),
            lambda e, r: a.at[4 * e + r],
            lambda ref: (ref.at[0], ref.at[1]), (c, dd, x, y, line), send, recv,
            lambda e, r: pltpu.make_async_copy(
                ff_block(gff_ref, at.chips[r], at.event[e], rows), a.at[4 * e + r],
                local.at[4 * e + r],
            ),
        )

        def start():
            at.barrier()
            reduce.send_along(2, lambda: acc_ref.at[1])
            for e in (1, 0):
                for r in (3, 1, 2, 0):
                    reduce.cross(e, r)

        schedule = [
            ((0, 0), start),
            ((0, 1), do(reduce.corner, 1)),
            ((0, 1), do(reduce.send_along, 3, lambda: acc_ref.at[0])),
            ((1, 1), do(reduce.plane, 1)),
            ((2, 0), do(reduce.corner, 0)),
            ((2, 1), do(reduce.along, 1)),
            ((3, 0), do(reduce.plane, 0)),
        ]

    pump(schedule, step, 0)
    d = normed_ref.shape[2]
    normed = normed_ref[0]
    score = router_score(normed, vec_ref)
    branch = branch_ref[0]
    standard, inverse = normalize(resid_ref[0])
    n2g = n2g_ref[0]
    cot = cotk_ref[0].astype(f32)
    resg = cot + norm_backward(n2g, standard, inverse, vec_ref[6:7])
    resg_ref[0] = resg
    bg = (score * resg).astype(bf16)
    rg = jnp.sum(resg * branch, axis=-1, keepdims=True) * score * (1.0 - score)
    rg_ref[0] = rg
    dp_ref[0, :, 3 * d :] = bg
    mg_s[...] = nn(bg, wout_ref[...]).astype(bf16)
    pump(schedule, step, 1)
    mrefs, vrefs = (m0_ref, m1_ref, m2_ref), (v0_ref, v1_ref, v2_ref)
    for pair in range(PAIRS):
        cols = lambda j: slice(j * d + pair * W2L, j * d + (pair + 1) * W2L)
        tails = [None] * 3
        for unit, (lo, hi) in enumerate(UNITS):
            qs = split_heads(proj_ref[0, lo:hi, cols(0)], HD ** -0.5)
            kk = proj_ref[0, lo:hi, cols(1)]
            pt = softmax_keys(nt(kk, qs) + mrefs[unit][...], vrefs[unit][0:1])
            ds = split_heads(mg_s[lo:hi, cols(0)], 1.0)
            gpt = nt(proj_ref[0, lo:hi, cols(2)], ds)
            sg = (pt * (gpt - jnp.sum(pt * gpt, axis=0, keepdims=True))).astype(bf16)
            grads = (
                join_heads(tn(sg, kk)) * HD ** -0.5, nn(sg, qs), nn(pt.astype(bf16), ds)
            )
            for j in range(3):
                tails[j] = store_window(dp_ref, 0, lo, hi, unit == 2, cols(j), grads[j], tails[j])
        if pair == 2:
            pump(schedule, step, 3)
    sums = jnp.concatenate(
        [
            colsum(rg * normed.astype(f32)),
            colsum(dp_ref[0, :, :d].astype(f32)),
            colsum(dp_ref[0, :, 2 * d : 3 * d].astype(f32)),
            colsum(bg.astype(f32)),
            colsum(n2g * standard),
            colsum(n2g),
            colsum(cot),
            jnp.zeros((1, d), f32),
        ],
        axis=0,
    )

    @pl.when(step == 0)
    def _():
        vecg_ref[...] = jnp.zeros_like(vecg_ref)

    vecg_ref[...] += sums
    if links:
        @pl.when(step == pl.num_programs(0) - 1)
        def _():
            reduce.gathered(0, *reduce.lines(), target=gout_ref)
            reduce.sends.finish()


def grads_kernel(
    links, dp_ref, normed_ref, mixed_ref, rg_ref, resg_ref, kept_ref, vec_ref, watt_ref,
    idx_ref, tok_ref, cot_ref, result_ref, *rest,
):
    if links:
        vecb_ref, bias_ref, ing_ref, out_ref, gout_ref, vecout_ref = rest[:6]
        gatt_s, vecg_s, *rest = rest[6:]
        c, dd, x, y, line, send, recv, vbuf, vsend, vrecv = rest[17:]
    else:
        ing_ref, out_ref, gatt_s, vecg_s, *rest = rest
    watt_s, dp_s, act_s, resg_s, kept_s, load, high_ref, low_ref, result_s = rest[:9]
    idx_s, col_s, tok_s, cot_s, ing_s, out_s, fetch, store = rest[9:17]
    step = pl.program_id(0)
    images, _, d = high_ref.shape
    last = 3 + images + 3
    total = images * RI
    chip, schedule = 0, []
    if links:
        at = Place()
        chip = lax.div(at.dp, 2)
        rows = gout_ref.shape[0]
        block = lambda e, dp: att_block(gatt_s, dp, at.event[e], rows)
        reduce = Reduce(
            at, block, lambda e, r: block(e, at.chips[r]), lambda ref: (ref,),
            (c, dd, x, y, line), send, recv,
        )

        def cross(r):
            for e in (3, 2, 1, 0):
                reduce.cross(e, r)

        exchange = lambda k, to: remote(
            vbuf.at[k + 1], vbuf.at[8 + k], vsend.at[k], vrecv.at[k], to
        )
        lines = [
            lambda k=k: remote(
                vbuf.at[0], vbuf.at[4 + at.z], vsend.at[2 + k], vrecv.at[3 + at.z],
                (at.dp, at.line[k]),
            )
            for k in range(1, MP)
        ]

        def spread_vectors():
            vbuf[0, 0:2] = vecg_s[0:2]
            vbuf[0, 2:9] = vecb_ref[0:7]
            vbuf[0, 9:13] = bias_ref[...]
            vbuf[0, 13:16] = jnp.zeros((3, d), f32)
            for make in lines:
                make().start()
            vbuf[4 + at.z] = vbuf[0]

        def line_vectors():
            for k in range(1, MP):
                zb = at.line[k]
                remote(
                    vbuf.at[0], vbuf.at[4 + zb], vsend.at[2 + k], vrecv.at[3 + zb], at.core
                ).wait_recv()
            vbuf[1] = vbuf[4] + vbuf[5] + vbuf[6] + vbuf[7]
            exchange(0, at.core).start()

        def core_vectors():
            exchange(0, at.core).wait()
            vbuf[2] = vbuf[1] + vbuf[8]
            exchange(1, at.x).start()

        def x_vectors():
            exchange(1, at.x).wait()
            vbuf[3] = vbuf[2] + vbuf[9]
            exchange(2, at.y).start()

        turns = (3 - chip, flip(chip, 1), flip(chip, 2), chip)
        schedule = [
            ((1, 2), do(cross, 3)),
            ((1, 2), do(cross, 1)),
            ((2, 2), do(reduce.corner, 3)),
            ((2, 2), do(cross, 2)),
            ((3, 2), do(cross, 0)),
            ((4, 1), do(reduce.plane, 3)),
            ((5, 0), do(reduce.corner, 2)),
            ((6, 0), do(reduce.corner, 1)),
            ((6, 0), do(reduce.along, 3)),
            ((7, 0), do(reduce.plane, 2)),
            ((8, 0), spread_vectors),
            ((8, 0), do(reduce.plane, 1)),
            ((8, 0), do(reduce.corner, 0)),
            ((8, 1), do(reduce.along, 2)),
            ((8, 2), line_vectors),
            ((9, 1), core_vectors),
            ((9, 1), do(reduce.along, 1)),
            ((9, 1), do(reduce.plane, 0)),
            ((9, 2), x_vectors),
        ]
    else:
        turns = (0, 1, 2, 3)
    turn = turns[3]
    for k in (2, 1, 0):
        turn = jnp.where(step == k, turns[k], turn)

    def columns(k):
        lanes = pl.ds(pl.multiple_of(turns[k] * d, 128), d) if links else pl.ds(k * d, d)
        return pltpu.make_async_copy(dp_ref.at[:, :, lanes], dp_s.at[turns[k]], load.at[k])

    acts = [
        pltpu.make_async_copy(normed_ref, act_s.at[0], load.at[4]),
        pltpu.make_async_copy(mixed_ref, act_s.at[1], load.at[5]),
    ]
    later = [
        pltpu.make_async_copy(watt_ref.at[: 3 * d], watt_s, load.at[6]),
        pltpu.make_async_copy(resg_ref, resg_s, load.at[7]),
        pltpu.make_async_copy(kept_ref, kept_s, load.at[8]),
        pltpu.make_async_copy(result_ref, result_s, load.at[9]),
    ]

    def crop_copies(crop, size):
        span = pl.ds(LG * crop, size)
        slot = lax.rem(crop, 2)
        here = pl.ds(0, size)
        return [
            pltpu.make_async_copy(cot_ref.at[span], cot_s.at[slot, here], fetch.at[0, slot]),
            pltpu.make_async_copy(tok_ref.at[span], tok_s.at[slot, here], fetch.at[1, slot]),
            pltpu.make_async_copy(ing_s.at[slot, here], ing_ref.at[span], store.at[0, slot]),
            pltpu.make_async_copy(out_s.at[slot, here], out_ref.at[span], store.at[1, slot]),
        ]

    def place(crop, local):
        hot, span, lo, n, count = one_hot(col_s, crop, images, local)
        size = count // images
        window = lambda ref: jnp.concatenate([ref[i, pl.ds(lo, n), :] for i in range(images)], axis=0)
        taken = tn(hot, jnp.ones((images * n, 128), bf16))[:, 0:1] > 0.5
        get_cot, get_tok, put_ing, put_out = crop_copies(crop, size)
        slot = lax.rem(crop, 2)
        get_tok.wait()
        old = tok_s[slot, 0:size].reshape(count, d).astype(f32)
        new = jnp.where(taken, tn(hot, window(result_s)), old).astype(bf16)
        out_s[slot, 0:size] = new.reshape(size, images, d)
        put_out.start()
        pump(schedule, step, 1)
        get_cot.wait()
        spread = tn(hot, window(high_ref)) + tn(hot, window(low_ref))
        old = cot_s[slot, 0:size].reshape(count, d).astype(f32)
        ing_s[slot, 0:size] = jnp.where(taken, spread, old).reshape(size, images, d)
        put_ing.start()

    @pl.when(step == 0)
    def _():
        columns(0).start()
        for copy in acts:
            copy.start()
        for k in (1, 2, 3):
            columns(k).start()
        for copy in later:
            copy.start()
        vecg_s[...] = jnp.zeros_like(vecg_s)
        if links:
            at.barrier()
        for copy in acts:
            copy.wait()

    for k in range(4):
        @pl.when(step == k)
        def _(k=k):
            columns(k).wait()

    @pl.when(step < 4)
    def _():
        which = jnp.where(turn == 3, 1, 0)
        where = pl.ds(pl.multiple_of(turn * d, 128), d)
        left = dp_s[turn].reshape(total, d)
        gatt_s[where, :] = tn(left, act_s[which].reshape(total, d)).astype(bf16)

    @pl.when(step == 4)
    def _():
        for copy in later:
            copy.wait()

    pump(schedule, step, 0)

    @pl.when((step > 3) & (step < 4 + images))
    def _():
        image = step - 4
        standard, inverse = normalize(kept_s[image].astype(f32))
        ng = rg_ref[image] * vec_ref[2:3]
        for j in range(3):
            ng += nn(dp_s[j, image], watt_s[j * d : (j + 1) * d, :])
        pump(schedule, step, 1)
        grad = resg_s[image] + norm_backward(ng, standard, inverse, vec_ref[0:1])
        high = grad.astype(bf16)
        high_ref[image] = high
        low_ref[image] = (grad - high.astype(f32)).astype(bf16)
        vecg_s[0:1] += colsum(ng * standard)
        vecg_s[1:2] += colsum(ng)

    first_crop = 4 + images

    @pl.when(step == 4)
    def _():
        token_columns(idx_ref, idx_s, col_s)
        for crop in range(2):
            for copy in crop_copies(crop, LG)[:2]:
                copy.start()

    @pl.when((step == first_crop) | (step == first_crop + 1))
    def _():
        place(step - first_crop, False)

    @pl.when(step == first_crop + 1)
    def _():
        for copy in crop_copies(2, 4 * LL)[:2]:
            copy.start()
        for copy in crop_copies(0, LG)[2:]:
            copy.wait()

    @pl.when(step == first_crop + 2)
    def _():
        place(2, True)

    pump(schedule, step, 2)

    @pl.when(step == last)
    def _():
        for copy in crop_copies(1, LG)[2:] + crop_copies(2, 4 * LL)[2:]:
            copy.wait()

    if links:
        @pl.when(step == last)
        def _():
            exchange(2, at.y).wait()
            full_sum = vbuf[3] + vbuf[10]
            vecout_ref[...] = full_sum[: vecout_ref.shape[0]]
            reduce.gathered(0, *reduce.lines(), target=gout_ref)
            for make in lines:
                make().wait_send()
            reduce.sends.finish()


def adamw(grad, first, second, master, average, rate, decay):
    first_new = 0.5 * first + 0.5 * grad
    second_new = 0.5 * second + 0.5 * grad * grad
    update = first_new / (jnp.sqrt(second_new) + 1e-08)
    master_new = master - rate * (update + decay * master)
    average_new = 0.9 * average + 0.1 * master_new
    return (first_new, second_new, master_new, average_new)


GROUPS = ((0.02, 0.05), (0.02, 0.05), (0.2, 0.0))


def final_kernel(*refs):
    groups_in, rest = refs[2:17], refs[19:]
    (ing_in, out_in), (ing_ref, out_ref) = refs[:2], refs[17:19]
    qb_ref, groups_out, rest = rest[0], rest[1:18], rest[18:]
    state_s, load, fresh, store, pass_on = rest[:15], rest[15], rest[16:30], rest[30], rest[31]
    bounce = rest[32:34]
    state = [
        pltpu.make_async_copy(src, dst, load.at[i])
        for i, (src, dst) in enumerate(zip(groups_in, state_s))
    ]
    for c in state:
        c.start()
    stores, passing = [], []
    for k, (a, b) in enumerate(CROPS):
        for j, (src, dst) in enumerate(((ing_in, ing_ref), (out_in, out_ref))):
            through = bounce[j].at[a:b]
            taken = pltpu.make_async_copy(src.at[a:b], through, pass_on.at[0, j, k])
            taken.start()
            given = pltpu.make_async_copy(through, dst.at[a:b], pass_on.at[1, j, k])
            passing.append((taken, given))
    for g in range(3):
        for taken, given in passing[2 * g : 2 * g + 2]:
            taken.wait()
            given.start()
            stores.append(given)
        for c in state[5 * g : 5 * g + 5]:
            c.wait()
        grad, first, second, master, average = [ref[...] for ref in state_s[5 * g : 5 * g + 5]]
        new = adamw(grad, first, second, master, average, *GROUPS[g])
        if g < 2:
            new = new + (new[2].astype(bf16),)
        base = 5 * g
        for i, value in enumerate(new):
            fresh[base + i][...] = value
        pairs = [(fresh[base + i], base + i) for i in range(len(new))] + [(state_s[5 * g], 14 + g)]
        for src, i in pairs:
            stores.append(pltpu.make_async_copy(src, groups_out[i], store.at[i]))
            stores[-1].start()
    qb_ref[...] = state_s[10][3]
    for c in stores:
        c.wait()


def sds(*shape_dtype):
    return jax.ShapeDtypeStruct(shape_dtype[:-1], shape_dtype[-1])


def scratch(*shape_dtype):
    return pltpu.VMEM(shape_dtype[:-1], shape_dtype[-1])


def dma(*shape):
    return pltpu.SemaphoreType.DMA(shape)


def per_device(
    tokens, cotangent, kept_index,
    attention_weights, attention_first, attention_second, attention_average,
    feedforward_weights, feedforward_first, feedforward_second, feedforward_average,
    vector_weights, vector_first, vector_second, vector_average,
):
    images, length, d = tokens.shape
    ndp, nmp = lax.axis_size("dp"), lax.axis_size("mp")
    links = (ndp, nmp) == (8, MP)
    vec = vector_weights
    rows, hb = feedforward_weights.shape[1:]
    hidden = nmp * hb
    mask = masks()
    mask_specs = [full(m.shape) for m in mask]
    tok, cot = tokens.transpose(1, 0, 2), cotangent.transpose(1, 0, 2)
    comm = (lambda i: dict(collective_id=i, has_side_effects=True)) if links else (lambda i: {})

    att, ff = attention_weights.T, feedforward_weights
    if not links:
        att, ff = att.astype(bf16), ff.astype(bf16)
        att = lax.all_gather(att, ("dp", "mp"), axis=0, tiled=True)
        wff = lax.all_gather(lax.all_gather(ff, "dp", axis=1, tiled=True), "mp", axis=0)
    now = lambda *s: pl.BlockSpec((1,) + s, lambda i: (jnp.maximum(i - 1, 0), 0, 0))
    whole = lambda *s: pl.BlockSpec(s, lambda j: (0,) * len(s), pipeline_mode=pl.Buffered(1))
    rowspec = (images, RI, d)
    outs = pl.pallas_call(
        functools.partial(forward_kernel, links),
        grid=(1 + images,),
        in_specs=[ANY, ANY, full(kept_index.shape), full(vec.shape), *mask_specs]
        + ([full(att.shape), full(ff.shape)] if links else [ANY, ANY]),
        out_specs=[ANY] * 4 + [now(RI, d)] * 4 + [ANY] + [ANY] * links,
        out_shape=[sds(*rowspec, bf16)] * 3 + [
            sds(images, RI, 3 * d, bf16), sds(*rowspec, bf16), sds(*rowspec, f32),
            sds(*rowspec, f32), sds(*rowspec, bf16), sds(4 * d, d, bf16),
        ] + [sds(nmp, 2, d, hb, bf16)] * links,
        scratch_shapes=[
            scratch(4 * d, d, bf16), scratch(length, images, d, bf16), scratch(length, images, d, bf16),
            scratch(8, 384, f32), scratch(384, 8, f32), dma(7),
            *[scratch(*rowspec, bf16)] * 3, scratch(images, RI, 3 * d, bf16),
        ] + (
            [scratch(rows, d, bf16), scratch(2, rows, hb, bf16)]
            + [dma(4, Gather.SLOTS), dma(4, Gather.SLOTS), dma(4, 1)] if links else []
        ),
        compiler_params=params(**comm(0)),
        name="forward",
    )(tok, cot, kept_index, vec, *mask, att, ff)
    kept, normed, cotk, proj, mixed, branch, resid, n2, watt = outs[:9]
    if links:
        wff = outs[9]

    outs = pl.pallas_call(
        functools.partial(feed_kernel, links),
        grid=(nmp,),
        in_specs=[
            whole(*rowspec), whole(*rowspec), ANY, ANY, full(vec.shape),
        ],
        out_specs=[ANY, ANY, ANY, full((nmp, hb))]
        + [full((2, 2, rows, hb))] * links,
        out_shape=[
            sds(*rowspec, bf16), sds(*rowspec, f32),
            sds(nmp, 2, d, hb, bf16), sds(nmp, hb, f32),
        ] + [sds(2, 2, rows, hb, bf16)] * links,
        scratch_shapes=[
            scratch(*rowspec, bf16), scratch(*rowspec, f32),
            scratch(*rowspec, f32), scratch(images * RI, hb, bf16), scratch(images * RI, hb, bf16),
            *[scratch(RI, hb, f32)] * 4,
            scratch(nmp, 2, d, hb, bf16), scratch(2, 2, d, hb, bf16), dma(nmp + 1), dma(4),
        ] + (
            [dma(Gather.SLOTS), dma(Gather.SLOTS), dma(4)]
            + [scratch(n, 2, rows, hb, bf16) for n in (8, 8, 2, 2, 2)]
            + [dma(Reduce.SLOTS), dma(Reduce.SLOTS), dma(8)] if links else []
        ),
        compiler_params=params(**comm(3)),
        name="feedforward",
    )(n2, cotk, resid, wff, vec)
    result, n2g, gff, bg = outs[:4]

    spans = (16, 16, 4, 4, 4, 4)
    outs = pl.pallas_call(
        functools.partial(backward_kernel, links),
        grid=(images,),
        in_specs=[
            per_image(RI, d), per_image(RI, d), per_image(RI, d), per_image(RI, d),
            per_image(RI, d), per_image(RI, 3 * d),
            pl.BlockSpec((d, d), lambda i: (3, 0)), full(vec.shape), *mask_specs,
        ] + [ANY, full((2, 2, rows, hb))] * links,
        out_specs=[per_image(RI, 4 * d), per_image(RI, d), per_image(RI, 1), full((8, d))]
        + [full((2, rows, hb))] * links,
        out_shape=[
            sds(images, RI, 4 * d, bf16), sds(*rowspec, f32), sds(images, RI, 1, f32), sds(8, d, f32),
        ] + [sds(2, rows, hb, f32)] * links,
        scratch_shapes=[scratch(RI, d, bf16)] + (
            [scratch(n, 2, rows, hb, bf16) for n in (8, 8, 2, 2, 2, 4)]
            + [dma(Reduce.SLOTS), dma(Reduce.SLOTS), dma(8)] if links else []
        ),
        compiler_params=params(**comm(1)),
        name="attention_backward",
    )(n2g, cotk, branch, resid, normed, proj, watt, vec, *mask, *([gff, outs[4]] if links else []))
    dp, resg, rg, vecg = outs[:4]
    if links:
        feedforward_gradient = outs[4]

    full_d = (4 * d, d)
    outs = pl.pallas_call(
        functools.partial(grads_kernel, links),
        grid=(4 + images + 3,),
        in_specs=[ANY, ANY, ANY, full((images, RI, 1)), ANY, ANY, full(vec.shape), ANY]
        + [full(kept_index.shape), ANY, ANY, ANY]
        + [full((8, d)), full((hidden // d, d))] * links,
        out_specs=[ANY, ANY]
        + ([full((rows, d)), full(vec.shape)] if links else [full(full_d), full((8, d))]),
        out_shape=[sds(length, images, d, f32), sds(length, images, d, bf16)]
        + ([sds(rows, d, f32), sds(*vec.shape, f32)] if links else [sds(*full_d, bf16), sds(8, d, f32)]),
        scratch_shapes=([scratch(*full_d, bf16), scratch(8, d, f32)] if links else []) + [
            scratch(3 * d, d, bf16), scratch(4, *rowspec, bf16), scratch(2, *rowspec, bf16),
            scratch(*rowspec, f32), scratch(*rowspec, bf16), dma(10),
            *[scratch(*rowspec, bf16)] * 3,
            scratch(8, 384, f32), scratch(384, 8, f32),
            scratch(2, LG, images, d, bf16), scratch(2, LG, images, d, bf16),
            scratch(2, LG, images, d, f32), scratch(2, LG, images, d, bf16), dma(2, 2), dma(2, 2),
        ] + (
            [scratch(n, rows, d, bf16) for n in spans[1:]]
            + [dma(Reduce.SLOTS), dma(Reduce.SLOTS), scratch(11, 16, d, f32), dma(8), dma(8)]
            if links else []
        ),
        compiler_params=params(60, **comm(2)),
        name="attention_grads",
    )(
        dp, normed, mixed, rg, resg, kept, vec, watt, kept_index, tok, cot, result,
        *([vecg, bg] if links else []),
    )
    ing, out = outs[:2]
    if links:
        gatt, vector_gradient = outs[2:]
    else:
        gatt, vecg_in = outs[2:]
        local = jnp.concatenate([vecg_in[:2], vecg[:7], bg], axis=0)
        gatt = lax.psum_scatter(gatt, ("dp", "mp"), scatter_dimension=0, tiled=True).astype(f32)
        gff = lax.psum_scatter(gff, "mp", scatter_dimension=0, tiled=False)
        gff = lax.psum_scatter(gff, "dp", scatter_dimension=1, tiled=True)
        feedforward_gradient, vector_gradient = gff.astype(f32), lax.psum(local, ("dp", "mp"))

    state = []
    for grad, *rest in (
        (gatt, attention_first.T, attention_second.T, attention_weights.T, attention_average.T),
        (
            feedforward_gradient, feedforward_first, feedforward_second, feedforward_weights,
            feedforward_average,
        ),
        (vector_gradient, vector_first, vector_second, vector_weights, vector_average),
    ):
        state += [grad, *rest]
    fresh = []
    for g in range(3):
        fresh += [(state[5 * g].shape, f32)] * 4 + [(state[5 * g].shape, bf16)] * (g < 2)
    ing, out, qb, *new = pl.pallas_call(
        final_kernel,
        in_specs=[ANY] * 17,
        out_specs=[ANY, ANY, pl.BlockSpec(memory_space=pltpu.VMEM)] + [ANY] * (len(fresh) + 3),
        out_shape=[sds(length, images, d, f32), sds(length, images, d, bf16), sds(d, f32)]
        + [jax.ShapeDtypeStruct(*f) for f in fresh]
        + [sds(*state[5 * g].shape, f32) for g in range(3)],
        scratch_shapes=[
            *[pltpu.VMEM(v.shape, f32) for v in state], dma(15),
            *[pltpu.VMEM(*f) for f in fresh], dma(len(fresh) + 3), dma(2, 2, 3),
            scratch(length, images, d, f32), scratch(length, images, d, bf16),
        ],
        compiler_params=params(),
        name="finish",
    )(ing, out, *state)
    att_new, ff_new, vec_new = [v.T for v in new[:5]], new[5:10], new[10:14]
    gatt, feedforward_gradient, vector_gradient = new[14:]
    return (
        out.transpose(1, 0, 2), ing.transpose(1, 0, 2),
        gatt.T, *att_new, feedforward_gradient, *ff_new, vector_gradient, *vec_new, qb,
    )


def solution(mesh):
    rows = P(("dp", "mp"), None, None)
    att = P(None, ("dp", "mp"))
    feed = P(None, "dp", "mp")
    in_specs = (rows, rows, P(("dp", "mp"), None)) + (att,) * 4 + (feed,) * 4 + (P(),) * 4
    out_specs = (rows, rows) + (att,) * 6 + (feed,) * 6 + (P(),) * 6
    return jax.shard_map(
        per_device, mesh=mesh, in_specs=in_specs, out_specs=out_specs, check_vma=False
    )
```

```python
import functools

import jax
import jax.numpy as jnp
import numpy as np
from jax import lax
from jax.experimental import pallas as pl
from jax.experimental.pallas import tpu as pltpu
from jax.sharding import PartitionSpec as P

H = 12
HD = 64
LG = 197
LL = 37
KG = LG // 2
KL = LL // 2
LOC = 4 * KL
KEPT = 2 * KG + LOC
RI = -(-KEPT // 16) * 16
SPANS = ((0, KG), (KG, 2 * KG), (2 * KG, KEPT))
UNITS = tuple((a // 16 * 16, -(-b // 16) * 16) for a, b in SPANS)
PAIRS = H // 2
W2L = 2 * HD

bf16 = jnp.bfloat16
f32 = jnp.float32


def params(limit=56, **kw):
    return pltpu.CompilerParams(vmem_limit_bytes=limit << 20, **kw)


def full(shape):
    return pl.BlockSpec(shape, lambda *_: (0,) * len(shape))


def per_image(*shape):
    return pl.BlockSpec((1,) + shape, lambda i, *_: (i,) + (0,) * len(shape))


def nn(a, b):
    return lax.dot_general(a, b, (((1,), (0,)), ((), ())), preferred_element_type=f32)


def nt(a, b):
    return lax.dot_general(a, b, (((1,), (1,)), ((), ())), preferred_element_type=f32)


def tn(a, b):
    return lax.dot_general(a, b, (((0,), (0,)), ((), ())), preferred_element_type=f32)


def normalize(rows):
    center = rows - jnp.mean(rows, axis=-1, keepdims=True)
    spread = jnp.mean(center * center, axis=-1, keepdims=True)
    inverse = lax.rsqrt(spread + 1e-06)
    return center * inverse, inverse


def norm_backward(upstream, standard, inverse, gain):
    scaled = upstream * gain
    return inverse * (
        scaled
        - jnp.mean(scaled, axis=-1, keepdims=True)
        - standard * jnp.mean(scaled * standard, axis=-1, keepdims=True)
    )


def colsum(v):
    return jnp.sum(v, axis=0, keepdims=True)


def masks():
    crop = np.full(RI, -1)
    crop[:KG], crop[KG : 2 * KG] = 0, 1
    for c in range(4):
        crop[2 * KG + c * KL : 2 * KG + (c + 1) * KL] = 2 + c
    adds, valids = [], []
    for (a, b), (lo, hi) in zip(SPANS, UNITS):
        rows = np.arange(lo, hi)
        inside = (rows >= a) & (rows < b)
        same = (crop[lo:hi, None] == crop[None, lo:hi]) & inside[:, None] & inside[None, :]
        adds.append(np.tile(np.where(same, 0.0, -1e9), (1, 2)).astype(np.float32))
        valids.append(np.tile(inside[None, :].astype(np.float32), (8, 2)))
    return [jnp.asarray(m) for m in adds + valids]


def lane_half(shape):
    return lax.broadcasted_iota(jnp.int32, shape, len(shape) - 1) < HD


def split_heads(v, scale):
    first = lane_half(v.shape)
    zero = jnp.zeros_like(v)
    if scale != 1.0:
        v = v * jnp.asarray(scale, v.dtype)
    return jnp.concatenate([jnp.where(first, v, zero), jnp.where(first, zero, v)], axis=0)


def join_heads(v):
    n = v.shape[0] // 2
    return jnp.where(lane_half((n, v.shape[1])), v[:n], v[n:])


def softmax_keys(st, valid):
    p = jnp.exp(st - jnp.max(st, axis=0, keepdims=True))
    return p * (valid / jnp.sum(p, axis=0, keepdims=True))


def store_window(ref, image, lo, hi, last, cols, value, tail):
    value = value.astype(bf16)
    if tail is not None:
        value = jnp.concatenate([value[:16] + tail, value[16:]], axis=0)
    end = hi if last else hi - 16
    ref[image, lo:end, cols] = value[: end - lo]
    return None if last else value[end - lo :]


MESH = pl.DeviceIdType.MESH
ANY = pl.BlockSpec(memory_space=pl.ANY)
MP = 4
CROPS = ((0, LG), (LG, 2 * LG), (2 * LG, 2 * LG + 4 * LL))
ORDER = ((0, 1, 2, 3), (1, 0, 1, 2), (2, 2, 3, 1), (3, 3, 0, 0))


def flip(index, bit):
    return index + bit * (1 - 2 * lax.rem(lax.div(index, bit), 2))


def remote(src, dst, send, recv, to):
    return pltpu.make_async_remote_copy(
        src_ref=src, dst_ref=dst, send_sem=send, recv_sem=recv, device_id=to, device_id_type=MESH
    )


class Sends:
    def __init__(self):
        self.made = []

    def start(self, make, when=None):
        def go():
            make().start()

        go() if when is None else pl.when(when)(go)
        self.made.append((make, when))

    def finish(self):
        for make, when in self.made:
            def wait(make=make):
                make().wait_send()

            wait() if when is None else pl.when(when)(wait)


class Place:
    def __init__(self):
        self.dp = lax.axis_index("dp")
        self.z = lax.axis_index("mp")
        x, y = flip(self.dp, 2), flip(self.dp, 4)
        self.core = (flip(self.dp, 1), self.z)
        self.x, self.y = (x, self.z), (y, self.z)
        self.chips = (self.dp, x, y, flip(x, 4))
        self.mates = tuple(flip(c, 1) for c in self.chips)
        power = (1 + 3 * lax.rem(self.z, 2)) * (1 + 15 * lax.div(self.z, 2))
        self.event = []
        for row in ORDER:
            code = sum(v << (2 * i) for i, v in enumerate(row))
            self.event.append(lax.rem(lax.div(0 * power + code, power), 4))
        self.low, self.high = self.z > 0, self.z < MP - 1
        self.middle = self.low & self.high
        self.line = [lax.rem(self.z + k, MP) for k in range(MP)]
        self.up, self.down = (self.dp, self.z + 1), (self.dp, self.z - 1)
        self.onward = (self.up, self.down, (self.dp, 3 * (self.z - 1)))

    def barrier(self):
        sem = pltpu.get_barrier_semaphore()
        others = [self.core, self.x, self.y]
        others += [(self.dp, k) for k in self.line[1:]]
        for other in others:
            pl.semaphore_signal(sem, inc=1, device_id=other, device_id_type=MESH)
        pl.semaphore_wait(sem, len(others))


def att_block(ref, dp, z, rows):
    return ref.at[pl.ds(pl.multiple_of((dp * MP + z) * rows, 32), rows), :]


def att_part(ref, dp, z, rows, h):
    half = rows // 2
    return ref.at[pl.ds(pl.multiple_of((dp * MP + z) * rows + h * half, 16), half), :]


def ff_part(ref, dp, z, rows, h):
    return ref.at[z, h, pl.ds(pl.multiple_of(dp * rows, 32), rows), :]


def ff_block(ref, dp, z, rows):
    return ref.at[z, :, pl.ds(pl.multiple_of(dp * rows, 32), rows), :]


class Gather:
    ALONG, X, Y, D, C, SLOTS = 0, 4, 8, 12, 16, 32

    def __init__(self, at, first, place, send, recv, local):
        self.at, self.first, self.place = at, first, place
        self.send, self.recv, self.local = send, recv, local
        self.sends = Sends()

    def copy(self, slot, e, r, to):
        slot = self.ALONG + self.at.event[e] if slot is None else slot
        dst = self.place(e, self.at.chips[r])
        src = self.first(e) if r == 0 else dst
        return remote(src, dst, self.send.at[slot], self.recv.at[slot], to)

    def put(self, slot, e, r, to, when=None):
        self.sends.start(lambda: self.copy(slot, e, r, to), when)

    def got(self, slot, e, dp):
        dst = self.place(e, dp)
        remote(dst, dst, self.send.at[slot], self.recv.at[slot], self.at.core).wait_recv()

    def keep(self, e):
        return pltpu.make_async_copy(self.first(e), self.place(e, self.at.dp), self.local.at[e])

    def spread(self, e):
        self.put(self.X + e, e, 0, self.at.x)
        self.put(self.Y + e, e, 0, self.at.y)
        self.put(self.C + 4 * e, e, 0, self.at.core)

    def begin(self):
        at = self.at
        self.keep(0).start()
        for to, when in ((at.up, at.high), (at.down, at.low)):
            self.put(None, 0, 0, to, when)
        self.spread(0)

    def direct(self):
        self.keep(0).start()
        for zb in self.at.line[1:]:
            self.put(None, 0, 0, (self.at.dp, zb))

    def arrived(self, e):
        self.got(self.ALONG + self.at.event[e], e, self.at.dp)

    def along(self, e):
        at = self.at
        self.arrived(e)
        self.put(None, e, 0, at.onward[e - 1], at.middle)
        self.spread(e)

    def plane(self, e):
        at = self.at
        self.got(self.X + e, e, at.chips[1])
        if e % 2 == 0:
            self.put(self.D + e, e, 1, at.y)
        self.put(self.C + 4 * e + 1, e, 1, at.core)
        self.got(self.Y + e, e, at.chips[2])
        if e % 2 == 1:
            self.put(self.D + e, e, 2, at.x)
        self.put(self.C + 4 * e + 2, e, 2, at.core)

    def corner(self, e):
        self.got(self.D + e, e, self.at.chips[3])
        self.put(self.C + 4 * e + 3, e, 3, self.at.core)

    def finish(self, e):
        for r in range(4):
            self.got(self.C + 4 * e + r, e, self.at.mates[r])


def add_into(target, first, *others):
    if len(others) == 1 and target.dtype == bf16:
        @pl.loop(0, first.shape[0] // 48)
        def _(i):
            s = pl.ds(pl.multiple_of(i * 48, 16), 48)
            target[s, :] = first[s, :] + others[0][s, :]

        return
    step = 48

    @pl.loop(0, first.shape[0] // step)
    def _(i):
        s = pl.ds(pl.multiple_of(i * step, 16), step)
        total = first[s, :].astype(f32)
        for ref in others:
            total = total + ref[s, :].astype(f32)
        target[s, :] = total.astype(target.dtype)


class Reduce:
    C, D, X, Y, ALONG, SLOTS = 0, 16, 20, 24, 28, 32

    def __init__(self, at, source, own, parts, bufs, send, recv, load=None, base=0):
        self.at, self.source, self.own, self.parts, self.base = at, source, own, parts, base
        self.c, self.d, self.x, self.y, self.line = bufs
        self.send, self.recv, self.load = send, recv, load
        self.sends = Sends()

    def put(self, slot, src, dst, to):
        self.sends.start(
            lambda: remote(src(), dst(), self.send.at[slot], self.recv.at[slot], to)
        )

    def got(self, slot, dst):
        remote(dst, dst, self.send.at[slot], self.recv.at[slot], self.at.core).wait_recv()

    def slot(self, e, r):
        return 4 * (e - self.base) + r

    def cross(self, e, r):
        i = self.slot(e, r)
        self.put(self.C + i, lambda: self.source(e, self.at.mates[r]), lambda: self.c.at[i], self.at.core)
        if self.load is not None:
            self.load(e, r).start()

    def add(self, e, r, *others, target=None):
        i = self.slot(e, r)
        self.got(self.C + i, self.c.at[i])
        if self.load is not None:
            self.load(e, r).wait()
        refs = [self.own(e, r), self.c.at[i]] + list(others)
        self.total(refs[0] if target is None else target, *refs)

    def total(self, target, *refs):
        for t, *rest in zip(self.parts(target), *[self.parts(ref) for ref in refs]):
            add_into(t, *rest)

    def corner(self, e):
        at, i = self.at, e - self.base
        self.add(e, 3)
        self.put(
            self.D + i, lambda: self.own(e, 3), lambda: self.d.at[i], at.x if e % 2 else at.y
        )
        r, slot, buf, to = (1, self.X, self.x, at.x) if e % 2 else (2, self.Y, self.y, at.y)
        self.add(e, r)
        self.put(slot + i, lambda: self.own(e, r), lambda: buf.at[i], to)

    def plane(self, e):
        at, i = self.at, e - self.base
        r, slot, buf, to = (2, self.Y, self.y, at.y) if e % 2 else (1, self.X, self.x, at.x)
        self.got(self.D + i, self.d.at[i])
        self.add(e, r, self.d.at[i])
        self.put(slot + i, lambda: self.own(e, r), lambda: buf.at[i], to)

    def gathered(self, e, *others, target=None):
        i = e - self.base
        self.got(self.X + i, self.x.at[i])
        self.got(self.Y + i, self.y.at[i])
        self.add(e, 0, self.x.at[i], self.y.at[i], *others, target=target)

    def send_along(self, e, src):
        at = self.at
        zb = at.event[e]
        self.sends.start(
            lambda: remote(
                src(), self.line.at[at.z], self.send.at[self.ALONG + zb],
                self.recv.at[self.ALONG + at.z], (at.dp, zb),
            )
        )

    def along(self, e):
        self.gathered(e)
        self.send_along(e, lambda: self.own(e, 0))

    def lines(self):
        got = []
        for zb in self.at.line[1:]:
            got.append(self.line.at[zb])
            self.got(self.ALONG + zb, got[-1])
        return got


def pump(schedule, step, point):
    for (s, p), action in schedule:
        if isinstance(point, int):
            if p == point:
                pl.when(step == s)(action)
        else:
            pl.when((step == s) & (point == p))(action)


def do(action, *args):
    return lambda: action(*args)


def token_columns(idx_ref, idx_s, col_s):
    idx_s[...] = jnp.full(idx_s.shape, -1.0, f32)
    idx_s[0 : idx_ref.shape[0], 0 : idx_ref.shape[1]] = idx_ref[...].astype(f32)
    col_s[...] = idx_s[...].T


def one_hot(col_s, crop, images, local):
    (a, b), (s, e), (lo, hi) = [v[2 if local else 0] for v in (CROPS, SPANS, UNITS)]
    n, size = hi - lo, b - a
    count = images * size
    if not local:
        a, s, e, lo = LG * crop, KG * crop, KG * (crop + 1), UNITS[1][0] * crop
        lo = pl.multiple_of(lo, 16)
    columns = col_s[pl.ds(lo, n), :]
    row = lax.broadcasted_iota(jnp.int32, (n, 1), 0) + lo
    pieces = []
    for i in range(images):
        place = (columns[:, i : i + 1].astype(jnp.int32) - a) * images + i
        pieces.append(jnp.where((row >= s) & (row < e), place, -1))
    index = jnp.concatenate(pieces, axis=0)
    hot = lax.broadcasted_iota(jnp.int32, (index.shape[0], count), 1) == index
    return hot.astype(f32).astype(bf16), pl.ds(a, size), lo, n, count


def forward_kernel(
    links, tok_ref, cot_ref, idx_ref, vec_ref, m0_ref, m1_ref, m2_ref, v0_ref, v1_ref, v2_ref,
    att_ref, ff_ref,
    kept_out, normed_out, cotk_out, proj_out, mixed_ref, branch_ref, resid_ref, n2_ref,
    watt_out, *rest,
):
    if links:
        wff_ref, *rest = rest
        att_s, ff_s, send, recv, local = rest[10:]
    watt_ref, tok_s, cot_s, idx_s, col_s, load, kept_ref, normed_ref, cotk_ref, proj_ref = rest[:10]
    step = pl.program_id(0)
    images, _, d = kept_ref.shape
    leave = [
        pltpu.make_async_copy(src, dst, load.at[3 + i])
        for i, (src, dst) in enumerate(
            (
                (kept_ref, kept_out), (normed_ref, normed_out), (cotk_ref, cotk_out),
                (proj_ref, proj_out),
            )
        )
    ]
    loads = [
        pltpu.make_async_copy(tok_ref, tok_s, load.at[0]),
        pltpu.make_async_copy(cot_ref, cot_s, load.at[1]),
    ]
    order = (0, 1, 2, 3)

    def clear(dst):
        for i in range(images):
            for _, hi in UNITS[:2]:
                dst[i, hi - 16 : hi] = jnp.zeros((16, d), bf16)

    def pick(crop, local, src, dst):
        hot, span, lo, n, k = one_hot(col_s, crop, images, local)
        got = nn(hot, src[span].reshape(k, d)).astype(bf16)
        for i in range(images):
            part = got[i * n : (i + 1) * n]
            head = pl.ds(lo, 16)
            if local:
                dst[i, head, :] = dst[i, head, :] + part[:16]
            else:
                old = jnp.where(crop == 0, jnp.zeros_like(part[:16]), dst[i, head, :])
                dst[i, head, :] = old + part[:16]
            dst[i, pl.ds(lo + 16, n - 16), :] = part[16:]

    def cot_rows():
        loads[1].wait()
        clear(cotk_ref)

        @pl.loop(0, 2)
        def _(crop):
            pick(crop, False, cot_s, cotk_ref)

        pick(2, True, cot_s, cotk_ref)

    def project(r):
        j = order[r]

        @pl.when(j < 3)
        def _():
            rows_j = pl.ds(pl.multiple_of(j * d, 128), d)
            bias = jnp.where(j == 1, 0.0, jnp.where(j == 0, vec_ref[3:4], vec_ref[4:5]))

            @pl.loop(0, images)
            def _(i):
                part = nt(normed_ref[i], watt_ref[rows_j, :]) + bias
                proj_ref[i, :, rows_j] = part.astype(bf16)

    acts, schedule = [[]] * 5 + [[cot_rows]], []
    if links:
        at = Place()
        rows = att_ref.shape[0]
        half = rows // 2

        def att_half(h):
            return Gather(
                at,
                lambda e: att_part(watt_ref, at.dp, at.event[e], rows, h) if e
                else att_s.at[h * half : (h + 1) * half],
                lambda e, dp: att_part(watt_ref, dp, at.event[e], rows, h),
                send.at[h], recv.at[h], local.at[h],
            )

        def feed_half(h):
            return Gather(
                at, lambda e: ff_part(wff_ref, at.dp, at.event[e], rows, h) if e else ff_s.at[h],
                lambda e, dp: ff_part(wff_ref, dp, at.event[e], rows, h),
                send.at[2 + h], recv.at[2 + h], local.at[2 + h],
            )

        (a0, a1), (f0, f1) = [att_half(h) for h in (0, 1)], [feed_half(h) for h in (0, 1)]
        chip = lax.div(at.dp, 2)
        order = (chip, flip(chip, 1), flip(chip, 2), 3 - chip)

        def ready(r):
            for part in (a0, a1):
                for e in range(4):
                    part.got(part.C + 4 * e + r, e, at.mates[r])
                if r == 0:
                    part.keep(0).wait()

        acts = [
            [a1.begin, a0.begin],
            [do(a1.along, 1), do(a1.plane, 0), do(a0.along, 1), do(a0.along, 2), do(a1.along, 2)],
            [do(a0.along, 3)],
            [do(a1.along, 3), f0.direct, f1.direct, do(a1.plane, 1), do(a0.plane, 2)],
            [do(a0.plane, 0)],
            [
                do(ready, 0), do(project, 0),
                do(a0.plane, 3), do(a0.plane, 1), do(a1.plane, 3), do(a1.plane, 2), cot_rows,
                do(ready, 1), do(project, 1),
                do(a0.corner, 0), do(a1.corner, 1), do(a0.corner, 3), do(a1.corner, 2),
                do(a1.corner, 0),
                do(ready, 2), do(project, 2),
                do(a0.corner, 1), do(a0.corner, 2), do(a1.corner, 3),
                do(f0.arrived, 2), do(f0.spread, 2), do(f0.arrived, 3), do(f0.spread, 3),
                do(ready, 3), do(project, 3),
            ],
        ]
        schedule = [
            ((1, 1), do(f1.arrived, 2)),
            ((1, 1), do(f1.spread, 2)),
            ((1, 1), do(f1.arrived, 3)),
            ((1, 1), do(f1.spread, 3)),
            ((2, 1), do(f0.plane, 2)),
            ((2, 1), do(f0.plane, 3)),
            ((3, 1), do(f1.plane, 2)),
            ((3, 1), do(f1.plane, 3)),
            ((4, 1), do(f0.corner, 2)),
            ((4, 1), do(f0.corner, 3)),
            ((4, 3), do(f1.corner, 2)),
            ((4, 3), do(f1.corner, 3)),
        ]
    else:
        fetch = pltpu.make_async_copy(att_ref, watt_ref, load.at[2])
    store = pltpu.make_async_copy(watt_ref, watt_out, load.at[2])

    def run(point):
        for action in acts[point]:
            action()

    @pl.when(step == 0)
    def _():
        if links:
            att_s[...] = att_ref[...].astype(bf16)
            at.barrier()
            run(0)
        else:
            fetch.start()
        for c in loads:
            c.start()
        if links:
            ff_s[...] = ff_ref[...].astype(bf16)
        token_columns(idx_ref, idx_s, col_s)
        loads[0].wait()
        clear(kept_ref)

        @pl.loop(0, 2)
        def _(crop):
            pick(crop, False, tok_s, kept_ref)
            for point in (1, 2):
                pl.when(crop == point - 1)(do(run, point))

        pick(2, True, tok_s, kept_ref)
        run(3)
        for i in range(images):
            standard, _ = normalize(kept_ref[i].astype(f32))
            normed_ref[i] = (standard * vec_ref[0:1] + vec_ref[1:2]).astype(bf16)
            if i == 1:
                run(4)
        run(5)
        if not links:
            fetch.wait()
            for r in range(3):
                project(r)
        store.start()
        for c in leave:
            c.start()

    pump(schedule, step, 0)

    @pl.when(step > 0)
    def _():
        image = step - 1
        normed = normed_ref[image]
        pump(schedule, step, 1)
        mrefs, vrefs = (m0_ref, m1_ref, m2_ref), (v0_ref, v1_ref, v2_ref)
        for pair in range(PAIRS):
            cols = lambda j: slice(j * d + pair * W2L, j * d + (pair + 1) * W2L)
            tail = None
            for unit, (lo, hi) in enumerate(UNITS):
                qs = split_heads(proj_ref[image, lo:hi, cols(0)], HD ** -0.5)
                st = nt(proj_ref[image, lo:hi, cols(1)], qs) + mrefs[unit][...]
                pt = softmax_keys(st, vrefs[unit][0:1]).astype(bf16)
                out = join_heads(tn(pt, proj_ref[image, lo:hi, cols(2)]))
                tail = store_window(mixed_ref, 0, lo, hi, unit == 2, cols(0), out, tail)
            if pair == 2:
                pump(schedule, step, 3)
        branch = nt(mixed_ref[0], watt_ref[3 * d :, :]) + vec_ref[5:6]
        branch_ref[0] = branch
        residual = kept_ref[image].astype(f32) + router_score(normed, vec_ref) * branch
        resid_ref[0] = residual
        standard, _ = normalize(residual)
        n2_ref[0] = (standard * vec_ref[6:7] + vec_ref[7:8]).astype(bf16)

    @pl.when(step == images)
    def _():
        if links:
            for feed in (f0, f1):
                feed.finish(2)
                feed.finish(3)
                feed.arrived(1)
                feed.keep(0).wait()
            for part in (a0, a1, f0, f1):
                part.sends.finish()
        for c in [store] + leave:
            c.wait()


def router_score(normed, vec_ref):
    logit = jnp.sum(normed.astype(f32) * vec_ref[2:3], axis=-1, keepdims=True)
    return jax.nn.sigmoid(logit)


def feed_kernel(
    links, n2_ref, cot_ref, resid_ref, w_ref, vec_ref,
    result_out, n2g_out, gff_ref, bg_ref, *rest,
):
    if links:
        acc_ref, *rest = rest
        send, recv, local, a, c, dd, x, y, rsend, rrecv, rlocal = rest[13:]
    result_ref, n2g_ref, out_s, act_s, ig_s, i0, i1, a0, a1, w_s, g_s, load, store = rest[:13]
    inner_s, ag_s = (i0, i1), (a0, a1)
    step = pl.program_id(0)
    last = pl.num_programs(0) - 1
    images, _, d = n2_ref.shape
    nload = w_s.shape[0]
    hb = w_ref.shape[3]
    block, schedule = step, []
    if links:
        at = Place()
        rows = acc_ref.shape[2]
        block = at.event[0]
        for e in (1, 2, 3):
            block = jnp.where(step == 3 - e, at.event[e], block)
        gather = Gather(
            at, lambda e: ff_block(w_ref, at.dp, at.event[e], rows),
            lambda e, dp: w_s.at[3 - e, :, pl.ds(pl.multiple_of(dp * rows, 32), rows), :],
            send, recv, local,
        )
        reduce = Reduce(
            at, lambda e, dp: ff_block(gff_ref, dp, at.event[e], rows),
            lambda e, r: a.at[4 * (e - 2) + r],
            lambda ref: (ref.at[0], ref.at[1]), (c, dd, x, y, None), rsend, rrecv,
            lambda e, r: pltpu.make_async_copy(
                ff_block(gff_ref, at.chips[r], at.event[e], rows), a.at[4 * (e - 2) + r],
                rlocal.at[4 * (e - 2) + r],
            ),
            2,
        )

        def start():
            at.barrier()
            for e in (1, 0):
                gather.spread(e)
                gather.keep(e).start()

        def ready(e):
            gather.finish(e)
            gather.keep(e).wait()

        def cross(e):
            for r in (3, 1, 2, 0):
                reduce.cross(e, r)

        schedule = [
            ((1, 0), do(gather.plane, 1)),
            ((1, 0), do(gather.plane, 0)),
            ((1, 0), do(cross, 3)),
            ((2, 0), do(gather.corner, 1)),
            ((2, 0), do(reduce.corner, 3)),
            ((2, 0), do(cross, 2)),
            ((2, 0), do(ready, 1)),
            ((2, 0), do(reduce.corner, 2)),
            ((2, 0), do(gather.corner, 0)),
            ((3, 0), do(reduce.plane, 3)),
            ((3, 0), do(ready, 0)),
            ((3, 0), do(reduce.plane, 2)),
        ]

    def fetch(e):
        return pltpu.make_async_copy(
            w_ref.at[at.event[3 - e] if links else e], w_s.at[e], load.at[e]
        )

    def save(slot, which):
        return pltpu.make_async_copy(g_s.at[slot], gff_ref.at[which], store.at[slot])

    residual = pltpu.make_async_copy(resid_ref, out_s, load.at[nload])
    early = (0, 1) if links else range(w_s.shape[0])

    @pl.when(step == 0)
    def _():
        for e in early:
            fetch(e).start()
        if links:
            start()
        residual.start()
        n2g_ref[...] = jnp.zeros_like(n2g_ref)
        bg_ref[...] = jnp.zeros_like(bg_ref)
        fetch(0).wait()
        residual.wait()

    for e in early[1:]:
        @pl.when(step == e)
        def _(e=e):
            fetch(e).wait()

    slot = lax.rem(step, 2)

    @pl.when(step > 0)
    def _():
        save(1 - slot, 0).wait()

    pump(schedule, step, 0)

    def first(i):
        inner_s[i % 2][...] = nn(n2_ref[i], w_s[step, 0]) + vec_ref[pl.ds(9 + block, 1), :]
        ag_s[i % 2][...] = nn(cot_ref[i], w_s[step, 1])

    def second(i):
        inner = inner_s[i % 2][...]
        phi = 0.5 * (1.0 + lax.erf(inner * 0.7071067811865476))
        act = (inner * phi).astype(bf16)
        slope = phi + inner * jnp.exp(-0.5 * inner * inner) * 0.3989422804014327
        ig = (ag_s[i % 2][...] * slope).astype(bf16)
        rows_i = slice(i * RI, (i + 1) * RI)
        act_s[rows_i, :] = act
        ig_s[rows_i, :] = ig
        bg_ref[pl.ds(block, 1), :] += colsum(ig.astype(f32))
        out_s[i] += nt(act, w_s[step, 1])
        n2g_ref[i] += nt(ig, w_s[step, 0])

    first(0)
    for i in range(images):
        pump(schedule, step, i + 1)
        if i + 1 < images:
            first(i + 1)
        second(i)

    leave = [
        pltpu.make_async_copy(n2g_ref, n2g_out, store.at[2]),
        pltpu.make_async_copy(result_ref, result_out, store.at[3]),
    ]

    @pl.when(step == last)
    def _():
        leave[0].start()
        result_ref[...] = (out_s[...] + vec_ref[8:9]).astype(bf16)
        leave[1].start()

    n2 = n2_ref[...].reshape(images * RI, d)
    cot = cot_ref[...].reshape(images * RI, d)
    g_s[slot, 0] = tn(n2, ig_s[...]).astype(bf16)
    g_s[slot, 1] = tn(cot, act_s[...]).astype(bf16)
    save(slot, block).start()

    @pl.when(step == last)
    def _():
        for c in leave:
            c.wait()
        if links:
            reduce.gathered(3, target=acc_ref.at[0])
            reduce.gathered(2, target=acc_ref.at[1])
            gather.sends.finish()
            reduce.sends.finish()
        save(slot, 0).wait()


def backward_kernel(
    links, n2g_ref, cotk_ref, branch_ref, resid_ref, normed_ref, proj_ref, wout_ref,
    vec_ref, m0_ref, m1_ref, m2_ref, v0_ref, v1_ref, v2_ref, *rest,
):
    if links:
        gff_ref, acc_ref, dp_ref, resg_ref, rg_ref, vecg_ref, gout_ref = rest[:7]
        mg_s, a, c, dd, x, y, line, send, recv, local = rest[7:]
    else:
        dp_ref, resg_ref, rg_ref, vecg_ref, mg_s = rest
    step = pl.program_id(0)
    schedule = []
    if links:
        at = Place()
        rows = gout_ref.shape[1]
        reduce = Reduce(
            at, lambda e, dp: ff_block(gff_ref, dp, at.event[e], rows),
            lambda e, r: a.at[4 * e + r],
            lambda ref: (ref.at[0], ref.at[1]), (c, dd, x, y, line), send, recv,
            lambda e, r: pltpu.make_async_copy(
                ff_block(gff_ref, at.chips[r], at.event[e], rows), a.at[4 * e + r],
                local.at[4 * e + r],
            ),
        )

        def start():
            at.barrier()
            reduce.send_along(2, lambda: acc_ref.at[1])
            for e in (1, 0):
                for r in (3, 1, 2, 0):
                    reduce.cross(e, r)

        schedule = [
            ((0, 0), start),
            ((0, 1), do(reduce.corner, 1)),
            ((0, 1), do(reduce.send_along, 3, lambda: acc_ref.at[0])),
            ((1, 1), do(reduce.plane, 1)),
            ((2, 0), do(reduce.corner, 0)),
            ((2, 1), do(reduce.along, 1)),
            ((3, 0), do(reduce.plane, 0)),
        ]

    pump(schedule, step, 0)
    d = normed_ref.shape[2]
    normed = normed_ref[0]
    score = router_score(normed, vec_ref)
    branch = branch_ref[0]
    standard, inverse = normalize(resid_ref[0])
    n2g = n2g_ref[0]
    cot = cotk_ref[0].astype(f32)
    resg = cot + norm_backward(n2g, standard, inverse, vec_ref[6:7])
    resg_ref[0] = resg
    bg = (score * resg).astype(bf16)
    rg = jnp.sum(resg * branch, axis=-1, keepdims=True) * score * (1.0 - score)
    rg_ref[0] = rg
    dp_ref[0, :, 3 * d :] = bg
    mg_s[...] = nn(bg, wout_ref[...]).astype(bf16)
    pump(schedule, step, 1)
    mrefs, vrefs = (m0_ref, m1_ref, m2_ref), (v0_ref, v1_ref, v2_ref)
    for pair in range(PAIRS):
        cols = lambda j: slice(j * d + pair * W2L, j * d + (pair + 1) * W2L)
        tails = [None] * 3
        for unit, (lo, hi) in enumerate(UNITS):
            qs = split_heads(proj_ref[0, lo:hi, cols(0)], HD ** -0.5)
            kk = proj_ref[0, lo:hi, cols(1)]
            pt = softmax_keys(nt(kk, qs) + mrefs[unit][...], vrefs[unit][0:1])
            ds = split_heads(mg_s[lo:hi, cols(0)], 1.0)
            gpt = nt(proj_ref[0, lo:hi, cols(2)], ds)
            sg = (pt * (gpt - jnp.sum(pt * gpt, axis=0, keepdims=True))).astype(bf16)
            grads = (
                join_heads(tn(sg, kk)) * HD ** -0.5, nn(sg, qs), nn(pt.astype(bf16), ds)
            )
            for j in range(3):
                tails[j] = store_window(dp_ref, 0, lo, hi, unit == 2, cols(j), grads[j], tails[j])
        if pair == 2:
            pump(schedule, step, 3)
    sums = jnp.concatenate(
        [
            colsum(rg * normed.astype(f32)),
            colsum(dp_ref[0, :, :d].astype(f32)),
            colsum(dp_ref[0, :, 2 * d : 3 * d].astype(f32)),
            colsum(bg.astype(f32)),
            colsum(n2g * standard),
            colsum(n2g),
            colsum(cot),
            jnp.zeros((1, d), f32),
        ],
        axis=0,
    )

    @pl.when(step == 0)
    def _():
        vecg_ref[...] = jnp.zeros_like(vecg_ref)

    vecg_ref[...] += sums
    if links:
        @pl.when(step == pl.num_programs(0) - 1)
        def _():
            reduce.gathered(0, *reduce.lines(), target=gout_ref)
            reduce.sends.finish()


def grads_kernel(
    links, dp_ref, normed_ref, mixed_ref, rg_ref, resg_ref, kept_ref, vec_ref, watt_ref,
    idx_ref, tok_ref, cot_ref, result_ref, *rest,
):
    if links:
        vecb_ref, bias_ref, ing_ref, out_ref, gout_ref, vecout_ref = rest[:6]
        gatt_s, vecg_s, *rest = rest[6:]
        c, dd, x, y, line, send, recv, vbuf, vsend, vrecv = rest[17:]
    else:
        ing_ref, out_ref, gatt_s, vecg_s, *rest = rest
    watt_s, dp_s, act_s, resg_s, kept_s, load, high_ref, low_ref, result_s = rest[:9]
    idx_s, col_s, tok_s, cot_s, ing_s, out_s, fetch, store = rest[9:17]
    step = pl.program_id(0)
    images, _, d = high_ref.shape
    last = 3 + images + 3
    total = images * RI
    chip, schedule = 0, []
    if links:
        at = Place()
        chip = lax.div(at.dp, 2)
        rows = gout_ref.shape[0]
        block = lambda e, dp: att_block(gatt_s, dp, at.event[e], rows)
        reduce = Reduce(
            at, block, lambda e, r: block(e, at.chips[r]), lambda ref: (ref,),
            (c, dd, x, y, line), send, recv,
        )

        def cross(r):
            for e in (3, 2, 1, 0):
                reduce.cross(e, r)

        exchange = lambda k, to: remote(
            vbuf.at[k + 1], vbuf.at[8 + k], vsend.at[k], vrecv.at[k], to
        )
        lines = [
            lambda k=k: remote(
                vbuf.at[0], vbuf.at[4 + at.z], vsend.at[2 + k], vrecv.at[3 + at.z],
                (at.dp, at.line[k]),
            )
            for k in range(1, MP)
        ]

        def spread_vectors():
            vbuf[0, 0:2] = vecg_s[0:2]
            vbuf[0, 2:9] = vecb_ref[0:7]
            vbuf[0, 9:13] = bias_ref[...]
            vbuf[0, 13:16] = jnp.zeros((3, d), f32)
            for make in lines:
                make().start()
            vbuf[4 + at.z] = vbuf[0]

        def line_vectors():
            for k in range(1, MP):
                zb = at.line[k]
                remote(
                    vbuf.at[0], vbuf.at[4 + zb], vsend.at[2 + k], vrecv.at[3 + zb], at.core
                ).wait_recv()
            vbuf[1] = vbuf[4] + vbuf[5] + vbuf[6] + vbuf[7]
            exchange(0, at.core).start()

        def core_vectors():
            exchange(0, at.core).wait()
            vbuf[2] = vbuf[1] + vbuf[8]
            exchange(1, at.x).start()

        def x_vectors():
            exchange(1, at.x).wait()
            vbuf[3] = vbuf[2] + vbuf[9]
            exchange(2, at.y).start()

        turns = (3 - chip, flip(chip, 1), flip(chip, 2), chip)
        schedule = [
            ((1, 2), do(cross, 3)),
            ((1, 2), do(cross, 1)),
            ((2, 2), do(reduce.corner, 3)),
            ((2, 2), do(cross, 2)),
            ((3, 2), do(cross, 0)),
            ((4, 1), do(reduce.plane, 3)),
            ((5, 0), do(reduce.corner, 2)),
            ((6, 0), do(reduce.corner, 1)),
            ((6, 0), do(reduce.along, 3)),
            ((7, 0), do(reduce.plane, 2)),
            ((8, 0), spread_vectors),
            ((8, 0), do(reduce.plane, 1)),
            ((8, 0), do(reduce.corner, 0)),
            ((8, 1), do(reduce.along, 2)),
            ((8, 2), line_vectors),
            ((9, 1), core_vectors),
            ((9, 1), do(reduce.along, 1)),
            ((9, 1), do(reduce.plane, 0)),
            ((9, 2), x_vectors),
        ]
    else:
        turns = (0, 1, 2, 3)
    turn = turns[3]
    for k in (2, 1, 0):
        turn = jnp.where(step == k, turns[k], turn)

    def columns(k):
        lanes = pl.ds(pl.multiple_of(turns[k] * d, 128), d) if links else pl.ds(k * d, d)
        return pltpu.make_async_copy(dp_ref.at[:, :, lanes], dp_s.at[turns[k]], load.at[k])

    acts = [
        pltpu.make_async_copy(normed_ref, act_s.at[0], load.at[4]),
        pltpu.make_async_copy(mixed_ref, act_s.at[1], load.at[5]),
    ]
    later = [
        pltpu.make_async_copy(watt_ref.at[: 3 * d], watt_s, load.at[6]),
        pltpu.make_async_copy(resg_ref, resg_s, load.at[7]),
        pltpu.make_async_copy(kept_ref, kept_s, load.at[8]),
        pltpu.make_async_copy(result_ref, result_s, load.at[9]),
    ]

    def crop_copies(crop, size):
        span = pl.ds(LG * crop, size)
        slot = lax.rem(crop, 2)
        here = pl.ds(0, size)
        return [
            pltpu.make_async_copy(cot_ref.at[span], cot_s.at[slot, here], fetch.at[0, slot]),
            pltpu.make_async_copy(tok_ref.at[span], tok_s.at[slot, here], fetch.at[1, slot]),
            pltpu.make_async_copy(ing_s.at[slot, here], ing_ref.at[span], store.at[0, slot]),
            pltpu.make_async_copy(out_s.at[slot, here], out_ref.at[span], store.at[1, slot]),
        ]

    def place(crop, local):
        hot, span, lo, n, count = one_hot(col_s, crop, images, local)
        size = count // images
        window = lambda ref: jnp.concatenate([ref[i, pl.ds(lo, n), :] for i in range(images)], axis=0)
        taken = tn(hot, jnp.ones((images * n, 128), bf16))[:, 0:1] > 0.5
        get_cot, get_tok, put_ing, put_out = crop_copies(crop, size)
        slot = lax.rem(crop, 2)
        get_tok.wait()
        old = tok_s[slot, 0:size].reshape(count, d).astype(f32)
        new = jnp.where(taken, tn(hot, window(result_s)), old).astype(bf16)
        out_s[slot, 0:size] = new.reshape(size, images, d)
        put_out.start()
        pump(schedule, step, 1)
        get_cot.wait()
        spread = tn(hot, window(high_ref)) + tn(hot, window(low_ref))
        old = cot_s[slot, 0:size].reshape(count, d).astype(f32)
        ing_s[slot, 0:size] = jnp.where(taken, spread, old).reshape(size, images, d)
        put_ing.start()

    @pl.when(step == 0)
    def _():
        columns(0).start()
        for copy in acts:
            copy.start()
        for k in (1, 2, 3):
            columns(k).start()
        for copy in later:
            copy.start()
        vecg_s[...] = jnp.zeros_like(vecg_s)
        if links:
            at.barrier()
        for copy in acts:
            copy.wait()

    for k in range(4):
        @pl.when(step == k)
        def _(k=k):
            columns(k).wait()

    @pl.when(step < 4)
    def _():
        which = jnp.where(turn == 3, 1, 0)
        where = pl.ds(pl.multiple_of(turn * d, 128), d)
        left = dp_s[turn].reshape(total, d)
        gatt_s[where, :] = tn(left, act_s[which].reshape(total, d)).astype(bf16)

    @pl.when(step == 4)
    def _():
        for copy in later:
            copy.wait()

    pump(schedule, step, 0)

    @pl.when((step > 3) & (step < 4 + images))
    def _():
        image = step - 4
        standard, inverse = normalize(kept_s[image].astype(f32))
        ng = rg_ref[image] * vec_ref[2:3]
        for j in range(3):
            ng += nn(dp_s[j, image], watt_s[j * d : (j + 1) * d, :])
        pump(schedule, step, 1)
        grad = resg_s[image] + norm_backward(ng, standard, inverse, vec_ref[0:1])
        high = grad.astype(bf16)
        high_ref[image] = high
        low_ref[image] = (grad - high.astype(f32)).astype(bf16)
        vecg_s[0:1] += colsum(ng * standard)
        vecg_s[1:2] += colsum(ng)

    first_crop = 4 + images

    @pl.when(step == 4)
    def _():
        token_columns(idx_ref, idx_s, col_s)
        for crop in range(2):
            for copy in crop_copies(crop, LG)[:2]:
                copy.start()

    @pl.when((step == first_crop) | (step == first_crop + 1))
    def _():
        place(step - first_crop, False)

    @pl.when(step == first_crop + 1)
    def _():
        for copy in crop_copies(2, 4 * LL)[:2]:
            copy.start()
        for copy in crop_copies(0, LG)[2:]:
            copy.wait()

    @pl.when(step == first_crop + 2)
    def _():
        place(2, True)

    pump(schedule, step, 2)

    @pl.when(step == last)
    def _():
        for copy in crop_copies(1, LG)[2:] + crop_copies(2, 4 * LL)[2:]:
            copy.wait()

    if links:
        @pl.when(step == last)
        def _():
            exchange(2, at.y).wait()
            full_sum = vbuf[3] + vbuf[10]
            vecout_ref[...] = full_sum[: vecout_ref.shape[0]]
            reduce.gathered(0, *reduce.lines(), target=gout_ref)
            for make in lines:
                make().wait_send()
            reduce.sends.finish()


def adamw(grad, first, second, master, average, rate, decay):
    first_new = 0.5 * first + 0.5 * grad
    second_new = 0.5 * second + 0.5 * grad * grad
    update = first_new / (jnp.sqrt(second_new) + 1e-08)
    master_new = master - rate * (update + decay * master)
    average_new = 0.9 * average + 0.1 * master_new
    return (first_new, second_new, master_new, average_new)


GROUPS = ((0.02, 0.05), (0.02, 0.05), (0.2, 0.0))


def final_kernel(*refs):
    groups_in, rest = refs[2:17], refs[19:]
    (ing_in, out_in), (ing_ref, out_ref) = refs[:2], refs[17:19]
    qb_ref, groups_out, rest = rest[0], rest[1:18], rest[18:]
    state_s, load, fresh, store, pass_on = rest[:15], rest[15], rest[16:30], rest[30], rest[31]
    bounce = rest[32:34]
    state = [
        pltpu.make_async_copy(src, dst, load.at[i])
        for i, (src, dst) in enumerate(zip(groups_in, state_s))
    ]
    for c in state:
        c.start()
    stores, passing = [], []
    for k, (a, b) in enumerate(CROPS):
        for j, (src, dst) in enumerate(((ing_in, ing_ref), (out_in, out_ref))):
            through = bounce[j].at[a:b]
            taken = pltpu.make_async_copy(src.at[a:b], through, pass_on.at[0, j, k])
            taken.start()
            given = pltpu.make_async_copy(through, dst.at[a:b], pass_on.at[1, j, k])
            passing.append((taken, given))
    for g in range(3):
        for taken, given in passing[2 * g : 2 * g + 2]:
            taken.wait()
            given.start()
            stores.append(given)
        for c in state[5 * g : 5 * g + 5]:
            c.wait()
        grad, first, second, master, average = [ref[...] for ref in state_s[5 * g : 5 * g + 5]]
        new = adamw(grad, first, second, master, average, *GROUPS[g])
        if g < 2:
            new = new + (new[2].astype(bf16),)
        base = 5 * g
        for i, value in enumerate(new):
            fresh[base + i][...] = value
        pairs = [(fresh[base + i], base + i) for i in range(len(new))] + [(state_s[5 * g], 14 + g)]
        for src, i in pairs:
            stores.append(pltpu.make_async_copy(src, groups_out[i], store.at[i]))
            stores[-1].start()
    qb_ref[...] = state_s[10][3]
    for c in stores:
        c.wait()


def sds(*shape_dtype):
    return jax.ShapeDtypeStruct(shape_dtype[:-1], shape_dtype[-1])


def scratch(*shape_dtype):
    return pltpu.VMEM(shape_dtype[:-1], shape_dtype[-1])


def dma(*shape):
    return pltpu.SemaphoreType.DMA(shape)


def per_device(
    tokens, cotangent, kept_index,
    attention_weights, attention_first, attention_second, attention_average,
    feedforward_weights, feedforward_first, feedforward_second, feedforward_average,
    vector_weights, vector_first, vector_second, vector_average,
):
    images, length, d = tokens.shape
    ndp, nmp = lax.axis_size("dp"), lax.axis_size("mp")
    links = (ndp, nmp) == (8, MP)
    vec = vector_weights
    rows, hb = feedforward_weights.shape[1:]
    hidden = nmp * hb
    mask = masks()
    mask_specs = [full(m.shape) for m in mask]
    tok, cot = tokens.transpose(1, 0, 2), cotangent.transpose(1, 0, 2)
    comm = (lambda i: dict(collective_id=i, has_side_effects=True)) if links else (lambda i: {})

    att, ff = attention_weights.T, feedforward_weights
    if not links:
        att, ff = att.astype(bf16), ff.astype(bf16)
        att = lax.all_gather(att, ("dp", "mp"), axis=0, tiled=True)
        wff = lax.all_gather(lax.all_gather(ff, "dp", axis=1, tiled=True), "mp", axis=0)
    now = lambda *s: pl.BlockSpec((1,) + s, lambda i: (jnp.maximum(i - 1, 0), 0, 0))
    whole = lambda *s: pl.BlockSpec(s, lambda j: (0,) * len(s), pipeline_mode=pl.Buffered(1))
    rowspec = (images, RI, d)
    outs = pl.pallas_call(
        functools.partial(forward_kernel, links),
        grid=(1 + images,),
        in_specs=[ANY, ANY, full(kept_index.shape), full(vec.shape), *mask_specs]
        + ([full(att.shape), full(ff.shape)] if links else [ANY, ANY]),
        out_specs=[ANY] * 4 + [now(RI, d)] * 4 + [ANY] + [ANY] * links,
        out_shape=[sds(*rowspec, bf16)] * 3 + [
            sds(images, RI, 3 * d, bf16), sds(*rowspec, bf16), sds(*rowspec, f32),
            sds(*rowspec, f32), sds(*rowspec, bf16), sds(4 * d, d, bf16),
        ] + [sds(nmp, 2, d, hb, bf16)] * links,
        scratch_shapes=[
            scratch(4 * d, d, bf16), scratch(length, images, d, bf16), scratch(length, images, d, bf16),
            scratch(8, 384, f32), scratch(384, 8, f32), dma(7),
            *[scratch(*rowspec, bf16)] * 3, scratch(images, RI, 3 * d, bf16),
        ] + (
            [scratch(rows, d, bf16), scratch(2, rows, hb, bf16)]
            + [dma(4, Gather.SLOTS), dma(4, Gather.SLOTS), dma(4, 1)] if links else []
        ),
        compiler_params=params(**comm(0)),
        name="forward",
    )(tok, cot, kept_index, vec, *mask, att, ff)
    kept, normed, cotk, proj, mixed, branch, resid, n2, watt = outs[:9]
    if links:
        wff = outs[9]

    outs = pl.pallas_call(
        functools.partial(feed_kernel, links),
        grid=(nmp,),
        in_specs=[
            whole(*rowspec), whole(*rowspec), ANY, ANY, full(vec.shape),
        ],
        out_specs=[ANY, ANY, ANY, full((nmp, hb))]
        + [full((2, 2, rows, hb))] * links,
        out_shape=[
            sds(*rowspec, bf16), sds(*rowspec, f32),
            sds(nmp, 2, d, hb, bf16), sds(nmp, hb, f32),
        ] + [sds(2, 2, rows, hb, bf16)] * links,
        scratch_shapes=[
            scratch(*rowspec, bf16), scratch(*rowspec, f32),
            scratch(*rowspec, f32), scratch(images * RI, hb, bf16), scratch(images * RI, hb, bf16),
            *[scratch(RI, hb, f32)] * 4,
            scratch(nmp, 2, d, hb, bf16), scratch(2, 2, d, hb, bf16), dma(nmp + 1), dma(4),
        ] + (
            [dma(Gather.SLOTS), dma(Gather.SLOTS), dma(4)]
            + [scratch(n, 2, rows, hb, bf16) for n in (8, 8, 2, 2, 2)]
            + [dma(Reduce.SLOTS), dma(Reduce.SLOTS), dma(8)] if links else []
        ),
        compiler_params=params(**comm(3)),
        name="feedforward",
    )(n2, cotk, resid, wff, vec)
    result, n2g, gff, bg = outs[:4]

    spans = (16, 16, 4, 4, 4, 4)
    outs = pl.pallas_call(
        functools.partial(backward_kernel, links),
        grid=(images,),
        in_specs=[
            per_image(RI, d), per_image(RI, d), per_image(RI, d), per_image(RI, d),
            per_image(RI, d), per_image(RI, 3 * d),
            pl.BlockSpec((d, d), lambda i: (3, 0)), full(vec.shape), *mask_specs,
        ] + [ANY, full((2, 2, rows, hb))] * links,
        out_specs=[per_image(RI, 4 * d), per_image(RI, d), per_image(RI, 1), full((8, d))]
        + [full((2, rows, hb))] * links,
        out_shape=[
            sds(images, RI, 4 * d, bf16), sds(*rowspec, f32), sds(images, RI, 1, f32), sds(8, d, f32),
        ] + [sds(2, rows, hb, f32)] * links,
        scratch_shapes=[scratch(RI, d, bf16)] + (
            [scratch(n, 2, rows, hb, bf16) for n in (8, 8, 2, 2, 2, 4)]
            + [dma(Reduce.SLOTS), dma(Reduce.SLOTS), dma(8)] if links else []
        ),
        compiler_params=params(**comm(1)),
        name="attention_backward",
    )(n2g, cotk, branch, resid, normed, proj, watt, vec, *mask, *([gff, outs[4]] if links else []))
    dp, resg, rg, vecg = outs[:4]
    if links:
        feedforward_gradient = outs[4]

    full_d = (4 * d, d)
    outs = pl.pallas_call(
        functools.partial(grads_kernel, links),
        grid=(4 + images + 3,),
        in_specs=[ANY, ANY, ANY, full((images, RI, 1)), ANY, ANY, full(vec.shape), ANY]
        + [full(kept_index.shape), ANY, ANY, ANY]
        + [full((8, d)), full((hidden // d, d))] * links,
        out_specs=[ANY, ANY]
        + ([full((rows, d)), full(vec.shape)] if links else [full(full_d), full((8, d))]),
        out_shape=[sds(length, images, d, f32), sds(length, images, d, bf16)]
        + ([sds(rows, d, f32), sds(*vec.shape, f32)] if links else [sds(*full_d, bf16), sds(8, d, f32)]),
        scratch_shapes=([scratch(*full_d, bf16), scratch(8, d, f32)] if links else []) + [
            scratch(3 * d, d, bf16), scratch(4, *rowspec, bf16), scratch(2, *rowspec, bf16),
            scratch(*rowspec, f32), scratch(*rowspec, bf16), dma(10),
            *[scratch(*rowspec, bf16)] * 3,
            scratch(8, 384, f32), scratch(384, 8, f32),
            scratch(2, LG, images, d, bf16), scratch(2, LG, images, d, bf16),
            scratch(2, LG, images, d, f32), scratch(2, LG, images, d, bf16), dma(2, 2), dma(2, 2),
        ] + (
            [scratch(n, rows, d, bf16) for n in spans[1:]]
            + [dma(Reduce.SLOTS), dma(Reduce.SLOTS), scratch(11, 16, d, f32), dma(8), dma(8)]
            if links else []
        ),
        compiler_params=params(60, **comm(2)),
        name="attention_grads",
    )(
        dp, normed, mixed, rg, resg, kept, vec, watt, kept_index, tok, cot, result,
        *([vecg, bg] if links else []),
    )
    ing, out = outs[:2]
    if links:
        gatt, vector_gradient = outs[2:]
    else:
        gatt, vecg_in = outs[2:]
        local = jnp.concatenate([vecg_in[:2], vecg[:7], bg], axis=0)
        gatt = lax.psum_scatter(gatt, ("dp", "mp"), scatter_dimension=0, tiled=True).astype(f32)
        gff = lax.psum_scatter(gff, "mp", scatter_dimension=0, tiled=False)
        gff = lax.psum_scatter(gff, "dp", scatter_dimension=1, tiled=True)
        feedforward_gradient, vector_gradient = gff.astype(f32), lax.psum(local, ("dp", "mp"))

    state = []
    for grad, *rest in (
        (gatt, attention_first.T, attention_second.T, attention_weights.T, attention_average.T),
        (
            feedforward_gradient, feedforward_first, feedforward_second, feedforward_weights,
            feedforward_average,
        ),
        (vector_gradient, vector_first, vector_second, vector_weights, vector_average),
    ):
        state += [grad, *rest]
    fresh = []
    for g in range(3):
        fresh += [(state[5 * g].shape, f32)] * 4 + [(state[5 * g].shape, bf16)] * (g < 2)
    ing, out, qb, *new = pl.pallas_call(
        final_kernel,
        in_specs=[ANY] * 17,
        out_specs=[ANY, ANY, pl.BlockSpec(memory_space=pltpu.VMEM)] + [ANY] * (len(fresh) + 3),
        out_shape=[sds(length, images, d, f32), sds(length, images, d, bf16), sds(d, f32)]
        + [jax.ShapeDtypeStruct(*f) for f in fresh]
        + [sds(*state[5 * g].shape, f32) for g in range(3)],
        scratch_shapes=[
            *[pltpu.VMEM(v.shape, f32) for v in state], dma(15),
            *[pltpu.VMEM(*f) for f in fresh], dma(len(fresh) + 3), dma(2, 2, 3),
            scratch(length, images, d, f32), scratch(length, images, d, bf16),
        ],
        compiler_params=params(),
        name="finish",
    )(ing, out, *state)
    att_new, ff_new, vec_new = [v.T for v in new[:5]], new[5:10], new[10:14]
    gatt, feedforward_gradient, vector_gradient = new[14:]
    return (
        out.transpose(1, 0, 2), ing.transpose(1, 0, 2),
        gatt.T, *att_new, feedforward_gradient, *ff_new, vector_gradient, *vec_new, qb,
    )


def solution(mesh):
    rows = P(("dp", "mp"), None, None)
    att = P(None, ("dp", "mp"))
    feed = P(None, "dp", "mp")
    in_specs = (rows, rows, P(("dp", "mp"), None)) + (att,) * 4 + (feed,) * 4 + (P(),) * 4
    out_specs = (rows, rows) + (att,) * 6 + (feed,) * 6 + (P(),) * 6
    return jax.shard_map(
        per_device, mesh=mesh, in_specs=in_specs, out_specs=out_specs, check_vma=False
    )
```
